32 devices in a mesh: dp: 8 (over y, x, core), tensor: 4 (over z).
Axes of the slice: x: 2, y: 2, z: 4, core: 2. Of those that a mesh axis runs over, the one named last changes fastest.
Arguments:
- residual: bfloat16 [8192, 2048], P(('dp', 'tensor')), may hold values from -6 to 6
- attn_gain: float32 [2048], replicated, may hold values from 0.5 to 1.5
- w_query: bfloat16 [2048, 2048], P('dp', 'tensor'), may hold values from -0.125 to 0.125
- w_key: bfloat16 [2048, 2048], P('dp', 'tensor'), may hold values from -0.125 to 0.125
- w_value: bfloat16 [2048, 2048], P('dp', 'tensor'), may hold values from -0.125 to 0.125
- query_gain: float32 [2048], replicated, may hold values from 0.5 to 1.5
- key_gain: float32 [2048], replicated, may hold values from 0.5 to 1.5
- w_out: bfloat16 [2048, 2048], P('tensor', 'dp'), may hold values from -2 to 2
- moe_gain: float32 [2048], replicated, may hold values from 0.5 to 1.5
- router: bfloat16 [2048, 64], replicated, may hold values from -0.15625 to 0.15625
- w_gate: bfloat16 [64, 2048, 1024], P('dp', None, 'tensor'), may hold values from -0.125 to 0.125
- w_up: bfloat16 [64, 2048, 1024], P('dp', None, 'tensor'), may hold values from -0.125 to 0.125
- w_down: bfloat16 [64, 1024, 2048], P('dp', 'tensor'), may hold values from -6 to 6
- segment_path: int32 [3, 8192], P(None, 'dp'), may hold values from 0 to 63, as said below
- token_valid: int32 [8192], P('dp'), may hold values from 0 to 1, as said below
- routes: int32 [8192, 8], P(('dp', 'tensor')), may hold values from 0 to 63, all different within a row
- route_order: int32 [8192, 8], P(('dp', 'tensor')), may hold values from 0 to 2047, as said below
- cotangent: bfloat16 [8192, 2048], P(('dp', 'tensor')), may hold values from -6 to 6
Outputs:
- block_out: bfloat16 [8192, 2048], P(('dp', 'tensor'))
- grad_input: float32 [8192, 2048], P(('dp', 'tensor'))
- grad_attn_gain: float32 [2048], replicated
- grad_w_query: float32 [2048, 2048], P('dp', 'tensor')
- grad_w_key: float32 [2048, 2048], P('dp', 'tensor')
- grad_w_value: float32 [2048, 2048], P('dp', 'tensor')
- grad_query_gain: float32 [2048], replicated
- grad_key_gain: float32 [2048], replicated
- grad_w_out: float32 [2048, 2048], P('tensor', 'dp')
- grad_moe_gain: float32 [2048], replicated
- grad_router: float32 [2048, 64], replicated
- grad_w_gate: float32 [64, 2048, 1024], P('dp', None, 'tensor')
- grad_w_up: float32 [64, 2048, 1024], P('dp', None, 'tensor')
- grad_w_down: float32 [64, 1024, 2048], P('dp', 'tensor')
The draws below stay inside these ranges and needn't reach their ends.
Inputs may be any that keep to these rules, and one draw needn't show every extreme that they name: `segment_path`: each group of 1024 consecutive tokens holds one tree in depth-first order: a trunk, then four branches, each followed by its two leaves, then padding tokens at the end. Row 0 is a token's segment id, row 1 its segment's parent's id (the trunk's own id on the trunk), row 2 the trunk's id. The 13 segment ids of a group are distinct. Padding tokens carry the path of the group's last leaf. `token_valid`: 1 on the tree's tokens, 0 on the padding tokens at the end of each group; every group has padding. `route_order`: within each aligned block of 256 tokens, the 2048 entries are a permutation of 0 to 2047.
All inputs are finite; a program needn't handle non-finite values.
Results may differ from the reference program's by a relative error of at most 0.02.
Values may be sent and summed in bfloat16 or wider, within the bound.
A program may use at most 448 MiB of HBM per device.

```python
import jax
import jax.numpy as jnp
import numpy as np
from jax import lax

D = 2048
H = 16
HD = 128
FF = 1024
EXPERTS = 64
TOP = 8
SEQ = 1024
SPAN = 64
TOK_DEV = 256
TOKENS = 8192
CAPD = 36


parent_table = np.array([0, 0, 1, 1, 0, 4, 4, 0, 7, 7, 0, 10, 10], dtype=np.int32)


def tree_layout(key):
    group_count = TOKENS // SEQ
    group_keys = jax.random.split(jax.random.fold_in(key, 7), group_count)

    def one_group(group_key):
        span_key, pad_key, label_key = jax.random.split(group_key, 3)
        branch_lengths = jax.random.randint(span_key, (12,), SPAN // 2, SPAN + 1).astype(jnp.int32)
        padding = jax.random.randint(pad_key, (1,), 1, SPAN + 1).astype(jnp.int32)
        labels = jax.random.permutation(label_key, 64)[:13].astype(jnp.int32)
        trunk_length = (SEQ - jnp.sum(branch_lengths) - padding).astype(jnp.int32)
        piece_ends = jnp.cumsum(jnp.concatenate((trunk_length, branch_lengths, padding))).astype(jnp.int32)
        places = jnp.arange(SEQ, dtype=jnp.int32)
        piece_index = jnp.sum((places[:, None] >= piece_ends[None, :]).astype(jnp.int32), axis=1).astype(jnp.int32)
        own_piece = jnp.minimum(piece_index, 12)
        parent_piece = jnp.asarray(parent_table)[own_piece]
        trunk_ids = jnp.zeros((SEQ,), jnp.int32) + labels[0]
        paths = jnp.stack((labels[own_piece], labels[parent_piece], trunk_ids))
        living = (piece_index < 13).astype(jnp.int32)
        return (paths, living)
    all_paths, all_living = jax.vmap(one_group)(group_keys)
    return (jnp.transpose(all_paths, (1, 0, 2)).reshape(3, TOKENS), all_living.reshape(TOKENS))


def draw_segment_path(key, part):
    return tree_layout(key)[0]


def draw_token_valid(key, part):
    return tree_layout(key)[1]


def draw_route_order(key, part):
    block_count = TOKENS // TOK_DEV
    block_keys = jax.random.split(jax.random.fold_in(key, 11), block_count)

    def one_block(block_key):
        return jax.random.permutation(block_key, TOK_DEV * TOP).astype(jnp.int32)
    return jax.vmap(one_block)(block_keys).reshape(TOKENS, TOP).astype(jnp.int32)


def levels(rng, shape, shards, low, top_value):
    loudness = 1.0
    for position, shards_of in shards:
        draws = jax.random.uniform(jax.random.fold_in(jax.random.fold_in(rng, 6), position), (shards_of,), jnp.float32, low / len(shards), top_value / len(shards))
        loudness = loudness * jnp.repeat(jnp.exp(draws), shape[position] // shards_of).reshape((-1,) + (1,) * (len(shape) - 1 - position))
    return loudness


def different_ones(stream_key, rows, number_of, top, lift):
    order = jax.random.permutation(jax.random.fold_in(stream_key, 1), number_of)
    pull = order
    for power in range(3):
        pull = pull * pull // number_of
    pull = pull * lift // number_of
    lots = jax.random.randint(jax.random.fold_in(stream_key, 2), (rows, number_of), 0, 4096) + pull
    sure = jax.random.permutation(jax.random.fold_in(stream_key, 3), rows)[jnp.arange(number_of) % rows]
    lots = jnp.where(jnp.arange(rows)[:, None] == sure[None, :], 1 << 14, lots)
    merit = lots * number_of + jnp.arange(number_of)
    return lax.top_k(merit.astype(jnp.int32), top)[1].astype(jnp.int32)


def noise(key, dims, scale, limit, cuts=(), held_as=jnp.bfloat16):
    drawn = jax.random.normal(key, dims, jnp.float32) * scale
    if len(cuts) > 0:
        drawn = levels(key, dims, cuts, -0.22, 0.18) * drawn
    return jnp.clip(drawn, min=-limit, max=limit).astype(held_as)


def setup_inputs(seed: int = 0) -> dict:
    streams_of = jax.random.split(jax.random.key(seed), 19)
    residual = noise(streams_of[0], (TOKENS, D), 1.0, 6.0, ((0, 32),))
    attn_gain = jnp.clip(1.0 + 0.1 * jax.random.normal(streams_of[1], (D,), jnp.float32), 0.5, 1.5)
    w_query = noise(streams_of[2], (D, H * HD), D ** -0.5, 0.125, ((0, 8), (1, 4)))
    w_key = noise(streams_of[3], (D, H * HD), D ** -0.5, 0.125, ((0, 8), (1, 4)))
    w_value = noise(streams_of[4], (D, H * HD), D ** -0.5, 0.125, ((0, 8), (1, 4)))
    query_gain = jnp.clip(1.0 + 0.1 * jax.random.normal(streams_of[5], (H * HD,), jnp.float32), 0.5, 1.5)
    key_gain = jnp.clip(1.0 + 0.1 * jax.random.normal(streams_of[6], (H * HD,), jnp.float32), 0.5, 1.5)
    w_out = noise(streams_of[7], (H * HD, D), (max(1, H * HD // 256)) ** -0.5, 2.0, ((0, 4), (1, 8)))
    moe_gain = jnp.clip(1.0 + 0.1 * jax.random.normal(streams_of[8], (D,), jnp.float32), 0.5, 1.5)
    router = noise(streams_of[9], (D, EXPERTS), (0.5 / D ** 0.5), 0.15625)
    w_gate = noise(streams_of[10], (EXPERTS, D, FF), D ** -0.5, 0.125, ((0, 8), (2, 4)))
    w_up = noise(streams_of[11], (EXPERTS, D, FF), D ** -0.5, 0.125, ((0, 8), (2, 4)))
    w_down = noise(streams_of[12], (EXPERTS, FF, D), 1 ** -0.5, 6.0, ((0, 8), (1, 4)))
    segment_path = draw_segment_path(jax.random.fold_in(streams_of[18], 71), 0)
    token_valid = draw_token_valid(jax.random.fold_in(streams_of[18], 71), 0)
    routes = different_ones(streams_of[15], TOKENS, EXPERTS, TOP, 1024)
    route_order = draw_route_order(jax.random.fold_in(streams_of[18], 71), 0)
    cotangent = noise(streams_of[17], (TOKENS, D), 1.0, 6.0, ((0, 32),))
    return dict(residual=residual, attn_gain=attn_gain, w_query=w_query, w_key=w_key, w_value=w_value, query_gain=query_gain, key_gain=key_gain, w_out=w_out, moe_gain=moe_gain, router=router, w_gate=w_gate, w_up=w_up, w_down=w_down, segment_path=segment_path, token_valid=token_valid, routes=routes, route_order=route_order, cotangent=cotangent)


norm_eps = 1e-05
rope_base = 10000.0
masked_score = -1e+30

@jax.custom_vjp
def low(v):
    return lax.optimization_barrier(v.astype(jnp.bfloat16)).astype(jnp.float32)

@jax.custom_vjp
def low_back(v):
    return v

def low_keep(v):
    return (low(v), None)

def low_pass(kept, grad):
    return (grad,)

def back_keep(v):
    return (v, None)

def back_low(kept, grad):
    return (low(grad),)
low.defvjp(low_keep, low_pass)
low_back.defvjp(back_keep, back_low)

def dot_high(left, right):
    return jnp.dot(left, right, precision=lax.Precision.HIGHEST)

def rms_scale(values, gain):
    return values * lax.rsqrt(lax.optimization_barrier(jnp.mean(values * values, axis=-1, keepdims=True)) + norm_eps) * gain

def slot_ranks(expert_ids, route_rank, live_pairs, experts, capacity):
    pairs = expert_ids.shape[0]
    by_order = jnp.zeros((pairs,), jnp.int32).at[route_rank].set(lax.iota(jnp.int32, pairs))
    sorted_ids = expert_ids[by_order]
    sorted_live = live_pairs[by_order]
    hits = ((sorted_ids[:, None] == lax.iota(jnp.int32, experts)[None, :]) & (sorted_live[:, None] == 1)).astype(jnp.int32)
    earlier = (jnp.cumsum(hits, axis=0) - hits).astype(jnp.int32)
    rank_sorted = lax.optimization_barrier(jnp.sum(earlier * hits, axis=1)).astype(jnp.int32)
    keep_sorted = ((sorted_live == 1) & (rank_sorted < capacity)).astype(jnp.int32)
    ranks = jnp.zeros((pairs,), jnp.int32).at[by_order].set(rank_sorted)
    kept = jnp.zeros((pairs,), jnp.int32).at[by_order].set(keep_sorted)
    return (ranks, kept)

def slot_tables(routes, route_order, token_valid):
    blocks = TOKENS // TOK_DEV
    pairs = TOK_DEV * TOP
    expert_ids = routes.reshape(blocks, pairs)
    live_pairs = jnp.repeat(token_valid, TOP).reshape(blocks, pairs)

    def one_block(ids, order, live):
        return slot_ranks(ids, order, live, EXPERTS, CAPD)
    ranks, kept = jax.vmap(one_block)(expert_ids, route_order.reshape(blocks, pairs), live_pairs)
    block_index = lax.iota(jnp.int32, blocks)[:, None]
    pair_index = lax.iota(jnp.int32, pairs)[None, :]
    slots_all = EXPERTS * blocks * CAPD
    target = jnp.where(kept == 1, expert_ids * (blocks * CAPD) + block_index * CAPD + ranks, slots_all).reshape(-1)
    token_index = (block_index * TOK_DEV + pair_index // TOP).reshape(-1)
    pair_global = (block_index * pairs + pair_index).reshape(-1)
    slot_token = jnp.full((slots_all + 1,), TOKENS, jnp.int32).at[target].set(token_index)[:slots_all]
    slot_pair = jnp.full((slots_all + 1,), TOKENS * TOP, jnp.int32).at[target].set(pair_global)[:slots_all]
    return (slot_token.reshape(EXPERTS, blocks * CAPD), slot_pair.reshape(EXPERTS, blocks * CAPD))

def tree_visible(row_paths, key_paths, key_valid, row_first):
    row_count = row_paths.shape[1]
    key_count = key_paths.shape[1]
    key_segment = key_paths[0][None, :]
    on_path = (key_segment == row_paths[0][:, None]) | (key_segment == row_paths[1][:, None]) | (key_segment == row_paths[2][:, None])
    row_place = row_first + lax.iota(jnp.int32, row_count)
    key_place = lax.iota(jnp.int32, key_count)
    earlier = key_place[None, :] <= row_place[:, None]
    return on_path & earlier & (key_valid[None, :] == 1) | (key_place[None, :] == row_place[:, None])

def rotation(positions):
    half = HD // 2
    freqs = jnp.exp(-jnp.log(rope_base) * 2.0 * lax.iota(jnp.float32, half) / HD)
    angles = positions.astype(jnp.float32)[:, None] * freqs[None, :]
    return (jnp.cos(angles), jnp.sin(angles))

def rotate(values, cosine, sine):
    half = values.shape[-1] // 2
    first = values[..., :half]
    second = values[..., half:]
    cosine = cosine[:, None, :]
    sine = sine[:, None, :]
    return jnp.concatenate((first * cosine - second * sine, second * cosine + first * sine), axis=-1)

def reference(residual, attn_gain, w_query, w_key, w_value, query_gain, key_gain, w_out, moe_gain, router, w_gate, w_up, w_down, segment_path, token_valid, routes, route_order, cotangent):
    group_count = TOKENS // SEQ
    slot_token, slot_pair = slot_tables(routes, route_order, token_valid)
    group_paths = jnp.transpose(segment_path.reshape(3, group_count, SEQ), (1, 0, 2))
    group_valid = token_valid.reshape(group_count, SEQ)

    def forward(residual, attn_gain, w_query, w_key, w_value, query_gain, key_gain, w_out, moe_gain, router, w_gate, w_up, w_down):
        hidden = low(rms_scale(residual, attn_gain))
        q_raw = low_back(dot_high(hidden, w_query))
        k_raw = low_back(dot_high(hidden, w_key))
        v_raw = low_back(dot_high(hidden, w_value))

        def attend(pieces):
            q_group, k_group, v_group, paths, valid_group = pieces
            visible = tree_visible(paths, paths, valid_group, 0)
            positions = lax.optimization_barrier(jnp.sum(visible.astype(jnp.int32), axis=1)).astype(jnp.int32) - 1
            cosine, sine = rotation(positions)
            query = low(rotate(rms_scale(q_group, query_gain).reshape(SEQ, H, HD), cosine, sine))
            key = low(rotate(rms_scale(k_group, key_gain).reshape(SEQ, H, HD), cosine, sine))
            value = low(v_group).reshape(SEQ, H, HD)
            scores = low_back(jnp.einsum('qhd,khd->hqk', query, key, precision=lax.Precision.HIGHEST) * HD ** (-0.5))
            weights = low(jax.nn.softmax(jnp.where(visible[None], scores, masked_score), axis=-1))
            mixed = jnp.einsum('hqk,khd->qhd', weights, value, precision=lax.Precision.HIGHEST)
            return low(low_back(mixed)).reshape(SEQ, H * HD)
        attn_mixed = lax.map(jax.checkpoint(attend), (q_raw.reshape(group_count, SEQ, H * HD), k_raw.reshape(group_count, SEQ, H * HD), v_raw.reshape(group_count, SEQ, H * HD), group_paths, group_valid)).reshape(TOKENS, H * HD)
        x_one = residual + low_back(dot_high(attn_mixed, w_out))
        hidden_two = low(rms_scale(x_one, moe_gain))
        probs = jax.nn.softmax(dot_high(hidden_two, router), axis=-1)
        gate_pad = jnp.concatenate((jnp.take_along_axis(probs, routes, axis=1).reshape(TOKENS * TOP), jnp.zeros((1,), jnp.float32)))
        row_pad = jnp.concatenate((hidden_two, jnp.zeros((1, D), jnp.float32)), axis=0)

        def expert(pieces):
            gate_weight, up_weight, down_weight, slot_tokens, slot_pairs = pieces
            expert_in = low_back(row_pad[slot_tokens])
            gate_pre = low_back(dot_high(expert_in, gate_weight))
            up_pre = low_back(dot_high(expert_in, up_weight))
            act = low(jax.nn.silu(gate_pre) * up_pre)
            expert_out = low_back(low(dot_high(act, down_weight)))
            return expert_out * gate_pad[slot_pairs][:, None]
        weighted = lax.map(jax.checkpoint(expert), (w_gate, w_up, w_down, slot_token, slot_pair))
        moe_out = jnp.zeros((TOKENS + 1, D), jnp.float32).at[slot_token.reshape(-1)].add(weighted.reshape(-1, D))[:TOKENS]
        return x_one + moe_out
    block_out, pullback = jax.vjp(forward, residual.astype(jnp.float32), attn_gain, w_query.astype(jnp.float32), w_key.astype(jnp.float32), w_value.astype(jnp.float32), query_gain, key_gain, w_out.astype(jnp.float32), moe_gain, router.astype(jnp.float32), w_gate.astype(jnp.float32), w_up.astype(jnp.float32), w_down.astype(jnp.float32))
    grads = pullback(cotangent.astype(jnp.float32))
    return (block_out.astype(jnp.bfloat16), grads[0], grads[1], grads[2], grads[3], grads[4], grads[5], grads[6], grads[7], grads[8], grads[9], grads[10], grads[11], grads[12])
```

```python
import functools

import jax
import jax.numpy as jnp
from jax import lax
from jax.experimental import pallas as pl
from jax.experimental.pallas import tpu as pltpu
from jax.sharding import PartitionSpec as P

H = 16
HD = 128


norm_eps = 1e-05
rope_base = 10000.0
masked_score = -1e30


def padded(count, step):
    return -(-count // step) * step


def slot_table(routes, route_order, valid, experts, capacity):
    far = jnp.int32(1 << 30)
    expert = lax.iota(jnp.int32, experts)[:, None, None]
    hits = (routes[None] == expert) & (valid[None, :, None] == 1)
    order = jnp.min(jnp.where(hits, route_order[None], far), axis=-1)
    ranks = jnp.sum((order[:, None, :] < order[:, :, None]).astype(jnp.int32), axis=-1)
    return jnp.where((order < far) & (ranks < capacity), ranks, -1)


def slot_hits(slots, expert, rows):
    tokens = slots.shape[-1]
    return lax.broadcasted_iota(jnp.int32, (rows, tokens), 0) == slots[expert : expert + 1, :]


def dispatch_kernel(slots_ref, gates_ref, rows_ref, cots_ref, x_ref, c_ref, gate_ref):
    pair, experts, tokens = slots_ref.shape
    rows = x_ref.shape[1] // pair
    width = rows_ref.shape[1]
    picks = []
    for b in range(pair):
        slots = slots_ref[b]
        pieces = []
        for e in range(experts):
            hit = slot_hits(slots, e, rows)
            pieces.append(hit.astype(jnp.float32))
            gate = jnp.sum(jnp.where(hit, gates_ref[b, e : e + 1, :], 0.0), axis=1, keepdims=True)
            gate_ref[e, b * rows : (b + 1) * rows, :] = jnp.broadcast_to(gate, (rows, 128))
        picks.append(jnp.concatenate(pieces, axis=0).astype(jnp.bfloat16))
    step = min(512, width)
    for source, target in ((rows_ref, x_ref), (cots_ref, c_ref)):
        for first in range(0, width, step):
            parts = [
                jnp.dot(
                    picks[b],
                    source[b * tokens : (b + 1) * tokens, first : first + step],
                    preferred_element_type=jnp.float32,
                )
                for b in range(pair)
            ]
            for e in range(experts):
                target[e, :, first : first + step] = jnp.concatenate(
                    [part[e * rows : (e + 1) * rows] for part in parts], axis=0
                ).astype(jnp.bfloat16)


def dispatch(slots, gates, rows_all, cots_all, rows):
    blocks, experts, tokens = slots.shape
    width = rows_all.shape[1]
    pair = 2
    out = jax.ShapeDtypeStruct((experts, blocks * rows, width), jnp.bfloat16)
    table = pl.BlockSpec((pair, experts, tokens), lambda i: (i, 0, 0))
    source = pl.BlockSpec((pair * tokens, width), lambda i: (i, 0))
    target = pl.BlockSpec((experts, pair * rows, width), lambda i: (0, i, 0))
    return pl.pallas_call(
        dispatch_kernel,
        grid=(blocks // pair,),
        out_shape=(out, out, jax.ShapeDtypeStruct((experts, blocks * rows, 128), jnp.float32)),
        in_specs=[table, table, source, source],
        out_specs=[target, target, pl.BlockSpec((experts, pair * rows, 128), lambda i: (0, i, 0))],
        compiler_params=pltpu.CompilerParams(vmem_limit_bytes=50 << 20),
        cost_estimate=pl.CostEstimate(
            flops=4 * blocks * experts * rows * tokens * width,
            bytes_accessed=4 * blocks * (tokens + experts * rows) * width,
            transcendentals=0,
        ),
        name="dispatch",
    )(slots, gates, rows_all, cots_all)


def turned(left, right):
    return lax.dot_general(left, right, (((0,), (0,)), ((), ())), preferred_element_type=jnp.float32)


def across(left, right):
    return lax.dot_general(left, right, (((1,), (1,)), ((), ())), preferred_element_type=jnp.float32)


def expert_kernel(rows, first_ref, x_ref, c_ref, gate_ref, wg_ref, wu_ref, wd_ref,
                  o_ref, dx_ref, dwg_ref, dwu_ref, dwd_ref):
    expert = pl.program_id(0)
    tile, width = x_ref.shape[1:]
    units = wg_ref.shape[2]
    room = o_ref.shape[2]
    blocks = tile // rows
    gate = gate_ref[0, :, 0:1]
    x = x_ref[0]
    c = c_ref[0]
    gate_pre = jnp.dot(x, wg_ref[0], preferred_element_type=jnp.float32)
    up_pre = jnp.dot(x, wu_ref[0], preferred_element_type=jnp.float32)
    back = across(c, wd_ref[0])
    sig = jax.nn.sigmoid(gate_pre)
    silu = gate_pre * sig
    act = (silu * up_pre).astype(jnp.bfloat16)
    act_float = act.astype(jnp.float32)
    grad_gate = jnp.sum(act_float * back, axis=1, keepdims=True)
    grad_act = back * gate
    grad_gate_pre = (grad_act * up_pre * sig * (1.0 + gate_pre * (1.0 - sig))).astype(jnp.bfloat16)
    grad_up_pre = (grad_act * silu).astype(jnp.bfloat16)
    gated = (act_float * gate).astype(jnp.bfloat16)

    def spread(values):
        values = values.reshape(blocks, rows, values.shape[1])
        if room > rows:
            empty = jnp.zeros((blocks, room - rows, values.shape[2]), jnp.float32)
            values = jnp.concatenate((values, empty), axis=1)
        return values.astype(jnp.bfloat16)

    step = min(512, width)
    for first in range(0, width, step):
        part = slice(first, first + step)
        out = jnp.dot(act, wd_ref[0, :, part], preferred_element_type=jnp.float32) * gate
        o_ref[:, 0, :, part] = spread(out)
        grad = across(grad_gate_pre, wg_ref[0, part, :]) + across(grad_up_pre, wu_ref[0, part, :])
        dx_ref[:, 0, :, part] = spread(grad)
    lanes = lax.broadcasted_iota(jnp.int32, (tile, 128), 1)
    dx_ref[:, 0, :, width:] = spread(jnp.where(lanes == first_ref[0] + expert, grad_gate, 0.0))

    @pl.when(pl.program_id(1) == 0)
    def _():
        for ref in (dwg_ref, dwu_ref, dwd_ref):
            ref[...] = jnp.zeros_like(ref)

    for first in range(0, width, step):
        part = slice(first, first + step)
        dwg_ref[0, part, :] += turned(x_ref[0, :, part], grad_gate_pre)
        dwu_ref[0, part, :] += turned(x_ref[0, :, part], grad_up_pre)
        dwd_ref[0, :, part] += turned(gated, c_ref[0, :, part])


def expert_pass(first_expert, x_slots, c_slots, gate_slots, w_gate, w_up, w_down, blocks, room):
    experts, total, width = x_slots.shape
    units = w_gate.shape[2]
    rows = total // blocks
    group = next(n for n in (16, 8, 4, 2, 1) if blocks % n == 0 and (n * rows <= 768 or n == 1))
    tile = group * rows
    extra = 128
    tall = pl.BlockSpec((1, width, units), lambda e, r, _: (e, 0, 0))
    wide = pl.BlockSpec((1, units, width), lambda e, r, _: (e, 0, 0))
    slot = pl.BlockSpec((1, tile, width), lambda e, r, _: (e, r, 0))
    kernel = functools.partial(expert_kernel, rows)
    return pl.pallas_call(
        kernel,
        grid_spec=pltpu.PrefetchScalarGridSpec(
            num_scalar_prefetch=1,
            grid=(experts, total // tile),
            in_specs=[slot, slot, pl.BlockSpec((1, tile, 128), lambda e, r, _: (e, r, 0)), tall, tall, wide],
            out_specs=[
                pl.BlockSpec((group, 1, room, width), lambda e, r, _: (r, e, 0, 0)),
                pl.BlockSpec((group, 1, room, width + extra), lambda e, r, _: (r, e, 0, 0)),
                tall, tall, wide,
            ],
        ),
        out_shape=(
            jax.ShapeDtypeStruct((blocks, experts, room, width), jnp.bfloat16),
            jax.ShapeDtypeStruct((blocks, experts, room, width + extra), jnp.bfloat16),
            jax.ShapeDtypeStruct(w_gate.shape, jnp.float32),
            jax.ShapeDtypeStruct(w_up.shape, jnp.float32),
            jax.ShapeDtypeStruct(w_down.shape, jnp.float32),
        ),
        compiler_params=pltpu.CompilerParams(vmem_limit_bytes=60 << 20),
        cost_estimate=pl.CostEstimate(
            flops=18 * experts * total * width * units,
            bytes_accessed=8 * experts * total * width + 18 * experts * width * units,
            transcendentals=experts * total * units,
        ),
        name="experts",
    )(first_expert, x_slots, c_slots, gate_slots, w_gate, w_up, w_down)


def combine_kernel(slots_ref, o_ref, dx_ref, out_ref, grad_ref):
    _, experts, tokens = slots_ref.shape
    room, width = o_ref.shape[2:]
    slots = slots_ref[0]
    picks = jnp.concatenate(
        [slot_hits(slots, e, room).astype(jnp.float32) for e in range(experts)], axis=0
    ).astype(jnp.bfloat16)
    for source, target in ((o_ref, out_ref), (dx_ref, grad_ref)):
        columns = target.shape[1]
        for first in range(0, columns, 512):
            part = slice(first, min(first + 512, columns))
            values = source[0, :, :, part].reshape(experts * room, part.stop - first)
            target[:, part] = turned(picks, values).astype(jnp.bfloat16)


def combine(slots, outs, grads):
    blocks, experts, tokens = slots.shape
    room, width = outs.shape[2:]
    wider = grads.shape[3]
    return pl.pallas_call(
        combine_kernel,
        grid=(blocks,),
        out_shape=(
            jax.ShapeDtypeStruct((blocks * tokens, width), jnp.bfloat16),
            jax.ShapeDtypeStruct((blocks * tokens, wider), jnp.bfloat16),
        ),
        in_specs=[
            pl.BlockSpec((1, experts, tokens), lambda i: (i, 0, 0)),
            pl.BlockSpec((1, experts, room, width), lambda i: (i, 0, 0, 0)),
            pl.BlockSpec((1, experts, room, wider), lambda i: (i, 0, 0, 0)),
        ],
        out_specs=[
            pl.BlockSpec((tokens, width), lambda i: (i, 0)),
            pl.BlockSpec((tokens, wider), lambda i: (i, 0)),
        ],
        compiler_params=pltpu.CompilerParams(vmem_limit_bytes=50 << 20),
        cost_estimate=pl.CostEstimate(
            flops=2 * blocks * experts * room * tokens * (width + wider),
            bytes_accessed=2 * blocks * (tokens + experts * room) * (width + wider),
            transcendentals=0,
        ),
        name="combine",
    )(slots, outs, grads)


def visible_block(row_paths, key_paths, key_valid, row_first):
    row_count = row_paths.shape[1]
    key_count = key_paths.shape[1]
    key_segment = key_paths[0][None, :]
    on_path = (
        (key_segment == row_paths[0][:, None])
        | (key_segment == row_paths[1][:, None])
        | (key_segment == row_paths[2][:, None])
    )
    row_place = row_first + lax.iota(jnp.int32, row_count)
    key_place = lax.iota(jnp.int32, key_count)
    earlier = key_place[None, :] <= row_place[:, None]
    return on_path & earlier & (key_valid[None, :] == 1) | (
        key_place[None, :] == row_place[:, None]
    )


def rotation(positions, head_dim):
    half = head_dim // 2
    freqs = jnp.exp(-jnp.log(rope_base) * 2.0 * lax.iota(jnp.float32, half) / head_dim)
    angles = positions.astype(jnp.float32)[:, None] * freqs[None, :]
    return (jnp.cos(angles), jnp.sin(angles))


def rotate(values, cosine, sine):
    half = values.shape[-1] // 2
    first = values[..., :half]
    second = values[..., half:]
    cosine = cosine[:, None, :]
    sine = sine[:, None, :]
    return jnp.concatenate(
        (first * cosine - second * sine, second * cosine + first * sine), axis=-1
    )


def unrotate(grads, cosine, sine):
    half = grads.shape[-1] // 2
    first = grads[..., :half]
    second = grads[..., half:]
    cosine = cosine[:, None, :]
    sine = sine[:, None, :]
    return jnp.concatenate(
        (first * cosine + second * sine, second * cosine - first * sine), axis=-1
    )


def rms_apply(values, gain):
    scale = lax.rsqrt(jnp.mean(values * values, axis=-1, keepdims=True) + norm_eps)
    return (values * scale * gain, scale)


def rms_grad(values, scale, gain, grads, inner, width):
    grad_values = scale * gain * grads - values * scale**3 * inner / width
    grad_gain = jnp.sum(grads * values * scale, axis=0)
    return (grad_values, grad_gain)


def tensor_sums(pair):
    return lax.psum((pair[0], pair[1]), "tensor")


def heads_to_rows(term, rows):
    return lax.psum_scatter(
        term(jnp.int32(0), rows * lax.axis_size("tensor")),
        "tensor",
        scatter_dimension=0,
        tiled=True,
    )


def sum_to_blocks(rows, tokens):
    dp = lax.axis_size("dp")
    pieces = rows.reshape(dp, rows.shape[0] // dp, rows.shape[1])
    part = lax.psum_scatter(pieces, "dp", scatter_dimension=0, tiled=False)
    return lax.psum_scatter(part, "tensor", scatter_dimension=0, tiled=True)


def body(
    residual,
    attn_gain,
    w_query,
    w_key,
    w_value,
    query_gain,
    key_gain,
    w_out,
    moe_gain,
    router,
    w_gate,
    w_up,
    w_down,
    segment_path,
    token_valid,
    routes,
    route_order,
    cotangent,
):
    tensor_rank = lax.axis_index("tensor")
    tok_dev, width = residual.shape
    seq_len = segment_path.shape[1]
    top_count = routes.shape[1]
    experts = router.shape[1]
    local_experts = w_gate.shape[0]
    dp_groups = experts // local_experts
    capacity = 9 * tok_dev * top_count // (8 * experts)
    full_width = H * HD
    block_rows = min(512, seq_len)
    block_count = seq_len // block_rows
    score_scale = HD ** (-0.5)
    gathered_query, gathered_key, gathered_value, gathered_out = (
        lax.all_gather(w_query, "dp", axis=0, tiled=True),
        lax.all_gather(w_key, "dp", axis=0, tiled=True),
        lax.all_gather(w_value, "dp", axis=0, tiled=True),
        lax.all_gather(w_out, "dp", axis=1, tiled=True),
    )
    head_cols = gathered_query.shape[1]
    local_heads = head_cols // HD
    joined_weight = jnp.concatenate((gathered_query, gathered_key, gathered_value), axis=1)
    residual_float = residual.astype(jnp.float32)
    normed_one, scale_one = rms_apply(residual_float, attn_gain)
    hidden = normed_one.astype(jnp.bfloat16)
    hidden_all = lax.all_gather(hidden, "tensor", axis=0, tiled=True)
    projected = jnp.dot(hidden_all, joined_weight, preferred_element_type=jnp.float32)
    q_raw = projected[:, :head_cols]
    k_raw = projected[:, head_cols : 2 * head_cols]
    value_low = projected[:, 2 * head_cols :].astype(jnp.bfloat16).reshape(seq_len, local_heads, HD)
    query_sq, key_sq = tensor_sums((jnp.sum(q_raw * q_raw, axis=1), jnp.sum(k_raw * k_raw, axis=1)))
    query_scale = lax.rsqrt(query_sq / full_width + norm_eps)[:, None]
    key_scale = lax.rsqrt(key_sq / full_width + norm_eps)[:, None]
    query_gain_dev = lax.dynamic_slice_in_dim(query_gain, tensor_rank * head_cols, head_cols)
    key_gain_dev = lax.dynamic_slice_in_dim(key_gain, tensor_rank * head_cols, head_cols)
    block_starts = lax.iota(jnp.int32, block_count) * block_rows

    def block_mask(row_first):
        row_paths = lax.dynamic_slice_in_dim(segment_path, row_first, block_rows, 1)
        return visible_block(row_paths, segment_path, token_valid, row_first)

    def count_seen(row_first):
        return jnp.sum(block_mask(row_first).astype(jnp.int32), axis=1)

    positions = lax.map(count_seen, block_starts).reshape(seq_len) - 1
    cosine, sine = rotation(positions, HD)
    query_low = rotate(
        (q_raw * query_scale * query_gain_dev).reshape(seq_len, local_heads, HD), cosine, sine
    ).astype(jnp.bfloat16)
    key_low = rotate(
        (k_raw * key_scale * key_gain_dev).reshape(seq_len, local_heads, HD), cosine, sine
    ).astype(jnp.bfloat16)

    def attend(row_first):
        visible = block_mask(row_first)
        query_block = lax.dynamic_slice_in_dim(query_low, row_first, block_rows, 0)
        scores = (
            jnp.einsum("qhd,khd->hqk", query_block, key_low, preferred_element_type=jnp.float32)
            * score_scale
        )
        scores = jnp.where(visible[None], scores, masked_score)
        top_score = jnp.max(scores, axis=-1, keepdims=True)
        exp_scores = jnp.exp(scores - top_score)
        total = jnp.sum(exp_scores, axis=-1, keepdims=True)
        weights_low = (exp_scores / total).astype(jnp.bfloat16)
        mixed_block = jnp.einsum(
            "hqk,khd->qhd", weights_low, value_low, preferred_element_type=jnp.float32
        )
        return (mixed_block.astype(jnp.bfloat16), (top_score + jnp.log(total))[..., 0])

    mixed_blocks, log_totals = lax.map(attend, block_starts)
    attn_mixed = mixed_blocks.reshape(seq_len, head_cols)

    def attn_term(first_row, row_count):
        return jnp.dot(attn_mixed, gathered_out, preferred_element_type=jnp.float32)

    x_one = residual_float + heads_to_rows(attn_term, tok_dev)
    normed_two, scale_two = rms_apply(x_one, moe_gain)
    hidden_two = normed_two.astype(jnp.bfloat16)
    logits = jnp.dot(hidden_two, router, preferred_element_type=jnp.float32)
    probs = jax.nn.softmax(logits, axis=-1)
    everyone = ("dp", "tensor")
    cots_all = lax.all_gather(cotangent, everyone, axis=0, tiled=True)
    valid_dev = lax.dynamic_slice_in_dim(token_valid, tensor_rank * tok_dev, tok_dev)
    slots_own = slot_table(routes, route_order, valid_dev, experts, capacity)
    slots_all = lax.all_gather(slots_own.astype(jnp.bfloat16), everyone, axis=0)
    first_expert = lax.axis_index("dp") * local_experts
    slots = lax.dynamic_slice_in_dim(slots_all, first_expert, local_experts, 1).astype(jnp.int32)
    gates_all = lax.all_gather(probs.T, everyone, axis=0)
    gates = lax.dynamic_slice_in_dim(gates_all, first_expert, local_experts, 1)
    rows_all = lax.all_gather(hidden_two, everyone, axis=0, tiled=True)
    blocks = slots.shape[0]
    slot_rows = padded(capacity, 8)
    x_slots, c_slots, gate_slots = dispatch(slots, gates, rows_all, cots_all, slot_rows)
    outs, grads, grad_w_gate, grad_w_up, grad_w_down = expert_pass(
        first_expert.reshape(1),
        x_slots,
        c_slots,
        gate_slots,
        w_gate,
        w_up,
        w_down,
        blocks,
        padded(slot_rows, 16),
    )
    out_part, grad_part = combine(slots, outs, grads)
    grad_rows = sum_to_blocks(grad_part, tok_dev).astype(jnp.float32)
    moe_out = sum_to_blocks(out_part, tok_dev).astype(jnp.float32)
    block_out = (x_one + moe_out).astype(jnp.bfloat16)
    grad_out = cotangent.astype(jnp.float32)
    grad_hidden_two = grad_rows[:, :width]
    grad_probs = grad_rows[:, width : width + experts]
    grad_logits = probs * (grad_probs - jnp.sum(probs * grad_probs, axis=-1, keepdims=True))
    router_float = router.astype(jnp.float32)
    grad_hidden_two = grad_hidden_two + lax.dot_general(
        grad_logits, router_float, (((1,), (1,)), ((), ())), precision=lax.Precision.HIGHEST
    )
    grad_router_part = lax.dot_general(
        hidden_two.astype(jnp.float32),
        grad_logits,
        (((0,), (0,)), ((), ())),
        precision=lax.Precision.HIGHEST,
    )
    inner_two = jnp.sum(grad_hidden_two * moe_gain * x_one, axis=-1, keepdims=True)
    grad_norm_two, grad_moe_gain_part = rms_grad(
        x_one, scale_two, moe_gain, grad_hidden_two, inner_two, width
    )
    grad_x_one = grad_out + grad_norm_two
    grad_attn_all = lax.all_gather(grad_x_one.astype(jnp.bfloat16), "tensor", axis=0, tiled=True)
    grad_out_weight = lax.dot_general(
        attn_mixed, grad_attn_all, (((0,), (0,)), ((), ())), preferred_element_type=jnp.float32
    )
    grad_mixed = (
        lax.dot_general(
            grad_attn_all,
            gathered_out,
            (((1,), (1,)), ((), ())),
            preferred_element_type=jnp.float32,
        )
        .astype(jnp.bfloat16)
        .reshape(seq_len, local_heads, HD)
    )

    def attend_back(carry, pieces):
        grad_key_sum, grad_value_sum = carry
        row_first, log_total = pieces
        visible = block_mask(row_first)
        query_block = lax.dynamic_slice_in_dim(query_low, row_first, block_rows, 0)
        grad_block = lax.dynamic_slice_in_dim(grad_mixed, row_first, block_rows, 0)
        scores = (
            jnp.einsum("qhd,khd->hqk", query_block, key_low, preferred_element_type=jnp.float32)
            * score_scale
        )
        scores = jnp.where(visible[None], scores, masked_score)
        weights = jnp.exp(scores - log_total[..., None])
        grad_weights = jnp.einsum(
            "qhd,khd->hqk", grad_block, value_low, preferred_element_type=jnp.float32
        )
        inner = jnp.sum(weights * grad_weights, axis=-1, keepdims=True)
        grad_scores = (weights * (grad_weights - inner)).astype(jnp.bfloat16)
        grad_query_block = (
            jnp.einsum("hqk,khd->qhd", grad_scores, key_low, preferred_element_type=jnp.float32)
            * score_scale
        )
        grad_key_sum = (
            grad_key_sum
            + jnp.einsum(
                "hqk,qhd->khd", grad_scores, query_block, preferred_element_type=jnp.float32
            )
            * score_scale
        )
        grad_value_sum = grad_value_sum + jnp.einsum(
            "hqk,qhd->khd",
            weights.astype(jnp.bfloat16),
            grad_block,
            preferred_element_type=jnp.float32,
        )
        return ((grad_key_sum, grad_value_sum), grad_query_block)

    zero_heads = jnp.zeros((seq_len, local_heads, HD), jnp.float32)
    (grad_key_all, grad_value_all), grad_query_blocks = lax.scan(
        attend_back, (zero_heads, zero_heads), (block_starts, log_totals)
    )
    grad_q_norm = unrotate(
        grad_query_blocks.reshape(seq_len, local_heads, HD), cosine, sine
    ).reshape(seq_len, head_cols)
    grad_k_norm = unrotate(grad_key_all, cosine, sine).reshape(seq_len, head_cols)
    query_inner, key_inner = tensor_sums(
        (
            jnp.sum(grad_q_norm * query_gain_dev * q_raw, axis=1),
            jnp.sum(grad_k_norm * key_gain_dev * k_raw, axis=1),
        )
    )
    grad_q_raw, grad_query_gain_dev = rms_grad(
        q_raw, query_scale, query_gain_dev, grad_q_norm, query_inner[:, None], full_width
    )
    grad_k_raw, grad_key_gain_dev = rms_grad(
        k_raw, key_scale, key_gain_dev, grad_k_norm, key_inner[:, None], full_width
    )
    grad_joined = jnp.concatenate(
        (grad_q_raw, grad_k_raw, grad_value_all.reshape(seq_len, head_cols)), axis=1
    ).astype(jnp.bfloat16)
    grad_joined_weight = lax.dot_general(
        hidden_all, grad_joined, (((0,), (0,)), ((), ())), preferred_element_type=jnp.float32
    )

    def back_term(first_row, row_count):
        return lax.dot_general(
            grad_joined, joined_weight, (((1,), (1,)), ((), ())), preferred_element_type=jnp.float32
        )

    grad_hidden = heads_to_rows(back_term, tok_dev)
    inner_one = jnp.sum(grad_hidden * attn_gain * residual_float, axis=-1, keepdims=True)
    grad_norm_one, grad_attn_gain_part = rms_grad(
        residual_float, scale_one, attn_gain, grad_hidden, inner_one, width
    )
    grad_input = grad_x_one + grad_norm_one
    grad_w_query, grad_w_key, grad_w_value, grad_w_out = (
        lax.psum_scatter(
            grad_joined_weight[:, :head_cols].astype(jnp.bfloat16),
            "dp",
            scatter_dimension=0,
            tiled=True,
        ).astype(jnp.float32),
        lax.psum_scatter(
            grad_joined_weight[:, head_cols : 2 * head_cols].astype(jnp.bfloat16),
            "dp",
            scatter_dimension=0,
            tiled=True,
        ).astype(jnp.float32),
        lax.psum_scatter(
            grad_joined_weight[:, 2 * head_cols :].astype(jnp.bfloat16),
            "dp",
            scatter_dimension=0,
            tiled=True,
        ).astype(jnp.float32),
        lax.psum_scatter(
            grad_out_weight.astype(jnp.bfloat16), "dp", scatter_dimension=1, tiled=True
        ).astype(jnp.float32),
    )
    zero_width = jnp.zeros((full_width,), jnp.float32)
    grad_query_full = lax.dynamic_update_slice_in_dim(
        zero_width, grad_query_gain_dev, tensor_rank * head_cols, 0
    )
    grad_key_full = lax.dynamic_update_slice_in_dim(
        zero_width, grad_key_gain_dev, tensor_rank * head_cols, 0
    )
    summed = lax.psum(
        (grad_attn_gain_part, grad_moe_gain_part, grad_query_full, grad_key_full, grad_router_part),
        ("dp", "tensor"),
    )
    return (
        block_out,
        grad_input,
        summed[0],
        grad_w_query,
        grad_w_key,
        grad_w_value,
        summed[2],
        summed[3],
        grad_w_out,
        summed[1],
        summed[4],
        grad_w_gate,
        grad_w_up,
        grad_w_down,
    )


def solution(mesh):
    in_specs = (
        P(("dp", "tensor"), None),
        P(),
        P("dp", "tensor"),
        P("dp", "tensor"),
        P("dp", "tensor"),
        P(),
        P(),
        P("tensor", "dp"),
        P(),
        P(),
        P("dp", None, "tensor"),
        P("dp", None, "tensor"),
        P("dp", "tensor", None),
        P(None, "dp"),
        P("dp"),
        P(("dp", "tensor"), None),
        P(("dp", "tensor"), None),
        P(("dp", "tensor"), None),
    )
    out_specs = (
        P(("dp", "tensor"), None),
        P(("dp", "tensor"), None),
        P(),
        P("dp", "tensor"),
        P("dp", "tensor"),
        P("dp", "tensor"),
        P(),
        P(),
        P("tensor", "dp"),
        P(),
        P(),
        P("dp", None, "tensor"),
        P("dp", None, "tensor"),
        P("dp", "tensor", None),
    )
    return jax.shard_map(body, mesh=mesh, in_specs=in_specs, out_specs=out_specs, check_vma=False)
```

```python
import functools

import jax
import jax.numpy as jnp
from jax import lax
from jax.experimental import pallas as pl
from jax.experimental.pallas import tpu as pltpu
from jax.sharding import PartitionSpec as P

H = 16
HD = 128


norm_eps = 1e-05
rope_base = 10000.0
masked_score = -1e30


def padded(count, step):
    return -(-count // step) * step


def slot_table(routes, route_order, valid, experts, capacity):
    far = jnp.int32(1 << 30)
    expert = lax.iota(jnp.int32, experts)[:, None, None]
    hits = (routes[None] == expert) & (valid[None, :, None] == 1)
    order = jnp.min(jnp.where(hits, route_order[None], far), axis=-1)
    ranks = jnp.sum((order[:, None, :] < order[:, :, None]).astype(jnp.int32), axis=-1)
    return jnp.where((order < far) & (ranks < capacity), ranks, -1)


def slot_hits(slots, expert, rows):
    tokens = slots.shape[-1]
    return lax.broadcasted_iota(jnp.int32, (rows, tokens), 0) == slots[expert : expert + 1, :]


def dispatch_kernel(slots_ref, gates_ref, rows_ref, x_ref, gate_ref):
    pair, experts, tokens = slots_ref.shape
    rows = x_ref.shape[1] // pair
    width = rows_ref.shape[1]
    picks = []
    for b in range(pair):
        slots = slots_ref[b]
        pieces = []
        for e in range(experts):
            hit = slot_hits(slots, e, rows)
            pieces.append(hit.astype(jnp.float32))
            if gate_ref is not None:
                gate = jnp.sum(jnp.where(hit, gates_ref[b, e : e + 1, :], 0.0), axis=1, keepdims=True)
                gate_ref[e, b * rows : (b + 1) * rows, :] = jnp.broadcast_to(gate, (rows, 128))
        picks.append(jnp.concatenate(pieces, axis=0).astype(jnp.bfloat16))
    step = min(512, width)
    for first in range(0, width, step):
        parts = [
            jnp.dot(
                picks[b],
                rows_ref[b * tokens : (b + 1) * tokens, first : first + step],
                preferred_element_type=jnp.float32,
            )
            for b in range(pair)
        ]
        for e in range(experts):
            x_ref[e, :, first : first + step] = jnp.concatenate(
                [part[e * rows : (e + 1) * rows] for part in parts], axis=0
            ).astype(jnp.bfloat16)


def plain_dispatch_kernel(slots_ref, rows_ref, x_ref):
    dispatch_kernel(slots_ref, None, rows_ref, x_ref, None)


def dispatch(slots, gates, rows_all, rows):
    blocks, experts, tokens = slots.shape
    width = rows_all.shape[1]
    pair = 2
    out = jax.ShapeDtypeStruct((experts, blocks * rows, width), jnp.bfloat16)
    table = pl.BlockSpec((pair, experts, tokens), lambda i: (i, 0, 0))
    source = pl.BlockSpec((pair * tokens, width), lambda i: (i, 0))
    target = pl.BlockSpec((experts, pair * rows, width), lambda i: (0, i, 0))
    settings = dict(
        grid=(blocks // pair,),
        compiler_params=pltpu.CompilerParams(vmem_limit_bytes=50 << 20),
        cost_estimate=pl.CostEstimate(
            flops=2 * blocks * experts * rows * tokens * width,
            bytes_accessed=2 * blocks * (tokens + experts * rows) * width,
            transcendentals=0,
        ),
    )
    if gates is None:
        return pl.pallas_call(
            plain_dispatch_kernel, out_shape=out, in_specs=[table, source], out_specs=target, name="pick", **settings
        )(slots, rows_all)
    return pl.pallas_call(
        dispatch_kernel,
        out_shape=(out, jax.ShapeDtypeStruct((experts, blocks * rows, 128), jnp.float32)),
        in_specs=[table, table, source],
        out_specs=[target, pl.BlockSpec((experts, pair * rows, 128), lambda i: (0, i, 0))],
        name="dispatch",
        **settings,
    )(slots, gates, rows_all)


def turned(left, right):
    return lax.dot_general(left, right, (((0,), (0,)), ((), ())), preferred_element_type=jnp.float32)


def across(left, right):
    return lax.dot_general(left, right, (((1,), (1,)), ((), ())), preferred_element_type=jnp.float32)


def expert_kernel(rows, first_ref, x_ref, c_ref, gate_ref, wg_ref, wu_ref, wd_ref,
                  o_ref, dx_ref, dwg_ref, dwu_ref, dwd_ref):
    expert = pl.program_id(0)
    tile, width = x_ref.shape[1:]
    units = wg_ref.shape[2]
    room = o_ref.shape[2]
    blocks = tile // rows
    gate = gate_ref[0, :, 0:1]
    x = x_ref[0]
    c = c_ref[0]
    gate_pre = jnp.dot(x, wg_ref[0], preferred_element_type=jnp.float32)
    up_pre = jnp.dot(x, wu_ref[0], preferred_element_type=jnp.float32)
    back = across(c, wd_ref[0])
    sig = jax.nn.sigmoid(gate_pre)
    silu = gate_pre * sig
    act = (silu * up_pre).astype(jnp.bfloat16)
    act_float = act.astype(jnp.float32)
    grad_gate = jnp.sum(act_float * back, axis=1, keepdims=True)
    grad_act = back * gate
    grad_gate_pre = (grad_act * up_pre * sig * (1.0 + gate_pre * (1.0 - sig))).astype(jnp.bfloat16)
    grad_up_pre = (grad_act * silu).astype(jnp.bfloat16)
    gated = (act_float * gate).astype(jnp.bfloat16)

    def spread(values):
        values = values.reshape(blocks, rows, values.shape[1])
        if room > rows:
            empty = jnp.zeros((blocks, room - rows, values.shape[2]), jnp.float32)
            values = jnp.concatenate((values, empty), axis=1)
        return values.astype(jnp.bfloat16)

    step = min(512, width)
    for first in range(0, width, step):
        part = slice(first, first + step)
        out = jnp.dot(act, wd_ref[0, :, part], preferred_element_type=jnp.float32) * gate
        o_ref[:, 0, :, part] = spread(out)
        grad = across(grad_gate_pre, wg_ref[0, part, :]) + across(grad_up_pre, wu_ref[0, part, :])
        dx_ref[:, 0, :, part] = spread(grad)
    lanes = lax.broadcasted_iota(jnp.int32, (tile, 128), 1)
    dx_ref[:, 0, :, width:] = spread(jnp.where(lanes == first_ref[0] + expert, grad_gate, 0.0))

    @pl.when(pl.program_id(1) == 0)
    def _():
        for ref in (dwg_ref, dwu_ref, dwd_ref):
            ref[...] = jnp.zeros_like(ref)

    for first in range(0, width, step):
        part = slice(first, first + step)
        dwg_ref[0, part, :] += turned(x_ref[0, :, part], grad_gate_pre)
        dwu_ref[0, part, :] += turned(x_ref[0, :, part], grad_up_pre)
        dwd_ref[0, :, part] += turned(gated, c_ref[0, :, part])


def expert_pass(first_expert, x_slots, c_slots, gate_slots, w_gate, w_up, w_down, blocks, room):
    experts, total, width = x_slots.shape
    units = w_gate.shape[2]
    rows = total // blocks
    group = next(n for n in (16, 8, 4, 2, 1) if blocks % n == 0 and (n * rows <= 768 or n == 1))
    tile = group * rows
    extra = 128
    tall = pl.BlockSpec((1, width, units), lambda e, r, _: (e, 0, 0))
    wide = pl.BlockSpec((1, units, width), lambda e, r, _: (e, 0, 0))
    slot = pl.BlockSpec((1, tile, width), lambda e, r, _: (e, r, 0))
    kernel = functools.partial(expert_kernel, rows)
    return pl.pallas_call(
        kernel,
        grid_spec=pltpu.PrefetchScalarGridSpec(
            num_scalar_prefetch=1,
            grid=(experts, total // tile),
            in_specs=[slot, slot, pl.BlockSpec((1, tile, 128), lambda e, r, _: (e, r, 0)), tall, tall, wide],
            out_specs=[
                pl.BlockSpec((group, 1, room, width), lambda e, r, _: (r, e, 0, 0)),
                pl.BlockSpec((group, 1, room, width + extra), lambda e, r, _: (r, e, 0, 0)),
                tall, tall, wide,
            ],
        ),
        out_shape=(
            jax.ShapeDtypeStruct((blocks, experts, room, width), jnp.bfloat16),
            jax.ShapeDtypeStruct((blocks, experts, room, width + extra), jnp.bfloat16),
            jax.ShapeDtypeStruct(w_gate.shape, jnp.float32),
            jax.ShapeDtypeStruct(w_up.shape, jnp.float32),
            jax.ShapeDtypeStruct(w_down.shape, jnp.float32),
        ),
        compiler_params=pltpu.CompilerParams(vmem_limit_bytes=60 << 20),
        cost_estimate=pl.CostEstimate(
            flops=18 * experts * total * width * units,
            bytes_accessed=8 * experts * total * width + 18 * experts * width * units,
            transcendentals=experts * total * units,
        ),
        name="experts",
    )(first_expert, x_slots, c_slots, gate_slots, w_gate, w_up, w_down)


def combine_kernel(slots_ref, o_ref, dx_ref, out_ref, grad_ref):
    _, experts, tokens = slots_ref.shape
    room, width = o_ref.shape[2:]
    slots = slots_ref[0]
    picks = jnp.concatenate(
        [slot_hits(slots, e, room).astype(jnp.float32) for e in range(experts)], axis=0
    ).astype(jnp.bfloat16)
    for source, target in ((o_ref, out_ref), (dx_ref, grad_ref)):
        columns = target.shape[1]
        for first in range(0, columns, 512):
            part = slice(first, min(first + 512, columns))
            values = source[0, :, :, part].reshape(experts * room, part.stop - first)
            target[:, part] = turned(picks, values).astype(jnp.bfloat16)


def combine(slots, outs, grads):
    blocks, experts, tokens = slots.shape
    room, width = outs.shape[2:]
    wider = grads.shape[3]
    return pl.pallas_call(
        combine_kernel,
        grid=(blocks,),
        out_shape=(
            jax.ShapeDtypeStruct((blocks * tokens, width), jnp.bfloat16),
            jax.ShapeDtypeStruct((blocks * tokens, wider), jnp.bfloat16),
        ),
        in_specs=[
            pl.BlockSpec((1, experts, tokens), lambda i: (i, 0, 0)),
            pl.BlockSpec((1, experts, room, width), lambda i: (i, 0, 0, 0)),
            pl.BlockSpec((1, experts, room, wider), lambda i: (i, 0, 0, 0)),
        ],
        out_specs=[
            pl.BlockSpec((tokens, width), lambda i: (i, 0)),
            pl.BlockSpec((tokens, wider), lambda i: (i, 0)),
        ],
        compiler_params=pltpu.CompilerParams(vmem_limit_bytes=50 << 20),
        cost_estimate=pl.CostEstimate(
            flops=2 * blocks * experts * room * tokens * (width + wider),
            bytes_accessed=2 * blocks * (tokens + experts * room) * (width + wider),
            transcendentals=0,
        ),
        name="combine",
    )(slots, outs, grads)


MESH = pl.DeviceIdType.MESH


def place():
    dp, z = lax.axis_index("dp"), lax.axis_index("tensor")
    return dp // 4, dp // 2 % 2, dp % 2, z


def peer(y, x, core, z):
    return (y * 4 + x * 2 + core, z)


def block_of(y, x, core, z):
    return (y * 4 + x * 2 + core) * 4 + z


def greet(line):
    y, x, core, z = place()
    barrier = pltpu.get_barrier_semaphore()
    for near in ((y, x, 1 - core, z), (y, 1 - x, core, z), (1 - y, x, core, z)):
        pl.semaphore_signal(barrier, inc=1, device_id=peer(*near), device_id_type=MESH)

    @pl.when(z > 0)
    def _():
        pl.semaphore_signal(barrier, inc=1, device_id=peer(y, x, core, z - 1), device_id_type=MESH)

    @pl.when(z < line - 1)
    def _():
        pl.semaphore_signal(barrier, inc=1, device_id=peer(y, x, core, z + 1), device_id_type=MESH)

    pl.semaphore_wait(barrier, 3 + (z + line - 1) // line + (2 * line - 2 - z) // line)


def gather_kernel(line, count, *refs):
    owns, outs = refs[:count], refs[count : 2 * count]
    local_sem, send_sem, recv_sem = refs[2 * count :]
    y, x, core, z = place()
    greet(line)
    waits = []
    sent = [0]

    def send(cond, n, block, source_own, target):
        rows = owns[n].shape[0]
        part = pl.ds(block * rows, rows)
        copy = pltpu.make_async_remote_copy(
            src_ref=owns[n] if source_own else outs[n].at[part],
            dst_ref=outs[n].at[part],
            send_sem=send_sem.at[sent[0]],
            recv_sem=recv_sem.at[n, block],
            device_id=peer(*target),
            device_id_type=MESH,
        )
        sent[0] += 1
        waits.append((cond, copy))
        if cond is None:
            copy.start()
        else:
            pl.when(cond)(copy.start)

    def arrive(n, block):
        rows = owns[n].shape[0]
        part = pl.ds(block * rows, rows)
        pltpu.make_async_copy(outs[n].at[part], outs[n].at[part], recv_sem.at[n, block]).wait()

    def both(a, b):
        return b if a is None else a & b

    sibling, near_x, near_y = (y, x, 1 - core, z), (y, 1 - x, core, z), (1 - y, x, core, z)
    mine = block_of(y, x, core, z)
    locals_ = []
    for n in range(count):
        rows = owns[n].shape[0]
        own_copy = pltpu.make_async_copy(owns[n], outs[n].at[pl.ds(mine * rows, rows)], local_sem.at[n])
        own_copy.start()
        locals_.append(own_copy)

    def own_column(n, step, sign):
        zz = z + sign * step
        valid = None if step == 0 else (zz >= 0) & (zz < line)
        block = block_of(y, x, core, zz)

        def fetch():
            if step:
                arrive(n, block)

        if step:
            pl.when(valid)(fetch)
        if step == 0:
            send(z > 0, n, block, True, (y, x, core, z - 1))
            send(z < line - 1, n, block, True, (y, x, core, z + 1))
        elif sign < 0:
            send(both(valid, z < line - 1), n, block, False, (y, x, core, z + 1))
        else:
            send(both(valid, z > 0), n, block, False, (y, x, core, z - 1))
        send(valid, n, block, step == 0, near_x)
        send(valid, n, block, step == 0, near_y)
        send(valid, n, block, step == 0, sibling)

    def next_column(n, step, sign, along_x):
        zz = z + sign * step
        valid = None if step == 0 else (zz >= 0) & (zz < line)
        yy, xx = (y, 1 - x) if along_x else (1 - y, x)
        block = block_of(yy, xx, core, zz)
        if step:
            pl.when(valid)(lambda: arrive(n, block))
        else:
            arrive(n, block)
        if step % 2 == (0 if along_x else 1):
            send(valid, n, block, False, near_y if along_x else near_x)
        send(valid, n, block, False, sibling)

    def far_column(n, step, sign):
        zz = z + sign * step
        valid = None if step == 0 else (zz >= 0) & (zz < line)
        block = block_of(1 - y, 1 - x, core, zz)
        if step:
            pl.when(valid)(lambda: arrive(n, block))
        else:
            arrive(n, block)
        send(valid, n, block, False, sibling)

    def signs(step):
        return (1,) if step == 0 else (-1, 1)

    for n in range(count):
        own_column(n, 0, 1)
    for step in range(line + 1):
        for n in range(count):
            if step + 1 < line:
                for sign in signs(step + 1):
                    own_column(n, step + 1, sign)
            if step < line:
                for sign in signs(step):
                    next_column(n, step, sign, True)
                    next_column(n, step, sign, False)
            if step:
                for sign in signs(step - 1):
                    far_column(n, step - 1, sign)
    for yy in range(2):
        for xx in range(2):
            for zz in range(line):
                for n in range(count):
                    arrive(n, block_of(yy, xx, 1 - core, zz))
    for cond, copy in waits:
        if cond is None:
            copy.wait_send()
        else:
            pl.when(cond)(copy.wait_send)
    for copy in locals_:
        copy.wait()


def gather_all(arrays, collective_id):
    count = len(arrays)
    any_ref = pl.BlockSpec(memory_space=pl.ANY)
    line = lax.axis_size("tensor")
    devices = 8 * line
    return pl.pallas_call(
        functools.partial(gather_kernel, line, count),
        out_shape=[jax.ShapeDtypeStruct((devices * a.shape[0],) + a.shape[1:], a.dtype) for a in arrays],
        in_specs=[any_ref] * count,
        out_specs=[any_ref] * count,
        scratch_shapes=[
            pltpu.SemaphoreType.DMA((count,)),
            pltpu.SemaphoreType.DMA((count * 80,)),
            pltpu.SemaphoreType.DMA((count, devices)),
        ],
        compiler_params=pltpu.CompilerParams(collective_id=collective_id, has_side_effects=True),
        name="gather_all",
    )(*arrays)


def reduce_kernel(line, slots_ref, grads_ref, outs_ref, sum_ref, part_ref,
                  grad_in, out_in, out_stage, stage, near, far_x, far_y, from_x, from_y, up, down,
                  in_sem, part_sem, stage_sem, near_sem, send_sem, far_sem, x_sem, y_sem, line_sem):
    y, x, core, z = place()
    tokens, width = sum_ref.shape
    half = tokens // 2
    experts, room = grads_ref.shape[1:3]
    rounds = line
    greet(line)

    def goal(r):
        early = 1 - r // 2
        return (line - 1) * (r % 2) * early + (r - 1) * (1 - early)

    def block_at(q):
        r, j = q // 8, q % 8
        column = j % 4
        dy, dx = (column + 1) % 2, 1 - column // 2
        own = j // 4
        target_core = core * own + (1 - core) * (1 - own)
        return block_of((y + dy) % 2, (x + dx) % 2, target_core, goal(r))

    def load(q):
        b = block_at(q)
        return (
            pltpu.make_async_copy(grads_ref.at[b], grad_in.at[q % 2], in_sem.at[0, q % 2]),
            pltpu.make_async_copy(outs_ref.at[b], out_in.at[q % 2], in_sem.at[1, q % 2]),
        )

    def to_part(q):
        b = block_at(q)
        return pltpu.make_async_copy(out_stage.at[q % 2], part_ref.at[pl.ds(b * tokens, tokens)], part_sem.at[q % 2])

    def to_sibling(r, j):
        return pltpu.make_async_remote_copy(
            src_ref=stage.at[j], dst_ref=near.at[r * 4 + j], send_sem=stage_sem.at[j], recv_sem=near_sem.at[r * 4 + j],
            device_id=peer(y, x, 1 - core, z), device_id_type=MESH,
        )

    near_x, near_y = peer(y, 1 - x, core, z), peer(1 - y, x, core, z)

    def rows(h):
        return pl.ds(h * half, half)

    def cross(kind, r):
        column, h, target, sem, index, lane = {
            "far_x": (0, 0, far_x.at[r], far_sem.at[0, r], near_x, 0),
            "far_y": (0, 1, far_y.at[r], far_sem.at[1, r], near_y, 1),
            "x0": (1, 0, from_x.at[r, rows(0)], x_sem.at[r, 0], near_x, 2),
            "x1": (1, 1, from_x.at[r, rows(1)], x_sem.at[r, 1], near_x, 3),
            "y0": (2, 0, from_y.at[r, rows(0)], y_sem.at[r, 0], near_y, 4),
            "y1": (2, 1, from_y.at[r, rows(1)], y_sem.at[r, 1], near_y, 5),
        }[kind]
        return pltpu.make_async_remote_copy(
            src_ref=near.at[r * 4 + column, rows(h)], dst_ref=target, send_sem=send_sem.at[lane, r], recv_sem=sem,
            device_id=index, device_id_type=MESH,
        )

    def along(sign, r):
        target = up if sign > 0 else down
        lane = 0 if sign > 0 else 1
        return pltpu.make_async_remote_copy(
            src_ref=near.at[r * 4 + 3], dst_ref=target.at[r], send_sem=send_sem.at[6 + lane, r], recv_sem=line_sem.at[lane, r],
            device_id=peer(y, x, core, z + sign), device_id_type=MESH,
        )

    def term(q, source, target_width, store):
        picks = jnp.concatenate(
            [slot_hits(slots_ref[block_at(q)], e, room).astype(jnp.float32) for e in range(experts)], axis=0
        ).astype(jnp.bfloat16)
        for first in range(0, target_width, 512):
            part = slice(first, min(first + 512, target_width))
            values = source[q % 2, :, :, part].reshape(experts * room, part.stop - first)
            store(part, turned(picks, values))

    for copy in load(0):
        copy.start()

    def one(r, j, own):
        q = r * 8 + own * 4 + j
        for copy in load(q):
            copy.wait()

        @pl.when(q + 1 < rounds * 8)
        def _():
            for copy in load(q + 1):
                copy.start()

        if own:
            near_slot = r * 4 + j
            to_sibling(r, j).wait_recv()

            def keep(part, value):
                near[near_slot, :, part] = (value + near[near_slot, :, part].astype(jnp.float32)).astype(jnp.bfloat16)

            term(q, grad_in, width, keep)
        else:

            @pl.when(r > 0)
            def _():
                to_sibling(r - 1, j).wait_send()

            def keep(part, value):
                stage[j, :, part] = value.astype(jnp.bfloat16)

            term(q, grad_in, width, keep)
            to_sibling(r, j).start()

        @pl.when(q >= 2)
        def _():
            to_part(q - 2).wait()

        def put(part, value):
            out_stage[q % 2, :, part] = value.astype(jnp.bfloat16)

        term(q, out_in, out_stage.shape[2], put)
        to_part(q).start()

    def add(target, h, *sources):
        for first in range(0, width, 512):
            part = slice(first, min(first + 512, width))
            total = near[target, h, part].astype(jnp.float32)
            for source in sources:
                total = total + source(part).astype(jnp.float32)
            near[target, h, part] = total.astype(jnp.bfloat16)

    def work(s, carry):
        @pl.when(s < rounds)
        def _():
            r = s
            lax.fori_loop(0, 4, lambda j, c: (one(r, j, 0), c)[1], 0)
            lax.fori_loop(0, 4, lambda j, c: (one(r, j, 1), c)[1], 0)
            for kind in ("far_x", "far_y", "x0", "y1"):
                cross(kind, r).start()
            cross("far_y", r).wait_recv()
            add(r * 4 + 1, rows(1), lambda part: far_y[r, :, part])
            cross("x1", r).start()
            cross("far_x", r).wait_recv()
            add(r * 4 + 2, rows(0), lambda part: far_x[r, :, part])
            cross("y0", r).start()

        @pl.when((s >= 1) & (s < rounds + 1))
        def _():
            r = s - 1
            for kind in ("x0", "x1", "y0", "y1"):
                cross(kind, r).wait_recv()
            for h in range(2):
                add(
                    r * 4 + 3,
                    rows(h),
                    lambda part: from_x[r, rows(h), part],
                    lambda part: from_y[r, rows(h), part],
                )

        for hop in range(line - 1):
            r = s - 1 - hop
            live = (r >= 0) & (r < rounds)
            held = r * live.astype(jnp.int32)

            @pl.when(live & (goal(held) > z) & (z == hop))
            def _():
                if hop:
                    along(1, held).wait_recv()
                    for h in range(2):
                        add(held * 4 + 3, rows(h), lambda part: up[held, rows(h), part])
                along(1, held).start()

            @pl.when(live & (goal(held) < z) & (line - 1 - z == hop))
            def _():
                if hop:
                    along(-1, held).wait_recv()
                    for h in range(2):
                        add(held * 4 + 3, rows(h), lambda part: down[held, rows(h), part])
                along(-1, held).start()

        return carry

    lax.fori_loop(0, rounds + line - 1, work, 0)

    mine = (z + (z + 2) // 3) % 4 + z // 3
    sum_ref[...] = near[mine * 4 + 3].astype(jnp.float32)

    @pl.when(z > 0)
    def _():
        along(1, mine).wait_recv()
        sum_ref[...] += up[mine].astype(jnp.float32)

    @pl.when(z < line - 1)
    def _():
        along(-1, mine).wait_recv()
        sum_ref[...] += down[mine].astype(jnp.float32)

    def finish(r, carry):
        for kind in ("far_x", "far_y", "x0", "x1", "y0", "y1"):
            cross(kind, r).wait_send()

        @pl.when(goal(r) > z)
        def _():
            along(1, r).wait_send()

        @pl.when(goal(r) < z)
        def _():
            along(-1, r).wait_send()

        return carry

    lax.fori_loop(0, rounds, finish, 0)
    for j in range(4):
        to_sibling(rounds - 1, j).wait_send()
    for q in (rounds * 8 - 2, rounds * 8 - 1):
        to_part(q).wait()


def reduce_all(slots, outs, grads, collective_id):
    blocks, experts, tokens = slots.shape
    room, width = outs.shape[2:]
    wider = grads.shape[3]
    line = 4
    low = jnp.bfloat16
    any_ref = pl.BlockSpec(memory_space=pl.ANY)
    vmem = pl.BlockSpec(memory_space=pltpu.VMEM)
    dma = pltpu.SemaphoreType.DMA
    return pl.pallas_call(
        functools.partial(reduce_kernel, line),
        out_shape=(
            jax.ShapeDtypeStruct((tokens, wider), jnp.float32),
            jax.ShapeDtypeStruct((blocks * tokens, width), low),
        ),
        in_specs=[vmem, any_ref, any_ref],
        out_specs=[vmem, any_ref],
        scratch_shapes=[
            pltpu.VMEM((2, experts, room, wider), low),
            pltpu.VMEM((2, experts, room, width), low),
            pltpu.VMEM((2, tokens, width), low),
            pltpu.VMEM((4, tokens, wider), low),
            pltpu.VMEM((line * 4, tokens, wider), low),
            pltpu.VMEM((line, tokens // 2, wider), low),
            pltpu.VMEM((line, tokens // 2, wider), low),
            pltpu.VMEM((line, tokens, wider), low),
            pltpu.VMEM((line, tokens, wider), low),
            pltpu.VMEM((line, tokens, wider), low),
            pltpu.VMEM((line, tokens, wider), low),
            dma((2, 2)),
            dma((2,)),
            dma((4,)),
            dma((line * 4,)),
            dma((8, line)),
            dma((2, line)),
            dma((line, 2)),
            dma((line, 2)),
            dma((2, line)),
        ],
        compiler_params=pltpu.CompilerParams(
            collective_id=collective_id, has_side_effects=True, vmem_limit_bytes=62 << 20
        ),
        cost_estimate=pl.CostEstimate(
            flops=2 * blocks * experts * room * tokens * (width + wider),
            bytes_accessed=2 * blocks * experts * room * (width + wider),
            transcendentals=0,
        ),
        name="reduce_all",
    )(slots, grads, outs)


def visible_block(row_paths, key_paths, key_valid, row_first):
    row_count = row_paths.shape[1]
    key_count = key_paths.shape[1]
    key_segment = key_paths[0][None, :]
    on_path = (
        (key_segment == row_paths[0][:, None])
        | (key_segment == row_paths[1][:, None])
        | (key_segment == row_paths[2][:, None])
    )
    row_place = row_first + lax.iota(jnp.int32, row_count)
    key_place = lax.iota(jnp.int32, key_count)
    earlier = key_place[None, :] <= row_place[:, None]
    return on_path & earlier & (key_valid[None, :] == 1) | (
        key_place[None, :] == row_place[:, None]
    )


def rotation(positions, head_dim):
    half = head_dim // 2
    freqs = jnp.exp(-jnp.log(rope_base) * 2.0 * lax.iota(jnp.float32, half) / head_dim)
    angles = positions.astype(jnp.float32)[:, None] * freqs[None, :]
    return (jnp.cos(angles), jnp.sin(angles))


def rotate(values, cosine, sine):
    half = values.shape[-1] // 2
    first = values[..., :half]
    second = values[..., half:]
    cosine = cosine[:, None, :]
    sine = sine[:, None, :]
    return jnp.concatenate(
        (first * cosine - second * sine, second * cosine + first * sine), axis=-1
    )


def unrotate(grads, cosine, sine):
    half = grads.shape[-1] // 2
    first = grads[..., :half]
    second = grads[..., half:]
    cosine = cosine[:, None, :]
    sine = sine[:, None, :]
    return jnp.concatenate(
        (first * cosine + second * sine, second * cosine - first * sine), axis=-1
    )


def rms_apply(values, gain):
    scale = lax.rsqrt(jnp.mean(values * values, axis=-1, keepdims=True) + norm_eps)
    return (values * scale * gain, scale)


def rms_grad(values, scale, gain, grads, inner, width):
    grad_values = scale * gain * grads - values * scale**3 * inner / width
    grad_gain = jnp.sum(grads * values * scale, axis=0)
    return (grad_values, grad_gain)


def tensor_sums(pair):
    return lax.psum((pair[0], pair[1]), "tensor")


def heads_to_rows(term, rows):
    return lax.psum_scatter(
        term(jnp.int32(0), rows * lax.axis_size("tensor")).astype(jnp.bfloat16),
        "tensor",
        scatter_dimension=0,
        tiled=True,
    ).astype(jnp.float32)


def sum_over_dp(rows):
    dp = lax.axis_size("dp")
    pieces = rows.reshape(dp, rows.shape[0] // dp, rows.shape[1])
    return lax.psum_scatter(pieces, "dp", scatter_dimension=0, tiled=False)


def sum_over_tensor(part):
    return lax.psum_scatter(part, "tensor", scatter_dimension=0, tiled=True)


def body(
    residual,
    attn_gain,
    w_query,
    w_key,
    w_value,
    query_gain,
    key_gain,
    w_out,
    moe_gain,
    router,
    w_gate,
    w_up,
    w_down,
    segment_path,
    token_valid,
    routes,
    route_order,
    cotangent,
):
    tensor_rank = lax.axis_index("tensor")
    tok_dev, width = residual.shape
    seq_len = segment_path.shape[1]
    top_count = routes.shape[1]
    experts = router.shape[1]
    local_experts = w_gate.shape[0]
    dp_groups = experts // local_experts
    capacity = 9 * tok_dev * top_count // (8 * experts)
    full_width = H * HD
    block_rows = min(512, seq_len)
    block_count = seq_len // block_rows
    score_scale = HD ** (-0.5)
    everyone = ("dp", "tensor")
    direct = dp_groups == 8 and lax.axis_size("tensor") == 4
    first_expert = lax.axis_index("dp") * local_experts
    slot_rows = padded(capacity, 8)
    valid_dev = lax.dynamic_slice_in_dim(token_valid, tensor_rank * tok_dev, tok_dev)
    slots_own = slot_table(routes, route_order, valid_dev, experts, capacity)
    slots_all = lax.all_gather(slots_own.astype(jnp.bfloat16), everyone, axis=0)
    slots = lax.dynamic_slice_in_dim(slots_all, first_expert, local_experts, 1).astype(jnp.int32)
    blocks = slots.shape[0]
    cots_all = lax.all_gather(cotangent, everyone, axis=0, tiled=True)
    c_slots = dispatch(slots, None, cots_all, slot_rows)
    gathered_query, gathered_key, gathered_value, gathered_out = (
        lax.all_gather(w_query, "dp", axis=0, tiled=True),
        lax.all_gather(w_key, "dp", axis=0, tiled=True),
        lax.all_gather(w_value, "dp", axis=0, tiled=True),
        lax.all_gather(w_out, "dp", axis=1, tiled=True),
    )
    head_cols = gathered_query.shape[1]
    local_heads = head_cols // HD
    joined_weight = jnp.concatenate((gathered_query, gathered_key, gathered_value), axis=1)
    residual_float = residual.astype(jnp.float32)
    normed_one, scale_one = rms_apply(residual_float, attn_gain)
    hidden = normed_one.astype(jnp.bfloat16)
    hidden_all = lax.all_gather(hidden, "tensor", axis=0, tiled=True)
    projected = jnp.dot(hidden_all, joined_weight, preferred_element_type=jnp.float32)
    q_raw = projected[:, :head_cols]
    k_raw = projected[:, head_cols : 2 * head_cols]
    value_low = projected[:, 2 * head_cols :].astype(jnp.bfloat16).reshape(seq_len, local_heads, HD)
    query_sq, key_sq = tensor_sums((jnp.sum(q_raw * q_raw, axis=1), jnp.sum(k_raw * k_raw, axis=1)))
    query_scale = lax.rsqrt(query_sq / full_width + norm_eps)[:, None]
    key_scale = lax.rsqrt(key_sq / full_width + norm_eps)[:, None]
    query_gain_dev = lax.dynamic_slice_in_dim(query_gain, tensor_rank * head_cols, head_cols)
    key_gain_dev = lax.dynamic_slice_in_dim(key_gain, tensor_rank * head_cols, head_cols)
    block_starts = lax.iota(jnp.int32, block_count) * block_rows

    def block_mask(row_first):
        row_paths = lax.dynamic_slice_in_dim(segment_path, row_first, block_rows, 1)
        return visible_block(row_paths, segment_path, token_valid, row_first)

    def count_seen(row_first):
        return jnp.sum(block_mask(row_first).astype(jnp.int32), axis=1)

    positions = lax.map(count_seen, block_starts).reshape(seq_len) - 1
    cosine, sine = rotation(positions, HD)
    query_low = rotate(
        (q_raw * query_scale * query_gain_dev).reshape(seq_len, local_heads, HD), cosine, sine
    ).astype(jnp.bfloat16)
    key_low = rotate(
        (k_raw * key_scale * key_gain_dev).reshape(seq_len, local_heads, HD), cosine, sine
    ).astype(jnp.bfloat16)

    def attend(row_first):
        visible = block_mask(row_first)
        query_block = lax.dynamic_slice_in_dim(query_low, row_first, block_rows, 0)
        scores = (
            jnp.einsum("qhd,khd->hqk", query_block, key_low, preferred_element_type=jnp.float32)
            * score_scale
        )
        scores = jnp.where(visible[None], scores, masked_score)
        top_score = jnp.max(scores, axis=-1, keepdims=True)
        exp_scores = jnp.exp(scores - top_score)
        total = jnp.sum(exp_scores, axis=-1, keepdims=True)
        weights_low = (exp_scores / total).astype(jnp.bfloat16)
        mixed_block = jnp.einsum(
            "hqk,khd->qhd", weights_low, value_low, preferred_element_type=jnp.float32
        )
        return (mixed_block.astype(jnp.bfloat16), (top_score + jnp.log(total))[..., 0])

    mixed_blocks, log_totals = lax.map(attend, block_starts)
    attn_mixed = mixed_blocks.reshape(seq_len, head_cols)

    def attn_term(first_row, row_count):
        return jnp.dot(attn_mixed, gathered_out, preferred_element_type=jnp.float32)

    x_one = residual_float + heads_to_rows(attn_term, tok_dev)
    x_one, c_slots = lax.optimization_barrier((x_one, c_slots))
    normed_two, scale_two = rms_apply(x_one, moe_gain)
    hidden_two = normed_two.astype(jnp.bfloat16)
    logits = jnp.dot(hidden_two, router, preferred_element_type=jnp.float32)
    probs = jax.nn.softmax(logits, axis=-1)
    gates_own = probs.T
    if direct:
        rows_all, gates_all = gather_all([hidden_two, gates_own], 1)
        gates_all = gates_all.reshape(-1, experts, tok_dev)
    else:
        gates_all = lax.all_gather(gates_own, everyone, axis=0)
        rows_all = lax.all_gather(hidden_two, everyone, axis=0, tiled=True)
    gates = lax.dynamic_slice_in_dim(gates_all, first_expert, local_experts, 1)
    x_slots, gate_slots = dispatch(slots, gates, rows_all, slot_rows)
    outs, grads, grad_w_gate, grad_w_up, grad_w_down = expert_pass(
        first_expert.reshape(1),
        x_slots,
        c_slots,
        gate_slots,
        w_gate,
        w_up,
        w_down,
        blocks,
        padded(slot_rows, 16),
    )
    if direct:
        grad_rows, out_part = reduce_all(slots, outs, grads, 2)
    else:
        out_part, grad_part = combine(slots, outs, grads)
        grad_rows = sum_over_tensor(sum_over_dp(grad_part)).astype(jnp.float32)
    out_part = sum_over_dp(out_part)
    grad_out = cotangent.astype(jnp.float32)
    grad_hidden_two = grad_rows[:, :width]
    grad_probs = grad_rows[:, width : width + experts]
    grad_logits = probs * (grad_probs - jnp.sum(probs * grad_probs, axis=-1, keepdims=True))
    router_float = router.astype(jnp.float32)
    grad_hidden_two = grad_hidden_two + lax.dot_general(
        grad_logits, router_float, (((1,), (1,)), ((), ())), precision=lax.Precision.HIGHEST
    )
    grad_router_part = lax.dot_general(
        hidden_two.astype(jnp.float32),
        grad_logits,
        (((0,), (0,)), ((), ())),
        precision=lax.Precision.HIGHEST,
    )
    inner_two = jnp.sum(grad_hidden_two * moe_gain * x_one, axis=-1, keepdims=True)
    grad_norm_two, grad_moe_gain_part = rms_grad(
        x_one, scale_two, moe_gain, grad_hidden_two, inner_two, width
    )
    grad_x_one = grad_out + grad_norm_two
    grad_attn_all = lax.all_gather(grad_x_one.astype(jnp.bfloat16), "tensor", axis=0, tiled=True)
    grad_out_weight = lax.dot_general(
        attn_mixed, grad_attn_all, (((0,), (0,)), ((), ())), preferred_element_type=jnp.float32
    )
    grad_mixed = (
        lax.dot_general(
            grad_attn_all,
            gathered_out,
            (((1,), (1,)), ((), ())),
            preferred_element_type=jnp.float32,
        )
        .astype(jnp.bfloat16)
        .reshape(seq_len, local_heads, HD)
    )

    def attend_back(carry, pieces):
        grad_key_sum, grad_value_sum = carry
        row_first, log_total = pieces
        visible = block_mask(row_first)
        query_block = lax.dynamic_slice_in_dim(query_low, row_first, block_rows, 0)
        grad_block = lax.dynamic_slice_in_dim(grad_mixed, row_first, block_rows, 0)
        scores = (
            jnp.einsum("qhd,khd->hqk", query_block, key_low, preferred_element_type=jnp.float32)
            * score_scale
        )
        scores = jnp.where(visible[None], scores, masked_score)
        weights = jnp.exp(scores - log_total[..., None])
        grad_weights = jnp.einsum(
            "qhd,khd->hqk", grad_block, value_low, preferred_element_type=jnp.float32
        )
        inner = jnp.sum(weights * grad_weights, axis=-1, keepdims=True)
        grad_scores = (weights * (grad_weights - inner)).astype(jnp.bfloat16)
        grad_query_block = (
            jnp.einsum("hqk,khd->qhd", grad_scores, key_low, preferred_element_type=jnp.float32)
            * score_scale
        )
        grad_key_sum = (
            grad_key_sum
            + jnp.einsum(
                "hqk,qhd->khd", grad_scores, query_block, preferred_element_type=jnp.float32
            )
            * score_scale
        )
        grad_value_sum = grad_value_sum + jnp.einsum(
            "hqk,qhd->khd",
            weights.astype(jnp.bfloat16),
            grad_block,
            preferred_element_type=jnp.float32,
        )
        return ((grad_key_sum, grad_value_sum), grad_query_block)

    zero_heads = jnp.zeros((seq_len, local_heads, HD), jnp.float32)
    (grad_key_all, grad_value_all), grad_query_blocks = lax.scan(
        attend_back, (zero_heads, zero_heads), (block_starts, log_totals)
    )
    grad_q_norm = unrotate(
        grad_query_blocks.reshape(seq_len, local_heads, HD), cosine, sine
    ).reshape(seq_len, head_cols)
    grad_k_norm = unrotate(grad_key_all, cosine, sine).reshape(seq_len, head_cols)
    query_inner, key_inner = tensor_sums(
        (
            jnp.sum(grad_q_norm * query_gain_dev * q_raw, axis=1),
            jnp.sum(grad_k_norm * key_gain_dev * k_raw, axis=1),
        )
    )
    grad_q_raw, grad_query_gain_dev = rms_grad(
        q_raw, query_scale, query_gain_dev, grad_q_norm, query_inner[:, None], full_width
    )
    grad_k_raw, grad_key_gain_dev = rms_grad(
        k_raw, key_scale, key_gain_dev, grad_k_norm, key_inner[:, None], full_width
    )
    grad_joined = jnp.concatenate(
        (grad_q_raw, grad_k_raw, grad_value_all.reshape(seq_len, head_cols)), axis=1
    ).astype(jnp.bfloat16)
    out_part, grad_joined = lax.optimization_barrier((out_part, grad_joined))
    block_out = (x_one + sum_over_tensor(out_part).astype(jnp.float32)).astype(jnp.bfloat16)
    grad_joined_weight = lax.dot_general(
        hidden_all, grad_joined, (((0,), (0,)), ((), ())), preferred_element_type=jnp.float32
    )

    def back_term(first_row, row_count):
        return lax.dot_general(
            grad_joined, joined_weight, (((1,), (1,)), ((), ())), preferred_element_type=jnp.float32
        )

    grad_hidden = heads_to_rows(back_term, tok_dev)
    inner_one = jnp.sum(grad_hidden * attn_gain * residual_float, axis=-1, keepdims=True)
    grad_norm_one, grad_attn_gain_part = rms_grad(
        residual_float, scale_one, attn_gain, grad_hidden, inner_one, width
    )
    grad_input = grad_x_one + grad_norm_one
    grad_w_query, grad_w_key, grad_w_value, grad_w_out = (
        lax.psum_scatter(
            grad_joined_weight[:, :head_cols].astype(jnp.bfloat16),
            "dp",
            scatter_dimension=0,
            tiled=True,
        ).astype(jnp.float32),
        lax.psum_scatter(
            grad_joined_weight[:, head_cols : 2 * head_cols].astype(jnp.bfloat16),
            "dp",
            scatter_dimension=0,
            tiled=True,
        ).astype(jnp.float32),
        lax.psum_scatter(
            grad_joined_weight[:, 2 * head_cols :].astype(jnp.bfloat16),
            "dp",
            scatter_dimension=0,
            tiled=True,
        ).astype(jnp.float32),
        lax.psum_scatter(
            grad_out_weight.astype(jnp.bfloat16), "dp", scatter_dimension=1, tiled=True
        ).astype(jnp.float32),
    )
    zero_width = jnp.zeros((full_width,), jnp.float32)
    grad_query_full = lax.dynamic_update_slice_in_dim(
        zero_width, grad_query_gain_dev, tensor_rank * head_cols, 0
    )
    grad_key_full = lax.dynamic_update_slice_in_dim(
        zero_width, grad_key_gain_dev, tensor_rank * head_cols, 0
    )
    summed = lax.psum(
        (grad_attn_gain_part, grad_moe_gain_part, grad_query_full, grad_key_full, grad_router_part),
        ("dp", "tensor"),
    )
    return (
        block_out,
        grad_input,
        summed[0],
        grad_w_query,
        grad_w_key,
        grad_w_value,
        summed[2],
        summed[3],
        grad_w_out,
        summed[1],
        summed[4],
        grad_w_gate,
        grad_w_up,
        grad_w_down,
    )


def solution(mesh):
    in_specs = (
        P(("dp", "tensor"), None),
        P(),
        P("dp", "tensor"),
        P("dp", "tensor"),
        P("dp", "tensor"),
        P(),
        P(),
        P("tensor", "dp"),
        P(),
        P(),
        P("dp", None, "tensor"),
        P("dp", None, "tensor"),
        P("dp", "tensor", None),
        P(None, "dp"),
        P("dp"),
        P(("dp", "tensor"), None),
        P(("dp", "tensor"), None),
        P(("dp", "tensor"), None),
    )
    out_specs = (
        P(("dp", "tensor"), None),
        P(("dp", "tensor"), None),
        P(),
        P("dp", "tensor"),
        P("dp", "tensor"),
        P("dp", "tensor"),
        P(),
        P(),
        P("tensor", "dp"),
        P(),
        P(),
        P("dp", None, "tensor"),
        P("dp", None, "tensor"),
        P("dp", "tensor", None),
    )
    return jax.shard_map(body, mesh=mesh, in_specs=in_specs, out_specs=out_specs, check_vma=False)
```

```python
import functools

import jax
import jax.numpy as jnp
from jax import lax
from jax.experimental import pallas as pl
from jax.experimental.pallas import tpu as pltpu
from jax.sharding import PartitionSpec as P

H = 16
HD = 128


norm_eps = 1e-05
rope_base = 10000.0
masked_score = -1e30


def padded(count, step):
    return -(-count // step) * step


def slot_table(routes, route_order, valid, experts, capacity):
    far = jnp.int32(1 << 30)
    expert = lax.iota(jnp.int32, experts)[:, None, None]
    hits = (routes[None] == expert) & (valid[None, :, None] == 1)
    order = jnp.min(jnp.where(hits, route_order[None], far), axis=-1)
    ranks = jnp.sum((order[:, None, :] < order[:, :, None]).astype(jnp.int32), axis=-1)
    return jnp.where((order < far) & (ranks < capacity), ranks, -1)


def slot_hits(slots, expert, rows):
    tokens = slots.shape[-1]
    return lax.broadcasted_iota(jnp.int32, (rows, tokens), 0) == slots[expert : expert + 1, :]


def dispatch_kernel(slots_ref, gates_ref, rows_ref, x_ref, gate_ref):
    pair, experts, tokens = slots_ref.shape
    rows = x_ref.shape[1] // pair
    width = rows_ref.shape[1]
    picks = []
    for b in range(pair):
        slots = slots_ref[b]
        pieces = []
        for e in range(experts):
            hit = slot_hits(slots, e, rows)
            pieces.append(hit.astype(jnp.float32))
            if gate_ref is not None:
                gate = jnp.sum(jnp.where(hit, gates_ref[b, e : e + 1, :], 0.0), axis=1, keepdims=True)
                gate_ref[e, b * rows : (b + 1) * rows, :] = jnp.broadcast_to(gate, (rows, 128))
        picks.append(jnp.concatenate(pieces, axis=0).astype(jnp.bfloat16))
    step = min(512, width)
    for first in range(0, width, step):
        parts = [
            jnp.dot(
                picks[b],
                rows_ref[b * tokens : (b + 1) * tokens, first : first + step],
                preferred_element_type=jnp.float32,
            )
            for b in range(pair)
        ]
        for e in range(experts):
            x_ref[e, :, first : first + step] = jnp.concatenate(
                [part[e * rows : (e + 1) * rows] for part in parts], axis=0
            ).astype(jnp.bfloat16)


def plain_dispatch_kernel(slots_ref, rows_ref, x_ref):
    dispatch_kernel(slots_ref, None, rows_ref, x_ref, None)


def dispatch(slots, gates, rows_all, rows):
    blocks, experts, tokens = slots.shape
    width = rows_all.shape[1]
    pair = 2
    out = jax.ShapeDtypeStruct((experts, blocks * rows, width), jnp.bfloat16)
    table = pl.BlockSpec((pair, experts, tokens), lambda i: (i, 0, 0))
    source = pl.BlockSpec((pair * tokens, width), lambda i: (i, 0))
    target = pl.BlockSpec((experts, pair * rows, width), lambda i: (0, i, 0))
    settings = dict(
        grid=(blocks // pair,),
        compiler_params=pltpu.CompilerParams(vmem_limit_bytes=50 << 20),
        cost_estimate=pl.CostEstimate(
            flops=2 * blocks * experts * rows * tokens * width,
            bytes_accessed=2 * blocks * (tokens + experts * rows) * width,
            transcendentals=0,
        ),
    )
    if gates is None:
        return pl.pallas_call(
            plain_dispatch_kernel, out_shape=out, in_specs=[table, source], out_specs=target, name="pick", **settings
        )(slots, rows_all)
    return pl.pallas_call(
        dispatch_kernel,
        out_shape=(out, jax.ShapeDtypeStruct((experts, blocks * rows, 128), jnp.float32)),
        in_specs=[table, table, source],
        out_specs=[target, pl.BlockSpec((experts, pair * rows, 128), lambda i: (0, i, 0))],
        name="dispatch",
        **settings,
    )(slots, gates, rows_all)


def turned(left, right):
    return lax.dot_general(left, right, (((0,), (0,)), ((), ())), preferred_element_type=jnp.float32)


def across(left, right):
    return lax.dot_general(left, right, (((1,), (1,)), ((), ())), preferred_element_type=jnp.float32)


def expert_kernel(rows, first_ref, x_ref, c_ref, gate_ref, wg_ref, wu_ref, wd_ref,
                  o_ref, dx_ref, dwg_ref, dwu_ref, dwd_ref):
    expert = pl.program_id(0)
    tile, width = x_ref.shape[1:]
    units = wg_ref.shape[2]
    room = o_ref.shape[2]
    blocks = tile // rows
    gate = gate_ref[0, :, 0:1]
    x = x_ref[0]
    c = c_ref[0]
    gate_pre = jnp.dot(x, wg_ref[0], preferred_element_type=jnp.float32)
    up_pre = jnp.dot(x, wu_ref[0], preferred_element_type=jnp.float32)
    back = across(c, wd_ref[0])
    sig = jax.nn.sigmoid(gate_pre)
    silu = gate_pre * sig
    act = (silu * up_pre).astype(jnp.bfloat16)
    act_float = act.astype(jnp.float32)
    grad_gate = jnp.sum(act_float * back, axis=1, keepdims=True)
    grad_act = back * gate
    grad_gate_pre = (grad_act * up_pre * sig * (1.0 + gate_pre * (1.0 - sig))).astype(jnp.bfloat16)
    grad_up_pre = (grad_act * silu).astype(jnp.bfloat16)
    gated = (act_float * gate).astype(jnp.bfloat16)

    def spread(values):
        values = values.reshape(blocks, rows, values.shape[1])
        if room > rows:
            empty = jnp.zeros((blocks, room - rows, values.shape[2]), jnp.float32)
            values = jnp.concatenate((values, empty), axis=1)
        return values.astype(jnp.bfloat16)

    step = min(512, width)
    for first in range(0, width, step):
        part = slice(first, first + step)
        out = jnp.dot(act, wd_ref[0, :, part], preferred_element_type=jnp.float32) * gate
        o_ref[:, 0, :, part] = spread(out)
        grad = across(grad_gate_pre, wg_ref[0, part, :]) + across(grad_up_pre, wu_ref[0, part, :])
        dx_ref[:, 0, :, part] = spread(grad)
    lanes = lax.broadcasted_iota(jnp.int32, (tile, 128), 1)
    dx_ref[:, 0, :, width:] = spread(jnp.where(lanes == first_ref[0] + expert, grad_gate, 0.0))

    @pl.when(pl.program_id(1) == 0)
    def _():
        for ref in (dwg_ref, dwu_ref, dwd_ref):
            ref[...] = jnp.zeros_like(ref)

    for first in range(0, width, step):
        part = slice(first, first + step)
        dwg_ref[0, part, :] += turned(x_ref[0, :, part], grad_gate_pre)
        dwu_ref[0, part, :] += turned(x_ref[0, :, part], grad_up_pre)
        dwd_ref[0, :, part] += turned(gated, c_ref[0, :, part])


def expert_pass(first_expert, x_slots, c_slots, gate_slots, w_gate, w_up, w_down, blocks, room):
    experts, total, width = x_slots.shape
    units = w_gate.shape[2]
    rows = total // blocks
    group = next(n for n in (16, 8, 4, 2, 1) if blocks % n == 0 and (n * rows <= 768 or n == 1))
    tile = group * rows
    extra = 128
    tall = pl.BlockSpec((1, width, units), lambda e, r, _: (e, 0, 0))
    wide = pl.BlockSpec((1, units, width), lambda e, r, _: (e, 0, 0))
    slot = pl.BlockSpec((1, tile, width), lambda e, r, _: (e, r, 0))
    kernel = functools.partial(expert_kernel, rows)
    return pl.pallas_call(
        kernel,
        grid_spec=pltpu.PrefetchScalarGridSpec(
            num_scalar_prefetch=1,
            grid=(experts, total // tile),
            in_specs=[slot, slot, pl.BlockSpec((1, tile, 128), lambda e, r, _: (e, r, 0)), tall, tall, wide],
            out_specs=[
                pl.BlockSpec((group, 1, room, width), lambda e, r, _: (r, e, 0, 0)),
                pl.BlockSpec((group, 1, room, width + extra), lambda e, r, _: (r, e, 0, 0)),
                tall, tall, wide,
            ],
        ),
        out_shape=(
            jax.ShapeDtypeStruct((blocks, experts, room, width), jnp.bfloat16),
            jax.ShapeDtypeStruct((blocks, experts, room, width + extra), jnp.bfloat16),
            jax.ShapeDtypeStruct(w_gate.shape, jnp.float32),
            jax.ShapeDtypeStruct(w_up.shape, jnp.float32),
            jax.ShapeDtypeStruct(w_down.shape, jnp.float32),
        ),
        compiler_params=pltpu.CompilerParams(vmem_limit_bytes=60 << 20),
        cost_estimate=pl.CostEstimate(
            flops=18 * experts * total * width * units,
            bytes_accessed=8 * experts * total * width + 18 * experts * width * units,
            transcendentals=experts * total * units,
        ),
        name="experts",
    )(first_expert, x_slots, c_slots, gate_slots, w_gate, w_up, w_down)


def combine_kernel(slots_ref, o_ref, dx_ref, out_ref, grad_ref):
    _, experts, tokens = slots_ref.shape
    room, width = o_ref.shape[2:]
    slots = slots_ref[0]
    picks = jnp.concatenate(
        [slot_hits(slots, e, room).astype(jnp.float32) for e in range(experts)], axis=0
    ).astype(jnp.bfloat16)
    for source, target in ((o_ref, out_ref), (dx_ref, grad_ref)):
        columns = target.shape[1]
        for first in range(0, columns, 512):
            part = slice(first, min(first + 512, columns))
            values = source[0, :, :, part].reshape(experts * room, part.stop - first)
            target[:, part] = turned(picks, values).astype(jnp.bfloat16)


def combine(slots, outs, grads):
    blocks, experts, tokens = slots.shape
    room, width = outs.shape[2:]
    wider = grads.shape[3]
    return pl.pallas_call(
        combine_kernel,
        grid=(blocks,),
        out_shape=(
            jax.ShapeDtypeStruct((blocks * tokens, width), jnp.bfloat16),
            jax.ShapeDtypeStruct((blocks * tokens, wider), jnp.bfloat16),
        ),
        in_specs=[
            pl.BlockSpec((1, experts, tokens), lambda i: (i, 0, 0)),
            pl.BlockSpec((1, experts, room, width), lambda i: (i, 0, 0, 0)),
            pl.BlockSpec((1, experts, room, wider), lambda i: (i, 0, 0, 0)),
        ],
        out_specs=[
            pl.BlockSpec((tokens, width), lambda i: (i, 0)),
            pl.BlockSpec((tokens, wider), lambda i: (i, 0)),
        ],
        compiler_params=pltpu.CompilerParams(vmem_limit_bytes=50 << 20),
        cost_estimate=pl.CostEstimate(
            flops=2 * blocks * experts * room * tokens * (width + wider),
            bytes_accessed=2 * blocks * (tokens + experts * room) * (width + wider),
            transcendentals=0,
        ),
        name="combine",
    )(slots, outs, grads)


MESH = pl.DeviceIdType.MESH


def place():
    dp, z = lax.axis_index("dp"), lax.axis_index("tensor")
    return dp // 4, dp // 2 % 2, dp % 2, z


def peer(y, x, core, z):
    return (y * 4 + x * 2 + core, z)


def block_of(y, x, core, z):
    return (y * 4 + x * 2 + core) * 4 + z


def greet(line):
    y, x, core, z = place()
    barrier = pltpu.get_barrier_semaphore()
    for near in ((y, x, 1 - core, z), (y, 1 - x, core, z), (1 - y, x, core, z)):
        pl.semaphore_signal(barrier, inc=1, device_id=peer(*near), device_id_type=MESH)

    @pl.when(z > 0)
    def _():
        pl.semaphore_signal(barrier, inc=1, device_id=peer(y, x, core, z - 1), device_id_type=MESH)

    @pl.when(z < line - 1)
    def _():
        pl.semaphore_signal(barrier, inc=1, device_id=peer(y, x, core, z + 1), device_id_type=MESH)

    pl.semaphore_wait(barrier, 3 + (z + line - 1) // line + (2 * line - 2 - z) // line)


def gather_kernel(line, count, *refs):
    owns, outs = refs[:count], refs[count : 2 * count]
    local_sem, send_sem, recv_sem = refs[2 * count :]
    y, x, core, z = place()
    greet(line)
    waits = []
    sent = [0]

    def send(cond, n, block, source_own, target):
        rows = owns[n].shape[0]
        part = pl.ds(block * rows, rows)
        copy = pltpu.make_async_remote_copy(
            src_ref=owns[n] if source_own else outs[n].at[part],
            dst_ref=outs[n].at[part],
            send_sem=send_sem.at[sent[0]],
            recv_sem=recv_sem.at[n, block],
            device_id=peer(*target),
            device_id_type=MESH,
        )
        sent[0] += 1
        waits.append((cond, copy))
        if cond is None:
            copy.start()
        else:
            pl.when(cond)(copy.start)

    def arrive(n, block):
        rows = owns[n].shape[0]
        part = pl.ds(block * rows, rows)
        pltpu.make_async_copy(outs[n].at[part], outs[n].at[part], recv_sem.at[n, block]).wait()

    def both(a, b):
        return b if a is None else a & b

    sibling, near_x, near_y = (y, x, 1 - core, z), (y, 1 - x, core, z), (1 - y, x, core, z)
    mine = block_of(y, x, core, z)
    locals_ = []
    for n in range(count):
        rows = owns[n].shape[0]
        own_copy = pltpu.make_async_copy(owns[n], outs[n].at[pl.ds(mine * rows, rows)], local_sem.at[n])
        own_copy.start()
        locals_.append(own_copy)

    def own_column(n, step, sign):
        zz = z + sign * step
        valid = None if step == 0 else (zz >= 0) & (zz < line)
        block = block_of(y, x, core, zz)

        def fetch():
            if step:
                arrive(n, block)

        if step:
            pl.when(valid)(fetch)
        if step == 0:
            send(z > 0, n, block, True, (y, x, core, z - 1))
            send(z < line - 1, n, block, True, (y, x, core, z + 1))
        elif sign < 0:
            send(both(valid, z < line - 1), n, block, False, (y, x, core, z + 1))
        else:
            send(both(valid, z > 0), n, block, False, (y, x, core, z - 1))
        send(valid, n, block, step == 0, near_x)
        send(valid, n, block, step == 0, near_y)
        send(valid, n, block, step == 0, sibling)

    def next_column(n, step, sign, along_x):
        zz = z + sign * step
        valid = None if step == 0 else (zz >= 0) & (zz < line)
        yy, xx = (y, 1 - x) if along_x else (1 - y, x)
        block = block_of(yy, xx, core, zz)
        if step:
            pl.when(valid)(lambda: arrive(n, block))
        else:
            arrive(n, block)
        if step % 2 == (0 if along_x else 1):
            send(valid, n, block, False, near_y if along_x else near_x)
        send(valid, n, block, False, sibling)

    def far_column(n, step, sign):
        zz = z + sign * step
        valid = None if step == 0 else (zz >= 0) & (zz < line)
        block = block_of(1 - y, 1 - x, core, zz)
        if step:
            pl.when(valid)(lambda: arrive(n, block))
        else:
            arrive(n, block)
        send(valid, n, block, False, sibling)

    def signs(step):
        return (1,) if step == 0 else (-1, 1)

    for n in range(count):
        own_column(n, 0, 1)
    for step in range(line + 1):
        for n in range(count):
            if step + 1 < line:
                for sign in signs(step + 1):
                    own_column(n, step + 1, sign)
            if step < line:
                for sign in signs(step):
                    next_column(n, step, sign, True)
                    next_column(n, step, sign, False)
            if step:
                for sign in signs(step - 1):
                    far_column(n, step - 1, sign)
    for yy in range(2):
        for xx in range(2):
            for zz in range(line):
                for n in range(count):
                    arrive(n, block_of(yy, xx, 1 - core, zz))
    for cond, copy in waits:
        if cond is None:
            copy.wait_send()
        else:
            pl.when(cond)(copy.wait_send)
    for copy in locals_:
        copy.wait()


def gather_all(arrays, collective_id):
    count = len(arrays)
    any_ref = pl.BlockSpec(memory_space=pl.ANY)
    line = lax.axis_size("tensor")
    devices = 8 * line
    return pl.pallas_call(
        functools.partial(gather_kernel, line, count),
        out_shape=[jax.ShapeDtypeStruct((devices * a.shape[0],) + a.shape[1:], a.dtype) for a in arrays],
        in_specs=[any_ref] * count,
        out_specs=[any_ref] * count,
        scratch_shapes=[
            pltpu.SemaphoreType.DMA((count,)),
            pltpu.SemaphoreType.DMA((count * 80,)),
            pltpu.SemaphoreType.DMA((count, devices)),
        ],
        compiler_params=pltpu.CompilerParams(collective_id=collective_id, has_side_effects=True),
        name="gather_all",
    )(*arrays)


def reduce_kernel(line, slots_ref, grads_ref, outs_ref, sum_ref, part_ref,
                  grad_in, out_in, out_stage, stage, near, far_x, far_y, from_x, from_y, up, down,
                  in_sem, part_sem, stage_sem, near_sem, send_sem, far_sem, x_sem, y_sem, line_sem):
    y, x, core, z = place()
    tokens, width = sum_ref.shape
    half = tokens // 2
    experts, room = grads_ref.shape[1:3]
    rounds = line
    greet(line)

    def goal(r):
        early = 1 - r // 2
        return (line - 1) * (r % 2) * early + (r - 1) * (1 - early)

    def block_at(q):
        r, j = q // 8, q % 8
        column = j % 4
        dy, dx = (column + 1) % 2, 1 - column // 2
        own = j // 4
        target_core = core * own + (1 - core) * (1 - own)
        return block_of((y + dy) % 2, (x + dx) % 2, target_core, goal(r))

    def load(q):
        b = block_at(q)
        return (
            pltpu.make_async_copy(grads_ref.at[b], grad_in.at[q % 2], in_sem.at[0, q % 2]),
            pltpu.make_async_copy(outs_ref.at[b], out_in.at[q % 2], in_sem.at[1, q % 2]),
        )

    def to_part(q):
        b = block_at(q)
        return pltpu.make_async_copy(out_stage.at[q % 2], part_ref.at[pl.ds(b * tokens, tokens)], part_sem.at[q % 2])

    def to_sibling(r, j):
        return pltpu.make_async_remote_copy(
            src_ref=stage.at[j], dst_ref=near.at[r * 4 + j], send_sem=stage_sem.at[j], recv_sem=near_sem.at[r * 4 + j],
            device_id=peer(y, x, 1 - core, z), device_id_type=MESH,
        )

    near_x, near_y = peer(y, 1 - x, core, z), peer(1 - y, x, core, z)

    def rows(h):
        return pl.ds(h * half, half)

    def cross(kind, r):
        column, h, target, sem, index, lane = {
            "far_x": (0, 0, far_x.at[r], far_sem.at[0, r], near_x, 0),
            "far_y": (0, 1, far_y.at[r], far_sem.at[1, r], near_y, 1),
            "x0": (1, 0, from_x.at[r, rows(0)], x_sem.at[r, 0], near_x, 2),
            "x1": (1, 1, from_x.at[r, rows(1)], x_sem.at[r, 1], near_x, 3),
            "y0": (2, 0, from_y.at[r, rows(0)], y_sem.at[r, 0], near_y, 4),
            "y1": (2, 1, from_y.at[r, rows(1)], y_sem.at[r, 1], near_y, 5),
        }[kind]
        return pltpu.make_async_remote_copy(
            src_ref=near.at[r * 4 + column, rows(h)], dst_ref=target, send_sem=send_sem.at[lane, r], recv_sem=sem,
            device_id=index, device_id_type=MESH,
        )

    def along(sign, r):
        target = up if sign > 0 else down
        lane = 0 if sign > 0 else 1
        return pltpu.make_async_remote_copy(
            src_ref=near.at[r * 4 + 3], dst_ref=target.at[r], send_sem=send_sem.at[6 + lane, r], recv_sem=line_sem.at[lane, r],
            device_id=peer(y, x, core, z + sign), device_id_type=MESH,
        )

    def term(q, source, target_width, store):
        picks = jnp.concatenate(
            [slot_hits(slots_ref[block_at(q)], e, room).astype(jnp.float32) for e in range(experts)], axis=0
        ).astype(jnp.bfloat16)
        for first in range(0, target_width, 512):
            part = slice(first, min(first + 512, target_width))
            values = source[q % 2, :, :, part].reshape(experts * room, part.stop - first)
            store(part, turned(picks, values))

    for copy in load(0):
        copy.start()

    def one(r, j, own):
        q = r * 8 + own * 4 + j
        for copy in load(q):
            copy.wait()

        @pl.when(q + 1 < rounds * 8)
        def _():
            for copy in load(q + 1):
                copy.start()

        if own:
            near_slot = r * 4 + j
            to_sibling(r, j).wait_recv()

            def keep(part, value):
                near[near_slot, :, part] = (value + near[near_slot, :, part].astype(jnp.float32)).astype(jnp.bfloat16)

            term(q, grad_in, width, keep)
        else:

            @pl.when(r > 0)
            def _():
                to_sibling(r - 1, j).wait_send()

            def keep(part, value):
                stage[j, :, part] = value.astype(jnp.bfloat16)

            term(q, grad_in, width, keep)
            to_sibling(r, j).start()

        @pl.when(q >= 2)
        def _():
            to_part(q - 2).wait()

        def put(part, value):
            out_stage[q % 2, :, part] = value.astype(jnp.bfloat16)

        term(q, out_in, out_stage.shape[2], put)
        to_part(q).start()

    def add(target, h, *sources):
        for first in range(0, width, 512):
            part = slice(first, min(first + 512, width))
            total = near[target, h, part].astype(jnp.float32)
            for source in sources:
                total = total + source(part).astype(jnp.float32)
            near[target, h, part] = total.astype(jnp.bfloat16)

    def work(s, carry):
        @pl.when(s < rounds)
        def _():
            r = s
            lax.fori_loop(0, 4, lambda j, c: (one(r, j, 0), c)[1], 0)
            lax.fori_loop(0, 4, lambda j, c: (one(r, j, 1), c)[1], 0)
            for kind in ("far_x", "far_y", "x0", "y1"):
                cross(kind, r).start()
            cross("far_y", r).wait_recv()
            add(r * 4 + 1, rows(1), lambda part: far_y[r, :, part])
            cross("x1", r).start()
            cross("far_x", r).wait_recv()
            add(r * 4 + 2, rows(0), lambda part: far_x[r, :, part])
            cross("y0", r).start()

        @pl.when((s >= 1) & (s < rounds + 1))
        def _():
            r = s - 1
            for kind in ("x0", "x1", "y0", "y1"):
                cross(kind, r).wait_recv()
            for h in range(2):
                add(
                    r * 4 + 3,
                    rows(h),
                    lambda part: from_x[r, rows(h), part],
                    lambda part: from_y[r, rows(h), part],
                )

        for hop in range(line - 1):
            r = s - 1 - hop
            live = (r >= 0) & (r < rounds)
            held = r * live.astype(jnp.int32)

            @pl.when(live & (goal(held) > z) & (z == hop))
            def _():
                if hop:
                    along(1, held).wait_recv()
                    for h in range(2):
                        add(held * 4 + 3, rows(h), lambda part: up[held, rows(h), part])
                along(1, held).start()

            @pl.when(live & (goal(held) < z) & (line - 1 - z == hop))
            def _():
                if hop:
                    along(-1, held).wait_recv()
                    for h in range(2):
                        add(held * 4 + 3, rows(h), lambda part: down[held, rows(h), part])
                along(-1, held).start()

        return carry

    lax.fori_loop(0, rounds + line - 1, work, 0)

    mine = (z + (z + 2) // 3) % 4 + z // 3
    sum_ref[...] = near[mine * 4 + 3].astype(jnp.float32)

    @pl.when(z > 0)
    def _():
        along(1, mine).wait_recv()
        sum_ref[...] += up[mine].astype(jnp.float32)

    @pl.when(z < line - 1)
    def _():
        along(-1, mine).wait_recv()
        sum_ref[...] += down[mine].astype(jnp.float32)

    def finish(r, carry):
        for kind in ("far_x", "far_y", "x0", "x1", "y0", "y1"):
            cross(kind, r).wait_send()

        @pl.when(goal(r) > z)
        def _():
            along(1, r).wait_send()

        @pl.when(goal(r) < z)
        def _():
            along(-1, r).wait_send()

        return carry

    lax.fori_loop(0, rounds, finish, 0)
    for j in range(4):
        to_sibling(rounds - 1, j).wait_send()
    for q in (rounds * 8 - 2, rounds * 8 - 1):
        to_part(q).wait()


def reduce_all(slots, outs, grads, collective_id):
    blocks, experts, tokens = slots.shape
    room, width = outs.shape[2:]
    wider = grads.shape[3]
    line = 4
    low = jnp.bfloat16
    any_ref = pl.BlockSpec(memory_space=pl.ANY)
    vmem = pl.BlockSpec(memory_space=pltpu.VMEM)
    dma = pltpu.SemaphoreType.DMA
    return pl.pallas_call(
        functools.partial(reduce_kernel, line),
        out_shape=(
            jax.ShapeDtypeStruct((tokens, wider), jnp.float32),
            jax.ShapeDtypeStruct((blocks * tokens, width), low),
        ),
        in_specs=[vmem, any_ref, any_ref],
        out_specs=[vmem, any_ref],
        scratch_shapes=[
            pltpu.VMEM((2, experts, room, wider), low),
            pltpu.VMEM((2, experts, room, width), low),
            pltpu.VMEM((2, tokens, width), low),
            pltpu.VMEM((4, tokens, wider), low),
            pltpu.VMEM((line * 4, tokens, wider), low),
            pltpu.VMEM((line, tokens // 2, wider), low),
            pltpu.VMEM((line, tokens // 2, wider), low),
            pltpu.VMEM((line, tokens, wider), low),
            pltpu.VMEM((line, tokens, wider), low),
            pltpu.VMEM((line, tokens, wider), low),
            pltpu.VMEM((line, tokens, wider), low),
            dma((2, 2)),
            dma((2,)),
            dma((4,)),
            dma((line * 4,)),
            dma((8, line)),
            dma((2, line)),
            dma((line, 2)),
            dma((line, 2)),
            dma((2, line)),
        ],
        compiler_params=pltpu.CompilerParams(
            collective_id=collective_id, has_side_effects=True, vmem_limit_bytes=62 << 20
        ),
        cost_estimate=pl.CostEstimate(
            flops=2 * blocks * experts * room * tokens * (width + wider),
            bytes_accessed=2 * blocks * experts * room * (width + wider),
            transcendentals=0,
        ),
        name="reduce_all",
    )(slots, grads, outs)


def either(first, second, take):
    return first * (1 - take) + second * take


def remote(source, target, send_sem, recv_sem, where):
    return pltpu.make_async_remote_copy(
        src_ref=source, dst_ref=target, send_sem=send_sem, recv_sem=recv_sem,
        device_id=peer(*where), device_id_type=MESH,
    )


def landed(target, sem):
    pltpu.make_async_copy(target, target, sem).wait()


class LineGather:
    def __init__(self, own, out, send_sem, recv_sem, line):
        self.own, self.out, self.send_sem, self.recv_sem, self.line = own, out, send_sem, recv_sem, line
        self.spot = place()
        self.rows = own.shape[0]

    def view(self, block):
        return self.out.at[pl.ds(block * self.rows, self.rows)]

    def inside(self, block):
        return (block >= 0) & (block < self.line)

    def copy(self, sign, step):
        y, x, core, z = self.spot
        block = z - sign * step
        lane = (1 - sign) // 2
        source = self.own if step == 0 else self.view(block)
        return remote(
            source, self.view(block), self.send_sem.at[lane, step], self.recv_sem.at[lane, step], (y, x, core, z + sign)
        )

    def sends(self, sign, step):
        z = self.spot[3]
        return self.inside(z - sign * step) & self.inside(z + sign)

    def begin(self):
        for sign in (1, -1):
            pl.when(self.sends(sign, 0))(self.copy(sign, 0).start)

    def advance(self, step):
        z = self.spot[3]
        for sign in (1, -1):
            block = z - sign * (step + 1)
            lane = (1 - sign) // 2

            @pl.when(self.inside(block))
            def _():
                landed(self.view(block), self.recv_sem.at[lane, step])

            if step + 1 < self.line - 1:
                pl.when(self.sends(sign, step + 1))(self.copy(sign, step + 1).start)

    def finish(self):
        for sign in (1, -1):
            for step in range(self.line - 1):
                pl.when(self.sends(sign, step))(self.copy(sign, step).wait_send)


def start_kernel(line, hidden_ref, wq_ref, wk_ref, wv_ref, wo_ref, hidden_out, joined_out, wo_out,
                 local_sem, line_send, line_recv, plane_send, plane_recv):
    y, x, core, z = place()
    owns = (wq_ref, wk_ref, wv_ref, wo_ref)
    near_x, near_y, sibling = (y, 1 - x, core, z), (1 - y, x, core, z), (y, x, 1 - core, z)

    def view(n, yy, xx, half=None):
        group = yy * 4 + xx * 2 + core
        rows, columns = owns[n].shape
        first, count = (0, rows) if half is None else (half * (rows // 2), rows // 2)
        if n < 3:
            return joined_out.at[pl.ds(group * rows + first, count), pl.ds(n * columns, columns)]
        return wo_out.at[pl.ds(first, count), pl.ds(pl.multiple_of(group * columns, columns), columns)]

    kinds = ("x", "y", "s", "fy", "fx", "sx", "sy", "sf")

    def copy(kind, n):
        source, target, where = {
            "x": (owns[n], view(n, y, x), near_x),
            "y": (owns[n], view(n, y, x), near_y),
            "s": (owns[n], view(n, y, x), sibling),
            "fy": (view(n, y, 1 - x, 0), view(n, y, 1 - x, 0), near_y),
            "fx": (view(n, 1 - y, x, 1), view(n, 1 - y, x, 1), near_x),
            "sx": (view(n, y, 1 - x), view(n, y, 1 - x), sibling),
            "sy": (view(n, 1 - y, x), view(n, 1 - y, x), sibling),
            "sf": (view(n, 1 - y, 1 - x), view(n, 1 - y, 1 - x), sibling),
        }[kind]
        lane = kinds.index(kind)
        return remote(source, target, plane_send.at[lane, n], plane_recv.at[lane, n], where)

    def other(n, yy, xx):
        group = yy * 4 + xx * 2 + 1 - core
        rows, columns = owns[n].shape
        if n < 3:
            return joined_out.at[pl.ds(group * rows, rows), pl.ds(n * columns, columns)]
        return wo_out.at[pl.ds(0, rows), pl.ds(pl.multiple_of(group * columns, columns), columns)]

    greet(line)
    hidden = LineGather(hidden_ref, hidden_out, line_send, line_recv, line)
    locals_ = [pltpu.make_async_copy(hidden_ref, hidden.view(z), local_sem.at[4])]
    locals_ += [pltpu.make_async_copy(owns[n], view(n, y, x), local_sem.at[n]) for n in range(4)]
    hidden.begin()
    for n in range(4):
        for kind in ("x", "y", "s"):
            copy(kind, n).start()
    for local in locals_:
        local.start()
    for n in range(4):
        landed(view(n, y, 1 - x), plane_recv.at[0, n])
        copy("fy", n).start()
        copy("sx", n).start()
        landed(view(n, 1 - y, x), plane_recv.at[1, n])
        copy("fx", n).start()
        copy("sy", n).start()
    hidden.advance(0)
    for n in range(4):
        landed(view(n, 1 - y, 1 - x, 0), plane_recv.at[3, n])
        landed(view(n, 1 - y, 1 - x, 1), plane_recv.at[4, n])
        copy("sf", n).start()
    for step in range(1, line - 1):
        hidden.advance(step)
    for n in range(4):
        landed(other(n, y, x), plane_recv.at[2, n])
        landed(other(n, y, 1 - x), plane_recv.at[5, n])
        landed(other(n, 1 - y, x), plane_recv.at[6, n])
        landed(other(n, 1 - y, 1 - x), plane_recv.at[7, n])
    hidden.finish()
    for n in range(4):
        for kind in kinds:
            copy(kind, n).wait_send()
    for local in locals_:
        local.wait()


def start_exchange(hidden, w_query, w_key, w_value, w_out, collective_id):
    line = 4
    any_ref = pl.BlockSpec(memory_space=pl.ANY)
    dma = pltpu.SemaphoreType.DMA
    rows, width = hidden.shape
    part, columns = w_query.shape
    low = jnp.bfloat16
    return pl.pallas_call(
        functools.partial(start_kernel, line),
        out_shape=(
            jax.ShapeDtypeStruct((line * rows, width), low),
            jax.ShapeDtypeStruct((8 * part, 3 * columns), low),
            jax.ShapeDtypeStruct((w_out.shape[0], 8 * w_out.shape[1]), low),
        ),
        in_specs=[any_ref] * 5,
        out_specs=[any_ref] * 3,
        scratch_shapes=[dma((5,)), dma((2, line)), dma((2, line)), dma((8, 4)), dma((8, 4))],
        compiler_params=pltpu.CompilerParams(collective_id=collective_id, has_side_effects=True),
        cost_estimate=pl.CostEstimate(flops=0, bytes_accessed=150 << 20, transcendentals=0),
        name="start_exchange",
    )(hidden, w_query, w_key, w_value, w_out)


def line_gather_kernel(line, own_ref, out_ref, local_sem, send_sem, recv_sem):
    greet(line)
    gather = LineGather(own_ref, out_ref, send_sem, recv_sem, line)
    local = pltpu.make_async_copy(own_ref, gather.view(gather.spot[3]), local_sem)
    gather.begin()
    local.start()
    for step in range(line - 1):
        gather.advance(step)
    gather.finish()
    local.wait()


def line_gather(own, collective_id):
    line = 4
    any_ref = pl.BlockSpec(memory_space=pl.ANY)
    dma = pltpu.SemaphoreType.DMA
    return pl.pallas_call(
        functools.partial(line_gather_kernel, line),
        out_shape=jax.ShapeDtypeStruct((line * own.shape[0], own.shape[1]), own.dtype),
        in_specs=[any_ref],
        out_specs=any_ref,
        scratch_shapes=[dma(()), dma((2, line)), dma((2, line))],
        compiler_params=pltpu.CompilerParams(collective_id=collective_id, has_side_effects=True),
        cost_estimate=pl.CostEstimate(flops=0, bytes_accessed=150 << 20, transcendentals=0),
        name="line_gather",
    )(own)


class LineReduce:
    def __init__(self, part, up, down, send_sem, recv_sem, line):
        self.part, self.up, self.down = part, up, down
        self.send_sem, self.recv_sem, self.line = send_sem, recv_sem, line
        self.spot = place()

    def copy(self, sign, goal):
        y, x, core, z = self.spot
        lane = (1 - sign) // 2
        target = self.up if sign > 0 else self.down
        return remote(
            self.part.at[goal], target.at[goal], self.send_sem.at[lane, goal], self.recv_sem.at[lane, goal],
            (y, x, core, z + sign),
        )

    def order(self, i):
        z = self.spot[3]
        return either(self.line - 1 - i, i, z * 2 // self.line)

    def lead(self, goal):
        z = self.spot[3]
        pl.when((z == 0) & (goal > 0))(self.copy(1, goal).start)
        pl.when((z == self.line - 1) & (goal < z))(self.copy(-1, goal).start)

    def advance(self, unit, total_ref):
        z, line = self.spot[3], self.line
        for sign in (1, -1):
            goal = line - 1 - unit + z if sign > 0 else unit - line + 1 + z
            live = ((z > 0) & (goal < line)) if sign > 0 else ((z < line - 1) & (goal >= 0))
            inbox = self.up if sign > 0 else self.down

            @pl.when(live)
            def _():
                self.copy(sign, goal).wait_recv()
                if unit < line - 1:
                    self.part[goal] = (
                        self.part[goal].astype(jnp.float32) + inbox[goal].astype(jnp.float32)
                    ).astype(jnp.bfloat16)
                    self.copy(sign, goal).start()
                else:
                    total_ref[...] += inbox[goal].astype(jnp.float32)

    def finish(self):
        z = self.spot[3]

        def step(goal, carry):
            pl.when(goal > z)(self.copy(1, goal).wait_send)
            pl.when(goal < z)(self.copy(-1, goal).wait_send)
            return carry

        lax.fori_loop(0, self.line, step, 0)


def mixed_out_kernel(line, mixed_ref, w_ref, residual_ref, gain_ref, router_ref,
                     x_ref, hidden_ref, probs_ref, part, up, down, send_sem, recv_sem):
    rows, width = x_ref.shape
    greet(line)
    reduce = LineReduce(part, up, down, send_sem, recv_sem, line)
    z = reduce.spot[3]

    def term(i, carry):
        goal = reduce.order(i)
        first = pl.multiple_of(goal * rows, rows)
        for column in range(0, width, 512):
            piece = slice(column, column + 512)
            value = jnp.dot(mixed_ref[pl.ds(first, rows), :], w_ref[:, piece], preferred_element_type=jnp.float32)

            @pl.when(goal == z)
            def _():
                x_ref[:, piece] = value

            part[goal, :, piece] = value.astype(jnp.bfloat16)
        reduce.lead(goal)
        return carry

    lax.fori_loop(0, line, term, 0)
    for unit in range(1, line):
        reduce.advance(unit, x_ref)
    x_one = x_ref[...] + residual_ref[...].astype(jnp.float32)
    x_ref[...] = x_one
    scale = lax.rsqrt(jnp.mean(x_one * x_one, axis=-1, keepdims=True) + norm_eps)
    hidden = (x_one * scale * gain_ref[...]).astype(jnp.bfloat16)
    hidden_ref[...] = hidden
    logits = lax.dot_general(
        router_ref[...], hidden, (((1,), (1,)), ((), ())), preferred_element_type=jnp.float32
    )
    shifted = jnp.exp(logits - jnp.max(logits, axis=0, keepdims=True))
    probs_ref[...] = shifted / jnp.sum(shifted, axis=0, keepdims=True)
    reduce.finish()


def mixed_out(mixed, w_out, residual, gain, router_turned, collective_id):
    line = 4
    rows, width = residual.shape
    experts = router_turned.shape[0]
    vmem = pl.BlockSpec(memory_space=pltpu.VMEM)
    dma = pltpu.SemaphoreType.DMA
    block = pltpu.VMEM((line, rows, width), jnp.bfloat16)
    return pl.pallas_call(
        functools.partial(mixed_out_kernel, line),
        out_shape=(
            jax.ShapeDtypeStruct((rows, width), jnp.float32),
            jax.ShapeDtypeStruct((rows, width), jnp.bfloat16),
            jax.ShapeDtypeStruct((experts, rows), jnp.float32),
        ),
        in_specs=[vmem] * 5,
        out_specs=[vmem] * 3,
        scratch_shapes=[block, block, block, dma((2, line)), dma((2, line))],
        compiler_params=pltpu.CompilerParams(
            collective_id=collective_id, has_side_effects=True, vmem_limit_bytes=56 << 20
        ),
        cost_estimate=pl.CostEstimate(flops=0, bytes_accessed=150 << 20, transcendentals=0),
        name="mixed_out",
    )(mixed, w_out, residual, gain.reshape(1, width), router_turned)


def visible_block(row_paths, key_paths, key_valid, row_first):
    row_count = row_paths.shape[1]
    key_count = key_paths.shape[1]
    key_segment = key_paths[0][None, :]
    on_path = (
        (key_segment == row_paths[0][:, None])
        | (key_segment == row_paths[1][:, None])
        | (key_segment == row_paths[2][:, None])
    )
    row_place = row_first + lax.iota(jnp.int32, row_count)
    key_place = lax.iota(jnp.int32, key_count)
    earlier = key_place[None, :] <= row_place[:, None]
    return on_path & earlier & (key_valid[None, :] == 1) | (
        key_place[None, :] == row_place[:, None]
    )


def rotation(positions, head_dim):
    half = head_dim // 2
    freqs = jnp.exp(-jnp.log(rope_base) * 2.0 * lax.iota(jnp.float32, half) / head_dim)
    angles = positions.astype(jnp.float32)[:, None] * freqs[None, :]
    return (jnp.cos(angles), jnp.sin(angles))


def rotate(values, cosine, sine):
    half = values.shape[-1] // 2
    first = values[..., :half]
    second = values[..., half:]
    cosine = cosine[:, None, :]
    sine = sine[:, None, :]
    return jnp.concatenate(
        (first * cosine - second * sine, second * cosine + first * sine), axis=-1
    )


def unrotate(grads, cosine, sine):
    half = grads.shape[-1] // 2
    first = grads[..., :half]
    second = grads[..., half:]
    cosine = cosine[:, None, :]
    sine = sine[:, None, :]
    return jnp.concatenate(
        (first * cosine + second * sine, second * cosine - first * sine), axis=-1
    )


def rms_apply(values, gain):
    scale = lax.rsqrt(jnp.mean(values * values, axis=-1, keepdims=True) + norm_eps)
    return (values * scale * gain, scale)


def rms_grad(values, scale, gain, grads, inner, width):
    grad_values = scale * gain * grads - values * scale**3 * inner / width
    grad_gain = jnp.sum(grads * values * scale, axis=0)
    return (grad_values, grad_gain)


def tensor_sums(pair):
    return lax.psum((pair[0], pair[1]), "tensor")


def heads_to_rows(term, rows):
    return lax.psum_scatter(
        term(jnp.int32(0), rows * lax.axis_size("tensor")).astype(jnp.bfloat16),
        "tensor",
        scatter_dimension=0,
        tiled=True,
    ).astype(jnp.float32)


def sum_over_dp(rows):
    dp = lax.axis_size("dp")
    pieces = rows.reshape(dp, rows.shape[0] // dp, rows.shape[1])
    return lax.psum_scatter(pieces, "dp", scatter_dimension=0, tiled=False)


def sum_over_tensor(part):
    return lax.psum_scatter(part, "tensor", scatter_dimension=0, tiled=True)


def body(
    residual,
    attn_gain,
    w_query,
    w_key,
    w_value,
    query_gain,
    key_gain,
    w_out,
    moe_gain,
    router,
    w_gate,
    w_up,
    w_down,
    segment_path,
    token_valid,
    routes,
    route_order,
    cotangent,
):
    tensor_rank = lax.axis_index("tensor")
    tok_dev, width = residual.shape
    seq_len = segment_path.shape[1]
    top_count = routes.shape[1]
    experts = router.shape[1]
    local_experts = w_gate.shape[0]
    dp_groups = experts // local_experts
    capacity = 9 * tok_dev * top_count // (8 * experts)
    full_width = H * HD
    block_rows = min(512, seq_len)
    block_count = seq_len // block_rows
    score_scale = HD ** (-0.5)
    everyone = ("dp", "tensor")
    direct = dp_groups == 8 and lax.axis_size("tensor") == 4
    first_expert = lax.axis_index("dp") * local_experts
    slot_rows = padded(capacity, 8)
    valid_dev = lax.dynamic_slice_in_dim(token_valid, tensor_rank * tok_dev, tok_dev)
    slots_own = slot_table(routes, route_order, valid_dev, experts, capacity)
    slots_all = lax.all_gather(slots_own.astype(jnp.bfloat16), everyone, axis=0)
    slots = lax.dynamic_slice_in_dim(slots_all, first_expert, local_experts, 1).astype(jnp.int32)
    blocks = slots.shape[0]
    cots_all = lax.all_gather(cotangent, everyone, axis=0, tiled=True)
    c_slots = dispatch(slots, None, cots_all, slot_rows)
    head_cols = w_query.shape[1]
    local_heads = head_cols // HD
    residual_float = residual.astype(jnp.float32)
    normed_one, scale_one = rms_apply(residual_float, attn_gain)
    hidden = normed_one.astype(jnp.bfloat16)
    if direct:
        hidden_all, joined_weight, gathered_out = start_exchange(hidden, w_query, w_key, w_value, w_out, 3)
    else:
        hidden_all = lax.all_gather(hidden, "tensor", axis=0, tiled=True)
        joined_weight = jnp.concatenate(
            [lax.all_gather(w, "dp", axis=0, tiled=True) for w in (w_query, w_key, w_value)], axis=1
        )
        gathered_out = lax.all_gather(w_out, "dp", axis=1, tiled=True)
    projected = jnp.dot(hidden_all, joined_weight, preferred_element_type=jnp.float32)
    q_raw = projected[:, :head_cols]
    k_raw = projected[:, head_cols : 2 * head_cols]
    value_low = projected[:, 2 * head_cols :].astype(jnp.bfloat16).reshape(seq_len, local_heads, HD)
    query_sq, key_sq = tensor_sums((jnp.sum(q_raw * q_raw, axis=1), jnp.sum(k_raw * k_raw, axis=1)))
    query_scale = lax.rsqrt(query_sq / full_width + norm_eps)[:, None]
    key_scale = lax.rsqrt(key_sq / full_width + norm_eps)[:, None]
    query_gain_dev = lax.dynamic_slice_in_dim(query_gain, tensor_rank * head_cols, head_cols)
    key_gain_dev = lax.dynamic_slice_in_dim(key_gain, tensor_rank * head_cols, head_cols)
    block_starts = lax.iota(jnp.int32, block_count) * block_rows

    def block_mask(row_first):
        row_paths = lax.dynamic_slice_in_dim(segment_path, row_first, block_rows, 1)
        return visible_block(row_paths, segment_path, token_valid, row_first)

    def count_seen(row_first):
        return jnp.sum(block_mask(row_first).astype(jnp.int32), axis=1)

    positions = lax.map(count_seen, block_starts).reshape(seq_len) - 1
    cosine, sine = rotation(positions, HD)
    query_low = rotate(
        (q_raw * query_scale * query_gain_dev).reshape(seq_len, local_heads, HD), cosine, sine
    ).astype(jnp.bfloat16)
    key_low = rotate(
        (k_raw * key_scale * key_gain_dev).reshape(seq_len, local_heads, HD), cosine, sine
    ).astype(jnp.bfloat16)

    def attend(row_first):
        visible = block_mask(row_first)
        query_block = lax.dynamic_slice_in_dim(query_low, row_first, block_rows, 0)
        scores = (
            jnp.einsum("qhd,khd->hqk", query_block, key_low, preferred_element_type=jnp.float32)
            * score_scale
        )
        scores = jnp.where(visible[None], scores, masked_score)
        top_score = jnp.max(scores, axis=-1, keepdims=True)
        exp_scores = jnp.exp(scores - top_score)
        total = jnp.sum(exp_scores, axis=-1, keepdims=True)
        weights_low = (exp_scores / total).astype(jnp.bfloat16)
        mixed_block = jnp.einsum(
            "hqk,khd->qhd", weights_low, value_low, preferred_element_type=jnp.float32
        )
        return (mixed_block.astype(jnp.bfloat16), (top_score + jnp.log(total))[..., 0])

    mixed_blocks, log_totals = lax.map(attend, block_starts)
    attn_mixed = mixed_blocks.reshape(seq_len, head_cols)

    if direct:
        x_one, hidden_two, gates_own = mixed_out(attn_mixed, gathered_out, residual, moe_gain, router.T, 4)
        probs = gates_own.T
    else:

        def attn_term(first_row, row_count):
            return jnp.dot(attn_mixed, gathered_out, preferred_element_type=jnp.float32)

        x_one = residual_float + heads_to_rows(attn_term, tok_dev)
        hidden_two = rms_apply(x_one, moe_gain)[0].astype(jnp.bfloat16)
        logits = jnp.dot(hidden_two, router, preferred_element_type=jnp.float32)
        probs = jax.nn.softmax(logits, axis=-1)
        gates_own = probs.T
    hidden_two, c_slots = lax.optimization_barrier((hidden_two, c_slots))
    scale_two = lax.rsqrt(jnp.mean(x_one * x_one, axis=-1, keepdims=True) + norm_eps)
    if direct:
        rows_all, gates_all = gather_all([hidden_two, gates_own], 1)
        gates_all = gates_all.reshape(-1, experts, tok_dev)
    else:
        gates_all = lax.all_gather(gates_own, everyone, axis=0)
        rows_all = lax.all_gather(hidden_two, everyone, axis=0, tiled=True)
    gates = lax.dynamic_slice_in_dim(gates_all, first_expert, local_experts, 1)
    x_slots, gate_slots = dispatch(slots, gates, rows_all, slot_rows)
    outs, grads, grad_w_gate, grad_w_up, grad_w_down = expert_pass(
        first_expert.reshape(1),
        x_slots,
        c_slots,
        gate_slots,
        w_gate,
        w_up,
        w_down,
        blocks,
        padded(slot_rows, 16),
    )
    if direct:
        grad_rows, out_part = reduce_all(slots, outs, grads, 2)
    else:
        out_part, grad_part = combine(slots, outs, grads)
        grad_rows = sum_over_tensor(sum_over_dp(grad_part)).astype(jnp.float32)
    out_part = sum_over_dp(out_part)
    grad_out = cotangent.astype(jnp.float32)
    grad_hidden_two = grad_rows[:, :width]
    grad_probs = grad_rows[:, width : width + experts]
    grad_logits = probs * (grad_probs - jnp.sum(probs * grad_probs, axis=-1, keepdims=True))
    router_float = router.astype(jnp.float32)
    grad_hidden_two = grad_hidden_two + lax.dot_general(
        grad_logits, router_float, (((1,), (1,)), ((), ())), precision=lax.Precision.HIGHEST
    )
    grad_router_part = lax.dot_general(
        hidden_two.astype(jnp.float32),
        grad_logits,
        (((0,), (0,)), ((), ())),
        precision=lax.Precision.HIGHEST,
    )
    inner_two = jnp.sum(grad_hidden_two * moe_gain * x_one, axis=-1, keepdims=True)
    grad_norm_two, grad_moe_gain_part = rms_grad(
        x_one, scale_two, moe_gain, grad_hidden_two, inner_two, width
    )
    grad_x_one = grad_out + grad_norm_two
    grad_attn_low = grad_x_one.astype(jnp.bfloat16)
    if direct:
        grad_attn_all = line_gather(grad_attn_low, 5)
    else:
        grad_attn_all = lax.all_gather(grad_attn_low, "tensor", axis=0, tiled=True)
    grad_out_weight = lax.dot_general(
        attn_mixed, grad_attn_all, (((0,), (0,)), ((), ())), preferred_element_type=jnp.float32
    )
    grad_mixed = (
        lax.dot_general(
            grad_attn_all,
            gathered_out,
            (((1,), (1,)), ((), ())),
            preferred_element_type=jnp.float32,
        )
        .astype(jnp.bfloat16)
        .reshape(seq_len, local_heads, HD)
    )

    def attend_back(carry, pieces):
        grad_key_sum, grad_value_sum = carry
        row_first, log_total = pieces
        visible = block_mask(row_first)
        query_block = lax.dynamic_slice_in_dim(query_low, row_first, block_rows, 0)
        grad_block = lax.dynamic_slice_in_dim(grad_mixed, row_first, block_rows, 0)
        scores = (
            jnp.einsum("qhd,khd->hqk", query_block, key_low, preferred_element_type=jnp.float32)
            * score_scale
        )
        scores = jnp.where(visible[None], scores, masked_score)
        weights = jnp.exp(scores - log_total[..., None])
        grad_weights = jnp.einsum(
            "qhd,khd->hqk", grad_block, value_low, preferred_element_type=jnp.float32
        )
        inner = jnp.sum(weights * grad_weights, axis=-1, keepdims=True)
        grad_scores = (weights * (grad_weights - inner)).astype(jnp.bfloat16)
        grad_query_block = (
            jnp.einsum("hqk,khd->qhd", grad_scores, key_low, preferred_element_type=jnp.float32)
            * score_scale
        )
        grad_key_sum = (
            grad_key_sum
            + jnp.einsum(
                "hqk,qhd->khd", grad_scores, query_block, preferred_element_type=jnp.float32
            )
            * score_scale
        )
        grad_value_sum = grad_value_sum + jnp.einsum(
            "hqk,qhd->khd",
            weights.astype(jnp.bfloat16),
            grad_block,
            preferred_element_type=jnp.float32,
        )
        return ((grad_key_sum, grad_value_sum), grad_query_block)

    zero_heads = jnp.zeros((seq_len, local_heads, HD), jnp.float32)
    (grad_key_all, grad_value_all), grad_query_blocks = lax.scan(
        attend_back, (zero_heads, zero_heads), (block_starts, log_totals)
    )
    grad_q_norm = unrotate(
        grad_query_blocks.reshape(seq_len, local_heads, HD), cosine, sine
    ).reshape(seq_len, head_cols)
    grad_k_norm = unrotate(grad_key_all, cosine, sine).reshape(seq_len, head_cols)
    query_inner, key_inner = tensor_sums(
        (
            jnp.sum(grad_q_norm * query_gain_dev * q_raw, axis=1),
            jnp.sum(grad_k_norm * key_gain_dev * k_raw, axis=1),
        )
    )
    grad_q_raw, grad_query_gain_dev = rms_grad(
        q_raw, query_scale, query_gain_dev, grad_q_norm, query_inner[:, None], full_width
    )
    grad_k_raw, grad_key_gain_dev = rms_grad(
        k_raw, key_scale, key_gain_dev, grad_k_norm, key_inner[:, None], full_width
    )
    grad_joined = jnp.concatenate(
        (grad_q_raw, grad_k_raw, grad_value_all.reshape(seq_len, head_cols)), axis=1
    ).astype(jnp.bfloat16)
    out_part, grad_joined = lax.optimization_barrier((out_part, grad_joined))
    block_out = (x_one + sum_over_tensor(out_part).astype(jnp.float32)).astype(jnp.bfloat16)
    grad_joined_weight = lax.dot_general(
        hidden_all, grad_joined, (((0,), (0,)), ((), ())), preferred_element_type=jnp.float32
    )

    def back_term(first_row, row_count):
        return lax.dot_general(
            grad_joined, joined_weight, (((1,), (1,)), ((), ())), preferred_element_type=jnp.float32
        )

    grad_hidden = heads_to_rows(back_term, tok_dev)
    inner_one = jnp.sum(grad_hidden * attn_gain * residual_float, axis=-1, keepdims=True)
    grad_norm_one, grad_attn_gain_part = rms_grad(
        residual_float, scale_one, attn_gain, grad_hidden, inner_one, width
    )
    grad_input = grad_x_one + grad_norm_one
    grad_w_query, grad_w_key, grad_w_value, grad_w_out = (
        lax.psum_scatter(
            grad_joined_weight[:, :head_cols].astype(jnp.bfloat16),
            "dp",
            scatter_dimension=0,
            tiled=True,
        ).astype(jnp.float32),
        lax.psum_scatter(
            grad_joined_weight[:, head_cols : 2 * head_cols].astype(jnp.bfloat16),
            "dp",
            scatter_dimension=0,
            tiled=True,
        ).astype(jnp.float32),
        lax.psum_scatter(
            grad_joined_weight[:, 2 * head_cols :].astype(jnp.bfloat16),
            "dp",
            scatter_dimension=0,
            tiled=True,
        ).astype(jnp.float32),
        lax.psum_scatter(
            grad_out_weight.astype(jnp.bfloat16), "dp", scatter_dimension=1, tiled=True
        ).astype(jnp.float32),
    )
    zero_width = jnp.zeros((full_width,), jnp.float32)
    grad_query_full = lax.dynamic_update_slice_in_dim(
        zero_width, grad_query_gain_dev, tensor_rank * head_cols, 0
    )
    grad_key_full = lax.dynamic_update_slice_in_dim(
        zero_width, grad_key_gain_dev, tensor_rank * head_cols, 0
    )
    summed = lax.psum(
        (grad_attn_gain_part, grad_moe_gain_part, grad_query_full, grad_key_full, grad_router_part),
        ("dp", "tensor"),
    )
    return (
        block_out,
        grad_input,
        summed[0],
        grad_w_query,
        grad_w_key,
        grad_w_value,
        summed[2],
        summed[3],
        grad_w_out,
        summed[1],
        summed[4],
        grad_w_gate,
        grad_w_up,
        grad_w_down,
    )


def solution(mesh):
    in_specs = (
        P(("dp", "tensor"), None),
        P(),
        P("dp", "tensor"),
        P("dp", "tensor"),
        P("dp", "tensor"),
        P(),
        P(),
        P("tensor", "dp"),
        P(),
        P(),
        P("dp", None, "tensor"),
        P("dp", None, "tensor"),
        P("dp", "tensor", None),
        P(None, "dp"),
        P("dp"),
        P(("dp", "tensor"), None),
        P(("dp", "tensor"), None),
        P(("dp", "tensor"), None),
    )
    out_specs = (
        P(("dp", "tensor"), None),
        P(("dp", "tensor"), None),
        P(),
        P("dp", "tensor"),
        P("dp", "tensor"),
        P("dp", "tensor"),
        P(),
        P(),
        P("tensor", "dp"),
        P(),
        P(),
        P("dp", None, "tensor"),
        P("dp", None, "tensor"),
        P("dp", "tensor", None),
    )
    return jax.shard_map(body, mesh=mesh, in_specs=in_specs, out_specs=out_specs, check_vma=False)
```

```python
import functools

import jax
import jax.numpy as jnp
from jax import lax
from jax.experimental import pallas as pl
from jax.experimental.pallas import tpu as pltpu
from jax.sharding import PartitionSpec as P

H = 16
HD = 128


norm_eps = 1e-05
rope_base = 10000.0
masked_score = -1e30


def padded(count, step):
    return -(-count // step) * step


def slot_table(routes, route_order, valid, experts, capacity):
    far = jnp.int32(1 << 30)
    expert = lax.iota(jnp.int32, experts)[:, None, None]
    hits = (routes[None] == expert) & (valid[None, :, None] == 1)
    order = jnp.min(jnp.where(hits, route_order[None], far), axis=-1)
    ranks = jnp.sum((order[:, None, :] < order[:, :, None]).astype(jnp.int32), axis=-1)
    return jnp.where((order < far) & (ranks < capacity), ranks, -1)


def slot_hits(slots, expert, rows):
    tokens = slots.shape[-1]
    return lax.broadcasted_iota(jnp.int32, (rows, tokens), 0) == slots[expert : expert + 1, :]


def dispatch_kernel(slots_ref, gates_ref, rows_ref, x_ref, gate_ref):
    pair, experts, tokens = slots_ref.shape
    rows = x_ref.shape[1] // pair
    width = rows_ref.shape[1]
    picks = []
    for b in range(pair):
        slots = slots_ref[b]
        pieces = []
        for e in range(experts):
            hit = slot_hits(slots, e, rows)
            pieces.append(hit.astype(jnp.float32))
            if gate_ref is not None:
                gate = jnp.sum(jnp.where(hit, gates_ref[b, e : e + 1, :], 0.0), axis=1, keepdims=True)
                gate_ref[e, b * rows : (b + 1) * rows, :] = jnp.broadcast_to(gate, (rows, 128))
        picks.append(jnp.concatenate(pieces, axis=0).astype(jnp.bfloat16))
    step = min(512, width)
    for first in range(0, width, step):
        parts = [
            jnp.dot(
                picks[b],
                rows_ref[b * tokens : (b + 1) * tokens, first : first + step],
                preferred_element_type=jnp.float32,
            )
            for b in range(pair)
        ]
        for e in range(experts):
            x_ref[e, :, first : first + step] = jnp.concatenate(
                [part[e * rows : (e + 1) * rows] for part in parts], axis=0
            ).astype(jnp.bfloat16)


def plain_dispatch_kernel(slots_ref, rows_ref, x_ref):
    dispatch_kernel(slots_ref, None, rows_ref, x_ref, None)


def dispatch(slots, gates, rows_all, rows):
    blocks, experts, tokens = slots.shape
    width = rows_all.shape[1]
    pair = 2
    out = jax.ShapeDtypeStruct((experts, blocks * rows, width), jnp.bfloat16)
    table = pl.BlockSpec((pair, experts, tokens), lambda i: (i, 0, 0))
    source = pl.BlockSpec((pair * tokens, width), lambda i: (i, 0))
    target = pl.BlockSpec((experts, pair * rows, width), lambda i: (0, i, 0))
    settings = dict(
        grid=(blocks // pair,),
        compiler_params=pltpu.CompilerParams(vmem_limit_bytes=50 << 20),
        cost_estimate=pl.CostEstimate(
            flops=2 * blocks * experts * rows * tokens * width,
            bytes_accessed=2 * blocks * (tokens + experts * rows) * width,
            transcendentals=0,
        ),
    )
    if gates is None:
        return pl.pallas_call(
            plain_dispatch_kernel, out_shape=out, in_specs=[table, source], out_specs=target, name="pick", **settings
        )(slots, rows_all)
    return pl.pallas_call(
        dispatch_kernel,
        out_shape=(out, jax.ShapeDtypeStruct((experts, blocks * rows, 128), jnp.float32)),
        in_specs=[table, table, source],
        out_specs=[target, pl.BlockSpec((experts, pair * rows, 128), lambda i: (0, i, 0))],
        name="dispatch",
        **settings,
    )(slots, gates, rows_all)


def turned(left, right):
    return lax.dot_general(left, right, (((0,), (0,)), ((), ())), preferred_element_type=jnp.float32)


def across(left, right):
    return lax.dot_general(left, right, (((1,), (1,)), ((), ())), preferred_element_type=jnp.float32)


def expert_kernel(rows, first_ref, x_ref, c_ref, gate_ref, wg_ref, wu_ref, wd_ref,
                  o_ref, dx_ref, dwg_ref, dwu_ref, dwd_ref):
    expert = pl.program_id(0)
    tile, width = x_ref.shape[1:]
    units = wg_ref.shape[2]
    room = o_ref.shape[2]
    blocks = tile // rows
    gate = gate_ref[0, :, 0:1]
    x = x_ref[0]
    c = c_ref[0]
    gate_pre = jnp.dot(x, wg_ref[0], preferred_element_type=jnp.float32)
    up_pre = jnp.dot(x, wu_ref[0], preferred_element_type=jnp.float32)
    back = across(c, wd_ref[0])
    sig = jax.nn.sigmoid(gate_pre)
    silu = gate_pre * sig
    act = (silu * up_pre).astype(jnp.bfloat16)
    act_float = act.astype(jnp.float32)
    grad_gate = jnp.sum(act_float * back, axis=1, keepdims=True)
    grad_act = back * gate
    grad_gate_pre = (grad_act * up_pre * sig * (1.0 + gate_pre * (1.0 - sig))).astype(jnp.bfloat16)
    grad_up_pre = (grad_act * silu).astype(jnp.bfloat16)
    gated = (act_float * gate).astype(jnp.bfloat16)

    def spread(values):
        values = values.reshape(blocks, rows, values.shape[1])
        if room > rows:
            empty = jnp.zeros((blocks, room - rows, values.shape[2]), jnp.float32)
            values = jnp.concatenate((values, empty), axis=1)
        return values.astype(jnp.bfloat16)

    step = min(512, width)
    for first in range(0, width, step):
        part = slice(first, first + step)
        out = jnp.dot(act, wd_ref[0, :, part], preferred_element_type=jnp.float32) * gate
        o_ref[:, 0, :, part] = spread(out)
        grad = across(grad_gate_pre, wg_ref[0, part, :]) + across(grad_up_pre, wu_ref[0, part, :])
        dx_ref[:, 0, :, part] = spread(grad)
    lanes = lax.broadcasted_iota(jnp.int32, (tile, 128), 1)
    dx_ref[:, 0, :, width:] = spread(jnp.where(lanes == first_ref[0] + expert, grad_gate, 0.0))

    @pl.when(pl.program_id(1) == 0)
    def _():
        for ref in (dwg_ref, dwu_ref, dwd_ref):
            ref[...] = jnp.zeros_like(ref)

    for first in range(0, width, step):
        part = slice(first, first + step)
        dwg_ref[0, part, :] += turned(x_ref[0, :, part], grad_gate_pre)
        dwu_ref[0, part, :] += turned(x_ref[0, :, part], grad_up_pre)
        dwd_ref[0, :, part] += turned(gated, c_ref[0, :, part])


def expert_pass(first_expert, x_slots, c_slots, gate_slots, w_gate, w_up, w_down, blocks, room):
    experts, total, width = x_slots.shape
    units = w_gate.shape[2]
    rows = total // blocks
    group = next(n for n in (16, 8, 4, 2, 1) if blocks % n == 0 and (n * rows <= 768 or n == 1))
    tile = group * rows
    extra = 128
    tall = pl.BlockSpec((1, width, units), lambda e, r, _: (e, 0, 0))
    wide = pl.BlockSpec((1, units, width), lambda e, r, _: (e, 0, 0))
    slot = pl.BlockSpec((1, tile, width), lambda e, r, _: (e, r, 0))
    kernel = functools.partial(expert_kernel, rows)
    return pl.pallas_call(
        kernel,
        grid_spec=pltpu.PrefetchScalarGridSpec(
            num_scalar_prefetch=1,
            grid=(experts, total // tile),
            in_specs=[slot, slot, pl.BlockSpec((1, tile, 128), lambda e, r, _: (e, r, 0)), tall, tall, wide],
            out_specs=[
                pl.BlockSpec((group, 1, room, width), lambda e, r, _: (r, e, 0, 0)),
                pl.BlockSpec((group, 1, room, width + extra), lambda e, r, _: (r, e, 0, 0)),
                tall, tall, wide,
            ],
        ),
        out_shape=(
            jax.ShapeDtypeStruct((blocks, experts, room, width), jnp.bfloat16),
            jax.ShapeDtypeStruct((blocks, experts, room, width + extra), jnp.bfloat16),
            jax.ShapeDtypeStruct(w_gate.shape, jnp.float32),
            jax.ShapeDtypeStruct(w_up.shape, jnp.float32),
            jax.ShapeDtypeStruct(w_down.shape, jnp.float32),
        ),
        compiler_params=pltpu.CompilerParams(vmem_limit_bytes=60 << 20),
        cost_estimate=pl.CostEstimate(
            flops=18 * experts * total * width * units,
            bytes_accessed=8 * experts * total * width + 18 * experts * width * units,
            transcendentals=experts * total * units,
        ),
        name="experts",
    )(first_expert, x_slots, c_slots, gate_slots, w_gate, w_up, w_down)


def combine_kernel(slots_ref, o_ref, dx_ref, out_ref, grad_ref):
    _, experts, tokens = slots_ref.shape
    room, width = o_ref.shape[2:]
    slots = slots_ref[0]
    picks = jnp.concatenate(
        [slot_hits(slots, e, room).astype(jnp.float32) for e in range(experts)], axis=0
    ).astype(jnp.bfloat16)
    for source, target in ((o_ref, out_ref), (dx_ref, grad_ref)):
        columns = target.shape[1]
        for first in range(0, columns, 512):
            part = slice(first, min(first + 512, columns))
            values = source[0, :, :, part].reshape(experts * room, part.stop - first)
            target[:, part] = turned(picks, values).astype(jnp.bfloat16)


def combine(slots, outs, grads):
    blocks, experts, tokens = slots.shape
    room, width = outs.shape[2:]
    wider = grads.shape[3]
    return pl.pallas_call(
        combine_kernel,
        grid=(blocks,),
        out_shape=(
            jax.ShapeDtypeStruct((blocks * tokens, width), jnp.bfloat16),
            jax.ShapeDtypeStruct((blocks * tokens, wider), jnp.bfloat16),
        ),
        in_specs=[
            pl.BlockSpec((1, experts, tokens), lambda i: (i, 0, 0)),
            pl.BlockSpec((1, experts, room, width), lambda i: (i, 0, 0, 0)),
            pl.BlockSpec((1, experts, room, wider), lambda i: (i, 0, 0, 0)),
        ],
        out_specs=[
            pl.BlockSpec((tokens, width), lambda i: (i, 0)),
            pl.BlockSpec((tokens, wider), lambda i: (i, 0)),
        ],
        compiler_params=pltpu.CompilerParams(vmem_limit_bytes=50 << 20),
        cost_estimate=pl.CostEstimate(
            flops=2 * blocks * experts * room * tokens * (width + wider),
            bytes_accessed=2 * blocks * (tokens + experts * room) * (width + wider),
            transcendentals=0,
        ),
        name="combine",
    )(slots, outs, grads)


MESH = pl.DeviceIdType.MESH


def place():
    dp, z = lax.axis_index("dp"), lax.axis_index("tensor")
    return dp // 4, dp // 2 % 2, dp % 2, z


def peer(y, x, core, z):
    return (y * 4 + x * 2 + core, z)


def block_of(y, x, core, z):
    return (y * 4 + x * 2 + core) * 4 + z


def greet(line):
    y, x, core, z = place()
    barrier = pltpu.get_barrier_semaphore()
    for near in ((y, x, 1 - core, z), (y, 1 - x, core, z), (1 - y, x, core, z)):
        pl.semaphore_signal(barrier, inc=1, device_id=peer(*near), device_id_type=MESH)

    @pl.when(z > 0)
    def _():
        pl.semaphore_signal(barrier, inc=1, device_id=peer(y, x, core, z - 1), device_id_type=MESH)

    @pl.when(z < line - 1)
    def _():
        pl.semaphore_signal(barrier, inc=1, device_id=peer(y, x, core, z + 1), device_id_type=MESH)

    pl.semaphore_wait(barrier, 3 + (z + line - 1) // line + (2 * line - 2 - z) // line)


def gather_kernel(line, count, *refs):
    owns, outs = refs[:count], refs[count : 2 * count]
    local_sem, send_sem, recv_sem = refs[2 * count :]
    y, x, core, z = place()
    greet(line)
    waits = []
    sent = [0]

    def send(cond, n, block, source_own, target):
        rows = owns[n].shape[0]
        part = pl.ds(block * rows, rows)
        copy = pltpu.make_async_remote_copy(
            src_ref=owns[n] if source_own else outs[n].at[part],
            dst_ref=outs[n].at[part],
            send_sem=send_sem.at[sent[0]],
            recv_sem=recv_sem.at[n, block],
            device_id=peer(*target),
            device_id_type=MESH,
        )
        sent[0] += 1
        waits.append((cond, copy))
        if cond is None:
            copy.start()
        else:
            pl.when(cond)(copy.start)

    def arrive(n, block):
        rows = owns[n].shape[0]
        part = pl.ds(block * rows, rows)
        pltpu.make_async_copy(outs[n].at[part], outs[n].at[part], recv_sem.at[n, block]).wait()

    def both(a, b):
        return b if a is None else a & b

    sibling, near_x, near_y = (y, x, 1 - core, z), (y, 1 - x, core, z), (1 - y, x, core, z)
    mine = block_of(y, x, core, z)
    locals_ = []
    for n in range(count):
        rows = owns[n].shape[0]
        own_copy = pltpu.make_async_copy(owns[n], outs[n].at[pl.ds(mine * rows, rows)], local_sem.at[n])
        own_copy.start()
        locals_.append(own_copy)

    def own_column(n, step, sign):
        zz = z + sign * step
        valid = None if step == 0 else (zz >= 0) & (zz < line)
        block = block_of(y, x, core, zz)

        def fetch():
            if step:
                arrive(n, block)

        if step:
            pl.when(valid)(fetch)
        if step == 0:
            send(z > 0, n, block, True, (y, x, core, z - 1))
            send(z < line - 1, n, block, True, (y, x, core, z + 1))
        elif sign < 0:
            send(both(valid, z < line - 1), n, block, False, (y, x, core, z + 1))
        else:
            send(both(valid, z > 0), n, block, False, (y, x, core, z - 1))
        send(valid, n, block, step == 0, near_x)
        send(valid, n, block, step == 0, near_y)
        send(valid, n, block, step == 0, sibling)

    def next_column(n, step, sign, along_x):
        zz = z + sign * step
        valid = None if step == 0 else (zz >= 0) & (zz < line)
        yy, xx = (y, 1 - x) if along_x else (1 - y, x)
        block = block_of(yy, xx, core, zz)
        if step:
            pl.when(valid)(lambda: arrive(n, block))
        else:
            arrive(n, block)
        if step % 2 == (0 if along_x else 1):
            send(valid, n, block, False, near_y if along_x else near_x)
        send(valid, n, block, False, sibling)

    def far_column(n, step, sign):
        zz = z + sign * step
        valid = None if step == 0 else (zz >= 0) & (zz < line)
        block = block_of(1 - y, 1 - x, core, zz)
        if step:
            pl.when(valid)(lambda: arrive(n, block))
        else:
            arrive(n, block)
        send(valid, n, block, False, sibling)

    def signs(step):
        return (1,) if step == 0 else (-1, 1)

    for n in range(count):
        own_column(n, 0, 1)
    for step in range(line + 1):
        for n in range(count):
            if step + 1 < line:
                for sign in signs(step + 1):
                    own_column(n, step + 1, sign)
            if step < line:
                for sign in signs(step):
                    next_column(n, step, sign, True)
                    next_column(n, step, sign, False)
            if step:
                for sign in signs(step - 1):
                    far_column(n, step - 1, sign)
    for yy in range(2):
        for xx in range(2):
            for zz in range(line):
                for n in range(count):
                    arrive(n, block_of(yy, xx, 1 - core, zz))
    for cond, copy in waits:
        if cond is None:
            copy.wait_send()
        else:
            pl.when(cond)(copy.wait_send)
    for copy in locals_:
        copy.wait()


def gather_all(arrays, collective_id):
    count = len(arrays)
    any_ref = pl.BlockSpec(memory_space=pl.ANY)
    line = lax.axis_size("tensor")
    devices = 8 * line
    return pl.pallas_call(
        functools.partial(gather_kernel, line, count),
        out_shape=[jax.ShapeDtypeStruct((devices * a.shape[0],) + a.shape[1:], a.dtype) for a in arrays],
        in_specs=[any_ref] * count,
        out_specs=[any_ref] * count,
        scratch_shapes=[
            pltpu.SemaphoreType.DMA((count,)),
            pltpu.SemaphoreType.DMA((count * 80,)),
            pltpu.SemaphoreType.DMA((count, devices)),
        ],
        compiler_params=pltpu.CompilerParams(collective_id=collective_id, has_side_effects=True),
        name="gather_all",
    )(*arrays)


def reduce_kernel(line, slots_ref, grads_ref, outs_ref, sum_ref, part_ref,
                  grad_in, out_in, out_stage, stage, near, far_x, far_y, from_x, from_y, up, down,
                  in_sem, part_sem, stage_sem, near_sem, send_sem, far_sem, x_sem, y_sem, line_sem):
    y, x, core, z = place()
    tokens, width = sum_ref.shape
    half = tokens // 2
    experts, room = grads_ref.shape[1:3]
    rounds = line
    greet(line)

    def goal(r):
        early = 1 - r // 2
        return (line - 1) * (r % 2) * early + (r - 1) * (1 - early)

    def block_at(q):
        r, j = q // 8, q % 8
        column = j % 4
        dy, dx = (column + 1) % 2, 1 - column // 2
        own = j // 4
        target_core = core * own + (1 - core) * (1 - own)
        return block_of((y + dy) % 2, (x + dx) % 2, target_core, goal(r))

    def load(q):
        b = block_at(q)
        return (
            pltpu.make_async_copy(grads_ref.at[b], grad_in.at[q % 2], in_sem.at[0, q % 2]),
            pltpu.make_async_copy(outs_ref.at[b], out_in.at[q % 2], in_sem.at[1, q % 2]),
        )

    def to_part(q):
        b = block_at(q)
        return pltpu.make_async_copy(out_stage.at[q % 2], part_ref.at[pl.ds(b * tokens, tokens)], part_sem.at[q % 2])

    def to_sibling(r, j):
        return pltpu.make_async_remote_copy(
            src_ref=stage.at[j], dst_ref=near.at[r * 4 + j], send_sem=stage_sem.at[j], recv_sem=near_sem.at[r * 4 + j],
            device_id=peer(y, x, 1 - core, z), device_id_type=MESH,
        )

    near_x, near_y = peer(y, 1 - x, core, z), peer(1 - y, x, core, z)

    def rows(h):
        return pl.ds(h * half, half)

    def cross(kind, r):
        column, h, target, sem, index, lane = {
            "far_x": (0, 0, far_x.at[r], far_sem.at[0, r], near_x, 0),
            "far_y": (0, 1, far_y.at[r], far_sem.at[1, r], near_y, 1),
            "x0": (1, 0, from_x.at[r, rows(0)], x_sem.at[r, 0], near_x, 2),
            "x1": (1, 1, from_x.at[r, rows(1)], x_sem.at[r, 1], near_x, 3),
            "y0": (2, 0, from_y.at[r, rows(0)], y_sem.at[r, 0], near_y, 4),
            "y1": (2, 1, from_y.at[r, rows(1)], y_sem.at[r, 1], near_y, 5),
        }[kind]
        return pltpu.make_async_remote_copy(
            src_ref=near.at[r * 4 + column, rows(h)], dst_ref=target, send_sem=send_sem.at[lane, r], recv_sem=sem,
            device_id=index, device_id_type=MESH,
        )

    def along(sign, r):
        target = up if sign > 0 else down
        lane = 0 if sign > 0 else 1
        return pltpu.make_async_remote_copy(
            src_ref=near.at[r * 4 + 3], dst_ref=target.at[r], send_sem=send_sem.at[6 + lane, r], recv_sem=line_sem.at[lane, r],
            device_id=peer(y, x, core, z + sign), device_id_type=MESH,
        )

    def term(q, source, target_width, store):
        picks = jnp.concatenate(
            [slot_hits(slots_ref[block_at(q)], e, room).astype(jnp.float32) for e in range(experts)], axis=0
        ).astype(jnp.bfloat16)
        for first in range(0, target_width, 512):
            part = slice(first, min(first + 512, target_width))
            values = source[q % 2, :, :, part].reshape(experts * room, part.stop - first)
            store(part, turned(picks, values))

    for copy in load(0):
        copy.start()

    def one(r, j, own):
        q = r * 8 + own * 4 + j
        for copy in load(q):
            copy.wait()

        @pl.when(q + 1 < rounds * 8)
        def _():
            for copy in load(q + 1):
                copy.start()

        if own:
            near_slot = r * 4 + j
            to_sibling(r, j).wait_recv()

            def keep(part, value):
                near[near_slot, :, part] = (value + near[near_slot, :, part].astype(jnp.float32)).astype(jnp.bfloat16)

            term(q, grad_in, width, keep)
        else:

            @pl.when(r > 0)
            def _():
                to_sibling(r - 1, j).wait_send()

            def keep(part, value):
                stage[j, :, part] = value.astype(jnp.bfloat16)

            term(q, grad_in, width, keep)
            to_sibling(r, j).start()

        @pl.when(q >= 2)
        def _():
            to_part(q - 2).wait()

        def put(part, value):
            out_stage[q % 2, :, part] = value.astype(jnp.bfloat16)

        term(q, out_in, out_stage.shape[2], put)
        to_part(q).start()

    def add(target, h, *sources):
        for first in range(0, width, 512):
            part = slice(first, min(first + 512, width))
            total = near[target, h, part].astype(jnp.float32)
            for source in sources:
                total = total + source(part).astype(jnp.float32)
            near[target, h, part] = total.astype(jnp.bfloat16)

    def work(s, carry):
        @pl.when(s < rounds)
        def _():
            r = s
            lax.fori_loop(0, 4, lambda j, c: (one(r, j, 0), c)[1], 0)
            lax.fori_loop(0, 4, lambda j, c: (one(r, j, 1), c)[1], 0)
            for kind in ("far_x", "far_y", "x0", "y1"):
                cross(kind, r).start()
            cross("far_y", r).wait_recv()
            add(r * 4 + 1, rows(1), lambda part: far_y[r, :, part])
            cross("x1", r).start()
            cross("far_x", r).wait_recv()
            add(r * 4 + 2, rows(0), lambda part: far_x[r, :, part])
            cross("y0", r).start()

        @pl.when((s >= 1) & (s < rounds + 1))
        def _():
            r = s - 1
            for kind in ("x0", "x1", "y0", "y1"):
                cross(kind, r).wait_recv()
            for h in range(2):
                add(
                    r * 4 + 3,
                    rows(h),
                    lambda part: from_x[r, rows(h), part],
                    lambda part: from_y[r, rows(h), part],
                )

        for hop in range(line - 1):
            r = s - 1 - hop
            live = (r >= 0) & (r < rounds)
            held = r * live.astype(jnp.int32)

            @pl.when(live & (goal(held) > z) & (z == hop))
            def _():
                if hop:
                    along(1, held).wait_recv()
                    for h in range(2):
                        add(held * 4 + 3, rows(h), lambda part: up[held, rows(h), part])
                along(1, held).start()

            @pl.when(live & (goal(held) < z) & (line - 1 - z == hop))
            def _():
                if hop:
                    along(-1, held).wait_recv()
                    for h in range(2):
                        add(held * 4 + 3, rows(h), lambda part: down[held, rows(h), part])
                along(-1, held).start()

        return carry

    lax.fori_loop(0, rounds + line - 1, work, 0)

    mine = (z + (z + 2) // 3) % 4 + z // 3
    sum_ref[...] = near[mine * 4 + 3].astype(jnp.float32)

    @pl.when(z > 0)
    def _():
        along(1, mine).wait_recv()
        sum_ref[...] += up[mine].astype(jnp.float32)

    @pl.when(z < line - 1)
    def _():
        along(-1, mine).wait_recv()
        sum_ref[...] += down[mine].astype(jnp.float32)

    def finish(r, carry):
        for kind in ("far_x", "far_y", "x0", "x1", "y0", "y1"):
            cross(kind, r).wait_send()

        @pl.when(goal(r) > z)
        def _():
            along(1, r).wait_send()

        @pl.when(goal(r) < z)
        def _():
            along(-1, r).wait_send()

        return carry

    lax.fori_loop(0, rounds, finish, 0)
    for j in range(4):
        to_sibling(rounds - 1, j).wait_send()
    for q in (rounds * 8 - 2, rounds * 8 - 1):
        to_part(q).wait()


def reduce_all(slots, outs, grads, collective_id):
    blocks, experts, tokens = slots.shape
    room, width = outs.shape[2:]
    wider = grads.shape[3]
    line = 4
    low = jnp.bfloat16
    any_ref = pl.BlockSpec(memory_space=pl.ANY)
    vmem = pl.BlockSpec(memory_space=pltpu.VMEM)
    dma = pltpu.SemaphoreType.DMA
    return pl.pallas_call(
        functools.partial(reduce_kernel, line),
        out_shape=(
            jax.ShapeDtypeStruct((tokens, wider), jnp.float32),
            jax.ShapeDtypeStruct((blocks * tokens, width), low),
        ),
        in_specs=[vmem, any_ref, any_ref],
        out_specs=[vmem, any_ref],
        scratch_shapes=[
            pltpu.VMEM((2, experts, room, wider), low),
            pltpu.VMEM((2, experts, room, width), low),
            pltpu.VMEM((2, tokens, width), low),
            pltpu.VMEM((4, tokens, wider), low),
            pltpu.VMEM((line * 4, tokens, wider), low),
            pltpu.VMEM((line, tokens // 2, wider), low),
            pltpu.VMEM((line, tokens // 2, wider), low),
            pltpu.VMEM((line, tokens, wider), low),
            pltpu.VMEM((line, tokens, wider), low),
            pltpu.VMEM((line, tokens, wider), low),
            pltpu.VMEM((line, tokens, wider), low),
            dma((2, 2)),
            dma((2,)),
            dma((4,)),
            dma((line * 4,)),
            dma((8, line)),
            dma((2, line)),
            dma((line, 2)),
            dma((line, 2)),
            dma((2, line)),
        ],
        compiler_params=pltpu.CompilerParams(
            collective_id=collective_id, has_side_effects=True, vmem_limit_bytes=62 << 20
        ),
        cost_estimate=pl.CostEstimate(
            flops=2 * blocks * experts * room * tokens * (width + wider),
            bytes_accessed=2 * blocks * experts * room * (width + wider),
            transcendentals=0,
        ),
        name="reduce_all",
    )(slots, grads, outs)


def either(first, second, take):
    return first * (1 - take) + second * take


def remote(source, target, send_sem, recv_sem, where):
    return pltpu.make_async_remote_copy(
        src_ref=source, dst_ref=target, send_sem=send_sem, recv_sem=recv_sem,
        device_id=peer(*where), device_id_type=MESH,
    )


def landed(target, sem):
    pltpu.make_async_copy(target, target, sem).wait()


class LineGather:
    def __init__(self, own, out, send_sem, recv_sem, line):
        self.own, self.out, self.send_sem, self.recv_sem, self.line = own, out, send_sem, recv_sem, line
        self.spot = place()
        self.rows = own.shape[0]

    def view(self, block):
        return self.out.at[pl.ds(block * self.rows, self.rows)]

    def inside(self, block):
        return (block >= 0) & (block < self.line)

    def copy(self, sign, step):
        y, x, core, z = self.spot
        block = z - sign * step
        lane = (1 - sign) // 2
        source = self.own if step == 0 else self.view(block)
        return remote(
            source, self.view(block), self.send_sem.at[lane, step], self.recv_sem.at[lane, step], (y, x, core, z + sign)
        )

    def sends(self, sign, step):
        z = self.spot[3]
        return self.inside(z - sign * step) & self.inside(z + sign)

    def begin(self):
        for sign in (1, -1):
            pl.when(self.sends(sign, 0))(self.copy(sign, 0).start)

    def advance(self, step):
        z = self.spot[3]
        for sign in (1, -1):
            block = z - sign * (step + 1)
            lane = (1 - sign) // 2

            @pl.when(self.inside(block))
            def _():
                landed(self.view(block), self.recv_sem.at[lane, step])

            if step + 1 < self.line - 1:
                pl.when(self.sends(sign, step + 1))(self.copy(sign, step + 1).start)

    def finish(self):
        for sign in (1, -1):
            for step in range(self.line - 1):
                pl.when(self.sends(sign, step))(self.copy(sign, step).wait_send)


def start_kernel(line, hidden_ref, wq_ref, wk_ref, wv_ref, wo_ref, hidden_out, joined_out, wo_out,
                 local_sem, line_send, line_recv, plane_send, plane_recv):
    y, x, core, z = place()
    owns = (wq_ref, wk_ref, wv_ref, wo_ref)
    near_x, near_y, sibling = (y, 1 - x, core, z), (1 - y, x, core, z), (y, x, 1 - core, z)

    def view(n, yy, xx, half=None):
        group = yy * 4 + xx * 2 + core
        rows, columns = owns[n].shape
        first, count = (0, rows) if half is None else (half * (rows // 2), rows // 2)
        if n < 3:
            return joined_out.at[pl.ds(group * rows + first, count), pl.ds(n * columns, columns)]
        return wo_out.at[pl.ds(first, count), pl.ds(pl.multiple_of(group * columns, columns), columns)]

    kinds = ("x", "y", "s", "fy", "fx", "sx", "sy", "sf")

    def copy(kind, n):
        source, target, where = {
            "x": (owns[n], view(n, y, x), near_x),
            "y": (owns[n], view(n, y, x), near_y),
            "s": (owns[n], view(n, y, x), sibling),
            "fy": (view(n, y, 1 - x, 0), view(n, y, 1 - x, 0), near_y),
            "fx": (view(n, 1 - y, x, 1), view(n, 1 - y, x, 1), near_x),
            "sx": (view(n, y, 1 - x), view(n, y, 1 - x), sibling),
            "sy": (view(n, 1 - y, x), view(n, 1 - y, x), sibling),
            "sf": (view(n, 1 - y, 1 - x), view(n, 1 - y, 1 - x), sibling),
        }[kind]
        lane = kinds.index(kind)
        return remote(source, target, plane_send.at[lane, n], plane_recv.at[lane, n], where)

    def other(n, yy, xx):
        group = yy * 4 + xx * 2 + 1 - core
        rows, columns = owns[n].shape
        if n < 3:
            return joined_out.at[pl.ds(group * rows, rows), pl.ds(n * columns, columns)]
        return wo_out.at[pl.ds(0, rows), pl.ds(pl.multiple_of(group * columns, columns), columns)]

    greet(line)
    hidden = LineGather(hidden_ref, hidden_out, line_send, line_recv, line)
    locals_ = [pltpu.make_async_copy(hidden_ref, hidden.view(z), local_sem.at[4])]
    locals_ += [pltpu.make_async_copy(owns[n], view(n, y, x), local_sem.at[n]) for n in range(4)]
    hidden.begin()
    for n in range(4):
        for kind in ("x", "y", "s"):
            copy(kind, n).start()
    for local in locals_:
        local.start()
    for n in range(4):
        landed(view(n, y, 1 - x), plane_recv.at[0, n])
        copy("fy", n).start()
        copy("sx", n).start()
        landed(view(n, 1 - y, x), plane_recv.at[1, n])
        copy("fx", n).start()
        copy("sy", n).start()
    hidden.advance(0)
    for n in range(4):
        landed(view(n, 1 - y, 1 - x, 0), plane_recv.at[3, n])
        landed(view(n, 1 - y, 1 - x, 1), plane_recv.at[4, n])
        copy("sf", n).start()
    for step in range(1, line - 1):
        hidden.advance(step)
    for n in range(4):
        landed(other(n, y, x), plane_recv.at[2, n])
        landed(other(n, y, 1 - x), plane_recv.at[5, n])
        landed(other(n, 1 - y, x), plane_recv.at[6, n])
        landed(other(n, 1 - y, 1 - x), plane_recv.at[7, n])
    hidden.finish()
    for n in range(4):
        for kind in kinds:
            copy(kind, n).wait_send()
    for local in locals_:
        local.wait()


def start_exchange(hidden, w_query, w_key, w_value, w_out, collective_id):
    line = 4
    any_ref = pl.BlockSpec(memory_space=pl.ANY)
    dma = pltpu.SemaphoreType.DMA
    rows, width = hidden.shape
    part, columns = w_query.shape
    low = jnp.bfloat16
    return pl.pallas_call(
        functools.partial(start_kernel, line),
        out_shape=(
            jax.ShapeDtypeStruct((line * rows, width), low),
            jax.ShapeDtypeStruct((8 * part, 3 * columns), low),
            jax.ShapeDtypeStruct((w_out.shape[0], 8 * w_out.shape[1]), low),
        ),
        in_specs=[any_ref] * 5,
        out_specs=[any_ref] * 3,
        scratch_shapes=[dma((5,)), dma((2, line)), dma((2, line)), dma((8, 4)), dma((8, 4))],
        compiler_params=pltpu.CompilerParams(collective_id=collective_id, has_side_effects=True),
        cost_estimate=pl.CostEstimate(flops=0, bytes_accessed=150 << 20, transcendentals=0),
        name="start_exchange",
    )(hidden, w_query, w_key, w_value, w_out)


class LineReduce:
    def __init__(self, part, up, down, send_sem, recv_sem, line):
        self.part, self.up, self.down = part, up, down
        self.send_sem, self.recv_sem, self.line = send_sem, recv_sem, line
        self.spot = place()

    def copy(self, sign, goal):
        y, x, core, z = self.spot
        lane = (1 - sign) // 2
        target = self.up if sign > 0 else self.down
        return remote(
            self.part.at[goal], target.at[goal], self.send_sem.at[lane, goal], self.recv_sem.at[lane, goal],
            (y, x, core, z + sign),
        )

    def order(self, i):
        z = self.spot[3]
        return either(self.line - 1 - i, i, z * 2 // self.line)

    def lead(self, goal):
        z = self.spot[3]
        pl.when((z == 0) & (goal > 0))(self.copy(1, goal).start)
        pl.when((z == self.line - 1) & (goal < z))(self.copy(-1, goal).start)

    def advance(self, unit, total_ref):
        z, line = self.spot[3], self.line
        for sign in (1, -1):
            goal = line - 1 - unit + z if sign > 0 else unit - line + 1 + z
            live = ((z > 0) & (goal < line)) if sign > 0 else ((z < line - 1) & (goal >= 0))
            inbox = self.up if sign > 0 else self.down

            @pl.when(live)
            def _():
                self.copy(sign, goal).wait_recv()
                if unit < line - 1:
                    self.part[goal] = (
                        self.part[goal].astype(jnp.float32) + inbox[goal].astype(jnp.float32)
                    ).astype(jnp.bfloat16)
                    self.copy(sign, goal).start()
                else:
                    total_ref[...] += inbox[goal].astype(jnp.float32)

    def finish(self):
        z = self.spot[3]

        def step(goal, carry):
            pl.when(goal > z)(self.copy(1, goal).wait_send)
            pl.when(goal < z)(self.copy(-1, goal).wait_send)
            return carry

        lax.fori_loop(0, self.line, step, 0)


def mixed_out_kernel(line, mixed_ref, w_ref, residual_ref, gain_ref, router_ref,
                     x_ref, hidden_ref, probs_ref, part, up, down, send_sem, recv_sem):
    rows, width = x_ref.shape
    greet(line)
    reduce = LineReduce(part, up, down, send_sem, recv_sem, line)
    z = reduce.spot[3]

    def term(i, carry):
        goal = reduce.order(i)
        first = pl.multiple_of(goal * rows, rows)
        for column in range(0, width, 512):
            piece = slice(column, column + 512)
            value = jnp.dot(mixed_ref[pl.ds(first, rows), :], w_ref[:, piece], preferred_element_type=jnp.float32)

            @pl.when(goal == z)
            def _():
                x_ref[:, piece] = value

            part[goal, :, piece] = value.astype(jnp.bfloat16)
        reduce.lead(goal)
        return carry

    lax.fori_loop(0, line, term, 0)
    for unit in range(1, line):
        reduce.advance(unit, x_ref)
    x_one = x_ref[...] + residual_ref[...].astype(jnp.float32)
    x_ref[...] = x_one
    scale = lax.rsqrt(jnp.mean(x_one * x_one, axis=-1, keepdims=True) + norm_eps)
    hidden = (x_one * scale * gain_ref[...]).astype(jnp.bfloat16)
    hidden_ref[...] = hidden
    logits = lax.dot_general(
        router_ref[...], hidden, (((1,), (1,)), ((), ())), preferred_element_type=jnp.float32
    )
    shifted = jnp.exp(logits - jnp.max(logits, axis=0, keepdims=True))
    probs_ref[...] = shifted / jnp.sum(shifted, axis=0, keepdims=True)
    reduce.finish()


def mixed_out(mixed, w_out, residual, gain, router_turned, collective_id):
    line = 4
    rows, width = residual.shape
    experts = router_turned.shape[0]
    vmem = pl.BlockSpec(memory_space=pltpu.VMEM)
    dma = pltpu.SemaphoreType.DMA
    block = pltpu.VMEM((line, rows, width), jnp.bfloat16)
    return pl.pallas_call(
        functools.partial(mixed_out_kernel, line),
        out_shape=(
            jax.ShapeDtypeStruct((rows, width), jnp.float32),
            jax.ShapeDtypeStruct((rows, width), jnp.bfloat16),
            jax.ShapeDtypeStruct((experts, rows), jnp.float32),
        ),
        in_specs=[vmem] * 5,
        out_specs=[vmem] * 3,
        scratch_shapes=[block, block, block, dma((2, line)), dma((2, line))],
        compiler_params=pltpu.CompilerParams(
            collective_id=collective_id, has_side_effects=True, vmem_limit_bytes=56 << 20
        ),
        cost_estimate=pl.CostEstimate(flops=0, bytes_accessed=150 << 20, transcendentals=0),
        name="mixed_out",
    )(mixed, w_out, residual, gain.reshape(1, width), router_turned)


class Butterfly:
    def __init__(self, data, total, from_core, from_x, from_y, from_z, sums, send_sem, recv_sem):
        self.data, self.total, self.sums = data, total, sums
        self.boxes = {"core": from_core, "x": from_x, "y": from_y}
        self.from_z, self.send_sem, self.recv_sem = from_z, send_sem, recv_sem
        y, x, core, z = self.spot = place()
        self.width = data.shape[1]
        self.near = {"core": (y, x, 1 - core, z), "x": (y, 1 - x, core, z), "y": (1 - y, x, core, z)}
        half, quarter, eighth = self.width // 2, self.width // 4, self.width // 8
        first = core * half
        self.kept = {"core": (first, half), "x": (first + x * quarter, quarter)}
        self.kept["y"] = (first + x * quarter + y * eighth, eighth)
        self.away = {
            "core": ((1 - core) * half, half),
            "x": (first + (1 - x) * quarter, quarter),
            "y": (first + x * quarter + (1 - y) * eighth, eighth),
        }

    def part(self, span):
        return pl.ds(pl.multiple_of(span[0], span[1]), span[1])

    def fold_copy(self, axis):
        lane = ("core", "x", "y").index(axis)
        return remote(
            self.data.at[:, self.part(self.away[axis])], self.boxes[axis], self.send_sem.at[lane],
            self.recv_sem.at[lane], self.near[axis],
        )

    def fold(self, axis):
        copy = self.fold_copy(axis)
        copy.start()
        copy.wait()
        self.data[:, self.part(self.kept[axis])] += self.boxes[axis][...]

    def line_step(self, step):
        y, x, core, z = self.spot
        other = (z + 1 - 2 * (z % 2)) if step == 0 else (z + 2) % 4
        piece = self.part(self.kept["y"])
        source = self.data.at[:, piece] if step == 0 else self.sums
        copy = remote(
            source, self.from_z.at[step], self.send_sem.at[3 + step], self.recv_sem.at[3 + step], (y, x, core, other)
        )
        copy.start()
        copy.wait()
        if step == 0:
            self.sums[...] = self.data[:, piece] + self.from_z[0]
        else:
            self.total[:, piece] = self.sums[...] + self.from_z[1]

    def unfold(self, axis):
        lane = 5 + ("core", "x", "y").index(axis)
        mine = self.total.at[:, self.part(self.kept[axis])]
        copy = remote(mine, mine, self.send_sem.at[lane], self.recv_sem.at[lane], self.near[axis])
        copy.start()
        copy.wait_send()
        landed(self.total.at[:, self.part(self.away[axis])], self.recv_sem.at[lane])

    def scratch(rows, width):
        low = jnp.float32
        return [
            pltpu.VMEM((rows, width // 2), low),
            pltpu.VMEM((rows, width // 4), low),
            pltpu.VMEM((rows, width // 8), low),
            pltpu.VMEM((2, rows, width // 8), low),
            pltpu.VMEM((rows, width // 8), low),
            pltpu.SemaphoreType.DMA((8,)),
            pltpu.SemaphoreType.DMA((8,)),
        ]


def greet_far(line):
    y, x, core, z = place()
    barrier = pltpu.get_barrier_semaphore()
    for near in ((y, x, 1 - core, z), (y, 1 - x, core, z), (1 - y, x, core, z)):
        pl.semaphore_signal(barrier, inc=1, device_id=peer(*near), device_id_type=MESH)
    for step in range(1, line):
        pl.semaphore_signal(barrier, inc=1, device_id=peer(y, x, core, (z + step) % line), device_id_type=MESH)
    pl.semaphore_wait(barrier, 3 + line - 1)


def back_gather_kernel(line, own_ref, sums_ref, out_ref, total_ref, data, local_sem, send_sem, recv_sem, *fly):
    greet_far(line)
    gather = LineGather(own_ref, out_ref, send_sem, recv_sem, line)
    local = pltpu.make_async_copy(own_ref, gather.view(gather.spot[3]), local_sem)
    gather.begin()
    local.start()
    data[...] = sums_ref[...]
    butterfly = Butterfly(data, total_ref, *fly)
    for axis in ("core", "x", "y"):
        butterfly.fold(axis)
    gather.advance(0)
    butterfly.line_step(0)
    gather.advance(1)
    butterfly.line_step(1)
    for axis in ("y", "x", "core"):
        butterfly.unfold(axis)
    gather.advance(2)
    gather.finish()
    local.wait()


def back_gather(own, sums, collective_id):
    line = 4
    any_ref = pl.BlockSpec(memory_space=pl.ANY)
    vmem = pl.BlockSpec(memory_space=pltpu.VMEM)
    dma = pltpu.SemaphoreType.DMA
    return pl.pallas_call(
        functools.partial(back_gather_kernel, line),
        out_shape=(
            jax.ShapeDtypeStruct((line * own.shape[0], own.shape[1]), own.dtype),
            jax.ShapeDtypeStruct(sums.shape, jnp.float32),
        ),
        in_specs=[any_ref, vmem],
        out_specs=[any_ref, vmem],
        scratch_shapes=[
            pltpu.VMEM(sums.shape, jnp.float32), dma(()), dma((2, line)), dma((2, line)),
            *Butterfly.scratch(*sums.shape),
        ],
        compiler_params=pltpu.CompilerParams(collective_id=collective_id, has_side_effects=True),
        cost_estimate=pl.CostEstimate(flops=0, bytes_accessed=150 << 20, transcendentals=0),
        name="back_gather",
    )(own, sums)


def last_kernel(line, joined_ref, weight_ref, hidden_ref, mixed_ref, attn_ref, residual_ref, gain_ref, x_grad_ref, gains_ref,
                input_ref, wq_ref, wk_ref, wv_ref, wo_ref, total_ref,
                part, up, down, stage, near, far_x, far_y, from_x, from_y, data,
                line_send, line_recv, stage_sem, near_sem, send_sem, recv_sem, *fly):
    y, x, core, z = place()
    rows, width = input_ref.shape
    columns = joined_ref.shape[1]
    half = rows // 2
    low = jnp.bfloat16
    greet_far(line)
    reduce = LineReduce(part, up, down, line_send, line_recv, line)

    def term(i, carry):
        goal = reduce.order(i)
        first = pl.multiple_of(goal * rows, rows)
        for column in range(0, width, 512):
            piece = slice(column, column + 512)
            value = across(joined_ref[pl.ds(first, rows), :], weight_ref[piece, :])

            @pl.when(goal == z)
            def _():
                input_ref[:, piece] = value

            part[goal, :, piece] = value.astype(low)
        reduce.lead(goal)
        return carry

    lax.fori_loop(0, line, term, 0)
    near_x, near_y, sibling = (y, 1 - x, core, z), (1 - y, x, core, z), (y, x, 1 - core, z)

    def terms(j, own, store):
        dy, dx = (j + 1) % 2, 1 - j // 2
        group = (y + dy) % 2 * 4 + (x + dx) % 2 * 2 + (core if own else 1 - core)
        span = pl.ds(pl.multiple_of(group * rows, rows), rows)
        turned_rows = hidden_ref[:, span]
        for column in range(0, columns, 512):
            piece = slice(column, column + 512)
            store(piece, turned(turned_rows, joined_ref[:, piece]))
        value = turned(mixed_ref[...], attn_ref[:, span])
        store(slice(columns, columns + rows), value[:rows])
        store(slice(columns + rows, columns + 2 * rows), value[rows:])

    def to_sibling(j):
        return remote(stage.at[j], near.at[j], stage_sem.at[j], near_sem.at[j], sibling)

    def away(j, carry):
        def store(piece, value):
            stage[j, :, piece] = value.astype(low)

        terms(j, False, store)
        to_sibling(j).start()
        return carry

    def own(j, carry):
        to_sibling(j).wait_recv()

        def store(piece, value):
            near[j, :, piece] = (value + near[j, :, piece].astype(jnp.float32)).astype(low)

        terms(j, True, store)
        return carry

    lax.fori_loop(0, 4, away, 0)
    lax.fori_loop(0, 4, own, 0)

    def line_rows(h):
        return pl.ds(h * half, half)

    def cross(kind):
        column, h, target, where = {
            "far_x": (0, 0, far_x, near_x),
            "far_y": (0, 1, far_y, near_y),
            "x0": (1, 0, from_x.at[line_rows(0)], near_x),
            "x1": (1, 1, from_x.at[line_rows(1)], near_x),
            "y0": (2, 0, from_y.at[line_rows(0)], near_y),
            "y1": (2, 1, from_y.at[line_rows(1)], near_y),
        }[kind]
        lane = kinds.index(kind)
        return remote(near.at[column, line_rows(h)], target, send_sem.at[lane], recv_sem.at[lane], where)

    kinds = ("far_x", "far_y", "x0", "y1", "x1", "y0")
    for kind in kinds[:4]:
        cross(kind).start()

    def add(column, h, source):
        near[column, line_rows(h), :] = (
            near[column, line_rows(h), :].astype(jnp.float32) + source[...].astype(jnp.float32)
        ).astype(low)

    reduce.advance(1, input_ref)
    cross("far_y").wait_recv()
    add(1, 1, far_y)
    cross("x1").start()
    cross("far_x").wait_recv()
    add(2, 0, far_x)
    cross("y0").start()
    reduce.advance(2, input_ref)
    for kind in kinds[2:]:
        cross(kind).wait_recv()
    for n, ref in enumerate((wq_ref, wk_ref, wv_ref, wo_ref, wo_ref)):
        count = columns // 3 if n < 3 else rows
        first = n * (columns // 3) if n < 3 else columns + (n - 3) * rows
        piece = slice(first, first + count)
        total = sum(r[:, piece].astype(jnp.float32) for r in (near.at[3], from_x, from_y))
        if n < 3:
            ref[...] = total
        else:
            ref[(n - 3) * rows : (n - 2) * rows, :] = total
    reduce.advance(3, input_ref)
    grad = input_ref[...]
    values = residual_ref[...].astype(jnp.float32)
    scale = lax.rsqrt(jnp.mean(values * values, axis=-1, keepdims=True) + norm_eps)
    gained = grad * gain_ref[...]
    inner = jnp.sum(gained * values, axis=-1, keepdims=True)
    data[...] = gains_ref[...]
    data[2:3, :] = jnp.sum(grad * values * scale, axis=0, keepdims=True)
    input_ref[...] = x_grad_ref[...] + scale * gained - values * (scale * scale * scale * inner / width)
    butterfly = Butterfly(data, total_ref, *fly)
    for axis in ("core", "x", "y"):
        butterfly.fold(axis)
    butterfly.line_step(0)
    butterfly.line_step(1)
    for axis in ("y", "x", "core"):
        butterfly.unfold(axis)
    reduce.finish()
    for j in range(4):
        to_sibling(j).wait_send()
    for kind in kinds:
        cross(kind).wait_send()


def last_exchange(joined, weight, hidden, mixed, attn, residual, gain, x_grad, gains, collective_id):
    line = 4
    rows, width = residual.shape
    columns = joined.shape[1] // 3
    low, wide = jnp.bfloat16, jnp.float32
    vmem = pl.BlockSpec(memory_space=pltpu.VMEM)
    dma = pltpu.SemaphoreType.DMA
    block = pltpu.VMEM((line, rows, width), low)
    one = pltpu.VMEM((rows, width), low)
    part = pltpu.VMEM((rows // 2, width), low)
    square = jax.ShapeDtypeStruct((rows, columns), wide)
    return pl.pallas_call(
        functools.partial(last_kernel, line),
        out_shape=(
            jax.ShapeDtypeStruct((rows, width), wide), square, square, square,
            jax.ShapeDtypeStruct((2 * rows, rows), wide),
            jax.ShapeDtypeStruct(gains.shape, wide),
        ),
        in_specs=[vmem] * 9,
        out_specs=[vmem] * 6,
        scratch_shapes=[
            block, block, block, pltpu.VMEM((4, rows, width), low), pltpu.VMEM((4, rows, width), low),
            part, part, one, one, pltpu.VMEM(gains.shape, wide),
            dma((2, line)), dma((2, line)), dma((4,)), dma((4,)), dma((6,)), dma((6,)),
            *Butterfly.scratch(*gains.shape),
        ],
        compiler_params=pltpu.CompilerParams(
            collective_id=collective_id, has_side_effects=True, vmem_limit_bytes=62 << 20
        ),
        cost_estimate=pl.CostEstimate(flops=0, bytes_accessed=250 << 20, transcendentals=0),
        name="last_exchange",
    )(joined, weight, hidden, mixed, attn, residual, gain.reshape(1, width), x_grad, gains)


def visible_block(row_paths, key_paths, key_valid, row_first):
    row_count = row_paths.shape[1]
    key_count = key_paths.shape[1]
    key_segment = key_paths[0][None, :]
    on_path = (
        (key_segment == row_paths[0][:, None])
        | (key_segment == row_paths[1][:, None])
        | (key_segment == row_paths[2][:, None])
    )
    row_place = row_first + lax.iota(jnp.int32, row_count)
    key_place = lax.iota(jnp.int32, key_count)
    earlier = key_place[None, :] <= row_place[:, None]
    return on_path & earlier & (key_valid[None, :] == 1) | (
        key_place[None, :] == row_place[:, None]
    )


def rotation(positions, head_dim):
    half = head_dim // 2
    freqs = jnp.exp(-jnp.log(rope_base) * 2.0 * lax.iota(jnp.float32, half) / head_dim)
    angles = positions.astype(jnp.float32)[:, None] * freqs[None, :]
    return (jnp.cos(angles), jnp.sin(angles))


def rotate(values, cosine, sine):
    half = values.shape[-1] // 2
    first = values[..., :half]
    second = values[..., half:]
    cosine = cosine[:, None, :]
    sine = sine[:, None, :]
    return jnp.concatenate(
        (first * cosine - second * sine, second * cosine + first * sine), axis=-1
    )


def unrotate(grads, cosine, sine):
    half = grads.shape[-1] // 2
    first = grads[..., :half]
    second = grads[..., half:]
    cosine = cosine[:, None, :]
    sine = sine[:, None, :]
    return jnp.concatenate(
        (first * cosine + second * sine, second * cosine - first * sine), axis=-1
    )


def rms_apply(values, gain):
    scale = lax.rsqrt(jnp.mean(values * values, axis=-1, keepdims=True) + norm_eps)
    return (values * scale * gain, scale)


def rms_grad(values, scale, gain, grads, inner, width):
    grad_values = scale * gain * grads - values * scale**3 * inner / width
    grad_gain = jnp.sum(grads * values * scale, axis=0)
    return (grad_values, grad_gain)


def tensor_sums(pair):
    return lax.psum((pair[0], pair[1]), "tensor")


def heads_to_rows(term, rows):
    return lax.psum_scatter(
        term(jnp.int32(0), rows * lax.axis_size("tensor")).astype(jnp.bfloat16),
        "tensor",
        scatter_dimension=0,
        tiled=True,
    ).astype(jnp.float32)


def sum_over_dp(rows):
    dp = lax.axis_size("dp")
    pieces = rows.reshape(dp, rows.shape[0] // dp, rows.shape[1])
    return lax.psum_scatter(pieces, "dp", scatter_dimension=0, tiled=False)


def sum_over_tensor(part):
    return lax.psum_scatter(part, "tensor", scatter_dimension=0, tiled=True)


def body(
    residual,
    attn_gain,
    w_query,
    w_key,
    w_value,
    query_gain,
    key_gain,
    w_out,
    moe_gain,
    router,
    w_gate,
    w_up,
    w_down,
    segment_path,
    token_valid,
    routes,
    route_order,
    cotangent,
):
    tensor_rank = lax.axis_index("tensor")
    tok_dev, width = residual.shape
    seq_len = segment_path.shape[1]
    top_count = routes.shape[1]
    experts = router.shape[1]
    local_experts = w_gate.shape[0]
    dp_groups = experts // local_experts
    capacity = 9 * tok_dev * top_count // (8 * experts)
    full_width = H * HD
    block_rows = min(512, seq_len)
    block_count = seq_len // block_rows
    score_scale = HD ** (-0.5)
    everyone = ("dp", "tensor")
    direct = dp_groups == 8 and lax.axis_size("tensor") == 4
    first_expert = lax.axis_index("dp") * local_experts
    slot_rows = padded(capacity, 8)
    valid_dev = lax.dynamic_slice_in_dim(token_valid, tensor_rank * tok_dev, tok_dev)
    slots_own = slot_table(routes, route_order, valid_dev, experts, capacity)
    slots_all = lax.all_gather(slots_own.astype(jnp.bfloat16), everyone, axis=0)
    slots = lax.dynamic_slice_in_dim(slots_all, first_expert, local_experts, 1).astype(jnp.int32)
    blocks = slots.shape[0]
    cots_all = lax.all_gather(cotangent, everyone, axis=0, tiled=True)
    c_slots = dispatch(slots, None, cots_all, slot_rows)
    head_cols = w_query.shape[1]
    local_heads = head_cols // HD
    residual_float = residual.astype(jnp.float32)
    normed_one, scale_one = rms_apply(residual_float, attn_gain)
    hidden = normed_one.astype(jnp.bfloat16)
    if direct:
        hidden_all, joined_weight, gathered_out = start_exchange(hidden, w_query, w_key, w_value, w_out, 3)
    else:
        hidden_all = lax.all_gather(hidden, "tensor", axis=0, tiled=True)
        joined_weight = jnp.concatenate(
            [lax.all_gather(w, "dp", axis=0, tiled=True) for w in (w_query, w_key, w_value)], axis=1
        )
        gathered_out = lax.all_gather(w_out, "dp", axis=1, tiled=True)
    projected = jnp.dot(hidden_all, joined_weight, preferred_element_type=jnp.float32)
    q_raw = projected[:, :head_cols]
    k_raw = projected[:, head_cols : 2 * head_cols]
    value_low = projected[:, 2 * head_cols :].astype(jnp.bfloat16).reshape(seq_len, local_heads, HD)
    query_sq, key_sq = tensor_sums((jnp.sum(q_raw * q_raw, axis=1), jnp.sum(k_raw * k_raw, axis=1)))
    query_scale = lax.rsqrt(query_sq / full_width + norm_eps)[:, None]
    key_scale = lax.rsqrt(key_sq / full_width + norm_eps)[:, None]
    query_gain_dev = lax.dynamic_slice_in_dim(query_gain, tensor_rank * head_cols, head_cols)
    key_gain_dev = lax.dynamic_slice_in_dim(key_gain, tensor_rank * head_cols, head_cols)
    block_starts = lax.iota(jnp.int32, block_count) * block_rows

    def block_mask(row_first):
        row_paths = lax.dynamic_slice_in_dim(segment_path, row_first, block_rows, 1)
        return visible_block(row_paths, segment_path, token_valid, row_first)

    def count_seen(row_first):
        return jnp.sum(block_mask(row_first).astype(jnp.int32), axis=1)

    positions = lax.map(count_seen, block_starts).reshape(seq_len) - 1
    cosine, sine = rotation(positions, HD)
    query_low = rotate(
        (q_raw * query_scale * query_gain_dev).reshape(seq_len, local_heads, HD), cosine, sine
    ).astype(jnp.bfloat16)
    key_low = rotate(
        (k_raw * key_scale * key_gain_dev).reshape(seq_len, local_heads, HD), cosine, sine
    ).astype(jnp.bfloat16)

    def attend(row_first):
        visible = block_mask(row_first)
        query_block = lax.dynamic_slice_in_dim(query_low, row_first, block_rows, 0)
        scores = (
            jnp.einsum("qhd,khd->hqk", query_block, key_low, preferred_element_type=jnp.float32)
            * score_scale
        )
        scores = jnp.where(visible[None], scores, masked_score)
        top_score = jnp.max(scores, axis=-1, keepdims=True)
        exp_scores = jnp.exp(scores - top_score)
        total = jnp.sum(exp_scores, axis=-1, keepdims=True)
        weights_low = (exp_scores / total).astype(jnp.bfloat16)
        mixed_block = jnp.einsum(
            "hqk,khd->qhd", weights_low, value_low, preferred_element_type=jnp.float32
        )
        return (mixed_block.astype(jnp.bfloat16), (top_score + jnp.log(total))[..., 0])

    mixed_blocks, log_totals = lax.map(attend, block_starts)
    attn_mixed = mixed_blocks.reshape(seq_len, head_cols)

    if direct:
        x_one, hidden_two, gates_own = mixed_out(attn_mixed, gathered_out, residual, moe_gain, router.T, 4)
        probs = gates_own.T
    else:

        def attn_term(first_row, row_count):
            return jnp.dot(attn_mixed, gathered_out, preferred_element_type=jnp.float32)

        x_one = residual_float + heads_to_rows(attn_term, tok_dev)
        hidden_two = rms_apply(x_one, moe_gain)[0].astype(jnp.bfloat16)
        logits = jnp.dot(hidden_two, router, preferred_element_type=jnp.float32)
        probs = jax.nn.softmax(logits, axis=-1)
        gates_own = probs.T
    hidden_two, c_slots = lax.optimization_barrier((hidden_two, c_slots))
    scale_two = lax.rsqrt(jnp.mean(x_one * x_one, axis=-1, keepdims=True) + norm_eps)
    if direct:
        rows_all, gates_all = gather_all([hidden_two, gates_own], 1)
        gates_all = gates_all.reshape(-1, experts, tok_dev)
    else:
        gates_all = lax.all_gather(gates_own, everyone, axis=0)
        rows_all = lax.all_gather(hidden_two, everyone, axis=0, tiled=True)
    gates = lax.dynamic_slice_in_dim(gates_all, first_expert, local_experts, 1)
    x_slots, gate_slots = dispatch(slots, gates, rows_all, slot_rows)
    outs, grads, grad_w_gate, grad_w_up, grad_w_down = expert_pass(
        first_expert.reshape(1),
        x_slots,
        c_slots,
        gate_slots,
        w_gate,
        w_up,
        w_down,
        blocks,
        padded(slot_rows, 16),
    )
    if direct:
        grad_rows, out_part = reduce_all(slots, outs, grads, 2)
    else:
        out_part, grad_part = combine(slots, outs, grads)
        grad_rows = sum_over_tensor(sum_over_dp(grad_part)).astype(jnp.float32)
    out_part = sum_over_dp(out_part)
    grad_out = cotangent.astype(jnp.float32)
    grad_hidden_two = grad_rows[:, :width]
    grad_probs = grad_rows[:, width : width + experts]
    grad_logits = probs * (grad_probs - jnp.sum(probs * grad_probs, axis=-1, keepdims=True))
    router_float = router.astype(jnp.float32)
    grad_hidden_two = grad_hidden_two + lax.dot_general(
        grad_logits, router_float, (((1,), (1,)), ((), ())), precision=lax.Precision.HIGHEST
    )
    grad_router_part = lax.dot_general(
        grad_logits,
        hidden_two.astype(jnp.float32),
        (((0,), (0,)), ((), ())),
        precision=lax.Precision.HIGHEST,
    )
    inner_two = jnp.sum(grad_hidden_two * moe_gain * x_one, axis=-1, keepdims=True)
    grad_norm_two, grad_moe_gain_part = rms_grad(
        x_one, scale_two, moe_gain, grad_hidden_two, inner_two, width
    )
    grad_x_one = grad_out + grad_norm_two
    grad_attn_low = grad_x_one.astype(jnp.bfloat16)
    early_sums = jnp.concatenate(
        (grad_router_part, grad_moe_gain_part[None], jnp.zeros((7, width), jnp.float32)), axis=0
    )
    if direct:
        grad_attn_all, early_sums = back_gather(grad_attn_low, early_sums, 5)
    else:
        grad_attn_all = lax.all_gather(grad_attn_low, "tensor", axis=0, tiled=True)
        early_sums = lax.psum(early_sums, everyone)
    grad_mixed = (
        lax.dot_general(
            grad_attn_all,
            gathered_out,
            (((1,), (1,)), ((), ())),
            preferred_element_type=jnp.float32,
        )
        .astype(jnp.bfloat16)
        .reshape(seq_len, local_heads, HD)
    )

    def attend_back(carry, pieces):
        grad_key_sum, grad_value_sum = carry
        row_first, log_total = pieces
        visible = block_mask(row_first)
        query_block = lax.dynamic_slice_in_dim(query_low, row_first, block_rows, 0)
        grad_block = lax.dynamic_slice_in_dim(grad_mixed, row_first, block_rows, 0)
        scores = (
            jnp.einsum("qhd,khd->hqk", query_block, key_low, preferred_element_type=jnp.float32)
            * score_scale
        )
        scores = jnp.where(visible[None], scores, masked_score)
        weights = jnp.exp(scores - log_total[..., None])
        grad_weights = jnp.einsum(
            "qhd,khd->hqk", grad_block, value_low, preferred_element_type=jnp.float32
        )
        inner = jnp.sum(weights * grad_weights, axis=-1, keepdims=True)
        grad_scores = (weights * (grad_weights - inner)).astype(jnp.bfloat16)
        grad_query_block = (
            jnp.einsum("hqk,khd->qhd", grad_scores, key_low, preferred_element_type=jnp.float32)
            * score_scale
        )
        grad_key_sum = (
            grad_key_sum
            + jnp.einsum(
                "hqk,qhd->khd", grad_scores, query_block, preferred_element_type=jnp.float32
            )
            * score_scale
        )
        grad_value_sum = grad_value_sum + jnp.einsum(
            "hqk,qhd->khd",
            weights.astype(jnp.bfloat16),
            grad_block,
            preferred_element_type=jnp.float32,
        )
        return ((grad_key_sum, grad_value_sum), grad_query_block)

    zero_heads = jnp.zeros((seq_len, local_heads, HD), jnp.float32)
    (grad_key_all, grad_value_all), grad_query_blocks = lax.scan(
        attend_back, (zero_heads, zero_heads), (block_starts, log_totals)
    )
    grad_q_norm = unrotate(
        grad_query_blocks.reshape(seq_len, local_heads, HD), cosine, sine
    ).reshape(seq_len, head_cols)
    grad_k_norm = unrotate(grad_key_all, cosine, sine).reshape(seq_len, head_cols)
    query_inner, key_inner = tensor_sums(
        (
            jnp.sum(grad_q_norm * query_gain_dev * q_raw, axis=1),
            jnp.sum(grad_k_norm * key_gain_dev * k_raw, axis=1),
        )
    )
    grad_q_raw, grad_query_gain_dev = rms_grad(
        q_raw, query_scale, query_gain_dev, grad_q_norm, query_inner[:, None], full_width
    )
    grad_k_raw, grad_key_gain_dev = rms_grad(
        k_raw, key_scale, key_gain_dev, grad_k_norm, key_inner[:, None], full_width
    )
    grad_joined = jnp.concatenate(
        (grad_q_raw, grad_k_raw, grad_value_all.reshape(seq_len, head_cols)), axis=1
    ).astype(jnp.bfloat16)
    out_part, grad_joined = lax.optimization_barrier((out_part, grad_joined))
    block_out = (x_one + sum_over_tensor(out_part).astype(jnp.float32)).astype(jnp.bfloat16)
    zero_width = jnp.zeros((full_width,), jnp.float32)
    grad_query_full = lax.dynamic_update_slice_in_dim(
        zero_width, grad_query_gain_dev, tensor_rank * head_cols, 0
    )
    grad_key_full = lax.dynamic_update_slice_in_dim(
        zero_width, grad_key_gain_dev, tensor_rank * head_cols, 0
    )
    if direct:
        gains = jnp.concatenate(
            (grad_query_full[None], grad_key_full[None], jnp.zeros((6, width), jnp.float32)), axis=0
        )
        grad_input, grad_w_query, grad_w_key, grad_w_value, grad_w_out, gains = last_exchange(
            grad_joined,
            joined_weight,
            hidden_all,
            attn_mixed,
            grad_attn_all,
            residual,
            attn_gain,
            grad_x_one,
            gains,
            6,
        )
    else:
        grad_joined_weight = lax.dot_general(
            hidden_all, grad_joined, (((0,), (0,)), ((), ())), preferred_element_type=jnp.float32
        ).astype(jnp.bfloat16)
        grad_out_weight = lax.dot_general(
            attn_mixed, grad_attn_all, (((0,), (0,)), ((), ())), preferred_element_type=jnp.float32
        ).astype(jnp.bfloat16)

        def back_term(first_row, row_count):
            return lax.dot_general(
                grad_joined, joined_weight, (((1,), (1,)), ((), ())), preferred_element_type=jnp.float32
            )

        grad_hidden = heads_to_rows(back_term, tok_dev)
        inner_one = jnp.sum(grad_hidden * attn_gain * residual_float, axis=-1, keepdims=True)
        grad_norm_one, grad_attn_gain_part = rms_grad(
            residual_float, scale_one, attn_gain, grad_hidden, inner_one, width
        )
        grad_input = grad_x_one + grad_norm_one
        grad_w_query, grad_w_key, grad_w_value = (
            lax.psum_scatter(
                grad_joined_weight[:, n * head_cols : (n + 1) * head_cols],
                "dp",
                scatter_dimension=0,
                tiled=True,
            ).astype(jnp.float32)
            for n in range(3)
        )
        grad_w_out = lax.psum_scatter(
            grad_out_weight, "dp", scatter_dimension=1, tiled=True
        ).astype(jnp.float32)
        gains = lax.psum(jnp.stack((grad_query_full, grad_key_full, grad_attn_gain_part)), everyone)
    return (
        block_out,
        grad_input,
        gains[2],
        grad_w_query,
        grad_w_key,
        grad_w_value,
        gains[0],
        gains[1],
        grad_w_out,
        early_sums[experts],
        early_sums[:experts].T,
        grad_w_gate,
        grad_w_up,
        grad_w_down,
    )


def solution(mesh):
    in_specs = (
        P(("dp", "tensor"), None),
        P(),
        P("dp", "tensor"),
        P("dp", "tensor"),
        P("dp", "tensor"),
        P(),
        P(),
        P("tensor", "dp"),
        P(),
        P(),
        P("dp", None, "tensor"),
        P("dp", None, "tensor"),
        P("dp", "tensor", None),
        P(None, "dp"),
        P("dp"),
        P(("dp", "tensor"), None),
        P(("dp", "tensor"), None),
        P(("dp", "tensor"), None),
    )
    out_specs = (
        P(("dp", "tensor"), None),
        P(("dp", "tensor"), None),
        P(),
        P("dp", "tensor"),
        P("dp", "tensor"),
        P("dp", "tensor"),
        P(),
        P(),
        P("tensor", "dp"),
        P(),
        P(),
        P("dp", None, "tensor"),
        P("dp", None, "tensor"),
        P("dp", "tensor", None),
    )
    return jax.shard_map(body, mesh=mesh, in_specs=in_specs, out_specs=out_specs, check_vma=False)
```

```python
import functools

import jax
import jax.numpy as jnp
from jax import lax
from jax.experimental import pallas as pl
from jax.experimental.pallas import tpu as pltpu
from jax.sharding import PartitionSpec as P

H = 16
HD = 128


norm_eps = 1e-05
rope_base = 10000.0
masked_score = -1e30


def padded(count, step):
    return -(-count // step) * step


def slot_table(routes, route_order, valid, experts, capacity):
    far = jnp.int32(1 << 30)
    expert = lax.iota(jnp.int32, experts)[:, None, None]
    hits = (routes[None] == expert) & (valid[None, :, None] == 1)
    order = jnp.min(jnp.where(hits, route_order[None], far), axis=-1)
    ranks = jnp.sum((order[:, None, :] < order[:, :, None]).astype(jnp.int32), axis=-1)
    return jnp.where((order < far) & (ranks < capacity), ranks, -1)


def slot_hits(slots, expert, rows):
    tokens = slots.shape[-1]
    return lax.broadcasted_iota(jnp.int32, (rows, tokens), 0) == slots[expert : expert + 1, :]


def dispatch_kernel(slots_ref, gates_ref, rows_ref, x_ref, gate_ref):
    pair, experts, tokens = slots_ref.shape
    rows = x_ref.shape[1] // pair
    width = rows_ref.shape[1]
    picks = []
    for b in range(pair):
        slots = slots_ref[b]
        pieces = []
        for e in range(experts):
            hit = slot_hits(slots, e, rows)
            pieces.append(hit.astype(jnp.float32))
            if gate_ref is not None:
                gate = jnp.sum(jnp.where(hit, gates_ref[b, e : e + 1, :], 0.0), axis=1, keepdims=True)
                gate_ref[e, b * rows : (b + 1) * rows, :] = jnp.broadcast_to(gate, (rows, 128))
        picks.append(jnp.concatenate(pieces, axis=0).astype(jnp.bfloat16))
    step = min(512, width)
    for first in range(0, width, step):
        parts = [
            jnp.dot(
                picks[b],
                rows_ref[b * tokens : (b + 1) * tokens, first : first + step],
                preferred_element_type=jnp.float32,
            )
            for b in range(pair)
        ]
        for e in range(experts):
            x_ref[e, :, first : first + step] = jnp.concatenate(
                [part[e * rows : (e + 1) * rows] for part in parts], axis=0
            ).astype(jnp.bfloat16)


def plain_dispatch_kernel(slots_ref, rows_ref, x_ref):
    dispatch_kernel(slots_ref, None, rows_ref, x_ref, None)


def dispatch(slots, gates, rows_all, rows):
    blocks, experts, tokens = slots.shape
    width = rows_all.shape[1]
    pair = 2
    out = jax.ShapeDtypeStruct((experts, blocks * rows, width), jnp.bfloat16)
    table = pl.BlockSpec((pair, experts, tokens), lambda i: (i, 0, 0))
    source = pl.BlockSpec((pair * tokens, width), lambda i: (i, 0))
    target = pl.BlockSpec((experts, pair * rows, width), lambda i: (0, i, 0))
    settings = dict(
        grid=(blocks // pair,),
        compiler_params=pltpu.CompilerParams(vmem_limit_bytes=50 << 20),
        cost_estimate=pl.CostEstimate(
            flops=2 * blocks * experts * rows * tokens * width,
            bytes_accessed=2 * blocks * (tokens + experts * rows) * width,
            transcendentals=0,
        ),
    )
    if gates is None:
        return pl.pallas_call(
            plain_dispatch_kernel, out_shape=out, in_specs=[table, source], out_specs=target, name="pick", **settings
        )(slots, rows_all)
    return pl.pallas_call(
        dispatch_kernel,
        out_shape=(out, jax.ShapeDtypeStruct((experts, blocks * rows, 128), jnp.float32)),
        in_specs=[table, table, source],
        out_specs=[target, pl.BlockSpec((experts, pair * rows, 128), lambda i: (0, i, 0))],
        name="dispatch",
        **settings,
    )(slots, gates, rows_all)


def turned(left, right):
    return lax.dot_general(left, right, (((0,), (0,)), ((), ())), preferred_element_type=jnp.float32)


def across(left, right):
    return lax.dot_general(left, right, (((1,), (1,)), ((), ())), preferred_element_type=jnp.float32)


def expert_kernel(rows, first_ref, x_ref, c_ref, gate_ref, wg_ref, wu_ref, wd_ref,
                  o_ref, dx_ref, dwg_ref, dwu_ref, dwd_ref):
    expert = pl.program_id(0)
    tile, width = x_ref.shape[1:]
    units = wg_ref.shape[2]
    room = o_ref.shape[2]
    blocks = tile // rows
    gate = gate_ref[0, :, 0:1]
    x = x_ref[0]
    c = c_ref[0]
    gate_pre = jnp.dot(x, wg_ref[0], preferred_element_type=jnp.float32)
    up_pre = jnp.dot(x, wu_ref[0], preferred_element_type=jnp.float32)
    back = across(c, wd_ref[0])
    sig = jax.nn.sigmoid(gate_pre)
    silu = gate_pre * sig
    act = (silu * up_pre).astype(jnp.bfloat16)
    act_float = act.astype(jnp.float32)
    grad_gate = jnp.sum(act_float * back, axis=1, keepdims=True)
    grad_act = back * gate
    grad_gate_pre = (grad_act * up_pre * sig * (1.0 + gate_pre * (1.0 - sig))).astype(jnp.bfloat16)
    grad_up_pre = (grad_act * silu).astype(jnp.bfloat16)
    gated = (act_float * gate).astype(jnp.bfloat16)

    def spread(values):
        values = values.reshape(blocks, rows, values.shape[1])
        if room > rows:
            empty = jnp.zeros((blocks, room - rows, values.shape[2]), jnp.float32)
            values = jnp.concatenate((values, empty), axis=1)
        return values.astype(jnp.bfloat16)

    step = min(512, width)
    for first in range(0, width, step):
        part = slice(first, first + step)
        out = jnp.dot(act, wd_ref[0, :, part], preferred_element_type=jnp.float32) * gate
        o_ref[:, 0, :, part] = spread(out)
        grad = across(grad_gate_pre, wg_ref[0, part, :]) + across(grad_up_pre, wu_ref[0, part, :])
        dx_ref[:, 0, :, part] = spread(grad)
    lanes = lax.broadcasted_iota(jnp.int32, (tile, 128), 1)
    dx_ref[:, 0, :, width:] = spread(jnp.where(lanes == first_ref[0] + expert, grad_gate, 0.0))

    @pl.when(pl.program_id(1) == 0)
    def _():
        for ref in (dwg_ref, dwu_ref, dwd_ref):
            ref[...] = jnp.zeros_like(ref)

    for first in range(0, width, step):
        part = slice(first, first + step)
        dwg_ref[0, part, :] += turned(x_ref[0, :, part], grad_gate_pre)
        dwu_ref[0, part, :] += turned(x_ref[0, :, part], grad_up_pre)
        dwd_ref[0, :, part] += turned(gated, c_ref[0, :, part])


def expert_pass(first_expert, x_slots, c_slots, gate_slots, w_gate, w_up, w_down, blocks, room):
    experts, total, width = x_slots.shape
    units = w_gate.shape[2]
    rows = total // blocks
    group = next(n for n in (16, 8, 4, 2, 1) if blocks % n == 0 and (n * rows <= 768 or n == 1))
    tile = group * rows
    extra = 128
    tall = pl.BlockSpec((1, width, units), lambda e, r, _: (e, 0, 0))
    wide = pl.BlockSpec((1, units, width), lambda e, r, _: (e, 0, 0))
    slot = pl.BlockSpec((1, tile, width), lambda e, r, _: (e, r, 0))
    kernel = functools.partial(expert_kernel, rows)
    return pl.pallas_call(
        kernel,
        grid_spec=pltpu.PrefetchScalarGridSpec(
            num_scalar_prefetch=1,
            grid=(experts, total // tile),
            in_specs=[slot, slot, pl.BlockSpec((1, tile, 128), lambda e, r, _: (e, r, 0)), tall, tall, wide],
            out_specs=[
                pl.BlockSpec((group, 1, room, width), lambda e, r, _: (r, e, 0, 0)),
                pl.BlockSpec((group, 1, room, width + extra), lambda e, r, _: (r, e, 0, 0)),
                tall, tall, wide,
            ],
        ),
        out_shape=(
            jax.ShapeDtypeStruct((blocks, experts, room, width), jnp.bfloat16),
            jax.ShapeDtypeStruct((blocks, experts, room, width + extra), jnp.bfloat16),
            jax.ShapeDtypeStruct(w_gate.shape, jnp.float32),
            jax.ShapeDtypeStruct(w_up.shape, jnp.float32),
            jax.ShapeDtypeStruct(w_down.shape, jnp.float32),
        ),
        compiler_params=pltpu.CompilerParams(vmem_limit_bytes=60 << 20),
        cost_estimate=pl.CostEstimate(
            flops=18 * experts * total * width * units,
            bytes_accessed=8 * experts * total * width + 18 * experts * width * units,
            transcendentals=experts * total * units,
        ),
        name="experts",
    )(first_expert, x_slots, c_slots, gate_slots, w_gate, w_up, w_down)


def combine_kernel(slots_ref, o_ref, dx_ref, out_ref, grad_ref):
    _, experts, tokens = slots_ref.shape
    room, width = o_ref.shape[2:]
    slots = slots_ref[0]
    picks = jnp.concatenate(
        [slot_hits(slots, e, room).astype(jnp.float32) for e in range(experts)], axis=0
    ).astype(jnp.bfloat16)
    for source, target in ((o_ref, out_ref), (dx_ref, grad_ref)):
        columns = target.shape[1]
        for first in range(0, columns, 512):
            part = slice(first, min(first + 512, columns))
            values = source[0, :, :, part].reshape(experts * room, part.stop - first)
            target[:, part] = turned(picks, values).astype(jnp.bfloat16)


def combine(slots, outs, grads):
    blocks, experts, tokens = slots.shape
    room, width = outs.shape[2:]
    wider = grads.shape[3]
    return pl.pallas_call(
        combine_kernel,
        grid=(blocks,),
        out_shape=(
            jax.ShapeDtypeStruct((blocks * tokens, width), jnp.bfloat16),
            jax.ShapeDtypeStruct((blocks * tokens, wider), jnp.bfloat16),
        ),
        in_specs=[
            pl.BlockSpec((1, experts, tokens), lambda i: (i, 0, 0)),
            pl.BlockSpec((1, experts, room, width), lambda i: (i, 0, 0, 0)),
            pl.BlockSpec((1, experts, room, wider), lambda i: (i, 0, 0, 0)),
        ],
        out_specs=[
            pl.BlockSpec((tokens, width), lambda i: (i, 0)),
            pl.BlockSpec((tokens, wider), lambda i: (i, 0)),
        ],
        compiler_params=pltpu.CompilerParams(vmem_limit_bytes=50 << 20),
        cost_estimate=pl.CostEstimate(
            flops=2 * blocks * experts * room * tokens * (width + wider),
            bytes_accessed=2 * blocks * (tokens + experts * room) * (width + wider),
            transcendentals=0,
        ),
        name="combine",
    )(slots, outs, grads)


MESH = pl.DeviceIdType.MESH


def place():
    dp, z = lax.axis_index("dp"), lax.axis_index("tensor")
    return dp // 4, dp // 2 % 2, dp % 2, z


def peer(y, x, core, z):
    return (y * 4 + x * 2 + core, z)


def block_of(y, x, core, z):
    return (y * 4 + x * 2 + core) * 4 + z


def greet(line):
    y, x, core, z = place()
    barrier = pltpu.get_barrier_semaphore()
    for near in ((y, x, 1 - core, z), (y, 1 - x, core, z), (1 - y, x, core, z)):
        pl.semaphore_signal(barrier, inc=1, device_id=peer(*near), device_id_type=MESH)

    @pl.when(z > 0)
    def _():
        pl.semaphore_signal(barrier, inc=1, device_id=peer(y, x, core, z - 1), device_id_type=MESH)

    @pl.when(z < line - 1)
    def _():
        pl.semaphore_signal(barrier, inc=1, device_id=peer(y, x, core, z + 1), device_id_type=MESH)

    pl.semaphore_wait(barrier, 3 + (z + line - 1) // line + (2 * line - 2 - z) // line)


def either(first, second, take):
    return first * (1 - take) + second * take


def remote(source, target, send_sem, recv_sem, where):
    return pltpu.make_async_remote_copy(
        src_ref=source, dst_ref=target, send_sem=send_sem, recv_sem=recv_sem,
        device_id=peer(*where), device_id_type=MESH,
    )


def landed(target, sem):
    pltpu.make_async_copy(target, target, sem).wait()


def slot_order(y, x, core, z):
    return ((y * 2 + x) * 4 + z) * 2 + core


def near_first(z, i):
    side = z // 2
    low = either(z, 3 - z, side)
    first, second = (4 - i) // 4, (5 - i) // 4 - (4 - i) // 4
    return either(i + low * (first - second), 3 - i - low * (first - second), side)


def gather_dispatch_kernel(line, rows, slots_ref, hidden_ref, gates_ref, cots_ref,
                           rows_out, gates_out, x_out, c_out, gate_out,
                           in_c, in_x, in_gate, stage_c, stage_x, stage_gate,
                           local_sem, send_sem, recv_sem, load_sem, store_sem):
    y, x, core, z = place()
    tokens, width = hidden_ref.shape
    experts = slots_ref.shape[1]
    first_expert = (y * 4 + x * 2 + core) * experts
    owns, outs = (hidden_ref, gates_ref), (rows_out, gates_out)
    near_x, near_y, sibling = (y, 1 - x, core, z), (1 - y, x, core, z), (y, x, 1 - core, z)
    last = 24
    greet(line)

    def span(n, block):
        count = owns[n].shape[0]
        return outs[n].at[pl.ds(block * count, count)]

    def spot(m):
        q = m % 4
        i = m // 4 - (q + 1) // 2
        live = (i >= 0) & (i < line)
        held = i * live.astype(jnp.int32)
        yy, xx = (y + q // 2) % 2, (x + q % 2) % 2
        return q, held, live, yy, xx, near_first(z, held)

    def sends(m):
        q, i, live, yy, xx, zz = spot(m)
        block = block_of(yy, xx, core, zz)
        own = live & (q == 0)
        table = (
            (own & (zz <= z) & (z < line - 1), (y, x, core, z + 1)),
            (own & (zz >= z) & (z > 0), (y, x, core, z - 1)),
            (own | (live & (q == 2) & (zz % 2 == 1)), near_x),
            (own | (live & (q == 1) & (zz % 2 == 0)), near_y),
            (live, sibling),
        )
        for lane, (wanted, where) in enumerate(table):
            for n in range(2):
                part = span(n, block)
                yield wanted, remote(part, part, send_sem.at[n, lane, m], recv_sem.at[n, block], where)

    def load_c(chip):
        yy, xx, zz = chip // 8, chip // 4 % 2, chip % 4
        for c in range(2):
            b = block_of(yy, xx, c, zz)
            yield pltpu.make_async_copy(
                cots_ref.at[pl.ds(b * tokens, tokens)], in_c.at[pl.ds(c * tokens, tokens)], load_sem.at[0, c]
            )

    def load_x(yy, xx, zz):
        for c in range(2):
            b = block_of(yy, xx, c, zz)
            yield pltpu.make_async_copy(
                rows_out.at[pl.ds(b * tokens, tokens)], in_x.at[pl.ds(c * tokens, tokens)], load_sem.at[1, c]
            )
            yield pltpu.make_async_copy(
                gates_out.at[pl.ds(b * gates_ref.shape[0] + first_expert, experts)], in_gate.at[c], load_sem.at[2, c]
            )

    def store(stage, target, lane, chip):
        return pltpu.make_async_copy(stage, target.at[:, pl.ds(chip * 2 * rows, 2 * rows)], store_sem.at[lane])

    def pick(source, target, yy, xx, zz, gated):
        picks = []
        for c in range(2):
            slots = slots_ref[block_of(yy, xx, c, zz)]
            pieces = []
            for e in range(experts):
                hit = slot_hits(slots, e, rows)
                pieces.append(hit.astype(jnp.float32))
                if gated:
                    gate = jnp.sum(jnp.where(hit, in_gate[c, e : e + 1, :], 0.0), axis=1, keepdims=True)
                    stage_gate[e, c * rows : (c + 1) * rows, :] = jnp.broadcast_to(gate, (rows, 128))
            picks.append(jnp.concatenate(pieces, axis=0).astype(jnp.bfloat16))
        step = min(512, width)
        for first in range(0, width, step):
            parts = [
                jnp.dot(
                    picks[c], source[c * tokens : (c + 1) * tokens, first : first + step],
                    preferred_element_type=jnp.float32,
                )
                for c in range(2)
            ]
            for e in range(experts):
                target[e, :, first : first + step] = jnp.concatenate(
                    [part[e * rows : (e + 1) * rows] for part in parts], axis=0
                ).astype(jnp.bfloat16)

    mine = block_of(y, x, core, z)
    local = [pltpu.make_async_copy(owns[n], span(n, mine), local_sem.at[n]) for n in range(2)]
    for copy in local:
        copy.start()
    for copy in load_c(0):
        copy.start()
    for copy in local:
        copy.wait()
    chips = 4 * line
    lag = 2

    def work(m, carry):
        q, i, live, yy, xx, zz = spot(m)

        @pl.when((m < last) & live & (q + i > 0))
        def _():
            for n in range(2):
                landed(span(n, block_of(yy, xx, core, zz)), recv_sem.at[n, block_of(yy, xx, core, zz)])

        for wanted, copy in sends(m):
            pl.when((m < last) & wanted)(copy.start)

        @pl.when(m < chips)
        def _():
            for copy in load_c(m):
                copy.wait()

            @pl.when(m > 0)
            def _():
                store(stage_c, c_out, 0, m - 1).wait()

            pick(in_c, stage_c, m // 8, m // 4 % 2, m % 4, False)
            store(stage_c, c_out, 0, m).start()

            @pl.when(m + 1 < chips)
            def _():
                for copy in load_c(m + 1):
                    copy.start()

        back = m - lag
        q = (back + 8) % 4
        i = (back + 8) // 4 - 2 - (q + 1) // 2
        live = (i >= 0) & (i < line)
        held = i * live.astype(jnp.int32)
        yy, xx = (y + q // 2) % 2, (x + q % 2) % 2
        zz = near_first(z, held)

        @pl.when(live)
        def _():
            block = block_of(yy, xx, 1 - core, zz)
            for n in range(2):
                landed(span(n, block), recv_sem.at[n, block])
            for copy in load_x(yy, xx, zz):
                copy.start()
            chip = (yy * 2 + xx) * 4 + zz

            @pl.when(q + held > 0)
            def _():
                store(stage_x, x_out, 1, chip).wait()
                store(stage_gate, gate_out, 2, chip).wait()

            for copy in load_x(yy, xx, zz):
                copy.wait()
            pick(in_x, stage_x, yy, xx, zz, True)
            store(stage_x, x_out, 1, chip).start()
            store(stage_gate, gate_out, 2, chip).start()

        return carry

    lax.fori_loop(0, last + lag, work, 0)
    store(stage_c, c_out, 0, chips - 1).wait()
    store(stage_x, x_out, 1, 0).wait()
    store(stage_gate, gate_out, 2, 0).wait()

    def finish(m, carry):
        for wanted, copy in sends(m):
            pl.when(wanted)(copy.wait_send)
        return carry

    lax.fori_loop(0, last, finish, 0)


def gather_dispatch(slots, hidden, gates, cots_all, rows, collective_id):
    line = 4
    blocks, experts, tokens = slots.shape
    width = hidden.shape[1]
    pair = 2 * rows
    low, wide = jnp.bfloat16, jnp.float32
    any_ref = pl.BlockSpec(memory_space=pl.ANY)
    vmem = pl.BlockSpec(memory_space=pltpu.VMEM)
    dma = pltpu.SemaphoreType.DMA
    slot_shape = jax.ShapeDtypeStruct((experts, blocks * rows, width), low)
    return pl.pallas_call(
        functools.partial(gather_dispatch_kernel, line, rows),
        out_shape=(
            jax.ShapeDtypeStruct((blocks * tokens, width), low),
            jax.ShapeDtypeStruct((blocks * gates.shape[0], tokens), wide),
            slot_shape,
            slot_shape,
            jax.ShapeDtypeStruct((experts, blocks * rows, 128), wide),
        ),
        in_specs=[vmem, any_ref, any_ref, any_ref],
        out_specs=[any_ref] * 5,
        scratch_shapes=[
            pltpu.VMEM((2 * tokens, width), low),
            pltpu.VMEM((2 * tokens, width), low),
            pltpu.VMEM((2, experts, tokens), wide),
            pltpu.VMEM((experts, pair, width), low),
            pltpu.VMEM((experts, pair, width), low),
            pltpu.VMEM((experts, pair, 128), wide),
            dma((2,)),
            dma((2, 5, 24)),
            dma((2, blocks)),
            dma((3, 2)),
            dma((3,)),
        ],
        compiler_params=pltpu.CompilerParams(
            collective_id=collective_id, has_side_effects=True, vmem_limit_bytes=40 << 20
        ),
        cost_estimate=pl.CostEstimate(
            flops=4 * blocks * experts * rows * tokens * width, bytes_accessed=200 << 20, transcendentals=0
        ),
        name="gather_dispatch",
    )(slots, hidden, gates, cots_all)[2:]


def reduce_kernel(line, slots_ref, grads_ref, outs_ref, sum_ref, part_ref,
                  grad_in, out_in, out_stage, stage, near, far_x, far_y, from_x, from_y, up, down,
                  in_sem, part_sem, stage_sem, near_sem, send_sem, far_sem, x_sem, y_sem, line_sem):
    y, x, core, z = place()
    tokens, width = sum_ref.shape
    half = tokens // 2
    experts, room = grads_ref.shape[1:3]
    rounds = line
    greet(line)

    def goal(r):
        early = 1 - r // 2
        return (line - 1) * (r % 2) * early + (r - 1) * (1 - early)

    def spot_at(q):
        r, j = q // 8, q % 8
        column = j % 4
        dy, dx = (column + 1) % 2, 1 - column // 2
        own = j // 4
        target_core = core * own + (1 - core) * (1 - own)
        return (y + dy) % 2, (x + dx) % 2, target_core, goal(r)

    def load(q):
        b = slot_order(*spot_at(q))
        return (
            pltpu.make_async_copy(grads_ref.at[b], grad_in.at[q % 2], in_sem.at[0, q % 2]),
            pltpu.make_async_copy(outs_ref.at[b], out_in.at[q % 2], in_sem.at[1, q % 2]),
        )

    def to_part(q):
        b = block_of(*spot_at(q))
        return pltpu.make_async_copy(out_stage.at[q % 2], part_ref.at[pl.ds(b * tokens, tokens)], part_sem.at[q % 2])

    def to_sibling(r, j):
        return pltpu.make_async_remote_copy(
            src_ref=stage.at[j], dst_ref=near.at[r * 4 + j], send_sem=stage_sem.at[j], recv_sem=near_sem.at[r * 4 + j],
            device_id=peer(y, x, 1 - core, z), device_id_type=MESH,
        )

    near_x, near_y = peer(y, 1 - x, core, z), peer(1 - y, x, core, z)

    def rows(h):
        return pl.ds(h * half, half)

    def cross(kind, r):
        column, h, target, sem, index, lane = {
            "far_x": (0, 0, far_x.at[r], far_sem.at[0, r], near_x, 0),
            "far_y": (0, 1, far_y.at[r], far_sem.at[1, r], near_y, 1),
            "x0": (1, 0, from_x.at[r, rows(0)], x_sem.at[r, 0], near_x, 2),
            "x1": (1, 1, from_x.at[r, rows(1)], x_sem.at[r, 1], near_x, 3),
            "y0": (2, 0, from_y.at[r, rows(0)], y_sem.at[r, 0], near_y, 4),
            "y1": (2, 1, from_y.at[r, rows(1)], y_sem.at[r, 1], near_y, 5),
        }[kind]
        return pltpu.make_async_remote_copy(
            src_ref=near.at[r * 4 + column, rows(h)], dst_ref=target, send_sem=send_sem.at[lane, r], recv_sem=sem,
            device_id=index, device_id_type=MESH,
        )

    def along(sign, r):
        target = up if sign > 0 else down
        lane = 0 if sign > 0 else 1
        return pltpu.make_async_remote_copy(
            src_ref=near.at[r * 4 + 3], dst_ref=target.at[r], send_sem=send_sem.at[6 + lane, r], recv_sem=line_sem.at[lane, r],
            device_id=peer(y, x, core, z + sign), device_id_type=MESH,
        )

    def term(q, source, target_width, store):
        picks = jnp.concatenate(
            [slot_hits(slots_ref[block_of(*spot_at(q))], e, room).astype(jnp.float32) for e in range(experts)], axis=0
        ).astype(jnp.bfloat16)
        for first in range(0, target_width, 512):
            part = slice(first, min(first + 512, target_width))
            values = source[q % 2, :, :, part].reshape(experts * room, part.stop - first)
            store(part, turned(picks, values))

    for copy in load(0):
        copy.start()

    def one(r, j, own):
        q = r * 8 + own * 4 + j
        for copy in load(q):
            copy.wait()

        @pl.when(q + 1 < rounds * 8)
        def _():
            for copy in load(q + 1):
                copy.start()

        if own:
            near_slot = r * 4 + j
            to_sibling(r, j).wait_recv()

            def keep(part, value):
                near[near_slot, :, part] = (value + near[near_slot, :, part].astype(jnp.float32)).astype(jnp.bfloat16)

            term(q, grad_in, width, keep)
        else:

            @pl.when(r > 0)
            def _():
                to_sibling(r - 1, j).wait_send()

            def keep(part, value):
                stage[j, :, part] = value.astype(jnp.bfloat16)

            term(q, grad_in, width, keep)
            to_sibling(r, j).start()

        @pl.when(q >= 2)
        def _():
            to_part(q - 2).wait()

        def put(part, value):
            out_stage[q % 2, :, part] = value.astype(jnp.bfloat16)

        term(q, out_in, out_stage.shape[2], put)
        to_part(q).start()

    def add(target, h, *sources):
        for first in range(0, width, 512):
            part = slice(first, min(first + 512, width))
            total = near[target, h, part].astype(jnp.float32)
            for source in sources:
                total = total + source(part).astype(jnp.float32)
            near[target, h, part] = total.astype(jnp.bfloat16)

    def work(s, carry):
        @pl.when(s < rounds)
        def _():
            r = s
            lax.fori_loop(0, 4, lambda j, c: (one(r, j, 0), c)[1], 0)
            lax.fori_loop(0, 4, lambda j, c: (one(r, j, 1), c)[1], 0)
            for kind in ("far_x", "far_y", "x0", "y1"):
                cross(kind, r).start()
            cross("far_y", r).wait_recv()
            add(r * 4 + 1, rows(1), lambda part: far_y[r, :, part])
            cross("x1", r).start()
            cross("far_x", r).wait_recv()
            add(r * 4 + 2, rows(0), lambda part: far_x[r, :, part])
            cross("y0", r).start()

        @pl.when((s >= 1) & (s < rounds + 1))
        def _():
            r = s - 1
            for kind in ("x0", "x1", "y0", "y1"):
                cross(kind, r).wait_recv()
            for h in range(2):
                add(
                    r * 4 + 3,
                    rows(h),
                    lambda part: from_x[r, rows(h), part],
                    lambda part: from_y[r, rows(h), part],
                )

        for hop in range(line - 1):
            r = s - 1 - hop
            live = (r >= 0) & (r < rounds)
            held = r * live.astype(jnp.int32)

            @pl.when(live & (goal(held) > z) & (z == hop))
            def _():
                if hop:
                    along(1, held).wait_recv()
                    for h in range(2):
                        add(held * 4 + 3, rows(h), lambda part: up[held, rows(h), part])
                along(1, held).start()

            @pl.when(live & (goal(held) < z) & (line - 1 - z == hop))
            def _():
                if hop:
                    along(-1, held).wait_recv()
                    for h in range(2):
                        add(held * 4 + 3, rows(h), lambda part: down[held, rows(h), part])
                along(-1, held).start()

        return carry

    lax.fori_loop(0, rounds + line - 1, work, 0)

    mine = (z + (z + 2) // 3) % 4 + z // 3
    sum_ref[...] = near[mine * 4 + 3].astype(jnp.float32)

    @pl.when(z > 0)
    def _():
        along(1, mine).wait_recv()
        sum_ref[...] += up[mine].astype(jnp.float32)

    @pl.when(z < line - 1)
    def _():
        along(-1, mine).wait_recv()
        sum_ref[...] += down[mine].astype(jnp.float32)

    def finish(r, carry):
        for kind in ("far_x", "far_y", "x0", "x1", "y0", "y1"):
            cross(kind, r).wait_send()

        @pl.when(goal(r) > z)
        def _():
            along(1, r).wait_send()

        @pl.when(goal(r) < z)
        def _():
            along(-1, r).wait_send()

        return carry

    lax.fori_loop(0, rounds, finish, 0)
    for j in range(4):
        to_sibling(rounds - 1, j).wait_send()
    for q in (rounds * 8 - 2, rounds * 8 - 1):
        to_part(q).wait()


def reduce_all(slots, outs, grads, collective_id):
    blocks, experts, tokens = slots.shape
    room, width = outs.shape[2:]
    wider = grads.shape[3]
    line = 4
    low = jnp.bfloat16
    any_ref = pl.BlockSpec(memory_space=pl.ANY)
    vmem = pl.BlockSpec(memory_space=pltpu.VMEM)
    dma = pltpu.SemaphoreType.DMA
    return pl.pallas_call(
        functools.partial(reduce_kernel, line),
        out_shape=(
            jax.ShapeDtypeStruct((tokens, wider), jnp.float32),
            jax.ShapeDtypeStruct((blocks * tokens, width), low),
        ),
        in_specs=[vmem, any_ref, any_ref],
        out_specs=[vmem, any_ref],
        scratch_shapes=[
            pltpu.VMEM((2, experts, room, wider), low),
            pltpu.VMEM((2, experts, room, width), low),
            pltpu.VMEM((2, tokens, width), low),
            pltpu.VMEM((4, tokens, wider), low),
            pltpu.VMEM((line * 4, tokens, wider), low),
            pltpu.VMEM((line, tokens // 2, wider), low),
            pltpu.VMEM((line, tokens // 2, wider), low),
            pltpu.VMEM((line, tokens, wider), low),
            pltpu.VMEM((line, tokens, wider), low),
            pltpu.VMEM((line, tokens, wider), low),
            pltpu.VMEM((line, tokens, wider), low),
            dma((2, 2)),
            dma((2,)),
            dma((4,)),
            dma((line * 4,)),
            dma((8, line)),
            dma((2, line)),
            dma((line, 2)),
            dma((line, 2)),
            dma((2, line)),
        ],
        compiler_params=pltpu.CompilerParams(
            collective_id=collective_id, has_side_effects=True, vmem_limit_bytes=62 << 20
        ),
        cost_estimate=pl.CostEstimate(
            flops=2 * blocks * experts * room * tokens * (width + wider),
            bytes_accessed=2 * blocks * experts * room * (width + wider),
            transcendentals=0,
        ),
        name="reduce_all",
    )(slots, grads, outs)


class LineGather:
    def __init__(self, own, out, send_sem, recv_sem, line):
        self.own, self.out, self.send_sem, self.recv_sem, self.line = own, out, send_sem, recv_sem, line
        self.spot = place()
        self.rows = own.shape[0]

    def view(self, block):
        return self.out.at[pl.ds(block * self.rows, self.rows)]

    def inside(self, block):
        return (block >= 0) & (block < self.line)

    def copy(self, sign, step):
        y, x, core, z = self.spot
        block = z - sign * step
        lane = (1 - sign) // 2
        source = self.own if step == 0 else self.view(block)
        return remote(
            source, self.view(block), self.send_sem.at[lane, step], self.recv_sem.at[lane, step], (y, x, core, z + sign)
        )

    def sends(self, sign, step):
        z = self.spot[3]
        return self.inside(z - sign * step) & self.inside(z + sign)

    def begin(self):
        for sign in (1, -1):
            pl.when(self.sends(sign, 0))(self.copy(sign, 0).start)

    def advance(self, step):
        z = self.spot[3]
        for sign in (1, -1):
            block = z - sign * (step + 1)
            lane = (1 - sign) // 2

            @pl.when(self.inside(block))
            def _():
                landed(self.view(block), self.recv_sem.at[lane, step])

            if step + 1 < self.line - 1:
                pl.when(self.sends(sign, step + 1))(self.copy(sign, step + 1).start)

    def finish(self):
        for sign in (1, -1):
            for step in range(self.line - 1):
                pl.when(self.sends(sign, step))(self.copy(sign, step).wait_send)


def start_kernel(line, hidden_ref, wq_ref, wk_ref, wv_ref, wo_ref, hidden_out, joined_out, wo_out,
                 local_sem, line_send, line_recv, plane_send, plane_recv):
    y, x, core, z = place()
    owns = (wq_ref, wk_ref, wv_ref, wo_ref)
    near_x, near_y, sibling = (y, 1 - x, core, z), (1 - y, x, core, z), (y, x, 1 - core, z)

    def view(n, yy, xx, half=None):
        group = yy * 4 + xx * 2 + core
        rows, columns = owns[n].shape
        first, count = (0, rows) if half is None else (half * (rows // 2), rows // 2)
        if n < 3:
            return joined_out.at[pl.ds(group * rows + first, count), pl.ds(n * columns, columns)]
        return wo_out.at[pl.ds(first, count), pl.ds(pl.multiple_of(group * columns, columns), columns)]

    kinds = ("x", "y", "s", "fy", "fx", "sx", "sy", "sf")

    def copy(kind, n):
        source, target, where = {
            "x": (owns[n], view(n, y, x), near_x),
            "y": (owns[n], view(n, y, x), near_y),
            "s": (owns[n], view(n, y, x), sibling),
            "fy": (view(n, y, 1 - x, 0), view(n, y, 1 - x, 0), near_y),
            "fx": (view(n, 1 - y, x, 1), view(n, 1 - y, x, 1), near_x),
            "sx": (view(n, y, 1 - x), view(n, y, 1 - x), sibling),
            "sy": (view(n, 1 - y, x), view(n, 1 - y, x), sibling),
            "sf": (view(n, 1 - y, 1 - x), view(n, 1 - y, 1 - x), sibling),
        }[kind]
        lane = kinds.index(kind)
        return remote(source, target, plane_send.at[lane, n], plane_recv.at[lane, n], where)

    def other(n, yy, xx):
        group = yy * 4 + xx * 2 + 1 - core
        rows, columns = owns[n].shape
        if n < 3:
            return joined_out.at[pl.ds(group * rows, rows), pl.ds(n * columns, columns)]
        return wo_out.at[pl.ds(0, rows), pl.ds(pl.multiple_of(group * columns, columns), columns)]

    greet(line)
    hidden = LineGather(hidden_ref, hidden_out, line_send, line_recv, line)
    locals_ = [pltpu.make_async_copy(hidden_ref, hidden.view(z), local_sem.at[4])]
    locals_ += [pltpu.make_async_copy(owns[n], view(n, y, x), local_sem.at[n]) for n in range(4)]
    hidden.begin()
    for n in range(4):
        for kind in ("x", "y", "s"):
            copy(kind, n).start()
    for local in locals_:
        local.start()
    for n in range(4):
        landed(view(n, y, 1 - x), plane_recv.at[0, n])
        copy("fy", n).start()
        copy("sx", n).start()
        landed(view(n, 1 - y, x), plane_recv.at[1, n])
        copy("fx", n).start()
        copy("sy", n).start()
    hidden.advance(0)
    for n in range(4):
        landed(view(n, 1 - y, 1 - x, 0), plane_recv.at[3, n])
        landed(view(n, 1 - y, 1 - x, 1), plane_recv.at[4, n])
        copy("sf", n).start()
    for step in range(1, line - 1):
        hidden.advance(step)
    for n in range(4):
        landed(other(n, y, x), plane_recv.at[2, n])
        landed(other(n, y, 1 - x), plane_recv.at[5, n])
        landed(other(n, 1 - y, x), plane_recv.at[6, n])
        landed(other(n, 1 - y, 1 - x), plane_recv.at[7, n])
    hidden.finish()
    for n in range(4):
        for kind in kinds:
            copy(kind, n).wait_send()
    for local in locals_:
        local.wait()


def start_exchange(hidden, w_query, w_key, w_value, w_out, collective_id):
    line = 4
    any_ref = pl.BlockSpec(memory_space=pl.ANY)
    dma = pltpu.SemaphoreType.DMA
    rows, width = hidden.shape
    part, columns = w_query.shape
    low = jnp.bfloat16
    return pl.pallas_call(
        functools.partial(start_kernel, line),
        out_shape=(
            jax.ShapeDtypeStruct((line * rows, width), low),
            jax.ShapeDtypeStruct((8 * part, 3 * columns), low),
            jax.ShapeDtypeStruct((w_out.shape[0], 8 * w_out.shape[1]), low),
        ),
        in_specs=[any_ref] * 5,
        out_specs=[any_ref] * 3,
        scratch_shapes=[dma((5,)), dma((2, line)), dma((2, line)), dma((8, 4)), dma((8, 4))],
        compiler_params=pltpu.CompilerParams(collective_id=collective_id, has_side_effects=True),
        cost_estimate=pl.CostEstimate(flops=0, bytes_accessed=150 << 20, transcendentals=0),
        name="start_exchange",
    )(hidden, w_query, w_key, w_value, w_out)


class LineReduce:
    def __init__(self, part, up, down, send_sem, recv_sem, line):
        self.part, self.up, self.down = part, up, down
        self.send_sem, self.recv_sem, self.line = send_sem, recv_sem, line
        self.spot = place()

    def copy(self, sign, goal):
        y, x, core, z = self.spot
        lane = (1 - sign) // 2
        target = self.up if sign > 0 else self.down
        return remote(
            self.part.at[goal], target.at[goal], self.send_sem.at[lane, goal], self.recv_sem.at[lane, goal],
            (y, x, core, z + sign),
        )

    def order(self, i):
        z = self.spot[3]
        return either(self.line - 1 - i, i, z * 2 // self.line)

    def lead(self, goal):
        z = self.spot[3]
        pl.when((z == 0) & (goal > 0))(self.copy(1, goal).start)
        pl.when((z == self.line - 1) & (goal < z))(self.copy(-1, goal).start)

    def advance(self, unit, total_ref):
        z, line = self.spot[3], self.line
        for sign in (1, -1):
            goal = line - 1 - unit + z if sign > 0 else unit - line + 1 + z
            live = ((z > 0) & (goal < line)) if sign > 0 else ((z < line - 1) & (goal >= 0))
            inbox = self.up if sign > 0 else self.down

            @pl.when(live)
            def _():
                self.copy(sign, goal).wait_recv()
                if unit < line - 1:
                    self.part[goal] = (
                        self.part[goal].astype(jnp.float32) + inbox[goal].astype(jnp.float32)
                    ).astype(jnp.bfloat16)
                    self.copy(sign, goal).start()
                else:
                    total_ref[...] += inbox[goal].astype(jnp.float32)

    def finish(self):
        z = self.spot[3]

        def step(goal, carry):
            pl.when(goal > z)(self.copy(1, goal).wait_send)
            pl.when(goal < z)(self.copy(-1, goal).wait_send)
            return carry

        lax.fori_loop(0, self.line, step, 0)


def mixed_out_kernel(line, mixed_ref, w_ref, residual_ref, gain_ref, router_ref,
                     x_ref, hidden_ref, probs_ref, part, up, down, send_sem, recv_sem):
    rows, width = x_ref.shape
    greet(line)
    reduce = LineReduce(part, up, down, send_sem, recv_sem, line)
    z = reduce.spot[3]

    def term(i, carry):
        goal = reduce.order(i)
        first = pl.multiple_of(goal * rows, rows)
        for column in range(0, width, 512):
            piece = slice(column, column + 512)
            value = jnp.dot(mixed_ref[pl.ds(first, rows), :], w_ref[:, piece], preferred_element_type=jnp.float32)

            @pl.when(goal == z)
            def _():
                x_ref[:, piece] = value

            part[goal, :, piece] = value.astype(jnp.bfloat16)
        reduce.lead(goal)
        return carry

    lax.fori_loop(0, line, term, 0)
    for unit in range(1, line):
        reduce.advance(unit, x_ref)
    x_one = x_ref[...] + residual_ref[...].astype(jnp.float32)
    x_ref[...] = x_one
    scale = lax.rsqrt(jnp.mean(x_one * x_one, axis=-1, keepdims=True) + norm_eps)
    hidden = (x_one * scale * gain_ref[...]).astype(jnp.bfloat16)
    hidden_ref[...] = hidden
    logits = lax.dot_general(
        router_ref[...], hidden, (((1,), (1,)), ((), ())), preferred_element_type=jnp.float32
    )
    shifted = jnp.exp(logits - jnp.max(logits, axis=0, keepdims=True))
    probs_ref[...] = shifted / jnp.sum(shifted, axis=0, keepdims=True)
    reduce.finish()


def mixed_out(mixed, w_out, residual, gain, router_turned, collective_id):
    line = 4
    rows, width = residual.shape
    experts = router_turned.shape[0]
    vmem = pl.BlockSpec(memory_space=pltpu.VMEM)
    dma = pltpu.SemaphoreType.DMA
    block = pltpu.VMEM((line, rows, width), jnp.bfloat16)
    return pl.pallas_call(
        functools.partial(mixed_out_kernel, line),
        out_shape=(
            jax.ShapeDtypeStruct((rows, width), jnp.float32),
            jax.ShapeDtypeStruct((rows, width), jnp.bfloat16),
            jax.ShapeDtypeStruct((experts, rows), jnp.float32),
        ),
        in_specs=[vmem] * 5,
        out_specs=[vmem] * 3,
        scratch_shapes=[block, block, block, dma((2, line)), dma((2, line))],
        compiler_params=pltpu.CompilerParams(
            collective_id=collective_id, has_side_effects=True, vmem_limit_bytes=56 << 20
        ),
        cost_estimate=pl.CostEstimate(flops=0, bytes_accessed=150 << 20, transcendentals=0),
        name="mixed_out",
    )(mixed, w_out, residual, gain.reshape(1, width), router_turned)


class Butterfly:
    def __init__(self, data, total, from_core, from_x, from_y, from_z, sums, send_sem, recv_sem):
        self.data, self.total, self.sums = data, total, sums
        self.boxes = {"core": from_core, "x": from_x, "y": from_y}
        self.from_z, self.send_sem, self.recv_sem = from_z, send_sem, recv_sem
        y, x, core, z = self.spot = place()
        self.width = data.shape[1]
        self.near = {"core": (y, x, 1 - core, z), "x": (y, 1 - x, core, z), "y": (1 - y, x, core, z)}
        half, quarter, eighth = self.width // 2, self.width // 4, self.width // 8
        first = core * half
        self.kept = {"core": (first, half), "x": (first + x * quarter, quarter)}
        self.kept["y"] = (first + x * quarter + y * eighth, eighth)
        self.away = {
            "core": ((1 - core) * half, half),
            "x": (first + (1 - x) * quarter, quarter),
            "y": (first + x * quarter + (1 - y) * eighth, eighth),
        }

    def part(self, span):
        return pl.ds(pl.multiple_of(span[0], span[1]), span[1])

    def fold_copy(self, axis):
        lane = ("core", "x", "y").index(axis)
        return remote(
            self.data.at[:, self.part(self.away[axis])], self.boxes[axis], self.send_sem.at[lane],
            self.recv_sem.at[lane], self.near[axis],
        )

    def fold(self, axis):
        copy = self.fold_copy(axis)
        copy.start()
        copy.wait()
        self.data[:, self.part(self.kept[axis])] += self.boxes[axis][...]

    def line_step(self, step):
        y, x, core, z = self.spot
        other = (z + 1 - 2 * (z % 2)) if step == 0 else (z + 2) % 4
        piece = self.part(self.kept["y"])
        source = self.data.at[:, piece] if step == 0 else self.sums
        copy = remote(
            source, self.from_z.at[step], self.send_sem.at[3 + step], self.recv_sem.at[3 + step], (y, x, core, other)
        )
        copy.start()
        copy.wait()
        if step == 0:
            self.sums[...] = self.data[:, piece] + self.from_z[0]
        else:
            self.total[:, piece] = self.sums[...] + self.from_z[1]

    def unfold(self, axis):
        lane = 5 + ("core", "x", "y").index(axis)
        mine = self.total.at[:, self.part(self.kept[axis])]
        copy = remote(mine, mine, self.send_sem.at[lane], self.recv_sem.at[lane], self.near[axis])
        copy.start()
        copy.wait_send()
        landed(self.total.at[:, self.part(self.away[axis])], self.recv_sem.at[lane])

    def scratch(rows, width):
        low = jnp.float32
        return [
            pltpu.VMEM((rows, width // 2), low),
            pltpu.VMEM((rows, width // 4), low),
            pltpu.VMEM((rows, width // 8), low),
            pltpu.VMEM((2, rows, width // 8), low),
            pltpu.VMEM((rows, width // 8), low),
            pltpu.SemaphoreType.DMA((8,)),
            pltpu.SemaphoreType.DMA((8,)),
        ]


def greet_far(line):
    y, x, core, z = place()
    barrier = pltpu.get_barrier_semaphore()
    for near in ((y, x, 1 - core, z), (y, 1 - x, core, z), (1 - y, x, core, z)):
        pl.semaphore_signal(barrier, inc=1, device_id=peer(*near), device_id_type=MESH)
    for step in range(1, line):
        pl.semaphore_signal(barrier, inc=1, device_id=peer(y, x, core, (z + step) % line), device_id_type=MESH)
    pl.semaphore_wait(barrier, 3 + line - 1)


def back_gather_kernel(line, own_ref, sums_ref, out_ref, total_ref, data, local_sem, send_sem, recv_sem, *fly):
    greet_far(line)
    gather = LineGather(own_ref, out_ref, send_sem, recv_sem, line)
    local = pltpu.make_async_copy(own_ref, gather.view(gather.spot[3]), local_sem)
    gather.begin()
    local.start()
    data[...] = sums_ref[...]
    butterfly = Butterfly(data, total_ref, *fly)
    for axis in ("core", "x", "y"):
        butterfly.fold(axis)
    gather.advance(0)
    butterfly.line_step(0)
    gather.advance(1)
    butterfly.line_step(1)
    for axis in ("y", "x", "core"):
        butterfly.unfold(axis)
    gather.advance(2)
    gather.finish()
    local.wait()


def back_gather(own, sums, collective_id):
    line = 4
    any_ref = pl.BlockSpec(memory_space=pl.ANY)
    vmem = pl.BlockSpec(memory_space=pltpu.VMEM)
    dma = pltpu.SemaphoreType.DMA
    return pl.pallas_call(
        functools.partial(back_gather_kernel, line),
        out_shape=(
            jax.ShapeDtypeStruct((line * own.shape[0], own.shape[1]), own.dtype),
            jax.ShapeDtypeStruct(sums.shape, jnp.float32),
        ),
        in_specs=[any_ref, vmem],
        out_specs=[any_ref, vmem],
        scratch_shapes=[
            pltpu.VMEM(sums.shape, jnp.float32), dma(()), dma((2, line)), dma((2, line)),
            *Butterfly.scratch(*sums.shape),
        ],
        compiler_params=pltpu.CompilerParams(collective_id=collective_id, has_side_effects=True),
        cost_estimate=pl.CostEstimate(flops=0, bytes_accessed=150 << 20, transcendentals=0),
        name="back_gather",
    )(own, sums)


def last_kernel(line, joined_ref, weight_ref, hidden_ref, mixed_ref, attn_ref, residual_ref, gain_ref, x_grad_ref, gains_ref,
                input_ref, wq_ref, wk_ref, wv_ref, wo_ref, total_ref,
                part, up, down, stage, near, far_x, far_y, from_x, from_y, data,
                line_send, line_recv, stage_sem, near_sem, send_sem, recv_sem, *fly):
    y, x, core, z = place()
    rows, width = input_ref.shape
    columns = joined_ref.shape[1]
    half = rows // 2
    low = jnp.bfloat16
    greet_far(line)
    reduce = LineReduce(part, up, down, line_send, line_recv, line)

    def term(i, carry):
        goal = reduce.order(i)
        first = pl.multiple_of(goal * rows, rows)
        for column in range(0, width, 512):
            piece = slice(column, column + 512)
            value = across(joined_ref[pl.ds(first, rows), :], weight_ref[piece, :])

            @pl.when(goal == z)
            def _():
                input_ref[:, piece] = value

            part[goal, :, piece] = value.astype(low)
        reduce.lead(goal)
        return carry

    lax.fori_loop(0, line, term, 0)
    near_x, near_y, sibling = (y, 1 - x, core, z), (1 - y, x, core, z), (y, x, 1 - core, z)

    def terms(j, own, store):
        dy, dx = (j + 1) % 2, 1 - j // 2
        group = (y + dy) % 2 * 4 + (x + dx) % 2 * 2 + (core if own else 1 - core)
        span = pl.ds(pl.multiple_of(group * rows, rows), rows)
        turned_rows = hidden_ref[:, span]
        for column in range(0, columns, 512):
            piece = slice(column, column + 512)
            store(piece, turned(turned_rows, joined_ref[:, piece]))
        value = turned(mixed_ref[...], attn_ref[:, span])
        store(slice(columns, columns + rows), value[:rows])
        store(slice(columns + rows, columns + 2 * rows), value[rows:])

    def to_sibling(j):
        return remote(stage.at[j], near.at[j], stage_sem.at[j], near_sem.at[j], sibling)

    def away(j, carry):
        def store(piece, value):
            stage[j, :, piece] = value.astype(low)

        terms(j, False, store)
        to_sibling(j).start()
        return carry

    def own(j, carry):
        to_sibling(j).wait_recv()

        def store(piece, value):
            near[j, :, piece] = (value + near[j, :, piece].astype(jnp.float32)).astype(low)

        terms(j, True, store)
        return carry

    lax.fori_loop(0, 4, away, 0)
    lax.fori_loop(0, 4, own, 0)

    def line_rows(h):
        return pl.ds(h * half, half)

    def cross(kind):
        column, h, target, where = {
            "far_x": (0, 0, far_x, near_x),
            "far_y": (0, 1, far_y, near_y),
            "x0": (1, 0, from_x.at[line_rows(0)], near_x),
            "x1": (1, 1, from_x.at[line_rows(1)], near_x),
            "y0": (2, 0, from_y.at[line_rows(0)], near_y),
            "y1": (2, 1, from_y.at[line_rows(1)], near_y),
        }[kind]
        lane = kinds.index(kind)
        return remote(near.at[column, line_rows(h)], target, send_sem.at[lane], recv_sem.at[lane], where)

    kinds = ("far_x", "far_y", "x0", "y1", "x1", "y0")
    for kind in kinds[:4]:
        cross(kind).start()

    def add(column, h, source):
        near[column, line_rows(h), :] = (
            near[column, line_rows(h), :].astype(jnp.float32) + source[...].astype(jnp.float32)
        ).astype(low)

    reduce.advance(1, input_ref)
    cross("far_y").wait_recv()
    add(1, 1, far_y)
    cross("x1").start()
    cross("far_x").wait_recv()
    add(2, 0, far_x)
    cross("y0").start()
    reduce.advance(2, input_ref)
    for kind in kinds[2:]:
        cross(kind).wait_recv()
    for n, ref in enumerate((wq_ref, wk_ref, wv_ref, wo_ref, wo_ref)):
        count = columns // 3 if n < 3 else rows
        first = n * (columns // 3) if n < 3 else columns + (n - 3) * rows
        piece = slice(first, first + count)
        total = sum(r[:, piece].astype(jnp.float32) for r in (near.at[3], from_x, from_y))
        if n < 3:
            ref[...] = total
        else:
            ref[(n - 3) * rows : (n - 2) * rows, :] = total
    reduce.advance(3, input_ref)
    grad = input_ref[...]
    values = residual_ref[...].astype(jnp.float32)
    scale = lax.rsqrt(jnp.mean(values * values, axis=-1, keepdims=True) + norm_eps)
    gained = grad * gain_ref[...]
    inner = jnp.sum(gained * values, axis=-1, keepdims=True)
    data[...] = gains_ref[...]
    data[2:3, :] = jnp.sum(grad * values * scale, axis=0, keepdims=True)
    input_ref[...] = x_grad_ref[...] + scale * gained - values * (scale * scale * scale * inner / width)
    butterfly = Butterfly(data, total_ref, *fly)
    for axis in ("core", "x", "y"):
        butterfly.fold(axis)
    butterfly.line_step(0)
    butterfly.line_step(1)
    for axis in ("y", "x", "core"):
        butterfly.unfold(axis)
    reduce.finish()
    for j in range(4):
        to_sibling(j).wait_send()
    for kind in kinds:
        cross(kind).wait_send()


def last_exchange(joined, weight, hidden, mixed, attn, residual, gain, x_grad, gains, collective_id):
    line = 4
    rows, width = residual.shape
    columns = joined.shape[1] // 3
    low, wide = jnp.bfloat16, jnp.float32
    vmem = pl.BlockSpec(memory_space=pltpu.VMEM)
    dma = pltpu.SemaphoreType.DMA
    block = pltpu.VMEM((line, rows, width), low)
    one = pltpu.VMEM((rows, width), low)
    part = pltpu.VMEM((rows // 2, width), low)
    square = jax.ShapeDtypeStruct((rows, columns), wide)
    return pl.pallas_call(
        functools.partial(last_kernel, line),
        out_shape=(
            jax.ShapeDtypeStruct((rows, width), wide), square, square, square,
            jax.ShapeDtypeStruct((2 * rows, rows), wide),
            jax.ShapeDtypeStruct(gains.shape, wide),
        ),
        in_specs=[vmem] * 9,
        out_specs=[vmem] * 6,
        scratch_shapes=[
            block, block, block, pltpu.VMEM((4, rows, width), low), pltpu.VMEM((4, rows, width), low),
            part, part, one, one, pltpu.VMEM(gains.shape, wide),
            dma((2, line)), dma((2, line)), dma((4,)), dma((4,)), dma((6,)), dma((6,)),
            *Butterfly.scratch(*gains.shape),
        ],
        compiler_params=pltpu.CompilerParams(
            collective_id=collective_id, has_side_effects=True, vmem_limit_bytes=62 << 20
        ),
        cost_estimate=pl.CostEstimate(flops=0, bytes_accessed=250 << 20, transcendentals=0),
        name="last_exchange",
    )(joined, weight, hidden, mixed, attn, residual, gain.reshape(1, width), x_grad, gains)


def visible_block(row_paths, key_paths, key_valid, row_first):
    row_count = row_paths.shape[1]
    key_count = key_paths.shape[1]
    key_segment = key_paths[0][None, :]
    on_path = (
        (key_segment == row_paths[0][:, None])
        | (key_segment == row_paths[1][:, None])
        | (key_segment == row_paths[2][:, None])
    )
    row_place = row_first + lax.iota(jnp.int32, row_count)
    key_place = lax.iota(jnp.int32, key_count)
    earlier = key_place[None, :] <= row_place[:, None]
    return on_path & earlier & (key_valid[None, :] == 1) | (
        key_place[None, :] == row_place[:, None]
    )


def rotation(positions, head_dim):
    half = head_dim // 2
    freqs = jnp.exp(-jnp.log(rope_base) * 2.0 * lax.iota(jnp.float32, half) / head_dim)
    angles = positions.astype(jnp.float32)[:, None] * freqs[None, :]
    return (jnp.cos(angles), jnp.sin(angles))


def rotate(values, cosine, sine):
    half = values.shape[-1] // 2
    first = values[..., :half]
    second = values[..., half:]
    cosine = cosine[:, None, :]
    sine = sine[:, None, :]
    return jnp.concatenate(
        (first * cosine - second * sine, second * cosine + first * sine), axis=-1
    )


def unrotate(grads, cosine, sine):
    half = grads.shape[-1] // 2
    first = grads[..., :half]
    second = grads[..., half:]
    cosine = cosine[:, None, :]
    sine = sine[:, None, :]
    return jnp.concatenate(
        (first * cosine + second * sine, second * cosine - first * sine), axis=-1
    )


def rms_apply(values, gain):
    scale = lax.rsqrt(jnp.mean(values * values, axis=-1, keepdims=True) + norm_eps)
    return (values * scale * gain, scale)


def rms_grad(values, scale, gain, grads, inner, width):
    grad_values = scale * gain * grads - values * scale**3 * inner / width
    grad_gain = jnp.sum(grads * values * scale, axis=0)
    return (grad_values, grad_gain)


def tensor_sums(pair):
    return lax.psum((pair[0], pair[1]), "tensor")


def heads_to_rows(term, rows):
    return lax.psum_scatter(
        term(jnp.int32(0), rows * lax.axis_size("tensor")).astype(jnp.bfloat16),
        "tensor",
        scatter_dimension=0,
        tiled=True,
    ).astype(jnp.float32)


def sum_over_dp(rows):
    dp = lax.axis_size("dp")
    pieces = rows.reshape(dp, rows.shape[0] // dp, rows.shape[1])
    return lax.psum_scatter(pieces, "dp", scatter_dimension=0, tiled=False)


def sum_over_tensor(part):
    return lax.psum_scatter(part, "tensor", scatter_dimension=0, tiled=True)


def body(
    residual,
    attn_gain,
    w_query,
    w_key,
    w_value,
    query_gain,
    key_gain,
    w_out,
    moe_gain,
    router,
    w_gate,
    w_up,
    w_down,
    segment_path,
    token_valid,
    routes,
    route_order,
    cotangent,
):
    tensor_rank = lax.axis_index("tensor")
    tok_dev, width = residual.shape
    seq_len = segment_path.shape[1]
    top_count = routes.shape[1]
    experts = router.shape[1]
    local_experts = w_gate.shape[0]
    dp_groups = experts // local_experts
    capacity = 9 * tok_dev * top_count // (8 * experts)
    full_width = H * HD
    block_rows = min(512, seq_len)
    block_count = seq_len // block_rows
    score_scale = HD ** (-0.5)
    everyone = ("dp", "tensor")
    direct = dp_groups == 8 and lax.axis_size("tensor") == 4
    first_expert = lax.axis_index("dp") * local_experts
    slot_rows = padded(capacity, 8)
    valid_dev = lax.dynamic_slice_in_dim(token_valid, tensor_rank * tok_dev, tok_dev)
    slots_own = slot_table(routes, route_order, valid_dev, experts, capacity)
    slots_all = lax.all_gather(slots_own.astype(jnp.bfloat16), everyone, axis=0)
    slots = lax.dynamic_slice_in_dim(slots_all, first_expert, local_experts, 1).astype(jnp.int32)
    blocks = slots.shape[0]
    cots_all = lax.all_gather(cotangent, everyone, axis=0, tiled=True)
    c_slots = None if direct else dispatch(slots, None, cots_all, slot_rows)
    head_cols = w_query.shape[1]
    local_heads = head_cols // HD
    residual_float = residual.astype(jnp.float32)
    normed_one, scale_one = rms_apply(residual_float, attn_gain)
    hidden = normed_one.astype(jnp.bfloat16)
    if direct:
        hidden_all, joined_weight, gathered_out = start_exchange(hidden, w_query, w_key, w_value, w_out, 3)
    else:
        hidden_all = lax.all_gather(hidden, "tensor", axis=0, tiled=True)
        joined_weight = jnp.concatenate(
            [lax.all_gather(w, "dp", axis=0, tiled=True) for w in (w_query, w_key, w_value)], axis=1
        )
        gathered_out = lax.all_gather(w_out, "dp", axis=1, tiled=True)
    projected = jnp.dot(hidden_all, joined_weight, preferred_element_type=jnp.float32)
    q_raw = projected[:, :head_cols]
    k_raw = projected[:, head_cols : 2 * head_cols]
    value_low = projected[:, 2 * head_cols :].astype(jnp.bfloat16).reshape(seq_len, local_heads, HD)
    query_sq, key_sq = tensor_sums((jnp.sum(q_raw * q_raw, axis=1), jnp.sum(k_raw * k_raw, axis=1)))
    query_scale = lax.rsqrt(query_sq / full_width + norm_eps)[:, None]
    key_scale = lax.rsqrt(key_sq / full_width + norm_eps)[:, None]
    query_gain_dev = lax.dynamic_slice_in_dim(query_gain, tensor_rank * head_cols, head_cols)
    key_gain_dev = lax.dynamic_slice_in_dim(key_gain, tensor_rank * head_cols, head_cols)
    block_starts = lax.iota(jnp.int32, block_count) * block_rows

    def block_mask(row_first):
        row_paths = lax.dynamic_slice_in_dim(segment_path, row_first, block_rows, 1)
        return visible_block(row_paths, segment_path, token_valid, row_first)

    def count_seen(row_first):
        return jnp.sum(block_mask(row_first).astype(jnp.int32), axis=1)

    positions = lax.map(count_seen, block_starts).reshape(seq_len) - 1
    cosine, sine = rotation(positions, HD)
    query_low = rotate(
        (q_raw * query_scale * query_gain_dev).reshape(seq_len, local_heads, HD), cosine, sine
    ).astype(jnp.bfloat16)
    key_low = rotate(
        (k_raw * key_scale * key_gain_dev).reshape(seq_len, local_heads, HD), cosine, sine
    ).astype(jnp.bfloat16)

    def attend(row_first):
        visible = block_mask(row_first)
        query_block = lax.dynamic_slice_in_dim(query_low, row_first, block_rows, 0)
        scores = (
            jnp.einsum("qhd,khd->hqk", query_block, key_low, preferred_element_type=jnp.float32)
            * score_scale
        )
        scores = jnp.where(visible[None], scores, masked_score)
        top_score = jnp.max(scores, axis=-1, keepdims=True)
        exp_scores = jnp.exp(scores - top_score)
        total = jnp.sum(exp_scores, axis=-1, keepdims=True)
        weights_low = (exp_scores / total).astype(jnp.bfloat16)
        mixed_block = jnp.einsum(
            "hqk,khd->qhd", weights_low, value_low, preferred_element_type=jnp.float32
        )
        return (mixed_block.astype(jnp.bfloat16), (top_score + jnp.log(total))[..., 0])

    mixed_blocks, log_totals = lax.map(attend, block_starts)
    attn_mixed = mixed_blocks.reshape(seq_len, head_cols)

    if direct:
        x_one, hidden_two, gates_own = mixed_out(attn_mixed, gathered_out, residual, moe_gain, router.T, 4)
        probs = gates_own.T
    else:

        def attn_term(first_row, row_count):
            return jnp.dot(attn_mixed, gathered_out, preferred_element_type=jnp.float32)

        x_one = residual_float + heads_to_rows(attn_term, tok_dev)
        hidden_two = rms_apply(x_one, moe_gain)[0].astype(jnp.bfloat16)
        logits = jnp.dot(hidden_two, router, preferred_element_type=jnp.float32)
        probs = jax.nn.softmax(logits, axis=-1)
        gates_own = probs.T
    scale_two = lax.rsqrt(jnp.mean(x_one * x_one, axis=-1, keepdims=True) + norm_eps)
    if direct:
        x_slots, c_slots, gate_slots = gather_dispatch(slots, hidden_two, gates_own, cots_all, slot_rows, 1)
    else:
        gates_all = lax.all_gather(gates_own, everyone, axis=0)
        rows_all = lax.all_gather(hidden_two, everyone, axis=0, tiled=True)
        gates = lax.dynamic_slice_in_dim(gates_all, first_expert, local_experts, 1)
        x_slots, gate_slots = dispatch(slots, gates, rows_all, slot_rows)
    outs, grads, grad_w_gate, grad_w_up, grad_w_down = expert_pass(
        first_expert.reshape(1),
        x_slots,
        c_slots,
        gate_slots,
        w_gate,
        w_up,
        w_down,
        blocks,
        padded(slot_rows, 16),
    )
    if direct:
        grad_rows, out_part = reduce_all(slots, outs, grads, 2)
    else:
        out_part, grad_part = combine(slots, outs, grads)
        grad_rows = sum_over_tensor(sum_over_dp(grad_part)).astype(jnp.float32)
    out_part = sum_over_dp(out_part)
    grad_out = cotangent.astype(jnp.float32)
    grad_hidden_two = grad_rows[:, :width]
    grad_probs = grad_rows[:, width : width + experts]
    grad_logits = probs * (grad_probs - jnp.sum(probs * grad_probs, axis=-1, keepdims=True))
    router_float = router.astype(jnp.float32)
    grad_hidden_two = grad_hidden_two + lax.dot_general(
        grad_logits, router_float, (((1,), (1,)), ((), ())), precision=lax.Precision.HIGHEST
    )
    grad_router_part = lax.dot_general(
        grad_logits,
        hidden_two.astype(jnp.float32),
        (((0,), (0,)), ((), ())),
        precision=lax.Precision.HIGHEST,
    )
    inner_two = jnp.sum(grad_hidden_two * moe_gain * x_one, axis=-1, keepdims=True)
    grad_norm_two, grad_moe_gain_part = rms_grad(
        x_one, scale_two, moe_gain, grad_hidden_two, inner_two, width
    )
    grad_x_one = grad_out + grad_norm_two
    grad_attn_low = grad_x_one.astype(jnp.bfloat16)
    early_sums = jnp.concatenate(
        (grad_router_part, grad_moe_gain_part[None], jnp.zeros((7, width), jnp.float32)), axis=0
    )
    if direct:
        grad_attn_all, early_sums = back_gather(grad_attn_low, early_sums, 5)
    else:
        grad_attn_all = lax.all_gather(grad_attn_low, "tensor", axis=0, tiled=True)
        early_sums = lax.psum(early_sums, everyone)
    grad_mixed = (
        lax.dot_general(
            grad_attn_all,
            gathered_out,
            (((1,), (1,)), ((), ())),
            preferred_element_type=jnp.float32,
        )
        .astype(jnp.bfloat16)
        .reshape(seq_len, local_heads, HD)
    )

    def attend_back(carry, pieces):
        grad_key_sum, grad_value_sum = carry
        row_first, log_total = pieces
        visible = block_mask(row_first)
        query_block = lax.dynamic_slice_in_dim(query_low, row_first, block_rows, 0)
        grad_block = lax.dynamic_slice_in_dim(grad_mixed, row_first, block_rows, 0)
        scores = (
            jnp.einsum("qhd,khd->hqk", query_block, key_low, preferred_element_type=jnp.float32)
            * score_scale
        )
        scores = jnp.where(visible[None], scores, masked_score)
        weights = jnp.exp(scores - log_total[..., None])
        grad_weights = jnp.einsum(
            "qhd,khd->hqk", grad_block, value_low, preferred_element_type=jnp.float32
        )
        inner = jnp.sum(weights * grad_weights, axis=-1, keepdims=True)
        grad_scores = (weights * (grad_weights - inner)).astype(jnp.bfloat16)
        grad_query_block = (
            jnp.einsum("hqk,khd->qhd", grad_scores, key_low, preferred_element_type=jnp.float32)
            * score_scale
        )
        grad_key_sum = (
            grad_key_sum
            + jnp.einsum(
                "hqk,qhd->khd", grad_scores, query_block, preferred_element_type=jnp.float32
            )
            * score_scale
        )
        grad_value_sum = grad_value_sum + jnp.einsum(
            "hqk,qhd->khd",
            weights.astype(jnp.bfloat16),
            grad_block,
            preferred_element_type=jnp.float32,
        )
        return ((grad_key_sum, grad_value_sum), grad_query_block)

    zero_heads = jnp.zeros((seq_len, local_heads, HD), jnp.float32)
    (grad_key_all, grad_value_all), grad_query_blocks = lax.scan(
        attend_back, (zero_heads, zero_heads), (block_starts, log_totals)
    )
    grad_q_norm = unrotate(
        grad_query_blocks.reshape(seq_len, local_heads, HD), cosine, sine
    ).reshape(seq_len, head_cols)
    grad_k_norm = unrotate(grad_key_all, cosine, sine).reshape(seq_len, head_cols)
    query_inner, key_inner = tensor_sums(
        (
            jnp.sum(grad_q_norm * query_gain_dev * q_raw, axis=1),
            jnp.sum(grad_k_norm * key_gain_dev * k_raw, axis=1),
        )
    )
    grad_q_raw, grad_query_gain_dev = rms_grad(
        q_raw, query_scale, query_gain_dev, grad_q_norm, query_inner[:, None], full_width
    )
    grad_k_raw, grad_key_gain_dev = rms_grad(
        k_raw, key_scale, key_gain_dev, grad_k_norm, key_inner[:, None], full_width
    )
    grad_joined = jnp.concatenate(
        (grad_q_raw, grad_k_raw, grad_value_all.reshape(seq_len, head_cols)), axis=1
    ).astype(jnp.bfloat16)
    out_part, grad_joined = lax.optimization_barrier((out_part, grad_joined))
    block_out = (x_one + sum_over_tensor(out_part).astype(jnp.float32)).astype(jnp.bfloat16)
    zero_width = jnp.zeros((full_width,), jnp.float32)
    grad_query_full = lax.dynamic_update_slice_in_dim(
        zero_width, grad_query_gain_dev, tensor_rank * head_cols, 0
    )
    grad_key_full = lax.dynamic_update_slice_in_dim(
        zero_width, grad_key_gain_dev, tensor_rank * head_cols, 0
    )
    if direct:
        gains = jnp.concatenate(
            (grad_query_full[None], grad_key_full[None], jnp.zeros((6, width), jnp.float32)), axis=0
        )
        grad_input, grad_w_query, grad_w_key, grad_w_value, grad_w_out, gains = last_exchange(
            grad_joined,
            joined_weight,
            hidden_all,
            attn_mixed,
            grad_attn_all,
            residual,
            attn_gain,
            grad_x_one,
            gains,
            6,
        )
    else:
        grad_joined_weight = lax.dot_general(
            hidden_all, grad_joined, (((0,), (0,)), ((), ())), preferred_element_type=jnp.float32
        ).astype(jnp.bfloat16)
        grad_out_weight = lax.dot_general(
            attn_mixed, grad_attn_all, (((0,), (0,)), ((), ())), preferred_element_type=jnp.float32
        ).astype(jnp.bfloat16)

        def back_term(first_row, row_count):
            return lax.dot_general(
                grad_joined, joined_weight, (((1,), (1,)), ((), ())), preferred_element_type=jnp.float32
            )

        grad_hidden = heads_to_rows(back_term, tok_dev)
        inner_one = jnp.sum(grad_hidden * attn_gain * residual_float, axis=-1, keepdims=True)
        grad_norm_one, grad_attn_gain_part = rms_grad(
            residual_float, scale_one, attn_gain, grad_hidden, inner_one, width
        )
        grad_input = grad_x_one + grad_norm_one
        grad_w_query, grad_w_key, grad_w_value = (
            lax.psum_scatter(
                grad_joined_weight[:, n * head_cols : (n + 1) * head_cols],
                "dp",
                scatter_dimension=0,
                tiled=True,
            ).astype(jnp.float32)
            for n in range(3)
        )
        grad_w_out = lax.psum_scatter(
            grad_out_weight, "dp", scatter_dimension=1, tiled=True
        ).astype(jnp.float32)
        gains = lax.psum(jnp.stack((grad_query_full, grad_key_full, grad_attn_gain_part)), everyone)
    return (
        block_out,
        grad_input,
        gains[2],
        grad_w_query,
        grad_w_key,
        grad_w_value,
        gains[0],
        gains[1],
        grad_w_out,
        early_sums[experts],
        early_sums[:experts].T,
        grad_w_gate,
        grad_w_up,
        grad_w_down,
    )


def solution(mesh):
    in_specs = (
        P(("dp", "tensor"), None),
        P(),
        P("dp", "tensor"),
        P("dp", "tensor"),
        P("dp", "tensor"),
        P(),
        P(),
        P("tensor", "dp"),
        P(),
        P(),
        P("dp", None, "tensor"),
        P("dp", None, "tensor"),
        P("dp", "tensor", None),
        P(None, "dp"),
        P("dp"),
        P(("dp", "tensor"), None),
        P(("dp", "tensor"), None),
        P(("dp", "tensor"), None),
    )
    out_specs = (
        P(("dp", "tensor"), None),
        P(("dp", "tensor"), None),
        P(),
        P("dp", "tensor"),
        P("dp", "tensor"),
        P("dp", "tensor"),
        P(),
        P(),
        P("tensor", "dp"),
        P(),
        P(),
        P("dp", None, "tensor"),
        P("dp", None, "tensor"),
        P("dp", "tensor", None),
    )
    return jax.shard_map(body, mesh=mesh, in_specs=in_specs, out_specs=out_specs, check_vma=False)
```

```python
import functools

import jax
import jax.numpy as jnp
from jax import lax
from jax.experimental import pallas as pl
from jax.experimental.pallas import tpu as pltpu
from jax.sharding import PartitionSpec as P

H = 16
HD = 128


norm_eps = 1e-05
rope_base = 10000.0
masked_score = -1e30


def padded(count, step):
    return -(-count // step) * step


def slot_table(routes, route_order, valid, experts, capacity):
    far = jnp.int32(1 << 30)
    expert = lax.iota(jnp.int32, experts)[:, None, None]
    hits = (routes[None] == expert) & (valid[None, :, None] == 1)
    order = jnp.min(jnp.where(hits, route_order[None], far), axis=-1)
    ranks = jnp.sum((order[:, None, :] < order[:, :, None]).astype(jnp.int32), axis=-1)
    return jnp.where((order < far) & (ranks < capacity), ranks, -1)


def slot_hits(slots, expert, rows):
    tokens = slots.shape[-1]
    return lax.broadcasted_iota(jnp.int32, (rows, tokens), 0) == slots[expert : expert + 1, :]


def dispatch_kernel(slots_ref, gates_ref, rows_ref, x_ref, gate_ref):
    pair, experts, tokens = slots_ref.shape
    rows = x_ref.shape[1] // pair
    width = rows_ref.shape[1]
    picks = []
    for b in range(pair):
        slots = slots_ref[b]
        pieces = []
        for e in range(experts):
            hit = slot_hits(slots, e, rows)
            pieces.append(hit.astype(jnp.float32))
            if gate_ref is not None:
                gate = jnp.sum(jnp.where(hit, gates_ref[b, e : e + 1, :], 0.0), axis=1, keepdims=True)
                gate_ref[e, b * rows : (b + 1) * rows, :] = jnp.broadcast_to(gate, (rows, 128))
        picks.append(jnp.concatenate(pieces, axis=0).astype(jnp.bfloat16))
    step = min(512, width)
    for first in range(0, width, step):
        parts = [
            jnp.dot(
                picks[b],
                rows_ref[b * tokens : (b + 1) * tokens, first : first + step],
                preferred_element_type=jnp.float32,
            )
            for b in range(pair)
        ]
        for e in range(experts):
            x_ref[e, :, first : first + step] = jnp.concatenate(
                [part[e * rows : (e + 1) * rows] for part in parts], axis=0
            ).astype(jnp.bfloat16)


def plain_dispatch_kernel(slots_ref, rows_ref, x_ref):
    dispatch_kernel(slots_ref, None, rows_ref, x_ref, None)


def dispatch(slots, gates, rows_all, rows):
    blocks, experts, tokens = slots.shape
    width = rows_all.shape[1]
    pair = 2
    out = jax.ShapeDtypeStruct((experts, blocks * rows, width), jnp.bfloat16)
    table = pl.BlockSpec((pair, experts, tokens), lambda i: (i, 0, 0))
    source = pl.BlockSpec((pair * tokens, width), lambda i: (i, 0))
    target = pl.BlockSpec((experts, pair * rows, width), lambda i: (0, i, 0))
    settings = dict(
        grid=(blocks // pair,),
        compiler_params=pltpu.CompilerParams(vmem_limit_bytes=50 << 20),
        cost_estimate=pl.CostEstimate(
            flops=2 * blocks * experts * rows * tokens * width,
            bytes_accessed=2 * blocks * (tokens + experts * rows) * width,
            transcendentals=0,
        ),
    )
    if gates is None:
        return pl.pallas_call(
            plain_dispatch_kernel, out_shape=out, in_specs=[table, source], out_specs=target, name="pick", **settings
        )(slots, rows_all)
    return pl.pallas_call(
        dispatch_kernel,
        out_shape=(out, jax.ShapeDtypeStruct((experts, blocks * rows, 128), jnp.float32)),
        in_specs=[table, table, source],
        out_specs=[target, pl.BlockSpec((experts, pair * rows, 128), lambda i: (0, i, 0))],
        name="dispatch",
        **settings,
    )(slots, gates, rows_all)


def turned(left, right):
    return lax.dot_general(left, right, (((0,), (0,)), ((), ())), preferred_element_type=jnp.float32)


def across(left, right):
    return lax.dot_general(left, right, (((1,), (1,)), ((), ())), preferred_element_type=jnp.float32)


def expert_kernel(rows, first_ref, x_ref, c_ref, gate_ref, wg_ref, wu_ref, wd_ref,
                  o_ref, dx_ref, dwg_ref, dwu_ref, dwd_ref):
    expert = pl.program_id(0)
    tile, width = x_ref.shape[1:]
    units = wg_ref.shape[2]
    room = o_ref.shape[2]
    blocks = tile // rows
    gate = gate_ref[0, :, 0:1]
    x = x_ref[0]
    c = c_ref[0]
    gate_pre = jnp.dot(x, wg_ref[0], preferred_element_type=jnp.float32)
    up_pre = jnp.dot(x, wu_ref[0], preferred_element_type=jnp.float32)
    back = across(c, wd_ref[0])
    sig = jax.nn.sigmoid(gate_pre)
    silu = gate_pre * sig
    act = (silu * up_pre).astype(jnp.bfloat16)
    act_float = act.astype(jnp.float32)
    grad_gate = jnp.sum(act_float * back, axis=1, keepdims=True)
    grad_act = back * gate
    grad_gate_pre = (grad_act * up_pre * sig * (1.0 + gate_pre * (1.0 - sig))).astype(jnp.bfloat16)
    grad_up_pre = (grad_act * silu).astype(jnp.bfloat16)
    gated = (act_float * gate).astype(jnp.bfloat16)

    def spread(values):
        values = values.reshape(blocks, rows, values.shape[1])
        if room > rows:
            empty = jnp.zeros((blocks, room - rows, values.shape[2]), jnp.float32)
            values = jnp.concatenate((values, empty), axis=1)
        return values.astype(jnp.bfloat16)

    step = min(512, width)
    for first in range(0, width, step):
        part = slice(first, first + step)
        out = jnp.dot(act, wd_ref[0, :, part], preferred_element_type=jnp.float32) * gate
        o_ref[:, 0, :, part] = spread(out)
        grad = across(grad_gate_pre, wg_ref[0, part, :]) + across(grad_up_pre, wu_ref[0, part, :])
        dx_ref[:, 0, :, part] = spread(grad)
    lanes = lax.broadcasted_iota(jnp.int32, (tile, 128), 1)
    dx_ref[:, 0, :, width:] = spread(jnp.where(lanes == first_ref[0] + expert, grad_gate, 0.0))

    @pl.when(pl.program_id(1) == 0)
    def _():
        for ref in (dwg_ref, dwu_ref, dwd_ref):
            ref[...] = jnp.zeros_like(ref)

    for first in range(0, width, step):
        part = slice(first, first + step)
        dwg_ref[0, part, :] += turned(x_ref[0, :, part], grad_gate_pre)
        dwu_ref[0, part, :] += turned(x_ref[0, :, part], grad_up_pre)
        dwd_ref[0, :, part] += turned(gated, c_ref[0, :, part])


def expert_pass(first_expert, x_slots, c_slots, gate_slots, w_gate, w_up, w_down, blocks, room):
    experts, total, width = x_slots.shape
    units = w_gate.shape[2]
    rows = total // blocks
    group = next(n for n in (16, 8, 4, 2, 1) if blocks % n == 0 and (n * rows <= 768 or n == 1))
    tile = group * rows
    extra = 128
    tall = pl.BlockSpec((1, width, units), lambda e, r, _: (e, 0, 0))
    wide = pl.BlockSpec((1, units, width), lambda e, r, _: (e, 0, 0))
    slot = pl.BlockSpec((1, tile, width), lambda e, r, _: (e, r, 0))
    kernel = functools.partial(expert_kernel, rows)
    return pl.pallas_call(
        kernel,
        grid_spec=pltpu.PrefetchScalarGridSpec(
            num_scalar_prefetch=1,
            grid=(experts, total // tile),
            in_specs=[slot, slot, pl.BlockSpec((1, tile, 128), lambda e, r, _: (e, r, 0)), tall, tall, wide],
            out_specs=[
                pl.BlockSpec((group, 1, room, width), lambda e, r, _: (r, e, 0, 0)),
                pl.BlockSpec((group, 1, room, width + extra), lambda e, r, _: (r, e, 0, 0)),
                tall, tall, wide,
            ],
        ),
        out_shape=(
            jax.ShapeDtypeStruct((blocks, experts, room, width), jnp.bfloat16),
            jax.ShapeDtypeStruct((blocks, experts, room, width + extra), jnp.bfloat16),
            jax.ShapeDtypeStruct(w_gate.shape, jnp.float32),
            jax.ShapeDtypeStruct(w_up.shape, jnp.float32),
            jax.ShapeDtypeStruct(w_down.shape, jnp.float32),
        ),
        compiler_params=pltpu.CompilerParams(vmem_limit_bytes=60 << 20),
        cost_estimate=pl.CostEstimate(
            flops=18 * experts * total * width * units,
            bytes_accessed=8 * experts * total * width + 18 * experts * width * units,
            transcendentals=experts * total * units,
        ),
        name="experts",
    )(first_expert, x_slots, c_slots, gate_slots, w_gate, w_up, w_down)


def combine_kernel(slots_ref, o_ref, dx_ref, out_ref, grad_ref):
    _, experts, tokens = slots_ref.shape
    room, width = o_ref.shape[2:]
    slots = slots_ref[0]
    picks = jnp.concatenate(
        [slot_hits(slots, e, room).astype(jnp.float32) for e in range(experts)], axis=0
    ).astype(jnp.bfloat16)
    for source, target in ((o_ref, out_ref), (dx_ref, grad_ref)):
        columns = target.shape[1]
        for first in range(0, columns, 512):
            part = slice(first, min(first + 512, columns))
            values = source[0, :, :, part].reshape(experts * room, part.stop - first)
            target[:, part] = turned(picks, values).astype(jnp.bfloat16)


def combine(slots, outs, grads):
    blocks, experts, tokens = slots.shape
    room, width = outs.shape[2:]
    wider = grads.shape[3]
    return pl.pallas_call(
        combine_kernel,
        grid=(blocks,),
        out_shape=(
            jax.ShapeDtypeStruct((blocks * tokens, width), jnp.bfloat16),
            jax.ShapeDtypeStruct((blocks * tokens, wider), jnp.bfloat16),
        ),
        in_specs=[
            pl.BlockSpec((1, experts, tokens), lambda i: (i, 0, 0)),
            pl.BlockSpec((1, experts, room, width), lambda i: (i, 0, 0, 0)),
            pl.BlockSpec((1, experts, room, wider), lambda i: (i, 0, 0, 0)),
        ],
        out_specs=[
            pl.BlockSpec((tokens, width), lambda i: (i, 0)),
            pl.BlockSpec((tokens, wider), lambda i: (i, 0)),
        ],
        compiler_params=pltpu.CompilerParams(vmem_limit_bytes=50 << 20),
        cost_estimate=pl.CostEstimate(
            flops=2 * blocks * experts * room * tokens * (width + wider),
            bytes_accessed=2 * blocks * (tokens + experts * room) * (width + wider),
            transcendentals=0,
        ),
        name="combine",
    )(slots, outs, grads)


MESH = pl.DeviceIdType.MESH


def place():
    dp, z = lax.axis_index("dp"), lax.axis_index("tensor")
    return dp // 4, dp // 2 % 2, dp % 2, z


def peer(y, x, core, z):
    return (y * 4 + x * 2 + core, z)


def block_of(y, x, core, z):
    return (y * 4 + x * 2 + core) * 4 + z


def greet(line):
    y, x, core, z = place()
    barrier = pltpu.get_barrier_semaphore()
    for near in ((y, x, 1 - core, z), (y, 1 - x, core, z), (1 - y, x, core, z)):
        pl.semaphore_signal(barrier, inc=1, device_id=peer(*near), device_id_type=MESH)

    @pl.when(z > 0)
    def _():
        pl.semaphore_signal(barrier, inc=1, device_id=peer(y, x, core, z - 1), device_id_type=MESH)

    @pl.when(z < line - 1)
    def _():
        pl.semaphore_signal(barrier, inc=1, device_id=peer(y, x, core, z + 1), device_id_type=MESH)

    pl.semaphore_wait(barrier, 3 + (z + line - 1) // line + (2 * line - 2 - z) // line)


def either(first, second, take):
    return first * (1 - take) + second * take


def remote(source, target, send_sem, recv_sem, where):
    return pltpu.make_async_remote_copy(
        src_ref=source, dst_ref=target, send_sem=send_sem, recv_sem=recv_sem,
        device_id=peer(*where), device_id_type=MESH,
    )


def landed(target, sem):
    pltpu.make_async_copy(target, target, sem).wait()


def slot_order(y, x, core, z):
    return ((y * 2 + x) * 4 + z) * 2 + core


def near_first(z, i):
    side = z // 2
    low = either(z, 3 - z, side)
    first, second = (4 - i) // 4, (5 - i) // 4 - (4 - i) // 4
    return either(i + low * (first - second), 3 - i - low * (first - second), side)


def gather_dispatch_kernel(line, rows, slots_ref, hidden_ref, gates_ref, cots_ref,
                           rows_out, gates_out, x_out, c_out, gate_out,
                           in_c, in_x, in_gate, stage_c, stage_x, stage_gate,
                           local_sem, send_sem, recv_sem, load_sem, store_sem):
    y, x, core, z = place()
    tokens, width = hidden_ref.shape
    experts = slots_ref.shape[1]
    first_expert = (y * 4 + x * 2 + core) * experts
    owns, outs = (hidden_ref, gates_ref), (rows_out, gates_out)
    near_x, near_y, sibling = (y, 1 - x, core, z), (1 - y, x, core, z), (y, x, 1 - core, z)
    last = 24
    greet(line)

    def span(n, block):
        count = owns[n].shape[0]
        return outs[n].at[pl.ds(block * count, count)]

    def spot(m):
        q = m % 4
        i = m // 4 - (q + 1) // 2
        live = (i >= 0) & (i < line)
        held = i * live.astype(jnp.int32)
        yy, xx = (y + q // 2) % 2, (x + q % 2) % 2
        return q, held, live, yy, xx, near_first(z, held)

    def sends(m):
        q, i, live, yy, xx, zz = spot(m)
        block = block_of(yy, xx, core, zz)
        own = live & (q == 0)
        table = (
            (own & (zz <= z) & (z < line - 1), (y, x, core, z + 1)),
            (own & (zz >= z) & (z > 0), (y, x, core, z - 1)),
            (own | (live & (q == 2) & (zz % 2 == 1)), near_x),
            (own | (live & (q == 1) & (zz % 2 == 0)), near_y),
            (live, sibling),
        )
        for lane, (wanted, where) in enumerate(table):
            for n in range(2):
                part = span(n, block)
                yield wanted, remote(part, part, send_sem.at[n, lane, m], recv_sem.at[n, block], where)

    def load_c(chip):
        yy, xx, zz = chip // 8, chip // 4 % 2, chip % 4
        for c in range(2):
            b = block_of(yy, xx, c, zz)
            yield pltpu.make_async_copy(
                cots_ref.at[pl.ds(b * tokens, tokens)], in_c.at[pl.ds(c * tokens, tokens)], load_sem.at[0, c]
            )

    def load_x(yy, xx, zz):
        for c in range(2):
            b = block_of(yy, xx, c, zz)
            yield pltpu.make_async_copy(
                rows_out.at[pl.ds(b * tokens, tokens)], in_x.at[pl.ds(c * tokens, tokens)], load_sem.at[1, c]
            )
            yield pltpu.make_async_copy(
                gates_out.at[pl.ds(b * gates_ref.shape[0] + first_expert, experts)], in_gate.at[c], load_sem.at[2, c]
            )

    def store(stage, target, lane, chip):
        return pltpu.make_async_copy(stage, target.at[:, pl.ds(chip * 2 * rows, 2 * rows)], store_sem.at[lane])

    def pick(source, target, yy, xx, zz, gated):
        picks = []
        for c in range(2):
            slots = slots_ref[block_of(yy, xx, c, zz)]
            pieces = []
            for e in range(experts):
                hit = slot_hits(slots, e, rows)
                pieces.append(hit.astype(jnp.float32))
                if gated:
                    gate = jnp.sum(jnp.where(hit, in_gate[c, e : e + 1, :], 0.0), axis=1, keepdims=True)
                    stage_gate[e, c * rows : (c + 1) * rows, :] = jnp.broadcast_to(gate, (rows, 128))
            picks.append(jnp.concatenate(pieces, axis=0).astype(jnp.bfloat16))
        step = min(512, width)
        for first in range(0, width, step):
            parts = [
                jnp.dot(
                    picks[c], source[c * tokens : (c + 1) * tokens, first : first + step],
                    preferred_element_type=jnp.float32,
                )
                for c in range(2)
            ]
            for e in range(experts):
                target[e, :, first : first + step] = jnp.concatenate(
                    [part[e * rows : (e + 1) * rows] for part in parts], axis=0
                ).astype(jnp.bfloat16)

    mine = block_of(y, x, core, z)
    local = [pltpu.make_async_copy(owns[n], span(n, mine), local_sem.at[n]) for n in range(2)]
    for copy in local:
        copy.start()
    for copy in load_c(0):
        copy.start()
    for copy in local:
        copy.wait()
    chips = 4 * line
    lag = 2

    def work(m, carry):
        q, i, live, yy, xx, zz = spot(m)

        @pl.when((m < last) & live & (q + i > 0))
        def _():
            for n in range(2):
                landed(span(n, block_of(yy, xx, core, zz)), recv_sem.at[n, block_of(yy, xx, core, zz)])

        for wanted, copy in sends(m):
            pl.when((m < last) & wanted)(copy.start)

        @pl.when(m < chips)
        def _():
            for copy in load_c(m):
                copy.wait()

            @pl.when(m > 0)
            def _():
                store(stage_c, c_out, 0, m - 1).wait()

            pick(in_c, stage_c, m // 8, m // 4 % 2, m % 4, False)
            store(stage_c, c_out, 0, m).start()

            @pl.when(m + 1 < chips)
            def _():
                for copy in load_c(m + 1):
                    copy.start()

        back = m - lag
        q = (back + 8) % 4
        i = (back + 8) // 4 - 2 - (q + 1) // 2
        live = (i >= 0) & (i < line)
        held = i * live.astype(jnp.int32)
        yy, xx = (y + q // 2) % 2, (x + q % 2) % 2
        zz = near_first(z, held)

        @pl.when(live)
        def _():
            block = block_of(yy, xx, 1 - core, zz)
            for n in range(2):
                landed(span(n, block), recv_sem.at[n, block])
            for copy in load_x(yy, xx, zz):
                copy.start()
            chip = (yy * 2 + xx) * 4 + zz

            @pl.when(q + held > 0)
            def _():
                store(stage_x, x_out, 1, chip).wait()
                store(stage_gate, gate_out, 2, chip).wait()

            for copy in load_x(yy, xx, zz):
                copy.wait()
            pick(in_x, stage_x, yy, xx, zz, True)
            store(stage_x, x_out, 1, chip).start()
            store(stage_gate, gate_out, 2, chip).start()

        return carry

    lax.fori_loop(0, last + lag, work, 0)
    store(stage_c, c_out, 0, chips - 1).wait()
    store(stage_x, x_out, 1, 0).wait()
    store(stage_gate, gate_out, 2, 0).wait()

    def finish(m, carry):
        for wanted, copy in sends(m):
            pl.when(wanted)(copy.wait_send)
        return carry

    lax.fori_loop(0, last, finish, 0)


def gather_dispatch(slots, hidden, gates, cots_all, rows, collective_id):
    line = 4
    blocks, experts, tokens = slots.shape
    width = hidden.shape[1]
    pair = 2 * rows
    low, wide = jnp.bfloat16, jnp.float32
    any_ref = pl.BlockSpec(memory_space=pl.ANY)
    vmem = pl.BlockSpec(memory_space=pltpu.VMEM)
    dma = pltpu.SemaphoreType.DMA
    slot_shape = jax.ShapeDtypeStruct((experts, blocks * rows, width), low)
    return pl.pallas_call(
        functools.partial(gather_dispatch_kernel, line, rows),
        out_shape=(
            jax.ShapeDtypeStruct((blocks * tokens, width), low),
            jax.ShapeDtypeStruct((blocks * gates.shape[0], tokens), wide),
            slot_shape,
            slot_shape,
            jax.ShapeDtypeStruct((experts, blocks * rows, 128), wide),
        ),
        in_specs=[vmem, any_ref, any_ref, any_ref],
        out_specs=[any_ref] * 5,
        scratch_shapes=[
            pltpu.VMEM((2 * tokens, width), low),
            pltpu.VMEM((2 * tokens, width), low),
            pltpu.VMEM((2, experts, tokens), wide),
            pltpu.VMEM((experts, pair, width), low),
            pltpu.VMEM((experts, pair, width), low),
            pltpu.VMEM((experts, pair, 128), wide),
            dma((2,)),
            dma((2, 5, 24)),
            dma((2, blocks)),
            dma((3, 2)),
            dma((3,)),
        ],
        compiler_params=pltpu.CompilerParams(
            collective_id=collective_id, has_side_effects=True, vmem_limit_bytes=40 << 20
        ),
        cost_estimate=pl.CostEstimate(
            flops=4 * blocks * experts * rows * tokens * width, bytes_accessed=200 << 20, transcendentals=0
        ),
        name="gather_dispatch",
    )(slots, hidden, gates, cots_all)[2:]


def reduce_kernel(line, slots_ref, grads_ref, outs_ref, sum_ref, part_ref,
                  grad_in, out_in, out_stage, stage, near, far_x, far_y, from_x, from_y, up, down,
                  in_sem, part_sem, stage_sem, near_sem, send_sem, far_sem, x_sem, y_sem, line_sem):
    y, x, core, z = place()
    tokens, width = sum_ref.shape
    half = tokens // 2
    experts, room = grads_ref.shape[1:3]
    rounds = line
    greet(line)

    def goal(r):
        early = 1 - r // 2
        return (line - 1) * (r % 2) * early + (r - 1) * (1 - early)

    def spot_at(q):
        r, p = q // 8, q % 8
        own = (1 - p % 2) * ((p + 7) // 8) + p // 7
        column = own * (p // 2 - 1 + p // 7) + (1 - own) * ((p + 1) // 2)
        dy, dx = (column + 1) % 2, 1 - column // 2
        target_core = core * own + (1 - core) * (1 - own)
        return (y + dy) % 2, (x + dx) % 2, target_core, goal(r)

    def load(q):
        b = slot_order(*spot_at(q))
        return (
            pltpu.make_async_copy(grads_ref.at[b], grad_in.at[q % 2], in_sem.at[0, q % 2]),
            pltpu.make_async_copy(outs_ref.at[b], out_in.at[q % 2], in_sem.at[1, q % 2]),
        )

    def to_part(q):
        b = block_of(*spot_at(q))
        return pltpu.make_async_copy(out_stage.at[q % 2], part_ref.at[pl.ds(b * tokens, tokens)], part_sem.at[q % 2])

    def to_sibling(r, j):
        return pltpu.make_async_remote_copy(
            src_ref=stage.at[j], dst_ref=near.at[r * 4 + j], send_sem=stage_sem.at[j], recv_sem=near_sem.at[r * 4 + j],
            device_id=peer(y, x, 1 - core, z), device_id_type=MESH,
        )

    near_x, near_y = peer(y, 1 - x, core, z), peer(1 - y, x, core, z)

    def rows(h):
        return pl.ds(h * half, half)

    def cross(kind, r):
        column, h, target, sem, index, lane = {
            "far_x": (0, 0, far_x.at[r], far_sem.at[0, r], near_x, 0),
            "far_y": (0, 1, far_y.at[r], far_sem.at[1, r], near_y, 1),
            "x0": (1, 0, from_x.at[r, rows(0)], x_sem.at[r, 0], near_x, 2),
            "x1": (1, 1, from_x.at[r, rows(1)], x_sem.at[r, 1], near_x, 3),
            "y0": (2, 0, from_y.at[r, rows(0)], y_sem.at[r, 0], near_y, 4),
            "y1": (2, 1, from_y.at[r, rows(1)], y_sem.at[r, 1], near_y, 5),
        }[kind]
        return pltpu.make_async_remote_copy(
            src_ref=near.at[r * 4 + column, rows(h)], dst_ref=target, send_sem=send_sem.at[lane, r], recv_sem=sem,
            device_id=index, device_id_type=MESH,
        )

    def along(sign, r):
        target = up if sign > 0 else down
        lane = 0 if sign > 0 else 1
        return pltpu.make_async_remote_copy(
            src_ref=near.at[r * 4 + 3], dst_ref=target.at[r], send_sem=send_sem.at[6 + lane, r], recv_sem=line_sem.at[lane, r],
            device_id=peer(y, x, core, z + sign), device_id_type=MESH,
        )

    def term(q, source, target_width, store):
        picks = jnp.concatenate(
            [slot_hits(slots_ref[block_of(*spot_at(q))], e, room).astype(jnp.float32) for e in range(experts)], axis=0
        ).astype(jnp.bfloat16)
        for first in range(0, target_width, 512):
            part = slice(first, min(first + 512, target_width))
            values = source[q % 2, :, :, part].reshape(experts * room, part.stop - first)
            store(part, turned(picks, values))

    for copy in load(0):
        copy.start()

    def one(r, p, j, own):
        q = r * 8 + p
        for copy in load(q):
            copy.wait()

        @pl.when(q + 1 < rounds * 8)
        def _():
            for copy in load(q + 1):
                copy.start()

        if own:
            near_slot = r * 4 + j
            to_sibling(r, j).wait_recv()

            def keep(part, value):
                near[near_slot, :, part] = (value + near[near_slot, :, part].astype(jnp.float32)).astype(jnp.bfloat16)

            term(q, grad_in, width, keep)
        else:

            @pl.when(r > 0)
            def _():
                to_sibling(r - 1, j).wait_send()

            def keep(part, value):
                stage[j, :, part] = value.astype(jnp.bfloat16)

            term(q, grad_in, width, keep)
            to_sibling(r, j).start()

        @pl.when(q >= 2)
        def _():
            to_part(q - 2).wait()

        def put(part, value):
            out_stage[q % 2, :, part] = value.astype(jnp.bfloat16)

        term(q, out_in, out_stage.shape[2], put)
        to_part(q).start()

    def add(target, h, *sources):
        for first in range(0, width, 512):
            part = slice(first, min(first + 512, width))
            total = near[target, h, part].astype(jnp.float32)
            for source in sources:
                total = total + source(part).astype(jnp.float32)
            near[target, h, part] = total.astype(jnp.bfloat16)

    def work(s, carry):
        @pl.when(s < rounds)
        def _():
            r = s
            one(r, 0, 0, 0)
            for j in range(4):
                if j < 3:
                    one(r, 2 * j + 1, j + 1, 0)
                one(r, min(2 * j + 2, 7), j, 1)
                for kind in (("far_x", "far_y"), ("x0",), ("y1",), ())[j]:
                    cross(kind, r).start()
            cross("far_y", r).wait_recv()
            add(r * 4 + 1, rows(1), lambda part: far_y[r, :, part])
            cross("x1", r).start()
            cross("far_x", r).wait_recv()
            add(r * 4 + 2, rows(0), lambda part: far_x[r, :, part])
            cross("y0", r).start()

        @pl.when((s >= 1) & (s < rounds + 1))
        def _():
            r = s - 1
            for kind in ("x0", "x1", "y0", "y1"):
                cross(kind, r).wait_recv()
            for h in range(2):
                add(
                    r * 4 + 3,
                    rows(h),
                    lambda part: from_x[r, rows(h), part],
                    lambda part: from_y[r, rows(h), part],
                )

        for hop in range(line - 1):
            r = s - 1 - hop
            live = (r >= 0) & (r < rounds)
            held = r * live.astype(jnp.int32)

            @pl.when(live & (goal(held) > z) & (z == hop))
            def _():
                if hop:
                    along(1, held).wait_recv()
                    for h in range(2):
                        add(held * 4 + 3, rows(h), lambda part: up[held, rows(h), part])
                along(1, held).start()

            @pl.when(live & (goal(held) < z) & (line - 1 - z == hop))
            def _():
                if hop:
                    along(-1, held).wait_recv()
                    for h in range(2):
                        add(held * 4 + 3, rows(h), lambda part: down[held, rows(h), part])
                along(-1, held).start()

        return carry

    lax.fori_loop(0, rounds + line - 1, work, 0)

    mine = (z + (z + 2) // 3) % 4 + z // 3
    sum_ref[...] = near[mine * 4 + 3].astype(jnp.float32)

    @pl.when(z > 0)
    def _():
        along(1, mine).wait_recv()
        sum_ref[...] += up[mine].astype(jnp.float32)

    @pl.when(z < line - 1)
    def _():
        along(-1, mine).wait_recv()
        sum_ref[...] += down[mine].astype(jnp.float32)

    def finish(r, carry):
        for kind in ("far_x", "far_y", "x0", "x1", "y0", "y1"):
            cross(kind, r).wait_send()

        @pl.when(goal(r) > z)
        def _():
            along(1, r).wait_send()

        @pl.when(goal(r) < z)
        def _():
            along(-1, r).wait_send()

        return carry

    lax.fori_loop(0, rounds, finish, 0)
    for j in range(4):
        to_sibling(rounds - 1, j).wait_send()
    for q in (rounds * 8 - 2, rounds * 8 - 1):
        to_part(q).wait()


def reduce_all(slots, outs, grads, collective_id):
    blocks, experts, tokens = slots.shape
    room, width = outs.shape[2:]
    wider = grads.shape[3]
    line = 4
    low = jnp.bfloat16
    any_ref = pl.BlockSpec(memory_space=pl.ANY)
    vmem = pl.BlockSpec(memory_space=pltpu.VMEM)
    dma = pltpu.SemaphoreType.DMA
    return pl.pallas_call(
        functools.partial(reduce_kernel, line),
        out_shape=(
            jax.ShapeDtypeStruct((tokens, wider), jnp.float32),
            jax.ShapeDtypeStruct((blocks * tokens, width), low),
        ),
        in_specs=[vmem, any_ref, any_ref],
        out_specs=[vmem, any_ref],
        scratch_shapes=[
            pltpu.VMEM((2, experts, room, wider), low),
            pltpu.VMEM((2, experts, room, width), low),
            pltpu.VMEM((2, tokens, width), low),
            pltpu.VMEM((4, tokens, wider), low),
            pltpu.VMEM((line * 4, tokens, wider), low),
            pltpu.VMEM((line, tokens // 2, wider), low),
            pltpu.VMEM((line, tokens // 2, wider), low),
            pltpu.VMEM((line, tokens, wider), low),
            pltpu.VMEM((line, tokens, wider), low),
            pltpu.VMEM((line, tokens, wider), low),
            pltpu.VMEM((line, tokens, wider), low),
            dma((2, 2)),
            dma((2,)),
            dma((4,)),
            dma((line * 4,)),
            dma((8, line)),
            dma((2, line)),
            dma((line, 2)),
            dma((line, 2)),
            dma((2, line)),
        ],
        compiler_params=pltpu.CompilerParams(
            collective_id=collective_id, has_side_effects=True, vmem_limit_bytes=62 << 20
        ),
        cost_estimate=pl.CostEstimate(
            flops=2 * blocks * experts * room * tokens * (width + wider),
            bytes_accessed=2 * blocks * experts * room * (width + wider),
            transcendentals=0,
        ),
        name="reduce_all",
    )(slots, grads, outs)


class LineGather:
    def __init__(self, own, out, send_sem, recv_sem, line):
        self.own, self.out, self.send_sem, self.recv_sem, self.line = own, out, send_sem, recv_sem, line
        self.spot = place()
        self.rows = own.shape[0]

    def view(self, block):
        return self.out.at[pl.ds(block * self.rows, self.rows)]

    def inside(self, block):
        return (block >= 0) & (block < self.line)

    def copy(self, sign, step):
        y, x, core, z = self.spot
        block = z - sign * step
        lane = (1 - sign) // 2
        source = self.own if step == 0 else self.view(block)
        return remote(
            source, self.view(block), self.send_sem.at[lane, step], self.recv_sem.at[lane, step], (y, x, core, z + sign)
        )

    def sends(self, sign, step):
        z = self.spot[3]
        return self.inside(z - sign * step) & self.inside(z + sign)

    def begin(self):
        for sign in (1, -1):
            pl.when(self.sends(sign, 0))(self.copy(sign, 0).start)

    def advance(self, step):
        z = self.spot[3]
        for sign in (1, -1):
            block = z - sign * (step + 1)
            lane = (1 - sign) // 2

            @pl.when(self.inside(block))
            def _():
                landed(self.view(block), self.recv_sem.at[lane, step])

            if step + 1 < self.line - 1:
                pl.when(self.sends(sign, step + 1))(self.copy(sign, step + 1).start)

    def finish(self):
        for sign in (1, -1):
            for step in range(self.line - 1):
                pl.when(self.sends(sign, step))(self.copy(sign, step).wait_send)


def start_kernel(line, hidden_ref, wq_ref, wk_ref, wv_ref, wo_ref, hidden_out, joined_out, wo_out,
                 local_sem, line_send, line_recv, plane_send, plane_recv):
    y, x, core, z = place()
    owns = (wq_ref, wk_ref, wv_ref, wo_ref)
    near_x, near_y, sibling = (y, 1 - x, core, z), (1 - y, x, core, z), (y, x, 1 - core, z)

    def view(n, yy, xx, half=None):
        group = yy * 4 + xx * 2 + core
        rows, columns = owns[n].shape
        first, count = (0, rows) if half is None else (half * (rows // 2), rows // 2)
        if n < 3:
            return joined_out.at[pl.ds(group * rows + first, count), pl.ds(n * columns, columns)]
        return wo_out.at[pl.ds(first, count), pl.ds(pl.multiple_of(group * columns, columns), columns)]

    kinds = ("x", "y", "s", "fy", "fx", "sx", "sy", "sf")

    def copy(kind, n):
        source, target, where = {
            "x": (owns[n], view(n, y, x), near_x),
            "y": (owns[n], view(n, y, x), near_y),
            "s": (owns[n], view(n, y, x), sibling),
            "fy": (view(n, y, 1 - x, 0), view(n, y, 1 - x, 0), near_y),
            "fx": (view(n, 1 - y, x, 1), view(n, 1 - y, x, 1), near_x),
            "sx": (view(n, y, 1 - x), view(n, y, 1 - x), sibling),
            "sy": (view(n, 1 - y, x), view(n, 1 - y, x), sibling),
            "sf": (view(n, 1 - y, 1 - x), view(n, 1 - y, 1 - x), sibling),
        }[kind]
        lane = kinds.index(kind)
        return remote(source, target, plane_send.at[lane, n], plane_recv.at[lane, n], where)

    def other(n, yy, xx):
        group = yy * 4 + xx * 2 + 1 - core
        rows, columns = owns[n].shape
        if n < 3:
            return joined_out.at[pl.ds(group * rows, rows), pl.ds(n * columns, columns)]
        return wo_out.at[pl.ds(0, rows), pl.ds(pl.multiple_of(group * columns, columns), columns)]

    greet(line)
    hidden = LineGather(hidden_ref, hidden_out, line_send, line_recv, line)
    locals_ = [pltpu.make_async_copy(hidden_ref, hidden.view(z), local_sem.at[4])]
    locals_ += [pltpu.make_async_copy(owns[n], view(n, y, x), local_sem.at[n]) for n in range(4)]
    hidden.begin()
    for n in range(4):
        for kind in ("x", "y", "s"):
            copy(kind, n).start()
    for local in locals_:
        local.start()
    for n in range(4):
        landed(view(n, y, 1 - x), plane_recv.at[0, n])
        copy("fy", n).start()
        copy("sx", n).start()
        landed(view(n, 1 - y, x), plane_recv.at[1, n])
        copy("fx", n).start()
        copy("sy", n).start()
    hidden.advance(0)
    for n in range(4):
        landed(view(n, 1 - y, 1 - x, 0), plane_recv.at[3, n])
        landed(view(n, 1 - y, 1 - x, 1), plane_recv.at[4, n])
        copy("sf", n).start()
    for step in range(1, line - 1):
        hidden.advance(step)
    for n in range(4):
        landed(other(n, y, x), plane_recv.at[2, n])
        landed(other(n, y, 1 - x), plane_recv.at[5, n])
        landed(other(n, 1 - y, x), plane_recv.at[6, n])
        landed(other(n, 1 - y, 1 - x), plane_recv.at[7, n])
    hidden.finish()
    for n in range(4):
        for kind in kinds:
            copy(kind, n).wait_send()
    for local in locals_:
        local.wait()


def start_exchange(hidden, w_query, w_key, w_value, w_out, collective_id):
    line = 4
    any_ref = pl.BlockSpec(memory_space=pl.ANY)
    dma = pltpu.SemaphoreType.DMA
    rows, width = hidden.shape
    part, columns = w_query.shape
    low = jnp.bfloat16
    return pl.pallas_call(
        functools.partial(start_kernel, line),
        out_shape=(
            jax.ShapeDtypeStruct((line * rows, width), low),
            jax.ShapeDtypeStruct((8 * part, 3 * columns), low),
            jax.ShapeDtypeStruct((w_out.shape[0], 8 * w_out.shape[1]), low),
        ),
        in_specs=[any_ref] * 5,
        out_specs=[any_ref] * 3,
        scratch_shapes=[dma((5,)), dma((2, line)), dma((2, line)), dma((8, 4)), dma((8, 4))],
        compiler_params=pltpu.CompilerParams(collective_id=collective_id, has_side_effects=True),
        cost_estimate=pl.CostEstimate(flops=0, bytes_accessed=150 << 20, transcendentals=0),
        name="start_exchange",
    )(hidden, w_query, w_key, w_value, w_out)


class LineReduce:
    def __init__(self, part, up, down, send_sem, recv_sem, line):
        self.part, self.up, self.down = part, up, down
        self.send_sem, self.recv_sem, self.line = send_sem, recv_sem, line
        self.spot = place()

    def copy(self, sign, goal):
        y, x, core, z = self.spot
        lane = (1 - sign) // 2
        target = self.up if sign > 0 else self.down
        return remote(
            self.part.at[goal], target.at[goal], self.send_sem.at[lane, goal], self.recv_sem.at[lane, goal],
            (y, x, core, z + sign),
        )

    def order(self, i):
        z = self.spot[3]
        return either(self.line - 1 - i, i, z * 2 // self.line)

    def lead(self, goal):
        z = self.spot[3]
        pl.when((z == 0) & (goal > 0))(self.copy(1, goal).start)
        pl.when((z == self.line - 1) & (goal < z))(self.copy(-1, goal).start)

    def advance(self, unit, total_ref):
        z, line = self.spot[3], self.line
        for sign in (1, -1):
            goal = line - 1 - unit + z if sign > 0 else unit - line + 1 + z
            live = ((z > 0) & (goal < line)) if sign > 0 else ((z < line - 1) & (goal >= 0))
            inbox = self.up if sign > 0 else self.down

            @pl.when(live)
            def _():
                self.copy(sign, goal).wait_recv()
                if unit < line - 1:
                    self.part[goal] = (
                        self.part[goal].astype(jnp.float32) + inbox[goal].astype(jnp.float32)
                    ).astype(jnp.bfloat16)
                    self.copy(sign, goal).start()
                else:
                    total_ref[...] += inbox[goal].astype(jnp.float32)

    def finish(self):
        z = self.spot[3]

        def step(goal, carry):
            pl.when(goal > z)(self.copy(1, goal).wait_send)
            pl.when(goal < z)(self.copy(-1, goal).wait_send)
            return carry

        lax.fori_loop(0, self.line, step, 0)


def mixed_out_kernel(line, mixed_ref, w_ref, residual_ref, gain_ref, router_ref,
                     x_ref, hidden_ref, probs_ref, part, up, down, send_sem, recv_sem):
    rows, width = x_ref.shape
    greet(line)
    reduce = LineReduce(part, up, down, send_sem, recv_sem, line)
    z = reduce.spot[3]

    def term(i, carry):
        goal = reduce.order(i)
        first = pl.multiple_of(goal * rows, rows)
        for column in range(0, width, 512):
            piece = slice(column, column + 512)
            value = jnp.dot(mixed_ref[pl.ds(first, rows), :], w_ref[:, piece], preferred_element_type=jnp.float32)

            @pl.when(goal == z)
            def _():
                x_ref[:, piece] = value

            part[goal, :, piece] = value.astype(jnp.bfloat16)
        reduce.lead(goal)
        return carry

    lax.fori_loop(0, line, term, 0)
    for unit in range(1, line):
        reduce.advance(unit, x_ref)
    x_one = x_ref[...] + residual_ref[...].astype(jnp.float32)
    x_ref[...] = x_one
    scale = lax.rsqrt(jnp.mean(x_one * x_one, axis=-1, keepdims=True) + norm_eps)
    hidden = (x_one * scale * gain_ref[...]).astype(jnp.bfloat16)
    hidden_ref[...] = hidden
    logits = lax.dot_general(
        router_ref[...], hidden, (((1,), (1,)), ((), ())), preferred_element_type=jnp.float32
    )
    shifted = jnp.exp(logits - jnp.max(logits, axis=0, keepdims=True))
    probs_ref[...] = shifted / jnp.sum(shifted, axis=0, keepdims=True)
    reduce.finish()


def mixed_out(mixed, w_out, residual, gain, router_turned, collective_id):
    line = 4
    rows, width = residual.shape
    experts = router_turned.shape[0]
    vmem = pl.BlockSpec(memory_space=pltpu.VMEM)
    dma = pltpu.SemaphoreType.DMA
    block = pltpu.VMEM((line, rows, width), jnp.bfloat16)
    return pl.pallas_call(
        functools.partial(mixed_out_kernel, line),
        out_shape=(
            jax.ShapeDtypeStruct((rows, width), jnp.float32),
            jax.ShapeDtypeStruct((rows, width), jnp.bfloat16),
            jax.ShapeDtypeStruct((experts, rows), jnp.float32),
        ),
        in_specs=[vmem] * 5,
        out_specs=[vmem] * 3,
        scratch_shapes=[block, block, block, dma((2, line)), dma((2, line))],
        compiler_params=pltpu.CompilerParams(
            collective_id=collective_id, has_side_effects=True, vmem_limit_bytes=56 << 20
        ),
        cost_estimate=pl.CostEstimate(flops=0, bytes_accessed=150 << 20, transcendentals=0),
        name="mixed_out",
    )(mixed, w_out, residual, gain.reshape(1, width), router_turned)


class Butterfly:
    def __init__(self, data, total, from_core, from_x, from_y, from_z, sums, send_sem, recv_sem):
        self.data, self.total, self.sums = data, total, sums
        self.boxes = {"core": from_core, "x": from_x, "y": from_y}
        self.from_z, self.send_sem, self.recv_sem = from_z, send_sem, recv_sem
        y, x, core, z = self.spot = place()
        self.width = data.shape[1]
        self.near = {"core": (y, x, 1 - core, z), "x": (y, 1 - x, core, z), "y": (1 - y, x, core, z)}
        half, quarter, eighth = self.width // 2, self.width // 4, self.width // 8
        first = core * half
        self.kept = {"core": (first, half), "x": (first + x * quarter, quarter)}
        self.kept["y"] = (first + x * quarter + y * eighth, eighth)
        self.away = {
            "core": ((1 - core) * half, half),
            "x": (first + (1 - x) * quarter, quarter),
            "y": (first + x * quarter + (1 - y) * eighth, eighth),
        }

    def part(self, span):
        return pl.ds(pl.multiple_of(span[0], span[1]), span[1])

    def fold_copy(self, axis):
        lane = ("core", "x", "y").index(axis)
        return remote(
            self.data.at[:, self.part(self.away[axis])], self.boxes[axis], self.send_sem.at[lane],
            self.recv_sem.at[lane], self.near[axis],
        )

    def fold(self, axis):
        copy = self.fold_copy(axis)
        copy.start()
        copy.wait()
        self.data[:, self.part(self.kept[axis])] += self.boxes[axis][...]

    def line_step(self, step):
        y, x, core, z = self.spot
        other = (z + 1 - 2 * (z % 2)) if step == 0 else (z + 2) % 4
        piece = self.part(self.kept["y"])
        source = self.data.at[:, piece] if step == 0 else self.sums
        copy = remote(
            source, self.from_z.at[step], self.send_sem.at[3 + step], self.recv_sem.at[3 + step], (y, x, core, other)
        )
        copy.start()
        copy.wait()
        if step == 0:
            self.sums[...] = self.data[:, piece] + self.from_z[0]
        else:
            self.total[:, piece] = self.sums[...] + self.from_z[1]

    def unfold(self, axis):
        lane = 5 + ("core", "x", "y").index(axis)
        mine = self.total.at[:, self.part(self.kept[axis])]
        copy = remote(mine, mine, self.send_sem.at[lane], self.recv_sem.at[lane], self.near[axis])
        copy.start()
        copy.wait_send()
        landed(self.total.at[:, self.part(self.away[axis])], self.recv_sem.at[lane])

    def scratch(rows, width):
        low = jnp.float32
        return [
            pltpu.VMEM((rows, width // 2), low),
            pltpu.VMEM((rows, width // 4), low),
            pltpu.VMEM((rows, width // 8), low),
            pltpu.VMEM((2, rows, width // 8), low),
            pltpu.VMEM((rows, width // 8), low),
            pltpu.SemaphoreType.DMA((8,)),
            pltpu.SemaphoreType.DMA((8,)),
        ]


def greet_far(line):
    y, x, core, z = place()
    barrier = pltpu.get_barrier_semaphore()
    for near in ((y, x, 1 - core, z), (y, 1 - x, core, z), (1 - y, x, core, z)):
        pl.semaphore_signal(barrier, inc=1, device_id=peer(*near), device_id_type=MESH)
    for step in range(1, line):
        pl.semaphore_signal(barrier, inc=1, device_id=peer(y, x, core, (z + step) % line), device_id_type=MESH)
    pl.semaphore_wait(barrier, 3 + line - 1)


def back_gather_kernel(line, own_ref, sums_ref, out_ref, total_ref, data, local_sem, send_sem, recv_sem, *fly):
    greet_far(line)
    gather = LineGather(own_ref, out_ref, send_sem, recv_sem, line)
    local = pltpu.make_async_copy(own_ref, gather.view(gather.spot[3]), local_sem)
    gather.begin()
    local.start()
    data[...] = sums_ref[...]
    butterfly = Butterfly(data, total_ref, *fly)
    for axis in ("core", "x", "y"):
        butterfly.fold(axis)
    gather.advance(0)
    butterfly.line_step(0)
    gather.advance(1)
    butterfly.line_step(1)
    for axis in ("y", "x", "core"):
        butterfly.unfold(axis)
    gather.advance(2)
    gather.finish()
    local.wait()


def back_gather(own, sums, collective_id):
    line = 4
    any_ref = pl.BlockSpec(memory_space=pl.ANY)
    vmem = pl.BlockSpec(memory_space=pltpu.VMEM)
    dma = pltpu.SemaphoreType.DMA
    return pl.pallas_call(
        functools.partial(back_gather_kernel, line),
        out_shape=(
            jax.ShapeDtypeStruct((line * own.shape[0], own.shape[1]), own.dtype),
            jax.ShapeDtypeStruct(sums.shape, jnp.float32),
        ),
        in_specs=[any_ref, vmem],
        out_specs=[any_ref, vmem],
        scratch_shapes=[
            pltpu.VMEM(sums.shape, jnp.float32), dma(()), dma((2, line)), dma((2, line)),
            *Butterfly.scratch(*sums.shape),
        ],
        compiler_params=pltpu.CompilerParams(collective_id=collective_id, has_side_effects=True),
        cost_estimate=pl.CostEstimate(flops=0, bytes_accessed=150 << 20, transcendentals=0),
        name="back_gather",
    )(own, sums)


def last_kernel(line, joined_ref, weight_ref, hidden_ref, mixed_ref, attn_ref, residual_ref, gain_ref, x_grad_ref, gains_ref,
                input_ref, wq_ref, wk_ref, wv_ref, wo_ref, total_ref,
                part, up, down, stage, near, far_x, far_y, from_x, from_y, data,
                line_send, line_recv, stage_sem, near_sem, send_sem, recv_sem, *fly):
    y, x, core, z = place()
    rows, width = input_ref.shape
    columns = joined_ref.shape[1]
    half = rows // 2
    low = jnp.bfloat16
    greet_far(line)
    reduce = LineReduce(part, up, down, line_send, line_recv, line)

    def term(i, carry):
        goal = reduce.order(i)
        first = pl.multiple_of(goal * rows, rows)
        for column in range(0, width, 512):
            piece = slice(column, column + 512)
            value = across(joined_ref[pl.ds(first, rows), :], weight_ref[piece, :])

            @pl.when(goal == z)
            def _():
                input_ref[:, piece] = value

            part[goal, :, piece] = value.astype(low)
        reduce.lead(goal)
        return carry

    lax.fori_loop(0, line, term, 0)
    near_x, near_y, sibling = (y, 1 - x, core, z), (1 - y, x, core, z), (y, x, 1 - core, z)

    def terms(j, own, store):
        dy, dx = (j + 1) % 2, 1 - j // 2
        group = (y + dy) % 2 * 4 + (x + dx) % 2 * 2 + (core if own else 1 - core)
        span = pl.ds(pl.multiple_of(group * rows, rows), rows)
        turned_rows = hidden_ref[:, span]
        for column in range(0, columns, 512):
            piece = slice(column, column + 512)
            store(piece, turned(turned_rows, joined_ref[:, piece]))
        value = turned(mixed_ref[...], attn_ref[:, span])
        store(slice(columns, columns + rows), value[:rows])
        store(slice(columns + rows, columns + 2 * rows), value[rows:])

    def to_sibling(j):
        return remote(stage.at[j], near.at[j], stage_sem.at[j], near_sem.at[j], sibling)

    def away(j, carry):
        def store(piece, value):
            stage[j, :, piece] = value.astype(low)

        terms(j, False, store)
        to_sibling(j).start()
        return carry

    def own(j, carry):
        to_sibling(j).wait_recv()

        def store(piece, value):
            near[j, :, piece] = (value + near[j, :, piece].astype(jnp.float32)).astype(low)

        terms(j, True, store)
        return carry

    lax.fori_loop(0, 4, away, 0)
    lax.fori_loop(0, 4, own, 0)

    def line_rows(h):
        return pl.ds(h * half, half)

    def cross(kind):
        column, h, target, where = {
            "far_x": (0, 0, far_x, near_x),
            "far_y": (0, 1, far_y, near_y),
            "x0": (1, 0, from_x.at[line_rows(0)], near_x),
            "x1": (1, 1, from_x.at[line_rows(1)], near_x),
            "y0": (2, 0, from_y.at[line_rows(0)], near_y),
            "y1": (2, 1, from_y.at[line_rows(1)], near_y),
        }[kind]
        lane = kinds.index(kind)
        return remote(near.at[column, line_rows(h)], target, send_sem.at[lane], recv_sem.at[lane], where)

    kinds = ("far_x", "far_y", "x0", "y1", "x1", "y0")
    for kind in kinds[:4]:
        cross(kind).start()

    def add(column, h, source):
        near[column, line_rows(h), :] = (
            near[column, line_rows(h), :].astype(jnp.float32) + source[...].astype(jnp.float32)
        ).astype(low)

    reduce.advance(1, input_ref)
    cross("far_y").wait_recv()
    add(1, 1, far_y)
    cross("x1").start()
    cross("far_x").wait_recv()
    add(2, 0, far_x)
    cross("y0").start()
    reduce.advance(2, input_ref)
    for kind in kinds[2:]:
        cross(kind).wait_recv()
    for n, ref in enumerate((wq_ref, wk_ref, wv_ref, wo_ref, wo_ref)):
        count = columns // 3 if n < 3 else rows
        first = n * (columns // 3) if n < 3 else columns + (n - 3) * rows
        piece = slice(first, first + count)
        total = sum(r[:, piece].astype(jnp.float32) for r in (near.at[3], from_x, from_y))
        if n < 3:
            ref[...] = total
        else:
            ref[(n - 3) * rows : (n - 2) * rows, :] = total
    reduce.advance(3, input_ref)
    grad = input_ref[...]
    values = residual_ref[...].astype(jnp.float32)
    scale = lax.rsqrt(jnp.mean(values * values, axis=-1, keepdims=True) + norm_eps)
    gained = grad * gain_ref[...]
    inner = jnp.sum(gained * values, axis=-1, keepdims=True)
    data[...] = gains_ref[...]
    data[2:3, :] = jnp.sum(grad * values * scale, axis=0, keepdims=True)
    input_ref[...] = x_grad_ref[...] + scale * gained - values * (scale * scale * scale * inner / width)
    butterfly = Butterfly(data, total_ref, *fly)
    for axis in ("core", "x", "y"):
        butterfly.fold(axis)
    butterfly.line_step(0)
    butterfly.line_step(1)
    for axis in ("y", "x", "core"):
        butterfly.unfold(axis)
    reduce.finish()
    for j in range(4):
        to_sibling(j).wait_send()
    for kind in kinds:
        cross(kind).wait_send()


def last_exchange(joined, weight, hidden, mixed, attn, residual, gain, x_grad, gains, collective_id):
    line = 4
    rows, width = residual.shape
    columns = joined.shape[1] // 3
    low, wide = jnp.bfloat16, jnp.float32
    vmem = pl.BlockSpec(memory_space=pltpu.VMEM)
    dma = pltpu.SemaphoreType.DMA
    block = pltpu.VMEM((line, rows, width), low)
    one = pltpu.VMEM((rows, width), low)
    part = pltpu.VMEM((rows // 2, width), low)
    square = jax.ShapeDtypeStruct((rows, columns), wide)
    return pl.pallas_call(
        functools.partial(last_kernel, line),
        out_shape=(
            jax.ShapeDtypeStruct((rows, width), wide), square, square, square,
            jax.ShapeDtypeStruct((2 * rows, rows), wide),
            jax.ShapeDtypeStruct(gains.shape, wide),
        ),
        in_specs=[vmem] * 9,
        out_specs=[vmem] * 6,
        scratch_shapes=[
            block, block, block, pltpu.VMEM((4, rows, width), low), pltpu.VMEM((4, rows, width), low),
            part, part, one, one, pltpu.VMEM(gains.shape, wide),
            dma((2, line)), dma((2, line)), dma((4,)), dma((4,)), dma((6,)), dma((6,)),
            *Butterfly.scratch(*gains.shape),
        ],
        compiler_params=pltpu.CompilerParams(
            collective_id=collective_id, has_side_effects=True, vmem_limit_bytes=62 << 20
        ),
        cost_estimate=pl.CostEstimate(flops=0, bytes_accessed=250 << 20, transcendentals=0),
        name="last_exchange",
    )(joined, weight, hidden, mixed, attn, residual, gain.reshape(1, width), x_grad, gains)


def visible_block(row_paths, key_paths, key_valid, row_first):
    row_count = row_paths.shape[1]
    key_count = key_paths.shape[1]
    key_segment = key_paths[0][None, :]
    on_path = (
        (key_segment == row_paths[0][:, None])
        | (key_segment == row_paths[1][:, None])
        | (key_segment == row_paths[2][:, None])
    )
    row_place = row_first + lax.iota(jnp.int32, row_count)
    key_place = lax.iota(jnp.int32, key_count)
    earlier = key_place[None, :] <= row_place[:, None]
    return on_path & earlier & (key_valid[None, :] == 1) | (
        key_place[None, :] == row_place[:, None]
    )


def rotation(positions, head_dim):
    half = head_dim // 2
    freqs = jnp.exp(-jnp.log(rope_base) * 2.0 * lax.iota(jnp.float32, half) / head_dim)
    angles = positions.astype(jnp.float32)[:, None] * freqs[None, :]
    return (jnp.cos(angles), jnp.sin(angles))


def visible_bias(row_first, row_paths, row_places, key_segment, key_valid, key_places):
    on_path = (key_segment == row_paths[0]) | (key_segment == row_paths[1]) | (key_segment == row_paths[2])
    seen = (on_path & (key_places <= row_places) & (key_valid == 1)) | (key_places == row_places)
    return jnp.where(seen, 0.0, masked_score)


def attend_kernel(step, raw_ref, scale_ref, gain_ref, cos_ref, sin_ref, column_ref, line_ref,
                  query_ref, key_ref, value_ref, mixed_ref, log_ref, bias, logs):
    seq, columns = query_ref.shape
    heads = columns // HD

    def prepare(i, carry):
        rows = pl.ds(pl.multiple_of(i * step, step), step)
        cosine, sine = cos_ref[rows, :], sin_ref[rows, :]
        for n, ref in enumerate((query_ref, key_ref)):
            scale = scale_ref[rows, n : n + 1]
            for h in range(heads):
                span = slice(h * HD, (h + 1) * HD)
                values = raw_ref[rows, n * columns + h * HD : n * columns + (h + 1) * HD]
                values = values * scale * gain_ref[n : n + 1, span]
                turn = pltpu.roll(values, HD // 2, 1)
                ref[rows, span] = (values * cosine + turn * sine).astype(jnp.bfloat16)
        value_ref[rows, :] = raw_ref[rows, 2 * columns :].astype(jnp.bfloat16)
        return carry

    lax.fori_loop(0, seq // step, prepare, 0)
    for i in range(seq // step):
        rows = slice(i * step, (i + 1) * step)
        wide = (i + 1) * step
        places = lax.broadcasted_iota(jnp.int32, (step, wide), 0) + i * step
        bias[:, :wide] = visible_bias(
            i * step,
            [column_ref[rows, n : n + 1] for n in range(3)],
            places,
            line_ref[0:1, :wide],
            line_ref[3:4, :wide],
            lax.broadcasted_iota(jnp.int32, (step, wide), 1),
        )

        def head(h, carry):
            span = pl.ds(pl.multiple_of(h * HD, HD), HD)
            scores = across(query_ref[rows, span], key_ref[:wide, span]) * HD ** (-0.5) + bias[:, :wide]
            top = jnp.max(scores, axis=1, keepdims=True)
            weights = jnp.exp(scores - top)
            total = jnp.sum(weights, axis=1, keepdims=True)
            low = (weights / total).astype(jnp.bfloat16)
            mixed = jnp.dot(low, value_ref[:wide, span], preferred_element_type=jnp.float32)
            mixed_ref[rows, span] = mixed.astype(jnp.bfloat16)
            lanes = lax.broadcasted_iota(jnp.int32, (step, 128), 1)
            logs[...] = jnp.where(lanes == h, top + jnp.log(total), logs[...])
            return carry

        logs[...] = jnp.zeros_like(logs)
        lax.fori_loop(0, heads, head, 0)
        log_ref[:, rows] = jnp.transpose(logs[...])[: log_ref.shape[0]]


def attend(raw, scales, gains, cosine, sine, path_columns, path_lines):
    seq = raw.shape[0]
    columns = raw.shape[1] // 3
    step = min(256, seq)
    vmem = pl.BlockSpec(memory_space=pltpu.VMEM)
    low = jax.ShapeDtypeStruct((seq, columns), jnp.bfloat16)
    return pl.pallas_call(
        functools.partial(attend_kernel, step),
        out_shape=(low, low, low, low, jax.ShapeDtypeStruct((8, seq), jnp.float32)),
        in_specs=[vmem] * 7,
        out_specs=[vmem] * 5,
        scratch_shapes=[pltpu.VMEM((step, seq), jnp.float32), pltpu.VMEM((step, 128), jnp.float32)],
        compiler_params=pltpu.CompilerParams(vmem_limit_bytes=50 << 20),
        cost_estimate=pl.CostEstimate(
            flops=4 * seq * seq * columns, bytes_accessed=16 * seq * columns, transcendentals=seq * seq
        ),
        name="attend",
    )(raw, scales, gains, cosine, sine, path_columns, path_lines)


def attend_back_kernel(step, grad_ref, w_ref, query_ref, key_ref, value_ref, log_ref, cos_ref, sin_ref,
                       column_ref, line_ref, dq_ref, dk_ref, dv_ref, bias, mixed):
    seq, columns = query_ref.shape
    heads = columns // HD
    dk_ref[...] = jnp.zeros_like(dk_ref)
    dv_ref[...] = jnp.zeros_like(dv_ref)

    def unturn(values, rows):
        return values * cos_ref[rows, :] - pltpu.roll(values, HD // 2, 1) * sin_ref[rows, :]

    for i in range(seq // step):
        rows = slice(i * step, (i + 1) * step)
        wide = (i + 1) * step
        mixed[...] = across(grad_ref[rows, :], w_ref[...]).astype(jnp.bfloat16)
        places = lax.broadcasted_iota(jnp.int32, (wide, step), 1) + i * step
        bias[:wide, :] = visible_bias(
            i * step,
            [line_ref[n : n + 1, rows] for n in range(3)],
            places,
            column_ref[:wide, 0:1],
            column_ref[:wide, 3:4],
            lax.broadcasted_iota(jnp.int32, (wide, step), 0),
        )

        def head(h, carry):
            span = pl.ds(pl.multiple_of(h * HD, HD), HD)
            query, key, grad = query_ref[rows, span], key_ref[:wide, span], mixed[:, span]
            scores = across(key, query) * HD ** (-0.5) + bias[:wide, :]
            weights = jnp.exp(scores - log_ref[pl.ds(h, 1), rows])
            grad_weights = across(value_ref[:wide, span], grad)
            inner = jnp.sum(weights * grad_weights, axis=0, keepdims=True)
            grad_scores = (weights * (grad_weights - inner)).astype(jnp.bfloat16)
            dq_ref[rows, span] = unturn(turned(grad_scores, key) * HD ** (-0.5), rows)
            dk_ref[:wide, span] += jnp.dot(grad_scores, query, preferred_element_type=jnp.float32)
            dv_ref[:wide, span] += jnp.dot(
                weights.astype(jnp.bfloat16), grad, preferred_element_type=jnp.float32
            )
            return carry

        lax.fori_loop(0, heads, head, 0)
    for i in range(seq // step):
        rows = slice(i * step, (i + 1) * step)
        for h in range(heads):
            span = slice(h * HD, (h + 1) * HD)
            dk_ref[rows, span] = unturn(dk_ref[rows, span] * HD ** (-0.5), rows)


def attend_back(grads, w_out, query, key, value, logs, cosine, sine, path_columns, path_lines):
    seq, columns = query.shape
    step = min(256, seq)
    vmem = pl.BlockSpec(memory_space=pltpu.VMEM)
    wide = jax.ShapeDtypeStruct((seq, columns), jnp.float32)
    return pl.pallas_call(
        functools.partial(attend_back_kernel, step),
        out_shape=(wide, wide, wide),
        in_specs=[vmem] * 10,
        out_specs=[vmem] * 3,
        scratch_shapes=[pltpu.VMEM((seq, step), jnp.float32), pltpu.VMEM((step, columns), jnp.bfloat16)],
        compiler_params=pltpu.CompilerParams(vmem_limit_bytes=56 << 20),
        cost_estimate=pl.CostEstimate(
            flops=10 * seq * seq * columns, bytes_accessed=24 * seq * columns, transcendentals=seq * seq
        ),
        name="attend_back",
    )(grads, w_out, query, key, value, logs, cosine, sine, path_columns, path_lines)


def rms_apply(values, gain):
    scale = lax.rsqrt(jnp.mean(values * values, axis=-1, keepdims=True) + norm_eps)
    return (values * scale * gain, scale)


def rms_grad(values, scale, gain, grads, inner, width):
    grad_values = scale * gain * grads - values * scale**3 * inner / width
    grad_gain = jnp.sum(grads * values * scale, axis=0)
    return (grad_values, grad_gain)


def tensor_sums(pair):
    return lax.psum((pair[0], pair[1]), "tensor")


def heads_to_rows(term, rows):
    return lax.psum_scatter(
        term(jnp.int32(0), rows * lax.axis_size("tensor")).astype(jnp.bfloat16),
        "tensor",
        scatter_dimension=0,
        tiled=True,
    ).astype(jnp.float32)


def sum_over_dp(rows):
    dp = lax.axis_size("dp")
    pieces = rows.reshape(dp, rows.shape[0] // dp, rows.shape[1])
    return lax.psum_scatter(pieces, "dp", scatter_dimension=0, tiled=False)


def sum_over_tensor(part):
    return lax.psum_scatter(part, "tensor", scatter_dimension=0, tiled=True)


def body(
    residual,
    attn_gain,
    w_query,
    w_key,
    w_value,
    query_gain,
    key_gain,
    w_out,
    moe_gain,
    router,
    w_gate,
    w_up,
    w_down,
    segment_path,
    token_valid,
    routes,
    route_order,
    cotangent,
):
    tensor_rank = lax.axis_index("tensor")
    tok_dev, width = residual.shape
    seq_len = segment_path.shape[1]
    top_count = routes.shape[1]
    experts = router.shape[1]
    local_experts = w_gate.shape[0]
    dp_groups = experts // local_experts
    capacity = 9 * tok_dev * top_count // (8 * experts)
    full_width = H * HD
    everyone = ("dp", "tensor")
    direct = dp_groups == 8 and lax.axis_size("tensor") == 4
    first_expert = lax.axis_index("dp") * local_experts
    slot_rows = padded(capacity, 8)
    valid_dev = lax.dynamic_slice_in_dim(token_valid, tensor_rank * tok_dev, tok_dev)
    slots_own = slot_table(routes, route_order, valid_dev, experts, capacity)
    slots_all = lax.all_gather(slots_own.astype(jnp.bfloat16), everyone, axis=0)
    slots = lax.dynamic_slice_in_dim(slots_all, first_expert, local_experts, 1).astype(jnp.int32)
    blocks = slots.shape[0]
    cots_all = lax.all_gather(cotangent, everyone, axis=0, tiled=True)
    c_slots = None if direct else dispatch(slots, None, cots_all, slot_rows)
    head_cols = w_query.shape[1]
    residual_float = residual.astype(jnp.float32)
    normed_one, scale_one = rms_apply(residual_float, attn_gain)
    hidden = normed_one.astype(jnp.bfloat16)
    path_lines = jnp.concatenate((segment_path, token_valid[None]), axis=0)
    path_columns = path_lines.T
    positions = jnp.sum(visible_block(segment_path, segment_path, token_valid, 0).astype(jnp.int32), axis=1) - 1
    cosine, sine = rotation(positions, HD)
    cosine = jnp.concatenate((cosine, cosine), axis=1)
    sine = jnp.concatenate((-sine, sine), axis=1)
    if direct:
        hidden_all, joined_weight, gathered_out = start_exchange(hidden, w_query, w_key, w_value, w_out, 3)
    else:
        hidden_all = lax.all_gather(hidden, "tensor", axis=0, tiled=True)
        joined_weight = jnp.concatenate(
            [lax.all_gather(w, "dp", axis=0, tiled=True) for w in (w_query, w_key, w_value)], axis=1
        )
        gathered_out = lax.all_gather(w_out, "dp", axis=1, tiled=True)
    projected = jnp.dot(hidden_all, joined_weight, preferred_element_type=jnp.float32)
    q_raw = projected[:, :head_cols]
    k_raw = projected[:, head_cols : 2 * head_cols]
    query_sq, key_sq = tensor_sums((jnp.sum(q_raw * q_raw, axis=1), jnp.sum(k_raw * k_raw, axis=1)))
    query_scale = lax.rsqrt(query_sq / full_width + norm_eps)[:, None]
    key_scale = lax.rsqrt(key_sq / full_width + norm_eps)[:, None]
    query_gain_dev = lax.dynamic_slice_in_dim(query_gain, tensor_rank * head_cols, head_cols)
    key_gain_dev = lax.dynamic_slice_in_dim(key_gain, tensor_rank * head_cols, head_cols)
    query_low, key_low, value_low, attn_mixed, log_totals = attend(
        projected,
        jnp.concatenate((query_scale, key_scale), axis=1),
        jnp.stack((query_gain_dev, key_gain_dev)),
        cosine,
        sine,
        path_columns,
        path_lines,
    )
    if direct:
        x_one, hidden_two, gates_own = mixed_out(attn_mixed, gathered_out, residual, moe_gain, router.T, 4)
        probs = gates_own.T
    else:

        def attn_term(first_row, row_count):
            return jnp.dot(attn_mixed, gathered_out, preferred_element_type=jnp.float32)

        x_one = residual_float + heads_to_rows(attn_term, tok_dev)
        hidden_two = rms_apply(x_one, moe_gain)[0].astype(jnp.bfloat16)
        logits = jnp.dot(hidden_two, router, preferred_element_type=jnp.float32)
        probs = jax.nn.softmax(logits, axis=-1)
        gates_own = probs.T
    scale_two = lax.rsqrt(jnp.mean(x_one * x_one, axis=-1, keepdims=True) + norm_eps)
    if direct:
        x_slots, c_slots, gate_slots = gather_dispatch(slots, hidden_two, gates_own, cots_all, slot_rows, 1)
    else:
        gates_all = lax.all_gather(gates_own, everyone, axis=0)
        rows_all = lax.all_gather(hidden_two, everyone, axis=0, tiled=True)
        gates = lax.dynamic_slice_in_dim(gates_all, first_expert, local_experts, 1)
        x_slots, gate_slots = dispatch(slots, gates, rows_all, slot_rows)
    outs, grads, grad_w_gate, grad_w_up, grad_w_down = expert_pass(
        first_expert.reshape(1),
        x_slots,
        c_slots,
        gate_slots,
        w_gate,
        w_up,
        w_down,
        blocks,
        padded(slot_rows, 16),
    )
    if direct:
        grad_rows, out_part = reduce_all(slots, outs, grads, 2)
    else:
        out_part, grad_part = combine(slots, outs, grads)
        grad_rows = sum_over_tensor(sum_over_dp(grad_part)).astype(jnp.float32)
    out_part = sum_over_dp(out_part)
    grad_out = cotangent.astype(jnp.float32)
    grad_hidden_two = grad_rows[:, :width]
    grad_probs = grad_rows[:, width : width + experts]
    grad_logits = probs * (grad_probs - jnp.sum(probs * grad_probs, axis=-1, keepdims=True))
    router_float = router.astype(jnp.float32)
    grad_hidden_two = grad_hidden_two + lax.dot_general(
        grad_logits, router_float, (((1,), (1,)), ((), ())), precision=lax.Precision.HIGHEST
    )
    grad_router_part = lax.dot_general(
        grad_logits,
        hidden_two.astype(jnp.float32),
        (((0,), (0,)), ((), ())),
        precision=lax.Precision.HIGHEST,
    )
    inner_two = jnp.sum(grad_hidden_two * moe_gain * x_one, axis=-1, keepdims=True)
    grad_norm_two, grad_moe_gain_part = rms_grad(
        x_one, scale_two, moe_gain, grad_hidden_two, inner_two, width
    )
    grad_x_one = grad_out + grad_norm_two
    grad_attn_low = grad_x_one.astype(jnp.bfloat16)
    early_sums = jnp.concatenate(
        (grad_router_part, grad_moe_gain_part[None], jnp.zeros((7, width), jnp.float32)), axis=0
    )
    if direct:
        grad_attn_all, early_sums = back_gather(grad_attn_low, early_sums, 5)
    else:
        grad_attn_all = lax.all_gather(grad_attn_low, "tensor", axis=0, tiled=True)
        early_sums = lax.psum(early_sums, everyone)
    grad_q_norm, grad_k_norm, grad_value_all = attend_back(
        grad_attn_all,
        gathered_out,
        query_low,
        key_low,
        value_low,
        log_totals,
        cosine,
        sine,
        path_columns,
        path_lines,
    )
    query_inner, key_inner = tensor_sums(
        (
            jnp.sum(grad_q_norm * query_gain_dev * q_raw, axis=1),
            jnp.sum(grad_k_norm * key_gain_dev * k_raw, axis=1),
        )
    )
    grad_q_raw, grad_query_gain_dev = rms_grad(
        q_raw, query_scale, query_gain_dev, grad_q_norm, query_inner[:, None], full_width
    )
    grad_k_raw, grad_key_gain_dev = rms_grad(
        k_raw, key_scale, key_gain_dev, grad_k_norm, key_inner[:, None], full_width
    )
    grad_joined = jnp.concatenate(
        (grad_q_raw, grad_k_raw, grad_value_all), axis=1
    ).astype(jnp.bfloat16)
    zero_width = jnp.zeros((full_width,), jnp.float32)
    grad_query_full = lax.dynamic_update_slice_in_dim(
        zero_width, grad_query_gain_dev, tensor_rank * head_cols, 0
    )
    grad_key_full = lax.dynamic_update_slice_in_dim(
        zero_width, grad_key_gain_dev, tensor_rank * head_cols, 0
    )
    if direct:
        gains = jnp.concatenate(
            (grad_query_full[None], grad_key_full[None], jnp.zeros((6, width), jnp.float32)), axis=0
        )
        grad_input, grad_w_query, grad_w_key, grad_w_value, grad_w_out, gains = last_exchange(
            grad_joined,
            joined_weight,
            hidden_all,
            attn_mixed,
            grad_attn_all,
            residual,
            attn_gain,
            grad_x_one,
            gains,
            6,
        )
    else:
        grad_joined_weight = lax.dot_general(
            hidden_all, grad_joined, (((0,), (0,)), ((), ())), preferred_element_type=jnp.float32
        ).astype(jnp.bfloat16)
        grad_out_weight = lax.dot_general(
            attn_mixed, grad_attn_all, (((0,), (0,)), ((), ())), preferred_element_type=jnp.float32
        ).astype(jnp.bfloat16)

        def back_term(first_row, row_count):
            return lax.dot_general(
                grad_joined, joined_weight, (((1,), (1,)), ((), ())), preferred_element_type=jnp.float32
            )

        grad_hidden = heads_to_rows(back_term, tok_dev)
        inner_one = jnp.sum(grad_hidden * attn_gain * residual_float, axis=-1, keepdims=True)
        grad_norm_one, grad_attn_gain_part = rms_grad(
            residual_float, scale_one, attn_gain, grad_hidden, inner_one, width
        )
        grad_input = grad_x_one + grad_norm_one
        grad_w_query, grad_w_key, grad_w_value = (
            lax.psum_scatter(
                grad_joined_weight[:, n * head_cols : (n + 1) * head_cols],
                "dp",
                scatter_dimension=0,
                tiled=True,
            ).astype(jnp.float32)
            for n in range(3)
        )
        grad_w_out = lax.psum_scatter(
            grad_out_weight, "dp", scatter_dimension=1, tiled=True
        ).astype(jnp.float32)
        gains = lax.psum(jnp.stack((grad_query_full, grad_key_full, grad_attn_gain_part)), everyone)
    out_part, grad_input = lax.optimization_barrier((out_part, grad_input))
    block_out = (x_one + sum_over_tensor(out_part).astype(jnp.float32)).astype(jnp.bfloat16)
    return (
        block_out,
        grad_input,
        gains[2],
        grad_w_query,
        grad_w_key,
        grad_w_value,
        gains[0],
        gains[1],
        grad_w_out,
        early_sums[experts],
        early_sums[:experts].T,
        grad_w_gate,
        grad_w_up,
        grad_w_down,
    )


def solution(mesh):
    in_specs = (
        P(("dp", "tensor"), None),
        P(),
        P("dp", "tensor"),
        P("dp", "tensor"),
        P("dp", "tensor"),
        P(),
        P(),
        P("tensor", "dp"),
        P(),
        P(),
        P("dp", None, "tensor"),
        P("dp", None, "tensor"),
        P("dp", "tensor", None),
        P(None, "dp"),
        P("dp"),
        P(("dp", "tensor"), None),
        P(("dp", "tensor"), None),
        P(("dp", "tensor"), None),
    )
    out_specs = (
        P(("dp", "tensor"), None),
        P(("dp", "tensor"), None),
        P(),
        P("dp", "tensor"),
        P("dp", "tensor"),
        P("dp", "tensor"),
        P(),
        P(),
        P("tensor", "dp"),
        P(),
        P(),
        P("dp", None, "tensor"),
        P("dp", None, "tensor"),
        P("dp", "tensor", None),
    )
    return jax.shard_map(body, mesh=mesh, in_specs=in_specs, out_specs=out_specs, check_vma=False)
```

```python
import functools

import jax
import jax.numpy as jnp
from jax import lax
from jax.experimental import pallas as pl
from jax.experimental.pallas import tpu as pltpu
from jax.sharding import PartitionSpec as P

H = 16
HD = 128


norm_eps = 1e-05
rope_base = 10000.0
masked_score = -1e30


def padded(count, step):
    return -(-count // step) * step


def slot_table(routes, route_order, valid, experts, capacity):
    far = jnp.int32(1 << 30)
    expert = lax.iota(jnp.int32, experts)[:, None, None]
    hits = (routes[None] == expert) & (valid[None, :, None] == 1)
    order = jnp.min(jnp.where(hits, route_order[None], far), axis=-1)
    ranks = jnp.sum((order[:, None, :] < order[:, :, None]).astype(jnp.int32), axis=-1)
    return jnp.where((order < far) & (ranks < capacity), ranks, -1)


def slot_hits(slots, expert, rows):
    tokens = slots.shape[-1]
    return lax.broadcasted_iota(jnp.int32, (rows, tokens), 0) == slots[expert : expert + 1, :]


def dispatch_kernel(slots_ref, gates_ref, rows_ref, x_ref, gate_ref):
    pair, experts, tokens = slots_ref.shape
    rows = x_ref.shape[1] // pair
    width = rows_ref.shape[1]
    picks = []
    for b in range(pair):
        slots = slots_ref[b]
        pieces = []
        for e in range(experts):
            hit = slot_hits(slots, e, rows)
            pieces.append(hit.astype(jnp.float32))
            if gate_ref is not None:
                gate = jnp.sum(jnp.where(hit, gates_ref[b, e : e + 1, :], 0.0), axis=1, keepdims=True)
                gate_ref[e, b * rows : (b + 1) * rows, :] = jnp.broadcast_to(gate, (rows, 128))
        picks.append(jnp.concatenate(pieces, axis=0).astype(jnp.bfloat16))
    step = min(512, width)
    for first in range(0, width, step):
        parts = [
            jnp.dot(
                picks[b],
                rows_ref[b * tokens : (b + 1) * tokens, first : first + step],
                preferred_element_type=jnp.float32,
            )
            for b in range(pair)
        ]
        for e in range(experts):
            x_ref[e, :, first : first + step] = jnp.concatenate(
                [part[e * rows : (e + 1) * rows] for part in parts], axis=0
            ).astype(jnp.bfloat16)


def plain_dispatch_kernel(slots_ref, rows_ref, x_ref):
    dispatch_kernel(slots_ref, None, rows_ref, x_ref, None)


def dispatch(slots, gates, rows_all, rows):
    blocks, experts, tokens = slots.shape
    width = rows_all.shape[1]
    pair = 2
    out = jax.ShapeDtypeStruct((experts, blocks * rows, width), jnp.bfloat16)
    table = pl.BlockSpec((pair, experts, tokens), lambda i: (i, 0, 0))
    source = pl.BlockSpec((pair * tokens, width), lambda i: (i, 0))
    target = pl.BlockSpec((experts, pair * rows, width), lambda i: (0, i, 0))
    settings = dict(
        grid=(blocks // pair,),
        compiler_params=pltpu.CompilerParams(vmem_limit_bytes=50 << 20),
        cost_estimate=pl.CostEstimate(
            flops=2 * blocks * experts * rows * tokens * width,
            bytes_accessed=2 * blocks * (tokens + experts * rows) * width,
            transcendentals=0,
        ),
    )
    if gates is None:
        return pl.pallas_call(
            plain_dispatch_kernel, out_shape=out, in_specs=[table, source], out_specs=target, name="pick", **settings
        )(slots, rows_all)
    return pl.pallas_call(
        dispatch_kernel,
        out_shape=(out, jax.ShapeDtypeStruct((experts, blocks * rows, 128), jnp.float32)),
        in_specs=[table, table, source],
        out_specs=[target, pl.BlockSpec((experts, pair * rows, 128), lambda i: (0, i, 0))],
        name="dispatch",
        **settings,
    )(slots, gates, rows_all)


def turned(left, right):
    return lax.dot_general(left, right, (((0,), (0,)), ((), ())), preferred_element_type=jnp.float32)


def across(left, right):
    return lax.dot_general(left, right, (((1,), (1,)), ((), ())), preferred_element_type=jnp.float32)


def expert_kernel(rows, first_ref, x_ref, c_ref, gate_ref, wg_ref, wu_ref, wd_ref,
                  o_ref, dx_ref, pre_ref, gated_ref):
    expert = pl.program_id(0)
    tile, width = x_ref.shape[1:]
    units = wg_ref.shape[2]
    room = o_ref.shape[2]
    blocks = tile // rows
    gate = gate_ref[0, :, 0:1]
    x = x_ref[0]
    c = c_ref[0]
    gate_pre = jnp.dot(x, wg_ref[0], preferred_element_type=jnp.float32)
    up_pre = jnp.dot(x, wu_ref[0], preferred_element_type=jnp.float32)
    back = across(c, wd_ref[0])
    sig = jax.nn.sigmoid(gate_pre)
    silu = gate_pre * sig
    act = (silu * up_pre).astype(jnp.bfloat16)
    act_float = act.astype(jnp.float32)
    grad_gate = jnp.sum(act_float * back, axis=1, keepdims=True)
    grad_act = back * gate
    grad_gate_pre = (grad_act * up_pre * sig * (1.0 + gate_pre * (1.0 - sig))).astype(jnp.bfloat16)
    grad_up_pre = (grad_act * silu).astype(jnp.bfloat16)
    gated = (act_float * gate).astype(jnp.bfloat16)

    def spread(values):
        values = values.reshape(blocks, rows, values.shape[1])
        if room > rows:
            empty = jnp.zeros((blocks, room - rows, values.shape[2]), jnp.float32)
            values = jnp.concatenate((values, empty), axis=1)
        return values.astype(jnp.bfloat16)

    step = min(512, width)
    for first in range(0, width, step):
        part = slice(first, first + step)
        out = jnp.dot(act, wd_ref[0, :, part], preferred_element_type=jnp.float32) * gate
        o_ref[:, 0, :, part] = spread(out)
        grad = across(grad_gate_pre, wg_ref[0, part, :]) + across(grad_up_pre, wu_ref[0, part, :])
        dx_ref[:, 0, :, part] = spread(grad)
    lanes = lax.broadcasted_iota(jnp.int32, (tile, 128), 1)
    dx_ref[:, 0, :, width:] = spread(jnp.where(lanes == first_ref[0] + expert, grad_gate, 0.0))

    pre_ref[0, :, :units] = grad_gate_pre
    pre_ref[0, :, units:] = grad_up_pre
    gated_ref[0] = gated


def weight_terms(x_ref, c_ref, pre_ref, gated_ref, gate_ref, up_ref, down_ref):
    units = gated_ref.shape[1]
    width = x_ref.shape[1]
    step = min(512, width)
    for first in range(0, width, step):
        part = slice(first, first + step)
        both = turned(x_ref[:, part], pre_ref[...])
        gate_ref[part, :] = both[:, :units]
        up_ref[part, :] = both[:, units:]
        down_ref[:, part] = turned(gated_ref[...], c_ref[:, part])


def weight_kernel(x_ref, c_ref, pre_ref, gated_ref, gate_ref, up_ref, down_ref):
    weight_terms(*(r.at[0] for r in (x_ref, c_ref, pre_ref, gated_ref, gate_ref, up_ref, down_ref)))


def weight_grads(x_slots, c_slots, pre, gated):
    experts, total, width = x_slots.shape
    units = gated.shape[2]
    step = min(512, width)
    part = pl.BlockSpec((1, total, step), lambda e, j: (e, 0, j))
    tall = pl.BlockSpec((1, step, units), lambda e, j: (e, j, 0))
    return pl.pallas_call(
        weight_kernel,
        grid=(experts, width // step),
        out_shape=(
            jax.ShapeDtypeStruct((experts, width, units), jnp.float32),
            jax.ShapeDtypeStruct((experts, width, units), jnp.float32),
            jax.ShapeDtypeStruct((experts, units, width), jnp.float32),
        ),
        in_specs=[
            part, part,
            pl.BlockSpec((1, total, 2 * units), lambda e, j: (e, 0, 0)),
            pl.BlockSpec((1, total, units), lambda e, j: (e, 0, 0)),
        ],
        out_specs=[tall, tall, pl.BlockSpec((1, units, step), lambda e, j: (e, 0, j))],
        compiler_params=pltpu.CompilerParams(vmem_limit_bytes=50 << 20),
        name="weight_grads",
    )(x_slots, c_slots, pre, gated)


def expert_pass(first_expert, x_slots, c_slots, gate_slots, w_gate, w_up, w_down, blocks, room):
    experts, total, width = x_slots.shape
    units = w_gate.shape[2]
    rows = total // blocks
    group = next(n for n in (16, 8, 4, 2, 1) if blocks % n == 0 and (n * rows <= 768 or n == 1))
    tile = group * rows
    extra = 128
    tall = pl.BlockSpec((1, width, units), lambda e, r, _: (e, 0, 0))
    wide = pl.BlockSpec((1, units, width), lambda e, r, _: (e, 0, 0))
    slot = pl.BlockSpec((1, tile, width), lambda e, r, _: (e, r, 0))
    kernel = functools.partial(expert_kernel, rows)
    return pl.pallas_call(
        kernel,
        grid_spec=pltpu.PrefetchScalarGridSpec(
            num_scalar_prefetch=1,
            grid=(experts, total // tile),
            in_specs=[slot, slot, pl.BlockSpec((1, tile, 128), lambda e, r, _: (e, r, 0)), tall, tall, wide],
            out_specs=[
                pl.BlockSpec((group, 1, room, width), lambda e, r, _: (r, e, 0, 0)),
                pl.BlockSpec((group, 1, room, width + extra), lambda e, r, _: (r, e, 0, 0)),
                pl.BlockSpec((1, tile, 2 * units), lambda e, r, _: (e, r, 0)),
                pl.BlockSpec((1, tile, units), lambda e, r, _: (e, r, 0)),
            ],
        ),
        out_shape=(
            jax.ShapeDtypeStruct((blocks, experts, room, width), jnp.bfloat16),
            jax.ShapeDtypeStruct((blocks, experts, room, width + extra), jnp.bfloat16),
            jax.ShapeDtypeStruct((experts, total, 2 * units), jnp.bfloat16),
            jax.ShapeDtypeStruct((experts, total, units), jnp.bfloat16),
        ),
        compiler_params=pltpu.CompilerParams(vmem_limit_bytes=60 << 20),
        cost_estimate=pl.CostEstimate(
            flops=12 * experts * total * width * units,
            bytes_accessed=8 * experts * total * width + 6 * experts * width * units,
            transcendentals=experts * total * units,
        ),
        name="experts",
    )(first_expert, x_slots, c_slots, gate_slots, w_gate, w_up, w_down)


def combine_kernel(slots_ref, o_ref, dx_ref, out_ref, grad_ref):
    _, experts, tokens = slots_ref.shape
    room, width = o_ref.shape[2:]
    slots = slots_ref[0]
    picks = jnp.concatenate(
        [slot_hits(slots, e, room).astype(jnp.float32) for e in range(experts)], axis=0
    ).astype(jnp.bfloat16)
    for source, target in ((o_ref, out_ref), (dx_ref, grad_ref)):
        columns = target.shape[1]
        for first in range(0, columns, 512):
            part = slice(first, min(first + 512, columns))
            values = source[0, :, :, part].reshape(experts * room, part.stop - first)
            target[:, part] = turned(picks, values).astype(jnp.bfloat16)


def combine(slots, outs, grads):
    blocks, experts, tokens = slots.shape
    room, width = outs.shape[2:]
    wider = grads.shape[3]
    return pl.pallas_call(
        combine_kernel,
        grid=(blocks,),
        out_shape=(
            jax.ShapeDtypeStruct((blocks * tokens, width), jnp.bfloat16),
            jax.ShapeDtypeStruct((blocks * tokens, wider), jnp.bfloat16),
        ),
        in_specs=[
            pl.BlockSpec((1, experts, tokens), lambda i: (i, 0, 0)),
            pl.BlockSpec((1, experts, room, width), lambda i: (i, 0, 0, 0)),
            pl.BlockSpec((1, experts, room, wider), lambda i: (i, 0, 0, 0)),
        ],
        out_specs=[
            pl.BlockSpec((tokens, width), lambda i: (i, 0)),
            pl.BlockSpec((tokens, wider), lambda i: (i, 0)),
        ],
        compiler_params=pltpu.CompilerParams(vmem_limit_bytes=50 << 20),
        cost_estimate=pl.CostEstimate(
            flops=2 * blocks * experts * room * tokens * (width + wider),
            bytes_accessed=2 * blocks * (tokens + experts * room) * (width + wider),
            transcendentals=0,
        ),
        name="combine",
    )(slots, outs, grads)


MESH = pl.DeviceIdType.MESH


def place():
    dp, z = lax.axis_index("dp"), lax.axis_index("tensor")
    return dp // 4, dp // 2 % 2, dp % 2, z


def peer(y, x, core, z):
    return (y * 4 + x * 2 + core, z)


def block_of(y, x, core, z):
    return (y * 4 + x * 2 + core) * 4 + z


def greet(line):
    y, x, core, z = place()
    barrier = pltpu.get_barrier_semaphore()
    for near in ((y, x, 1 - core, z), (y, 1 - x, core, z), (1 - y, x, core, z)):
        pl.semaphore_signal(barrier, inc=1, device_id=peer(*near), device_id_type=MESH)

    @pl.when(z > 0)
    def _():
        pl.semaphore_signal(barrier, inc=1, device_id=peer(y, x, core, z - 1), device_id_type=MESH)

    @pl.when(z < line - 1)
    def _():
        pl.semaphore_signal(barrier, inc=1, device_id=peer(y, x, core, z + 1), device_id_type=MESH)

    pl.semaphore_wait(barrier, 3 + (z + line - 1) // line + (2 * line - 2 - z) // line)


def either(first, second, take):
    return first * (1 - take) + second * take


def remote(source, target, send_sem, recv_sem, where):
    return pltpu.make_async_remote_copy(
        src_ref=source, dst_ref=target, send_sem=send_sem, recv_sem=recv_sem,
        device_id=peer(*where), device_id_type=MESH,
    )


def landed(target, sem):
    pltpu.make_async_copy(target, target, sem).wait()


def slot_order(y, x, core, z):
    return ((y * 2 + x) * 4 + z) * 2 + core


def near_first(z, i):
    side = z // 2
    low = either(z, 3 - z, side)
    first, second = (4 - i) // 4, (5 - i) // 4 - (4 - i) // 4
    return either(i + low * (first - second), 3 - i - low * (first - second), side)


def gather_dispatch_kernel(line, rows, slots_ref, hidden_ref, gates_ref, cots_ref,
                           rows_out, gates_out, x_out, c_out, gate_out,
                           in_c, in_x, in_gate, stage_c, stage_x, stage_gate,
                           local_sem, send_sem, recv_sem, load_sem, store_sem):
    y, x, core, z = place()
    tokens, width = hidden_ref.shape
    experts = slots_ref.shape[1]
    first_expert = (y * 4 + x * 2 + core) * experts
    owns, outs = (hidden_ref, gates_ref), (rows_out, gates_out)
    near_x, near_y, sibling = (y, 1 - x, core, z), (1 - y, x, core, z), (y, x, 1 - core, z)
    last = 24
    greet(line)

    def span(n, block):
        count = owns[n].shape[0]
        return outs[n].at[pl.ds(block * count, count)]

    def spot(m):
        q = m % 4
        i = m // 4 - (q + 1) // 2
        live = (i >= 0) & (i < line)
        held = i * live.astype(jnp.int32)
        yy, xx = (y + q // 2) % 2, (x + q % 2) % 2
        return q, held, live, yy, xx, near_first(z, held)

    def sends(m):
        q, i, live, yy, xx, zz = spot(m)
        block = block_of(yy, xx, core, zz)
        own = live & (q == 0)
        table = (
            (own & (zz <= z) & (z < line - 1), (y, x, core, z + 1)),
            (own & (zz >= z) & (z > 0), (y, x, core, z - 1)),
            (own | (live & (q == 2) & (zz % 2 == 1)), near_x),
            (own | (live & (q == 1) & (zz % 2 == 0)), near_y),
            (live, sibling),
        )
        for lane, (wanted, where) in enumerate(table):
            for n in range(2):
                part = span(n, block)
                yield wanted, remote(part, part, send_sem.at[n, lane, m], recv_sem.at[n, block], where)

    def load_c(chip):
        yy, xx, zz = chip // 8, chip // 4 % 2, chip % 4
        for c in range(2):
            b = block_of(yy, xx, c, zz)
            yield pltpu.make_async_copy(
                cots_ref.at[pl.ds(b * tokens, tokens)], in_c.at[pl.ds(c * tokens, tokens)], load_sem.at[0, c]
            )

    def load_x(yy, xx, zz):
        for c in range(2):
            b = block_of(yy, xx, c, zz)
            yield pltpu.make_async_copy(
                rows_out.at[pl.ds(b * tokens, tokens)], in_x.at[pl.ds(c * tokens, tokens)], load_sem.at[1, c]
            )
            yield pltpu.make_async_copy(
                gates_out.at[pl.ds(b * gates_ref.shape[0] + first_expert, experts)], in_gate.at[c], load_sem.at[2, c]
            )

    def store(stage, target, lane, chip):
        return pltpu.make_async_copy(stage, target.at[:, pl.ds(chip * 2 * rows, 2 * rows)], store_sem.at[lane])

    def pick(source, target, yy, xx, zz, gated):
        picks = []
        for c in range(2):
            slots = slots_ref[block_of(yy, xx, c, zz)]
            pieces = []
            for e in range(experts):
                hit = slot_hits(slots, e, rows)
                pieces.append(hit.astype(jnp.float32))
                if gated:
                    gate = jnp.sum(jnp.where(hit, in_gate[c, e : e + 1, :], 0.0), axis=1, keepdims=True)
                    stage_gate[e, c * rows : (c + 1) * rows, :] = jnp.broadcast_to(gate, (rows, 128))
            picks.append(jnp.concatenate(pieces, axis=0).astype(jnp.bfloat16))
        step = min(512, width)
        for first in range(0, width, step):
            parts = [
                jnp.dot(
                    picks[c], source[c * tokens : (c + 1) * tokens, first : first + step],
                    preferred_element_type=jnp.float32,
                )
                for c in range(2)
            ]
            for e in range(experts):
                target[e, :, first : first + step] = jnp.concatenate(
                    [part[e * rows : (e + 1) * rows] for part in parts], axis=0
                ).astype(jnp.bfloat16)

    mine = block_of(y, x, core, z)
    local = [pltpu.make_async_copy(owns[n], span(n, mine), local_sem.at[n]) for n in range(2)]
    for copy in local:
        copy.start()
    for copy in load_c(0):
        copy.start()
    for copy in local:
        copy.wait()
    chips = 4 * line
    lag = 2

    def work(m, carry):
        q, i, live, yy, xx, zz = spot(m)

        @pl.when((m < last) & live & (q + i > 0))
        def _():
            for n in range(2):
                landed(span(n, block_of(yy, xx, core, zz)), recv_sem.at[n, block_of(yy, xx, core, zz)])

        for wanted, copy in sends(m):
            pl.when((m < last) & wanted)(copy.start)

        back = m - lag
        q = (back + 8) % 4
        i = (back + 8) // 4 - 2 - (q + 1) // 2
        live = (i >= 0) & (i < line)
        held = i * live.astype(jnp.int32)
        yy, xx = (y + q // 2) % 2, (x + q % 2) % 2
        zz = near_first(z, held)
        chip = (yy * 2 + xx) * 4 + zz

        @pl.when(live)
        def _():
            block = block_of(yy, xx, 1 - core, zz)
            for n in range(2):
                landed(span(n, block), recv_sem.at[n, block])
            for copy in load_x(yy, xx, zz):
                copy.start()

        @pl.when(m < chips)
        def _():
            for copy in load_c(m):
                copy.wait()

            @pl.when(m > 0)
            def _():
                store(stage_c, c_out, 0, m - 1).wait()

            pick(in_c, stage_c, m // 8, m // 4 % 2, m % 4, False)
            store(stage_c, c_out, 0, m).start()

            @pl.when(m + 1 < chips)
            def _():
                for copy in load_c(m + 1):
                    copy.start()

        @pl.when(live)
        def _():
            @pl.when(q + held > 0)
            def _():
                store(stage_x, x_out, 1, chip).wait()
                store(stage_gate, gate_out, 2, chip).wait()

            for copy in load_x(yy, xx, zz):
                copy.wait()
            pick(in_x, stage_x, yy, xx, zz, True)
            store(stage_x, x_out, 1, chip).start()
            store(stage_gate, gate_out, 2, chip).start()

        return carry

    lax.fori_loop(0, last + lag, work, 0)
    store(stage_c, c_out, 0, chips - 1).wait()
    store(stage_x, x_out, 1, 0).wait()
    store(stage_gate, gate_out, 2, 0).wait()

    def finish(m, carry):
        for wanted, copy in sends(m):
            pl.when(wanted)(copy.wait_send)
        return carry

    lax.fori_loop(0, last, finish, 0)


def gather_dispatch(slots, hidden, gates, cots_all, rows, collective_id):
    line = 4
    blocks, experts, tokens = slots.shape
    width = hidden.shape[1]
    pair = 2 * rows
    low, wide = jnp.bfloat16, jnp.float32
    any_ref = pl.BlockSpec(memory_space=pl.ANY)
    vmem = pl.BlockSpec(memory_space=pltpu.VMEM)
    dma = pltpu.SemaphoreType.DMA
    slot_shape = jax.ShapeDtypeStruct((experts, blocks * rows, width), low)
    return pl.pallas_call(
        functools.partial(gather_dispatch_kernel, line, rows),
        out_shape=(
            jax.ShapeDtypeStruct((blocks * tokens, width), low),
            jax.ShapeDtypeStruct((blocks * gates.shape[0], tokens), wide),
            slot_shape,
            slot_shape,
            jax.ShapeDtypeStruct((experts, blocks * rows, 128), wide),
        ),
        in_specs=[vmem, any_ref, any_ref, any_ref],
        out_specs=[any_ref] * 5,
        scratch_shapes=[
            pltpu.VMEM((2 * tokens, width), low),
            pltpu.VMEM((2 * tokens, width), low),
            pltpu.VMEM((2, experts, tokens), wide),
            pltpu.VMEM((experts, pair, width), low),
            pltpu.VMEM((experts, pair, width), low),
            pltpu.VMEM((experts, pair, 128), wide),
            dma((2,)),
            dma((2, 5, 24)),
            dma((2, blocks)),
            dma((3, 2)),
            dma((3,)),
        ],
        compiler_params=pltpu.CompilerParams(
            collective_id=collective_id, has_side_effects=True, vmem_limit_bytes=40 << 20
        ),
        cost_estimate=pl.CostEstimate(
            flops=4 * blocks * experts * rows * tokens * width, bytes_accessed=200 << 20, transcendentals=0
        ),
        name="gather_dispatch",
    )(slots, hidden, gates, cots_all)[2:]


def reduce_kernel(line, slots_ref, grads_ref, outs_ref, sum_ref, part_ref,
                  grad_in, out_in, out_stage, stage, near, far_x, far_y, from_x, from_y, up, down,
                  in_sem, part_sem, stage_sem, near_sem, send_sem, far_sem, x_sem, y_sem, line_sem):
    y, x, core, z = place()
    tokens, width = sum_ref.shape
    half = tokens // 2
    experts, room = grads_ref.shape[1:3]
    rounds = line
    greet(line)

    def goal(r):
        early = 1 - r // 2
        return (line - 1) * (r % 2) * early + (r - 1) * (1 - early)

    def spot_at(q):
        r, p = q // 8, q % 8
        own = (1 - p % 2) * ((p + 7) // 8) + p // 7
        column = own * (p // 2 - 1 + p // 7) + (1 - own) * ((p + 1) // 2)
        dy, dx = (column + 1) % 2, 1 - column // 2
        target_core = core * own + (1 - core) * (1 - own)
        return (y + dy) % 2, (x + dx) % 2, target_core, goal(r)

    def load(q):
        b = slot_order(*spot_at(q))
        return (
            pltpu.make_async_copy(grads_ref.at[b], grad_in.at[q % 2], in_sem.at[0, q % 2]),
            pltpu.make_async_copy(outs_ref.at[b], out_in.at[q % 2], in_sem.at[1, q % 2]),
        )

    def to_part(q):
        b = block_of(*spot_at(q))
        return pltpu.make_async_copy(out_stage.at[q % 2], part_ref.at[pl.ds(b * tokens, tokens)], part_sem.at[q % 2])

    def to_sibling(r, j):
        return pltpu.make_async_remote_copy(
            src_ref=stage.at[j], dst_ref=near.at[r * 4 + j], send_sem=stage_sem.at[j], recv_sem=near_sem.at[r * 4 + j],
            device_id=peer(y, x, 1 - core, z), device_id_type=MESH,
        )

    near_x, near_y = peer(y, 1 - x, core, z), peer(1 - y, x, core, z)

    def rows(h):
        return pl.ds(h * half, half)

    def cross(kind, r):
        column, h, target, sem, index, lane = {
            "far_x": (0, 0, far_x.at[r], far_sem.at[0, r], near_x, 0),
            "far_y": (0, 1, far_y.at[r], far_sem.at[1, r], near_y, 1),
            "x0": (1, 0, from_x.at[r, rows(0)], x_sem.at[r, 0], near_x, 2),
            "x1": (1, 1, from_x.at[r, rows(1)], x_sem.at[r, 1], near_x, 3),
            "y0": (2, 0, from_y.at[r, rows(0)], y_sem.at[r, 0], near_y, 4),
            "y1": (2, 1, from_y.at[r, rows(1)], y_sem.at[r, 1], near_y, 5),
        }[kind]
        return pltpu.make_async_remote_copy(
            src_ref=near.at[r * 4 + column, rows(h)], dst_ref=target, send_sem=send_sem.at[lane, r], recv_sem=sem,
            device_id=index, device_id_type=MESH,
        )

    def along(sign, r):
        target = up if sign > 0 else down
        lane = 0 if sign > 0 else 1
        return pltpu.make_async_remote_copy(
            src_ref=near.at[r * 4 + 3], dst_ref=target.at[r], send_sem=send_sem.at[6 + lane, r], recv_sem=line_sem.at[lane, r],
            device_id=peer(y, x, core, z + sign), device_id_type=MESH,
        )

    def term(q, source, target_width, store):
        picks = jnp.concatenate(
            [slot_hits(slots_ref[block_of(*spot_at(q))], e, room).astype(jnp.float32) for e in range(experts)], axis=0
        ).astype(jnp.bfloat16)
        for first in range(0, target_width, 512):
            part = slice(first, min(first + 512, target_width))
            values = source[q % 2, :, :, part].reshape(experts * room, part.stop - first)
            store(part, turned(picks, values))

    for copy in load(0):
        copy.start()

    def one(r, p, j, own):
        q = r * 8 + p
        for copy in load(q):
            copy.wait()

        @pl.when(q + 1 < rounds * 8)
        def _():
            for copy in load(q + 1):
                copy.start()

        if own:
            near_slot = r * 4 + j
            to_sibling(r, j).wait_recv()

            def keep(part, value):
                near[near_slot, :, part] = (value + near[near_slot, :, part].astype(jnp.float32)).astype(jnp.bfloat16)

            term(q, grad_in, width, keep)
        else:

            @pl.when(r > 0)
            def _():
                to_sibling(r - 1, j).wait_send()

            def keep(part, value):
                stage[j, :, part] = value.astype(jnp.bfloat16)

            term(q, grad_in, width, keep)
            to_sibling(r, j).start()

        @pl.when(q >= 2)
        def _():
            to_part(q - 2).wait()

        def put(part, value):
            out_stage[q % 2, :, part] = value.astype(jnp.bfloat16)

        term(q, out_in, out_stage.shape[2], put)
        to_part(q).start()

    def add(target, h, *sources):
        for first in range(0, width, 512):
            part = slice(first, min(first + 512, width))
            total = near[target, h, part].astype(jnp.float32)
            for source in sources:
                total = total + source(part).astype(jnp.float32)
            near[target, h, part] = total.astype(jnp.bfloat16)

    def work(s, carry):
        @pl.when(s < rounds)
        def _():
            r = s
            one(r, 0, 0, 0)
            for j in range(4):
                if j < 3:
                    one(r, 2 * j + 1, j + 1, 0)
                one(r, min(2 * j + 2, 7), j, 1)
                for kind in (("far_x", "far_y"), ("x0",), ("y1",), ())[j]:
                    cross(kind, r).start()
            cross("far_y", r).wait_recv()
            add(r * 4 + 1, rows(1), lambda part: far_y[r, :, part])
            cross("x1", r).start()
            cross("far_x", r).wait_recv()
            add(r * 4 + 2, rows(0), lambda part: far_x[r, :, part])
            cross("y0", r).start()

        @pl.when((s >= 1) & (s < rounds + 1))
        def _():
            r = s - 1
            for kind in ("x0", "x1", "y0", "y1"):
                cross(kind, r).wait_recv()
            for h in range(2):
                add(
                    r * 4 + 3,
                    rows(h),
                    lambda part: from_x[r, rows(h), part],
                    lambda part: from_y[r, rows(h), part],
                )

        for hop in range(line - 1):
            r = s - 1 - hop
            live = (r >= 0) & (r < rounds)
            held = r * live.astype(jnp.int32)

            @pl.when(live & (goal(held) > z) & (z == hop))
            def _():
                if hop:
                    along(1, held).wait_recv()
                    for h in range(2):
                        add(held * 4 + 3, rows(h), lambda part: up[held, rows(h), part])
                along(1, held).start()

            @pl.when(live & (goal(held) < z) & (line - 1 - z == hop))
            def _():
                if hop:
                    along(-1, held).wait_recv()
                    for h in range(2):
                        add(held * 4 + 3, rows(h), lambda part: down[held, rows(h), part])
                along(-1, held).start()

        return carry

    lax.fori_loop(0, rounds + line - 1, work, 0)

    mine = (z + (z + 2) // 3) % 4 + z // 3
    sum_ref[...] = near[mine * 4 + 3].astype(jnp.float32)

    @pl.when(z > 0)
    def _():
        along(1, mine).wait_recv()
        sum_ref[...] += up[mine].astype(jnp.float32)

    @pl.when(z < line - 1)
    def _():
        along(-1, mine).wait_recv()
        sum_ref[...] += down[mine].astype(jnp.float32)

    def finish(r, carry):
        for kind in ("far_x", "far_y", "x0", "x1", "y0", "y1"):
            cross(kind, r).wait_send()

        @pl.when(goal(r) > z)
        def _():
            along(1, r).wait_send()

        @pl.when(goal(r) < z)
        def _():
            along(-1, r).wait_send()

        return carry

    lax.fori_loop(0, rounds, finish, 0)
    for j in range(4):
        to_sibling(rounds - 1, j).wait_send()
    for q in (rounds * 8 - 2, rounds * 8 - 1):
        to_part(q).wait()


def reduce_all(slots, outs, grads, collective_id):
    blocks, experts, tokens = slots.shape
    room, width = outs.shape[2:]
    wider = grads.shape[3]
    line = 4
    low = jnp.bfloat16
    any_ref = pl.BlockSpec(memory_space=pl.ANY)
    vmem = pl.BlockSpec(memory_space=pltpu.VMEM)
    dma = pltpu.SemaphoreType.DMA
    return pl.pallas_call(
        functools.partial(reduce_kernel, line),
        out_shape=(
            jax.ShapeDtypeStruct((tokens, wider), jnp.float32),
            jax.ShapeDtypeStruct((blocks * tokens, width), low),
        ),
        in_specs=[vmem, any_ref, any_ref],
        out_specs=[vmem, any_ref],
        scratch_shapes=[
            pltpu.VMEM((2, experts, room, wider), low),
            pltpu.VMEM((2, experts, room, width), low),
            pltpu.VMEM((2, tokens, width), low),
            pltpu.VMEM((4, tokens, wider), low),
            pltpu.VMEM((line * 4, tokens, wider), low),
            pltpu.VMEM((line, tokens // 2, wider), low),
            pltpu.VMEM((line, tokens // 2, wider), low),
            pltpu.VMEM((line, tokens, wider), low),
            pltpu.VMEM((line, tokens, wider), low),
            pltpu.VMEM((line, tokens, wider), low),
            pltpu.VMEM((line, tokens, wider), low),
            dma((2, 2)),
            dma((2,)),
            dma((4,)),
            dma((line * 4,)),
            dma((8, line)),
            dma((2, line)),
            dma((line, 2)),
            dma((line, 2)),
            dma((2, line)),
        ],
        compiler_params=pltpu.CompilerParams(
            collective_id=collective_id, has_side_effects=True, vmem_limit_bytes=62 << 20
        ),
        cost_estimate=pl.CostEstimate(
            flops=2 * blocks * experts * room * tokens * (width + wider),
            bytes_accessed=2 * blocks * experts * room * (width + wider),
            transcendentals=0,
        ),
        name="reduce_all",
    )(slots, grads, outs)


class LineGather:
    def __init__(self, own, out, send_sem, recv_sem, line):
        self.own, self.out, self.send_sem, self.recv_sem, self.line = own, out, send_sem, recv_sem, line
        self.spot = place()
        self.rows = own.shape[0]

    def view(self, block):
        return self.out.at[pl.ds(block * self.rows, self.rows)]

    def inside(self, block):
        return (block >= 0) & (block < self.line)

    def copy(self, sign, step):
        y, x, core, z = self.spot
        block = z - sign * step
        lane = (1 - sign) // 2
        source = self.own if step == 0 else self.view(block)
        return remote(
            source, self.view(block), self.send_sem.at[lane, step], self.recv_sem.at[lane, step], (y, x, core, z + sign)
        )

    def sends(self, sign, step):
        z = self.spot[3]
        return self.inside(z - sign * step) & self.inside(z + sign)

    def begin(self):
        for sign in (1, -1):
            pl.when(self.sends(sign, 0))(self.copy(sign, 0).start)

    def advance(self, step):
        z = self.spot[3]
        for sign in (1, -1):
            block = z - sign * (step + 1)
            lane = (1 - sign) // 2

            @pl.when(self.inside(block))
            def _():
                landed(self.view(block), self.recv_sem.at[lane, step])

            if step + 1 < self.line - 1:
                pl.when(self.sends(sign, step + 1))(self.copy(sign, step + 1).start)

    def finish(self):
        for sign in (1, -1):
            for step in range(self.line - 1):
                pl.when(self.sends(sign, step))(self.copy(sign, step).wait_send)


def start_kernel(line, hidden_ref, wq_ref, wk_ref, wv_ref, wo_ref, slots_ref, hidden_out, joined_out, wo_out, slots_out,
                 local_sem, line_send, line_recv, plane_send, plane_recv, slot_send, slot_recv, slot_line_send, slot_line_recv):
    y, x, core, z = place()
    owns = (wq_ref, wk_ref, wv_ref, wo_ref)
    near_x, near_y, sibling = (y, 1 - x, core, z), (1 - y, x, core, z), (y, x, 1 - core, z)

    def view(n, yy, xx, half=None):
        group = yy * 4 + xx * 2 + core
        rows, columns = owns[n].shape
        first, count = (0, rows) if half is None else (half * (rows // 2), rows // 2)
        if n < 3:
            return joined_out.at[pl.ds(group * rows + first, count), pl.ds(n * columns, columns)]
        return wo_out.at[pl.ds(first, count), pl.ds(pl.multiple_of(group * columns, columns), columns)]

    kinds = ("x", "y", "s", "fy", "fx", "sx", "sy", "sf")

    def copy(kind, n):
        source, target, where = {
            "x": (owns[n], view(n, y, x), near_x),
            "y": (owns[n], view(n, y, x), near_y),
            "s": (owns[n], view(n, y, x), sibling),
            "fy": (view(n, y, 1 - x, 0), view(n, y, 1 - x, 0), near_y),
            "fx": (view(n, 1 - y, x, 1), view(n, 1 - y, x, 1), near_x),
            "sx": (view(n, y, 1 - x), view(n, y, 1 - x), sibling),
            "sy": (view(n, 1 - y, x), view(n, 1 - y, x), sibling),
            "sf": (view(n, 1 - y, 1 - x), view(n, 1 - y, 1 - x), sibling),
        }[kind]
        lane = kinds.index(kind)
        return remote(source, target, plane_send.at[lane, n], plane_recv.at[lane, n], where)

    def other(n, yy, xx):
        group = yy * 4 + xx * 2 + 1 - core
        rows, columns = owns[n].shape
        if n < 3:
            return joined_out.at[pl.ds(group * rows, rows), pl.ds(n * columns, columns)]
        return wo_out.at[pl.ds(0, rows), pl.ds(pl.multiple_of(group * columns, columns), columns)]

    barrier = pltpu.get_barrier_semaphore()
    shifts = [(dy, dx, dc) for dy in range(2) for dx in range(2) for dc in range(2) if dy + dx + dc]
    plane = [((y + dy) % 2, (x + dx) % 2, (core + dc) % 2, z) for dy, dx, dc in shifts]
    for other_spot in plane:
        pl.semaphore_signal(barrier, inc=1, device_id=peer(*other_spot), device_id_type=MESH)
    for step in (-1, 1):

        @pl.when((z + step >= 0) & (z + step < line))
        def _():
            pl.semaphore_signal(barrier, inc=1, device_id=peer(y, x, core, z + step), device_id_type=MESH)

    pl.semaphore_wait(barrier, 7 + (z + line - 1) // line + (2 * line - 2 - z) // line)
    experts = slots_out.shape[1]
    group = peer(y, x, core, z)[0]
    slot_copies = []
    for n, other_spot in enumerate(plane):
        their_group = peer(*other_spot)[0]
        slot_copies.append(
            remote(
                slots_ref.at[pl.ds(their_group * experts, experts)], slots_out.at[z * 8 + group],
                slot_send.at[n], slot_recv.at[group], other_spot,
            )
        )
    own_slots = pltpu.make_async_copy(
        slots_ref.at[pl.ds(group * experts, experts)], slots_out.at[z * 8 + group], local_sem.at[5]
    )
    own_slots.start()
    slot_line = LineGather(slots_out.at[pl.ds(z * 8, 8)], slots_out, slot_line_send, slot_line_recv, line)
    hidden = LineGather(hidden_ref, hidden_out, line_send, line_recv, line)
    locals_ = [pltpu.make_async_copy(hidden_ref, hidden.view(z), local_sem.at[4])]
    locals_ += [pltpu.make_async_copy(owns[n], view(n, y, x), local_sem.at[n]) for n in range(4)]
    for slot_copy in slot_copies:
        slot_copy.start()
    hidden.begin()
    for n in range(4):
        for kind in ("x", "y", "s"):
            copy(kind, n).start()
    for local in locals_:
        local.start()
    for n in range(4):
        landed(view(n, y, 1 - x), plane_recv.at[0, n])
        copy("fy", n).start()
        copy("sx", n).start()
        landed(view(n, 1 - y, x), plane_recv.at[1, n])
        copy("fx", n).start()
        copy("sy", n).start()
    own_slots.wait()
    for other_spot in plane:
        their_group = peer(*other_spot)[0]
        landed(slots_out.at[z * 8 + their_group], slot_recv.at[their_group])
    slot_line.begin()
    hidden.advance(0)
    slot_line.advance(0)
    for n in range(4):
        landed(view(n, 1 - y, 1 - x, 0), plane_recv.at[3, n])
        landed(view(n, 1 - y, 1 - x, 1), plane_recv.at[4, n])
        copy("sf", n).start()
    for step in range(1, line - 1):
        slot_line.advance(step)
        hidden.advance(step)
    for n in range(4):
        landed(other(n, y, x), plane_recv.at[2, n])
        landed(other(n, y, 1 - x), plane_recv.at[5, n])
        landed(other(n, 1 - y, x), plane_recv.at[6, n])
        landed(other(n, 1 - y, 1 - x), plane_recv.at[7, n])
    hidden.finish()
    slot_line.finish()
    for slot_copy in slot_copies:
        slot_copy.wait_send()
    for n in range(4):
        for kind in kinds:
            copy(kind, n).wait_send()
    for local in locals_:
        local.wait()


def start_exchange(hidden, w_query, w_key, w_value, w_out, slots, collective_id):
    line = 4
    any_ref = pl.BlockSpec(memory_space=pl.ANY)
    dma = pltpu.SemaphoreType.DMA
    rows, width = hidden.shape
    part, columns = w_query.shape
    low = jnp.bfloat16
    return pl.pallas_call(
        functools.partial(start_kernel, line),
        out_shape=(
            jax.ShapeDtypeStruct((line * rows, width), low),
            jax.ShapeDtypeStruct((8 * part, 3 * columns), low),
            jax.ShapeDtypeStruct((w_out.shape[0], 8 * w_out.shape[1]), low),
            jax.ShapeDtypeStruct((line * 8, slots.shape[0] // 8, slots.shape[1]), slots.dtype),
        ),
        in_specs=[any_ref] * 6,
        out_specs=[any_ref] * 4,
        scratch_shapes=[
            dma((6,)), dma((2, line)), dma((2, line)), dma((8, 4)), dma((8, 4)),
            dma((7,)), dma((8,)), dma((2, line)), dma((2, line)),
        ],
        compiler_params=pltpu.CompilerParams(collective_id=collective_id, has_side_effects=True),
        cost_estimate=pl.CostEstimate(flops=0, bytes_accessed=150 << 20, transcendentals=0),
        name="start_exchange",
    )(hidden, w_query, w_key, w_value, w_out, slots)


class LineReduce:
    def __init__(self, part, up, down, send_sem, recv_sem, line):
        self.part, self.up, self.down = part, up, down
        self.send_sem, self.recv_sem, self.line = send_sem, recv_sem, line
        self.spot = place()

    def copy(self, sign, goal):
        y, x, core, z = self.spot
        lane = (1 - sign) // 2
        target = self.up if sign > 0 else self.down
        return remote(
            self.part.at[goal], target.at[goal], self.send_sem.at[lane, goal], self.recv_sem.at[lane, goal],
            (y, x, core, z + sign),
        )

    def order(self, i):
        z = self.spot[3]
        return either(self.line - 1 - i, i, z * 2 // self.line)

    def lead(self, goal):
        z = self.spot[3]
        pl.when((z == 0) & (goal > 0))(self.copy(1, goal).start)
        pl.when((z == self.line - 1) & (goal < z))(self.copy(-1, goal).start)

    def advance(self, unit, total_ref):
        z, line = self.spot[3], self.line
        for sign in (1, -1):
            goal = line - 1 - unit + z if sign > 0 else unit - line + 1 + z
            live = ((z > 0) & (goal < line)) if sign > 0 else ((z < line - 1) & (goal >= 0))
            inbox = self.up if sign > 0 else self.down

            @pl.when(live)
            def _():
                self.copy(sign, goal).wait_recv()
                if unit < line - 1:
                    self.part[goal] = (
                        self.part[goal].astype(jnp.float32) + inbox[goal].astype(jnp.float32)
                    ).astype(jnp.bfloat16)
                    self.copy(sign, goal).start()
                else:
                    total_ref[...] += inbox[goal].astype(jnp.float32)

    def finish(self):
        z = self.spot[3]

        def step(goal, carry):
            pl.when(goal > z)(self.copy(1, goal).wait_send)
            pl.when(goal < z)(self.copy(-1, goal).wait_send)
            return carry

        lax.fori_loop(0, self.line, step, 0)


def mixed_out_kernel(line, mixed_ref, w_ref, residual_ref, gain_ref, router_ref,
                     x_ref, hidden_ref, probs_ref, part, up, down, send_sem, recv_sem):
    rows, width = x_ref.shape
    greet(line)
    reduce = LineReduce(part, up, down, send_sem, recv_sem, line)
    z = reduce.spot[3]

    def term(i, carry):
        goal = reduce.order(i)
        first = pl.multiple_of(goal * rows, rows)
        for column in range(0, width, 512):
            piece = slice(column, column + 512)
            value = jnp.dot(mixed_ref[pl.ds(first, rows), :], w_ref[:, piece], preferred_element_type=jnp.float32)

            @pl.when(goal == z)
            def _():
                x_ref[:, piece] = value

            part[goal, :, piece] = value.astype(jnp.bfloat16)
        reduce.lead(goal)
        return carry

    lax.fori_loop(0, line, term, 0)
    for unit in range(1, line):
        reduce.advance(unit, x_ref)
    x_one = x_ref[...] + residual_ref[...].astype(jnp.float32)
    x_ref[...] = x_one
    scale = lax.rsqrt(jnp.mean(x_one * x_one, axis=-1, keepdims=True) + norm_eps)
    hidden = (x_one * scale * gain_ref[...]).astype(jnp.bfloat16)
    hidden_ref[...] = hidden
    logits = lax.dot_general(
        router_ref[...], hidden, (((1,), (1,)), ((), ())), preferred_element_type=jnp.float32
    )
    shifted = jnp.exp(logits - jnp.max(logits, axis=0, keepdims=True))
    probs_ref[...] = shifted / jnp.sum(shifted, axis=0, keepdims=True)
    reduce.finish()


def mixed_out(mixed, w_out, residual, gain, router_turned, collective_id):
    line = 4
    rows, width = residual.shape
    experts = router_turned.shape[0]
    vmem = pl.BlockSpec(memory_space=pltpu.VMEM)
    dma = pltpu.SemaphoreType.DMA
    block = pltpu.VMEM((line, rows, width), jnp.bfloat16)
    return pl.pallas_call(
        functools.partial(mixed_out_kernel, line),
        out_shape=(
            jax.ShapeDtypeStruct((rows, width), jnp.float32),
            jax.ShapeDtypeStruct((rows, width), jnp.bfloat16),
            jax.ShapeDtypeStruct((experts, rows), jnp.float32),
        ),
        in_specs=[vmem] * 5,
        out_specs=[vmem] * 3,
        scratch_shapes=[block, block, block, dma((2, line)), dma((2, line))],
        compiler_params=pltpu.CompilerParams(
            collective_id=collective_id, has_side_effects=True, vmem_limit_bytes=56 << 20
        ),
        cost_estimate=pl.CostEstimate(flops=0, bytes_accessed=150 << 20, transcendentals=0),
        name="mixed_out",
    )(mixed, w_out, residual, gain.reshape(1, width), router_turned)


class Butterfly:
    def __init__(self, data, total, from_core, from_x, from_y, from_z, sums, send_sem, recv_sem):
        self.data, self.total, self.sums = data, total, sums
        self.boxes = {"core": from_core, "x": from_x, "y": from_y}
        self.from_z, self.send_sem, self.recv_sem = from_z, send_sem, recv_sem
        y, x, core, z = self.spot = place()
        self.width = data.shape[1]
        self.near = {"core": (y, x, 1 - core, z), "x": (y, 1 - x, core, z), "y": (1 - y, x, core, z)}
        half, quarter, eighth = self.width // 2, self.width // 4, self.width // 8
        first = core * half
        self.kept = {"core": (first, half), "x": (first + x * quarter, quarter)}
        self.kept["y"] = (first + x * quarter + y * eighth, eighth)
        self.away = {
            "core": ((1 - core) * half, half),
            "x": (first + (1 - x) * quarter, quarter),
            "y": (first + x * quarter + (1 - y) * eighth, eighth),
        }

    def part(self, span):
        return pl.ds(pl.multiple_of(span[0], span[1]), span[1])

    def fold_copy(self, axis):
        lane = ("core", "x", "y").index(axis)
        return remote(
            self.data.at[:, self.part(self.away[axis])], self.boxes[axis], self.send_sem.at[lane],
            self.recv_sem.at[lane], self.near[axis],
        )

    def fold(self, axis):
        copy = self.fold_copy(axis)
        copy.start()
        copy.wait()
        self.data[:, self.part(self.kept[axis])] += self.boxes[axis][...]

    def line_step(self, step):
        y, x, core, z = self.spot
        other = (z + 1 - 2 * (z % 2)) if step == 0 else (z + 2) % 4
        piece = self.part(self.kept["y"])
        source = self.data.at[:, piece] if step == 0 else self.sums
        copy = remote(
            source, self.from_z.at[step], self.send_sem.at[3 + step], self.recv_sem.at[3 + step], (y, x, core, other)
        )
        copy.start()
        copy.wait()
        if step == 0:
            self.sums[...] = self.data[:, piece] + self.from_z[0]
        else:
            self.total[:, piece] = self.sums[...] + self.from_z[1]

    def unfold(self, axis):
        lane = 5 + ("core", "x", "y").index(axis)
        mine = self.total.at[:, self.part(self.kept[axis])]
        copy = remote(mine, mine, self.send_sem.at[lane], self.recv_sem.at[lane], self.near[axis])
        copy.start()
        copy.wait_send()
        landed(self.total.at[:, self.part(self.away[axis])], self.recv_sem.at[lane])

    def scratch(rows, width):
        low = jnp.float32
        return [
            pltpu.VMEM((rows, width // 2), low),
            pltpu.VMEM((rows, width // 4), low),
            pltpu.VMEM((rows, width // 8), low),
            pltpu.VMEM((2, rows, width // 8), low),
            pltpu.VMEM((rows, width // 8), low),
            pltpu.SemaphoreType.DMA((8,)),
            pltpu.SemaphoreType.DMA((8,)),
        ]


def greet_far(line):
    y, x, core, z = place()
    barrier = pltpu.get_barrier_semaphore()
    for near in ((y, x, 1 - core, z), (y, 1 - x, core, z), (1 - y, x, core, z)):
        pl.semaphore_signal(barrier, inc=1, device_id=peer(*near), device_id_type=MESH)
    for step in range(1, line):
        pl.semaphore_signal(barrier, inc=1, device_id=peer(y, x, core, (z + step) % line), device_id_type=MESH)
    pl.semaphore_wait(barrier, 3 + line - 1)


def back_gather_kernel(line, own_ref, sums_ref, x_ref, c_ref, pre_ref, gated_ref,
                       out_ref, total_ref, gate_ref, up_ref, down_ref,
                       data, x_in, c_in, pre_in, gated_in, gate_out, up_out, down_out,
                       local_sem, send_sem, recv_sem, load_sem, store_sem, *fly):
    experts = x_ref.shape[0]
    half = x_in.shape[2]
    steps = 2 * experts
    greet_far(line)
    gather = LineGather(own_ref, out_ref, send_sem, recv_sem, line)
    local = pltpu.make_async_copy(own_ref, gather.view(gather.spot[3]), local_sem)
    gather.begin()
    local.start()
    data[...] = sums_ref[...]
    butterfly = Butterfly(data, total_ref, *fly)

    def loads(t):
        e, slot = t // 2, t % 2
        columns = pl.ds(pl.multiple_of(t % 2 * half, half), half)
        return (
            pltpu.make_async_copy(x_ref.at[e, :, columns], x_in.at[slot], load_sem.at[0, slot]),
            pltpu.make_async_copy(c_ref.at[e, :, columns], c_in.at[slot], load_sem.at[1, slot]),
            pltpu.make_async_copy(pre_ref.at[e], pre_in.at[slot], load_sem.at[2, slot]),
            pltpu.make_async_copy(gated_ref.at[e], gated_in.at[slot], load_sem.at[3, slot]),
        )

    def stores(t):
        e, slot = t // 2, t % 2
        columns = pl.ds(pl.multiple_of(t % 2 * half, half), half)
        return (
            pltpu.make_async_copy(gate_out.at[slot], gate_ref.at[e, columns], store_sem.at[0, slot]),
            pltpu.make_async_copy(up_out.at[slot], up_ref.at[e, columns], store_sem.at[1, slot]),
            pltpu.make_async_copy(down_out.at[slot], down_ref.at[e, :, columns], store_sem.at[2, slot]),
        )

    for copy in loads(0):
        copy.start()
    events = {
        1: lambda: butterfly.fold("core"),
        2: lambda: butterfly.fold("x"),
        4: lambda: butterfly.fold("y"),
        5: lambda: gather.advance(0),
        6: lambda: butterfly.line_step(0),
        9: lambda: gather.advance(1),
        10: lambda: butterfly.line_step(1),
        12: lambda: butterfly.unfold("y"),
        13: lambda: butterfly.unfold("x"),
        14: lambda: butterfly.unfold("core"),
    }

    def work(t, carry):
        for when, event in events.items():
            pl.when(t == when)(event)
        for copy in loads(t):
            copy.wait()

        @pl.when(t + 1 < steps)
        def _():
            for copy in loads(t + 1):
                copy.start()

        @pl.when(t >= 2)
        def _():
            for copy in stores(t - 2):
                copy.wait()

        slot = t % 2
        weight_terms(
            *(r.at[slot] for r in (x_in, c_in, pre_in, gated_in, gate_out, up_out, down_out))
        )
        for copy in stores(t):
            copy.start()
        return carry

    lax.fori_loop(0, steps, work, 0)
    gather.advance(2)
    for t in (steps - 2, steps - 1):
        for copy in stores(t):
            copy.wait()
    gather.finish()
    local.wait()


def back_gather(own, sums, x_slots, c_slots, pre, gated, collective_id):
    line = 4
    experts, total, width = x_slots.shape
    units = gated.shape[2]
    half = width // 2
    low, wide = jnp.bfloat16, jnp.float32
    any_ref = pl.BlockSpec(memory_space=pl.ANY)
    vmem = pl.BlockSpec(memory_space=pltpu.VMEM)
    dma = pltpu.SemaphoreType.DMA
    return pl.pallas_call(
        functools.partial(back_gather_kernel, line),
        out_shape=(
            jax.ShapeDtypeStruct((line * own.shape[0], own.shape[1]), own.dtype),
            jax.ShapeDtypeStruct(sums.shape, wide),
            jax.ShapeDtypeStruct((experts, width, units), wide),
            jax.ShapeDtypeStruct((experts, width, units), wide),
            jax.ShapeDtypeStruct((experts, units, width), wide),
        ),
        in_specs=[any_ref, vmem] + [any_ref] * 4,
        out_specs=[any_ref, vmem] + [any_ref] * 3,
        scratch_shapes=[
            pltpu.VMEM(sums.shape, wide),
            pltpu.VMEM((2, total, half), low),
            pltpu.VMEM((2, total, half), low),
            pltpu.VMEM((2, total, 2 * units), low),
            pltpu.VMEM((2, total, units), low),
            pltpu.VMEM((2, half, units), wide),
            pltpu.VMEM((2, half, units), wide),
            pltpu.VMEM((2, units, half), wide),
            dma(()), dma((2, line)), dma((2, line)), dma((4, 2)), dma((3, 2)),
            *Butterfly.scratch(*sums.shape),
        ],
        compiler_params=pltpu.CompilerParams(
            collective_id=collective_id, has_side_effects=True, vmem_limit_bytes=50 << 20
        ),
        cost_estimate=pl.CostEstimate(
            flops=6 * experts * total * width * units, bytes_accessed=180 << 20, transcendentals=0
        ),
        name="back_gather",
    )(own, sums, x_slots, c_slots, pre, gated)


def last_kernel(line, joined_ref, weight_ref, hidden_ref, mixed_ref, attn_ref, residual_ref, gain_ref, x_grad_ref, gains_ref,
                input_ref, wq_ref, wk_ref, wv_ref, wo_ref, total_ref,
                part, up, down, stage, near, far_x, far_y, from_x, from_y, data,
                line_send, line_recv, stage_sem, near_sem, send_sem, recv_sem, *fly):
    y, x, core, z = place()
    rows, width = input_ref.shape
    columns = joined_ref.shape[1]
    half = rows // 2
    low = jnp.bfloat16
    greet_far(line)
    reduce = LineReduce(part, up, down, line_send, line_recv, line)

    def term(i, carry):
        goal = reduce.order(i)
        first = pl.multiple_of(goal * rows, rows)
        for column in range(0, width, 512):
            piece = slice(column, column + 512)
            value = across(joined_ref[pl.ds(first, rows), :], weight_ref[piece, :])

            @pl.when(goal == z)
            def _():
                input_ref[:, piece] = value

            part[goal, :, piece] = value.astype(low)
        reduce.lead(goal)
        return carry

    lax.fori_loop(0, line, term, 0)
    near_x, near_y, sibling = (y, 1 - x, core, z), (1 - y, x, core, z), (y, x, 1 - core, z)

    def terms(j, own, store):
        dy, dx = (j + 1) % 2, 1 - j // 2
        group = (y + dy) % 2 * 4 + (x + dx) % 2 * 2 + (core if own else 1 - core)
        span = pl.ds(pl.multiple_of(group * rows, rows), rows)
        turned_rows = hidden_ref[:, span]
        for column in range(0, columns, 512):
            piece = slice(column, column + 512)
            store(piece, turned(turned_rows, joined_ref[:, piece]))
        value = turned(mixed_ref[...], attn_ref[:, span])
        store(slice(columns, columns + rows), value[:rows])
        store(slice(columns + rows, columns + 2 * rows), value[rows:])

    def to_sibling(j):
        return remote(stage.at[j], near.at[j], stage_sem.at[j], near_sem.at[j], sibling)

    def away(j, carry):
        def store(piece, value):
            stage[j, :, piece] = value.astype(low)

        terms(j, False, store)
        to_sibling(j).start()
        return carry

    def own(j, carry):
        to_sibling(j).wait_recv()

        def store(piece, value):
            near[j, :, piece] = (value + near[j, :, piece].astype(jnp.float32)).astype(low)

        terms(j, True, store)
        return carry

    lax.fori_loop(0, 4, away, 0)
    lax.fori_loop(0, 4, own, 0)

    def line_rows(h):
        return pl.ds(h * half, half)

    def cross(kind):
        column, h, target, where = {
            "far_x": (0, 0, far_x, near_x),
            "far_y": (0, 1, far_y, near_y),
            "x0": (1, 0, from_x.at[line_rows(0)], near_x),
            "x1": (1, 1, from_x.at[line_rows(1)], near_x),
            "y0": (2, 0, from_y.at[line_rows(0)], near_y),
            "y1": (2, 1, from_y.at[line_rows(1)], near_y),
        }[kind]
        lane = kinds.index(kind)
        return remote(near.at[column, line_rows(h)], target, send_sem.at[lane], recv_sem.at[lane], where)

    kinds = ("far_x", "far_y", "x0", "y1", "x1", "y0")
    for kind in kinds[:4]:
        cross(kind).start()

    def add(column, h, source):
        near[column, line_rows(h), :] = (
            near[column, line_rows(h), :].astype(jnp.float32) + source[...].astype(jnp.float32)
        ).astype(low)

    reduce.advance(1, input_ref)
    cross("far_y").wait_recv()
    add(1, 1, far_y)
    cross("x1").start()
    cross("far_x").wait_recv()
    add(2, 0, far_x)
    cross("y0").start()
    reduce.advance(2, input_ref)
    for kind in kinds[2:]:
        cross(kind).wait_recv()
    for n, ref in enumerate((wq_ref, wk_ref, wv_ref, wo_ref, wo_ref)):
        count = columns // 3 if n < 3 else rows
        first = n * (columns // 3) if n < 3 else columns + (n - 3) * rows
        piece = slice(first, first + count)
        total = sum(r[:, piece].astype(jnp.float32) for r in (near.at[3], from_x, from_y))
        if n < 3:
            ref[...] = total
        else:
            ref[(n - 3) * rows : (n - 2) * rows, :] = total
    reduce.advance(3, input_ref)
    grad = input_ref[...]
    values = residual_ref[...].astype(jnp.float32)
    scale = lax.rsqrt(jnp.mean(values * values, axis=-1, keepdims=True) + norm_eps)
    gained = grad * gain_ref[...]
    inner = jnp.sum(gained * values, axis=-1, keepdims=True)
    data[...] = gains_ref[...]
    data[2:3, :] = jnp.sum(grad * values * scale, axis=0, keepdims=True)
    input_ref[...] = x_grad_ref[...] + scale * gained - values * (scale * scale * scale * inner / width)
    butterfly = Butterfly(data, total_ref, *fly)
    for axis in ("core", "x", "y"):
        butterfly.fold(axis)
    butterfly.line_step(0)
    butterfly.line_step(1)
    for axis in ("y", "x", "core"):
        butterfly.unfold(axis)
    reduce.finish()
    for j in range(4):
        to_sibling(j).wait_send()
    for kind in kinds:
        cross(kind).wait_send()


def last_exchange(joined, weight, hidden, mixed, attn, residual, gain, x_grad, gains, collective_id):
    line = 4
    rows, width = residual.shape
    columns = joined.shape[1] // 3
    low, wide = jnp.bfloat16, jnp.float32
    vmem = pl.BlockSpec(memory_space=pltpu.VMEM)
    dma = pltpu.SemaphoreType.DMA
    block = pltpu.VMEM((line, rows, width), low)
    one = pltpu.VMEM((rows, width), low)
    part = pltpu.VMEM((rows // 2, width), low)
    square = jax.ShapeDtypeStruct((rows, columns), wide)
    return pl.pallas_call(
        functools.partial(last_kernel, line),
        out_shape=(
            jax.ShapeDtypeStruct((rows, width), wide), square, square, square,
            jax.ShapeDtypeStruct((2 * rows, rows), wide),
            jax.ShapeDtypeStruct(gains.shape, wide),
        ),
        in_specs=[vmem] * 9,
        out_specs=[vmem] * 6,
        scratch_shapes=[
            block, block, block, pltpu.VMEM((4, rows, width), low), pltpu.VMEM((4, rows, width), low),
            part, part, one, one, pltpu.VMEM(gains.shape, wide),
            dma((2, line)), dma((2, line)), dma((4,)), dma((4,)), dma((6,)), dma((6,)),
            *Butterfly.scratch(*gains.shape),
        ],
        compiler_params=pltpu.CompilerParams(
            collective_id=collective_id, has_side_effects=True, vmem_limit_bytes=62 << 20
        ),
        cost_estimate=pl.CostEstimate(flops=0, bytes_accessed=250 << 20, transcendentals=0),
        name="last_exchange",
    )(joined, weight, hidden, mixed, attn, residual, gain.reshape(1, width), x_grad, gains)


def visible_block(row_paths, key_paths, key_valid, row_first):
    row_count = row_paths.shape[1]
    key_count = key_paths.shape[1]
    key_segment = key_paths[0][None, :]
    on_path = (
        (key_segment == row_paths[0][:, None])
        | (key_segment == row_paths[1][:, None])
        | (key_segment == row_paths[2][:, None])
    )
    row_place = row_first + lax.iota(jnp.int32, row_count)
    key_place = lax.iota(jnp.int32, key_count)
    earlier = key_place[None, :] <= row_place[:, None]
    return on_path & earlier & (key_valid[None, :] == 1) | (
        key_place[None, :] == row_place[:, None]
    )


def rotation(positions, head_dim):
    half = head_dim // 2
    freqs = jnp.exp(-jnp.log(rope_base) * 2.0 * lax.iota(jnp.float32, half) / head_dim)
    angles = positions.astype(jnp.float32)[:, None] * freqs[None, :]
    return (jnp.cos(angles), jnp.sin(angles))


def visible_bias(row_first, row_paths, row_places, key_segment, key_valid, key_places):
    on_path = (key_segment == row_paths[0]) | (key_segment == row_paths[1]) | (key_segment == row_paths[2])
    seen = (on_path & (key_places <= row_places) & (key_valid == 1)) | (key_places == row_places)
    return jnp.where(seen, 0.0, masked_score)


def attend_kernel(step, raw_ref, scale_ref, gain_ref, cos_ref, sin_ref, column_ref, line_ref,
                  query_ref, key_ref, value_ref, mixed_ref, log_ref, bias, logs):
    seq, columns = query_ref.shape
    heads = columns // HD

    def prepare(i, carry):
        rows = pl.ds(pl.multiple_of(i * step, step), step)
        cosine, sine = cos_ref[rows, :], sin_ref[rows, :]
        for n, ref in enumerate((query_ref, key_ref)):
            scale = scale_ref[rows, n : n + 1]
            for h in range(heads):
                span = slice(h * HD, (h + 1) * HD)
                values = raw_ref[rows, n * columns + h * HD : n * columns + (h + 1) * HD]
                values = values * scale * gain_ref[n : n + 1, span]
                turn = pltpu.roll(values, HD // 2, 1)
                ref[rows, span] = (values * cosine + turn * sine).astype(jnp.bfloat16)
        value_ref[rows, :] = raw_ref[rows, 2 * columns :].astype(jnp.bfloat16)
        return carry

    lax.fori_loop(0, seq // step, prepare, 0)
    for i in range(seq // step):
        rows = slice(i * step, (i + 1) * step)
        wide = (i + 1) * step
        places = lax.broadcasted_iota(jnp.int32, (step, wide), 0) + i * step
        bias[:, :wide] = visible_bias(
            i * step,
            [column_ref[rows, n : n + 1] for n in range(3)],
            places,
            line_ref[0:1, :wide],
            line_ref[3:4, :wide],
            lax.broadcasted_iota(jnp.int32, (step, wide), 1),
        )

        def head(h, carry):
            span = pl.ds(pl.multiple_of(h * HD, HD), HD)
            scores = across(query_ref[rows, span], key_ref[:wide, span]) * HD ** (-0.5) + bias[:, :wide]
            top = jnp.max(scores, axis=1, keepdims=True)
            weights = jnp.exp(scores - top)
            total = jnp.sum(weights, axis=1, keepdims=True)
            low = (weights / total).astype(jnp.bfloat16)
            mixed = jnp.dot(low, value_ref[:wide, span], preferred_element_type=jnp.float32)
            mixed_ref[rows, span] = mixed.astype(jnp.bfloat16)
            lanes = lax.broadcasted_iota(jnp.int32, (step, 128), 1)
            logs[...] = jnp.where(lanes == h, top + jnp.log(total), logs[...])
            return carry

        logs[...] = jnp.zeros_like(logs)
        lax.fori_loop(0, heads, head, 0)
        log_ref[:, rows] = jnp.transpose(logs[...])[: log_ref.shape[0]]


def attend(raw, scales, gains, cosine, sine, path_columns, path_lines):
    seq = raw.shape[0]
    columns = raw.shape[1] // 3
    step = min(256, seq)
    vmem = pl.BlockSpec(memory_space=pltpu.VMEM)
    low = jax.ShapeDtypeStruct((seq, columns), jnp.bfloat16)
    return pl.pallas_call(
        functools.partial(attend_kernel, step),
        out_shape=(low, low, low, low, jax.ShapeDtypeStruct((8, seq), jnp.float32)),
        in_specs=[vmem] * 7,
        out_specs=[vmem] * 5,
        scratch_shapes=[pltpu.VMEM((step, seq), jnp.float32), pltpu.VMEM((step, 128), jnp.float32)],
        compiler_params=pltpu.CompilerParams(vmem_limit_bytes=50 << 20),
        cost_estimate=pl.CostEstimate(
            flops=4 * seq * seq * columns, bytes_accessed=16 * seq * columns, transcendentals=seq * seq
        ),
        name="attend",
    )(raw, scales, gains, cosine, sine, path_columns, path_lines)


def attend_back_kernel(step, grad_ref, w_ref, query_ref, key_ref, value_ref, log_ref, cos_ref, sin_ref,
                       column_ref, line_ref, dq_ref, dk_ref, dv_ref, bias, mixed):
    seq, columns = query_ref.shape
    heads = columns // HD
    dk_ref[...] = jnp.zeros_like(dk_ref)
    dv_ref[...] = jnp.zeros_like(dv_ref)

    def unturn(values, rows):
        return values * cos_ref[rows, :] - pltpu.roll(values, HD // 2, 1) * sin_ref[rows, :]

    for i in range(seq // step):
        rows = slice(i * step, (i + 1) * step)
        wide = (i + 1) * step
        mixed[...] = across(grad_ref[rows, :], w_ref[...]).astype(jnp.bfloat16)
        places = lax.broadcasted_iota(jnp.int32, (wide, step), 1) + i * step
        bias[:wide, :] = visible_bias(
            i * step,
            [line_ref[n : n + 1, rows] for n in range(3)],
            places,
            column_ref[:wide, 0:1],
            column_ref[:wide, 3:4],
            lax.broadcasted_iota(jnp.int32, (wide, step), 0),
        )

        def head(h, carry):
            span = pl.ds(pl.multiple_of(h * HD, HD), HD)
            query, key, grad = query_ref[rows, span], key_ref[:wide, span], mixed[:, span]
            scores = across(key, query) * HD ** (-0.5) + bias[:wide, :]
            weights = jnp.exp(scores - log_ref[pl.ds(h, 1), rows])
            grad_weights = across(value_ref[:wide, span], grad)
            inner = jnp.sum(weights * grad_weights, axis=0, keepdims=True)
            grad_scores = (weights * (grad_weights - inner)).astype(jnp.bfloat16)
            dq_ref[rows, span] = unturn(turned(grad_scores, key) * HD ** (-0.5), rows)
            dk_ref[:wide, span] += jnp.dot(grad_scores, query, preferred_element_type=jnp.float32)
            dv_ref[:wide, span] += jnp.dot(
                weights.astype(jnp.bfloat16), grad, preferred_element_type=jnp.float32
            )
            return carry

        lax.fori_loop(0, heads, head, 0)
    for i in range(seq // step):
        rows = slice(i * step, (i + 1) * step)
        for h in range(heads):
            span = slice(h * HD, (h + 1) * HD)
            dk_ref[rows, span] = unturn(dk_ref[rows, span] * HD ** (-0.5), rows)


def attend_back(grads, w_out, query, key, value, logs, cosine, sine, path_columns, path_lines):
    seq, columns = query.shape
    step = min(256, seq)
    vmem = pl.BlockSpec(memory_space=pltpu.VMEM)
    wide = jax.ShapeDtypeStruct((seq, columns), jnp.float32)
    return pl.pallas_call(
        functools.partial(attend_back_kernel, step),
        out_shape=(wide, wide, wide),
        in_specs=[vmem] * 10,
        out_specs=[vmem] * 3,
        scratch_shapes=[pltpu.VMEM((seq, step), jnp.float32), pltpu.VMEM((step, columns), jnp.bfloat16)],
        compiler_params=pltpu.CompilerParams(vmem_limit_bytes=56 << 20),
        cost_estimate=pl.CostEstimate(
            flops=10 * seq * seq * columns, bytes_accessed=24 * seq * columns, transcendentals=seq * seq
        ),
        name="attend_back",
    )(grads, w_out, query, key, value, logs, cosine, sine, path_columns, path_lines)


def rms_apply(values, gain):
    scale = lax.rsqrt(jnp.mean(values * values, axis=-1, keepdims=True) + norm_eps)
    return (values * scale * gain, scale)


def rms_grad(values, scale, gain, grads, inner, width):
    grad_values = scale * gain * grads - values * scale**3 * inner / width
    grad_gain = jnp.sum(grads * values * scale, axis=0)
    return (grad_values, grad_gain)


def tensor_sums(pair):
    return lax.psum((pair[0], pair[1]), "tensor")


def heads_to_rows(term, rows):
    return lax.psum_scatter(
        term(jnp.int32(0), rows * lax.axis_size("tensor")).astype(jnp.bfloat16),
        "tensor",
        scatter_dimension=0,
        tiled=True,
    ).astype(jnp.float32)


def sum_over_dp(rows):
    dp = lax.axis_size("dp")
    pieces = rows.reshape(dp, rows.shape[0] // dp, rows.shape[1])
    return lax.psum_scatter(pieces, "dp", scatter_dimension=0, tiled=False)


def sum_over_tensor(part):
    return lax.psum_scatter(part, "tensor", scatter_dimension=0, tiled=True)


def body(
    residual,
    attn_gain,
    w_query,
    w_key,
    w_value,
    query_gain,
    key_gain,
    w_out,
    moe_gain,
    router,
    w_gate,
    w_up,
    w_down,
    segment_path,
    token_valid,
    routes,
    route_order,
    cotangent,
):
    tensor_rank = lax.axis_index("tensor")
    tok_dev, width = residual.shape
    seq_len = segment_path.shape[1]
    top_count = routes.shape[1]
    experts = router.shape[1]
    local_experts = w_gate.shape[0]
    dp_groups = experts // local_experts
    capacity = 9 * tok_dev * top_count // (8 * experts)
    full_width = H * HD
    everyone = ("dp", "tensor")
    direct = dp_groups == 8 and lax.axis_size("tensor") == 4
    first_expert = lax.axis_index("dp") * local_experts
    slot_rows = padded(capacity, 8)
    valid_dev = lax.dynamic_slice_in_dim(token_valid, tensor_rank * tok_dev, tok_dev)
    slots_own = slot_table(routes, route_order, valid_dev, experts, capacity)
    cots_all = lax.all_gather(cotangent, everyone, axis=0, tiled=True)
    head_cols = w_query.shape[1]
    residual_float = residual.astype(jnp.float32)
    normed_one, scale_one = rms_apply(residual_float, attn_gain)
    hidden = normed_one.astype(jnp.bfloat16)
    path_lines = jnp.concatenate((segment_path, token_valid[None]), axis=0)
    path_columns = path_lines.T
    positions = jnp.sum(visible_block(segment_path, segment_path, token_valid, 0).astype(jnp.int32), axis=1) - 1
    cosine, sine = rotation(positions, HD)
    cosine = jnp.concatenate((cosine, cosine), axis=1)
    sine = jnp.concatenate((-sine, sine), axis=1)
    if direct:
        hidden_all, joined_weight, gathered_out, slots = start_exchange(
            hidden, w_query, w_key, w_value, w_out, slots_own, 3
        )
        slots = jnp.swapaxes(slots.reshape(4, 8, local_experts, tok_dev), 0, 1).reshape(32, local_experts, tok_dev)
    else:
        hidden_all = lax.all_gather(hidden, "tensor", axis=0, tiled=True)
        joined_weight = jnp.concatenate(
            [lax.all_gather(w, "dp", axis=0, tiled=True) for w in (w_query, w_key, w_value)], axis=1
        )
        gathered_out = lax.all_gather(w_out, "dp", axis=1, tiled=True)
        slots_all = lax.all_gather(slots_own.astype(jnp.bfloat16), everyone, axis=0)
        slots = lax.dynamic_slice_in_dim(slots_all, first_expert, local_experts, 1).astype(jnp.int32)
    projected = jnp.dot(hidden_all, joined_weight, preferred_element_type=jnp.float32)
    blocks = slots.shape[0]
    q_raw = projected[:, :head_cols]
    k_raw = projected[:, head_cols : 2 * head_cols]
    query_sq, key_sq = tensor_sums((jnp.sum(q_raw * q_raw, axis=1), jnp.sum(k_raw * k_raw, axis=1)))
    query_scale = lax.rsqrt(query_sq / full_width + norm_eps)[:, None]
    key_scale = lax.rsqrt(key_sq / full_width + norm_eps)[:, None]
    query_gain_dev = lax.dynamic_slice_in_dim(query_gain, tensor_rank * head_cols, head_cols)
    key_gain_dev = lax.dynamic_slice_in_dim(key_gain, tensor_rank * head_cols, head_cols)
    query_low, key_low, value_low, attn_mixed, log_totals = attend(
        projected,
        jnp.concatenate((query_scale, key_scale), axis=1),
        jnp.stack((query_gain_dev, key_gain_dev)),
        cosine,
        sine,
        path_columns,
        path_lines,
    )
    if direct:
        x_one, hidden_two, gates_own = mixed_out(attn_mixed, gathered_out, residual, moe_gain, router.T, 4)
        probs = gates_own.T
    else:

        def attn_term(first_row, row_count):
            return jnp.dot(attn_mixed, gathered_out, preferred_element_type=jnp.float32)

        x_one = residual_float + heads_to_rows(attn_term, tok_dev)
        hidden_two = rms_apply(x_one, moe_gain)[0].astype(jnp.bfloat16)
        logits = jnp.dot(hidden_two, router, preferred_element_type=jnp.float32)
        probs = jax.nn.softmax(logits, axis=-1)
        gates_own = probs.T
    scale_two = lax.rsqrt(jnp.mean(x_one * x_one, axis=-1, keepdims=True) + norm_eps)
    if direct:
        x_slots, c_slots, gate_slots = gather_dispatch(slots, hidden_two, gates_own, cots_all, slot_rows, 1)
    else:
        gates_all = lax.all_gather(gates_own, everyone, axis=0)
        rows_all = lax.all_gather(hidden_two, everyone, axis=0, tiled=True)
        gates = lax.dynamic_slice_in_dim(gates_all, first_expert, local_experts, 1)
        x_slots, gate_slots = dispatch(slots, gates, rows_all, slot_rows)
        c_slots = dispatch(slots, None, cots_all, slot_rows)
    outs, grads, pre, gated = expert_pass(
        first_expert.reshape(1),
        x_slots,
        c_slots,
        gate_slots,
        w_gate,
        w_up,
        w_down,
        blocks,
        padded(slot_rows, 16),
    )
    if direct:
        grad_rows, out_part = reduce_all(slots, outs, grads, 2)
    else:
        out_part, grad_part = combine(slots, outs, grads)
        grad_rows = sum_over_tensor(sum_over_dp(grad_part)).astype(jnp.float32)
    out_part = sum_over_dp(out_part)
    grad_out = cotangent.astype(jnp.float32)
    grad_hidden_two = grad_rows[:, :width]
    grad_probs = grad_rows[:, width : width + experts]
    grad_logits = probs * (grad_probs - jnp.sum(probs * grad_probs, axis=-1, keepdims=True))
    router_float = router.astype(jnp.float32)
    grad_hidden_two = grad_hidden_two + lax.dot_general(
        grad_logits, router_float, (((1,), (1,)), ((), ())), precision=lax.Precision.HIGHEST
    )
    grad_router_part = lax.dot_general(
        grad_logits,
        hidden_two.astype(jnp.float32),
        (((0,), (0,)), ((), ())),
        precision=lax.Precision.HIGHEST,
    )
    inner_two = jnp.sum(grad_hidden_two * moe_gain * x_one, axis=-1, keepdims=True)
    grad_norm_two, grad_moe_gain_part = rms_grad(
        x_one, scale_two, moe_gain, grad_hidden_two, inner_two, width
    )
    grad_x_one = grad_out + grad_norm_two
    grad_attn_low = grad_x_one.astype(jnp.bfloat16)
    early_sums = jnp.concatenate(
        (grad_router_part, grad_moe_gain_part[None], jnp.zeros((7, width), jnp.float32)), axis=0
    )
    if direct:
        grad_attn_all, early_sums, grad_w_gate, grad_w_up, grad_w_down = back_gather(
            grad_attn_low, early_sums, x_slots, c_slots, pre, gated, 5
        )
    else:
        grad_attn_all = lax.all_gather(grad_attn_low, "tensor", axis=0, tiled=True)
        early_sums = lax.psum(early_sums, everyone)
        grad_w_gate, grad_w_up, grad_w_down = weight_grads(x_slots, c_slots, pre, gated)
    grad_q_norm, grad_k_norm, grad_value_all = attend_back(
        grad_attn_all,
        gathered_out,
        query_low,
        key_low,
        value_low,
        log_totals,
        cosine,
        sine,
        path_columns,
        path_lines,
    )
    query_inner, key_inner = tensor_sums(
        (
            jnp.sum(grad_q_norm * query_gain_dev * q_raw, axis=1),
            jnp.sum(grad_k_norm * key_gain_dev * k_raw, axis=1),
        )
    )
    grad_q_raw, grad_query_gain_dev = rms_grad(
        q_raw, query_scale, query_gain_dev, grad_q_norm, query_inner[:, None], full_width
    )
    grad_k_raw, grad_key_gain_dev = rms_grad(
        k_raw, key_scale, key_gain_dev, grad_k_norm, key_inner[:, None], full_width
    )
    grad_joined = jnp.concatenate(
        (grad_q_raw, grad_k_raw, grad_value_all), axis=1
    ).astype(jnp.bfloat16)
    zero_width = jnp.zeros((full_width,), jnp.float32)
    grad_query_full = lax.dynamic_update_slice_in_dim(
        zero_width, grad_query_gain_dev, tensor_rank * head_cols, 0
    )
    grad_key_full = lax.dynamic_update_slice_in_dim(
        zero_width, grad_key_gain_dev, tensor_rank * head_cols, 0
    )
    if direct:
        gains = jnp.concatenate(
            (grad_query_full[None], grad_key_full[None], jnp.zeros((6, width), jnp.float32)), axis=0
        )
        grad_input, grad_w_query, grad_w_key, grad_w_value, grad_w_out, gains = last_exchange(
            grad_joined,
            joined_weight,
            hidden_all,
            attn_mixed,
            grad_attn_all,
            residual,
            attn_gain,
            grad_x_one,
            gains,
            6,
        )
    else:
        grad_joined_weight = lax.dot_general(
            hidden_all, grad_joined, (((0,), (0,)), ((), ())), preferred_element_type=jnp.float32
        ).astype(jnp.bfloat16)
        grad_out_weight = lax.dot_general(
            attn_mixed, grad_attn_all, (((0,), (0,)), ((), ())), preferred_element_type=jnp.float32
        ).astype(jnp.bfloat16)

        def back_term(first_row, row_count):
            return lax.dot_general(
                grad_joined, joined_weight, (((1,), (1,)), ((), ())), preferred_element_type=jnp.float32
            )

        grad_hidden = heads_to_rows(back_term, tok_dev)
        inner_one = jnp.sum(grad_hidden * attn_gain * residual_float, axis=-1, keepdims=True)
        grad_norm_one, grad_attn_gain_part = rms_grad(
            residual_float, scale_one, attn_gain, grad_hidden, inner_one, width
        )
        grad_input = grad_x_one + grad_norm_one
        grad_w_query, grad_w_key, grad_w_value = (
            lax.psum_scatter(
                grad_joined_weight[:, n * head_cols : (n + 1) * head_cols],
                "dp",
                scatter_dimension=0,
                tiled=True,
            ).astype(jnp.float32)
            for n in range(3)
        )
        grad_w_out = lax.psum_scatter(
            grad_out_weight, "dp", scatter_dimension=1, tiled=True
        ).astype(jnp.float32)
        gains = lax.psum(jnp.stack((grad_query_full, grad_key_full, grad_attn_gain_part)), everyone)
    out_part, grad_input = lax.optimization_barrier((out_part, grad_input))
    block_out = (x_one + sum_over_tensor(out_part).astype(jnp.float32)).astype(jnp.bfloat16)
    return (
        block_out,
        grad_input,
        gains[2],
        grad_w_query,
        grad_w_key,
        grad_w_value,
        gains[0],
        gains[1],
        grad_w_out,
        early_sums[experts],
        early_sums[:experts].T,
        grad_w_gate,
        grad_w_up,
        grad_w_down,
    )


def solution(mesh):
    in_specs = (
        P(("dp", "tensor"), None),
        P(),
        P("dp", "tensor"),
        P("dp", "tensor"),
        P("dp", "tensor"),
        P(),
        P(),
        P("tensor", "dp"),
        P(),
        P(),
        P("dp", None, "tensor"),
        P("dp", None, "tensor"),
        P("dp", "tensor", None),
        P(None, "dp"),
        P("dp"),
        P(("dp", "tensor"), None),
        P(("dp", "tensor"), None),
        P(("dp", "tensor"), None),
    )
    out_specs = (
        P(("dp", "tensor"), None),
        P(("dp", "tensor"), None),
        P(),
        P("dp", "tensor"),
        P("dp", "tensor"),
        P("dp", "tensor"),
        P(),
        P(),
        P("tensor", "dp"),
        P(),
        P(),
        P("dp", None, "tensor"),
        P("dp", None, "tensor"),
        P("dp", "tensor", None),
    )
    return jax.shard_map(body, mesh=mesh, in_specs=in_specs, out_specs=out_specs, check_vma=False)
```

```python
import functools

import jax
import jax.numpy as jnp
from jax import lax
from jax.experimental import pallas as pl
from jax.experimental.pallas import tpu as pltpu
from jax.sharding import PartitionSpec as P

H = 16
HD = 128


norm_eps = 1e-05
rope_base = 10000.0
masked_score = -1e30


def padded(count, step):
    return -(-count // step) * step


def slot_table(routes, route_order, valid, experts, capacity):
    far = jnp.int32(1 << 30)
    expert = lax.iota(jnp.int32, experts)[:, None, None]
    hits = (routes[None] == expert) & (valid[None, :, None] == 1)
    order = jnp.min(jnp.where(hits, route_order[None], far), axis=-1)
    ranks = jnp.sum((order[:, None, :] < order[:, :, None]).astype(jnp.int32), axis=-1)
    return jnp.where((order < far) & (ranks < capacity), ranks, -1)


def slot_hits(slots, expert, rows):
    tokens = slots.shape[-1]
    return lax.broadcasted_iota(jnp.int32, (rows, tokens), 0) == slots[expert : expert + 1, :]


def dispatch_kernel(slots_ref, gates_ref, rows_ref, x_ref, gate_ref):
    pair, experts, tokens = slots_ref.shape
    rows = x_ref.shape[1] // pair
    width = rows_ref.shape[1]
    picks = []
    for b in range(pair):
        slots = slots_ref[b]
        pieces = []
        for e in range(experts):
            hit = slot_hits(slots, e, rows)
            pieces.append(hit.astype(jnp.float32))
            if gate_ref is not None:
                gate = jnp.sum(jnp.where(hit, gates_ref[b, e : e + 1, :], 0.0), axis=1, keepdims=True)
                gate_ref[e, b * rows : (b + 1) * rows, :] = jnp.broadcast_to(gate, (rows, 128))
        picks.append(jnp.concatenate(pieces, axis=0).astype(jnp.bfloat16))
    step = min(512, width)
    for first in range(0, width, step):
        parts = [
            jnp.dot(
                picks[b],
                rows_ref[b * tokens : (b + 1) * tokens, first : first + step],
                preferred_element_type=jnp.float32,
            )
            for b in range(pair)
        ]
        for e in range(experts):
            x_ref[e, :, first : first + step] = jnp.concatenate(
                [part[e * rows : (e + 1) * rows] for part in parts], axis=0
            ).astype(jnp.bfloat16)


def plain_dispatch_kernel(slots_ref, rows_ref, x_ref):
    dispatch_kernel(slots_ref, None, rows_ref, x_ref, None)


def dispatch(slots, gates, rows_all, rows):
    blocks, experts, tokens = slots.shape
    width = rows_all.shape[1]
    pair = 2
    out = jax.ShapeDtypeStruct((experts, blocks * rows, width), jnp.bfloat16)
    table = pl.BlockSpec((pair, experts, tokens), lambda i: (i, 0, 0))
    source = pl.BlockSpec((pair * tokens, width), lambda i: (i, 0))
    target = pl.BlockSpec((experts, pair * rows, width), lambda i: (0, i, 0))
    settings = dict(
        grid=(blocks // pair,),
        compiler_params=pltpu.CompilerParams(vmem_limit_bytes=50 << 20),
        cost_estimate=pl.CostEstimate(
            flops=2 * blocks * experts * rows * tokens * width,
            bytes_accessed=2 * blocks * (tokens + experts * rows) * width,
            transcendentals=0,
        ),
    )
    if gates is None:
        return pl.pallas_call(
            plain_dispatch_kernel, out_shape=out, in_specs=[table, source], out_specs=target, name="pick", **settings
        )(slots, rows_all)
    return pl.pallas_call(
        dispatch_kernel,
        out_shape=(out, jax.ShapeDtypeStruct((experts, blocks * rows, 128), jnp.float32)),
        in_specs=[table, table, source],
        out_specs=[target, pl.BlockSpec((experts, pair * rows, 128), lambda i: (0, i, 0))],
        name="dispatch",
        **settings,
    )(slots, gates, rows_all)


def turned(left, right):
    return lax.dot_general(left, right, (((0,), (0,)), ((), ())), preferred_element_type=jnp.float32)


def across(left, right):
    return lax.dot_general(left, right, (((1,), (1,)), ((), ())), preferred_element_type=jnp.float32)


def expert_kernel(rows, first_ref, x_ref, c_ref, gate_ref, wg_ref, wu_ref, wd_ref,
                  o_ref, dx_ref, pre_ref, gated_ref):
    expert = pl.program_id(0)
    tile, width = x_ref.shape[1:]
    units = wg_ref.shape[2]
    room = o_ref.shape[2]
    blocks = tile // rows
    gate = gate_ref[0, :, 0:1]
    x = x_ref[0]
    c = c_ref[0]
    gate_pre = jnp.dot(x, wg_ref[0], preferred_element_type=jnp.float32)
    up_pre = jnp.dot(x, wu_ref[0], preferred_element_type=jnp.float32)
    back = across(c, wd_ref[0])
    sig = jax.nn.sigmoid(gate_pre)
    silu = gate_pre * sig
    act = (silu * up_pre).astype(jnp.bfloat16)
    act_float = act.astype(jnp.float32)
    grad_gate = jnp.sum(act_float * back, axis=1, keepdims=True)
    grad_act = back * gate
    grad_gate_pre = (grad_act * up_pre * sig * (1.0 + gate_pre * (1.0 - sig))).astype(jnp.bfloat16)
    grad_up_pre = (grad_act * silu).astype(jnp.bfloat16)
    gated = (act_float * gate).astype(jnp.bfloat16)

    def spread(values):
        values = values.reshape(blocks, rows, values.shape[1])
        if room > rows:
            empty = jnp.zeros((blocks, room - rows, values.shape[2]), jnp.float32)
            values = jnp.concatenate((values, empty), axis=1)
        return values.astype(jnp.bfloat16)

    step = min(512, width)
    for first in range(0, width, step):
        part = slice(first, first + step)
        out = jnp.dot(act, wd_ref[0, :, part], preferred_element_type=jnp.float32) * gate
        o_ref[:, 0, :, part] = spread(out)
        grad = across(grad_gate_pre, wg_ref[0, part, :]) + across(grad_up_pre, wu_ref[0, part, :])
        dx_ref[:, 0, :, part] = spread(grad)
    lanes = lax.broadcasted_iota(jnp.int32, (tile, 128), 1)
    dx_ref[:, 0, :, width:] = spread(jnp.where(lanes == first_ref[0] + expert, grad_gate, 0.0))

    pre_ref[0, :, :units] = grad_gate_pre
    pre_ref[0, :, units:] = grad_up_pre
    gated_ref[0] = gated


def weight_terms(x_ref, c_ref, pre_ref, gated_ref, gate_ref, up_ref, down_ref):
    units = gated_ref.shape[1]
    width = x_ref.shape[1]
    step = min(512, width)
    for first in range(0, width, step):
        part = slice(first, first + step)
        both = turned(x_ref[:, part], pre_ref[...])
        gate_ref[part, :] = both[:, :units]
        up_ref[part, :] = both[:, units:]
        down_ref[:, part] = turned(gated_ref[...], c_ref[:, part])


def weight_kernel(x_ref, c_ref, pre_ref, gated_ref, gate_ref, up_ref, down_ref):
    weight_terms(*(r.at[0] for r in (x_ref, c_ref, pre_ref, gated_ref, gate_ref, up_ref, down_ref)))


def weight_grads(x_slots, c_slots, pre, gated):
    experts, total, width = x_slots.shape
    units = gated.shape[2]
    step = min(512, width)
    part = pl.BlockSpec((1, total, step), lambda e, j: (e, 0, j))
    tall = pl.BlockSpec((1, step, units), lambda e, j: (e, j, 0))
    return pl.pallas_call(
        weight_kernel,
        grid=(experts, width // step),
        out_shape=(
            jax.ShapeDtypeStruct((experts, width, units), jnp.float32),
            jax.ShapeDtypeStruct((experts, width, units), jnp.float32),
            jax.ShapeDtypeStruct((experts, units, width), jnp.float32),
        ),
        in_specs=[
            part, part,
            pl.BlockSpec((1, total, 2 * units), lambda e, j: (e, 0, 0)),
            pl.BlockSpec((1, total, units), lambda e, j: (e, 0, 0)),
        ],
        out_specs=[tall, tall, pl.BlockSpec((1, units, step), lambda e, j: (e, 0, j))],
        compiler_params=pltpu.CompilerParams(vmem_limit_bytes=50 << 20),
        cost_estimate=pl.CostEstimate(
            flops=6 * experts * total * width * units,
            bytes_accessed=4 * experts * total * width + 12 * experts * width * units,
            transcendentals=0,
        ),
        name="weight_grads",
    )(x_slots, c_slots, pre, gated)


def expert_pass(first_expert, x_slots, c_slots, gate_slots, w_gate, w_up, w_down, blocks, room):
    experts, total, width = x_slots.shape
    units = w_gate.shape[2]
    rows = total // blocks
    group = next(n for n in (16, 8, 4, 2, 1) if blocks % n == 0 and (n * rows <= 768 or n == 1))
    tile = group * rows
    extra = 128
    tall = pl.BlockSpec((1, width, units), lambda e, r, _: (e, 0, 0))
    wide = pl.BlockSpec((1, units, width), lambda e, r, _: (e, 0, 0))
    slot = pl.BlockSpec((1, tile, width), lambda e, r, _: (e, r, 0))
    kernel = functools.partial(expert_kernel, rows)
    return pl.pallas_call(
        kernel,
        grid_spec=pltpu.PrefetchScalarGridSpec(
            num_scalar_prefetch=1,
            grid=(experts, total // tile),
            in_specs=[slot, slot, pl.BlockSpec((1, tile, 128), lambda e, r, _: (e, r, 0)), tall, tall, wide],
            out_specs=[
                pl.BlockSpec((group, 1, room, width), lambda e, r, _: (r, e, 0, 0)),
                pl.BlockSpec((group, 1, room, width + extra), lambda e, r, _: (r, e, 0, 0)),
                pl.BlockSpec((1, tile, 2 * units), lambda e, r, _: (e, r, 0)),
                pl.BlockSpec((1, tile, units), lambda e, r, _: (e, r, 0)),
            ],
        ),
        out_shape=(
            jax.ShapeDtypeStruct((blocks, experts, room, width), jnp.bfloat16),
            jax.ShapeDtypeStruct((blocks, experts, room, width + extra), jnp.bfloat16),
            jax.ShapeDtypeStruct((experts, total, 2 * units), jnp.bfloat16),
            jax.ShapeDtypeStruct((experts, total, units), jnp.bfloat16),
        ),
        compiler_params=pltpu.CompilerParams(vmem_limit_bytes=60 << 20),
        cost_estimate=pl.CostEstimate(
            flops=12 * experts * total * width * units,
            bytes_accessed=8 * experts * total * width + 6 * experts * width * units,
            transcendentals=experts * total * units,
        ),
        name="experts",
    )(first_expert, x_slots, c_slots, gate_slots, w_gate, w_up, w_down)


def combine_kernel(slots_ref, o_ref, dx_ref, out_ref, grad_ref):
    _, experts, tokens = slots_ref.shape
    room, width = o_ref.shape[2:]
    slots = slots_ref[0]
    picks = jnp.concatenate(
        [slot_hits(slots, e, room).astype(jnp.float32) for e in range(experts)], axis=0
    ).astype(jnp.bfloat16)
    for source, target in ((o_ref, out_ref), (dx_ref, grad_ref)):
        columns = target.shape[1]
        for first in range(0, columns, 512):
            part = slice(first, min(first + 512, columns))
            values = source[0, :, :, part].reshape(experts * room, part.stop - first)
            target[:, part] = turned(picks, values).astype(jnp.bfloat16)


def combine(slots, outs, grads):
    blocks, experts, tokens = slots.shape
    room, width = outs.shape[2:]
    wider = grads.shape[3]
    return pl.pallas_call(
        combine_kernel,
        grid=(blocks,),
        out_shape=(
            jax.ShapeDtypeStruct((blocks * tokens, width), jnp.bfloat16),
            jax.ShapeDtypeStruct((blocks * tokens, wider), jnp.bfloat16),
        ),
        in_specs=[
            pl.BlockSpec((1, experts, tokens), lambda i: (i, 0, 0)),
            pl.BlockSpec((1, experts, room, width), lambda i: (i, 0, 0, 0)),
            pl.BlockSpec((1, experts, room, wider), lambda i: (i, 0, 0, 0)),
        ],
        out_specs=[
            pl.BlockSpec((tokens, width), lambda i: (i, 0)),
            pl.BlockSpec((tokens, wider), lambda i: (i, 0)),
        ],
        compiler_params=pltpu.CompilerParams(vmem_limit_bytes=50 << 20),
        cost_estimate=pl.CostEstimate(
            flops=2 * blocks * experts * room * tokens * (width + wider),
            bytes_accessed=2 * blocks * (tokens + experts * room) * (width + wider),
            transcendentals=0,
        ),
        name="combine",
    )(slots, outs, grads)


MESH = pl.DeviceIdType.MESH


def place():
    dp, z = lax.axis_index("dp"), lax.axis_index("tensor")
    return dp // 4, dp // 2 % 2, dp % 2, z


def peer(y, x, core, z):
    return (y * 4 + x * 2 + core, z)


def block_of(y, x, core, z):
    return (y * 4 + x * 2 + core) * 4 + z


def greet(line):
    y, x, core, z = place()
    barrier = pltpu.get_barrier_semaphore()
    for near in ((y, x, 1 - core, z), (y, 1 - x, core, z), (1 - y, x, core, z)):
        pl.semaphore_signal(barrier, inc=1, device_id=peer(*near), device_id_type=MESH)

    @pl.when(z > 0)
    def _():
        pl.semaphore_signal(barrier, inc=1, device_id=peer(y, x, core, z - 1), device_id_type=MESH)

    @pl.when(z < line - 1)
    def _():
        pl.semaphore_signal(barrier, inc=1, device_id=peer(y, x, core, z + 1), device_id_type=MESH)

    pl.semaphore_wait(barrier, 3 + (z + line - 1) // line + (2 * line - 2 - z) // line)


def either(first, second, take):
    return first * (1 - take) + second * take


def remote(source, target, send_sem, recv_sem, where):
    return pltpu.make_async_remote_copy(
        src_ref=source, dst_ref=target, send_sem=send_sem, recv_sem=recv_sem,
        device_id=peer(*where), device_id_type=MESH,
    )


def landed(target, sem):
    pltpu.make_async_copy(target, target, sem).wait()


def slot_order(y, x, core, z):
    return ((y * 2 + x) * 4 + z) * 2 + core


def near_first(z, i):
    side = z // 2
    low = either(z, 3 - z, side)
    first, second = (4 - i) // 4, (5 - i) // 4 - (4 - i) // 4
    return either(i + low * (first - second), 3 - i - low * (first - second), side)


def gather_dispatch_kernel(line, rows, slots_ref, hidden_ref, gates_ref, cots_ref,
                           rows_out, gates_out, x_out, c_out, gate_out,
                           in_c, in_x, in_gate, stage_c, stage_x, stage_gate,
                           local_sem, send_sem, recv_sem, load_sem, store_sem):
    y, x, core, z = place()
    tokens, width = hidden_ref.shape
    experts = slots_ref.shape[1]
    first_expert = (y * 4 + x * 2 + core) * experts
    owns, outs = (hidden_ref, gates_ref), (rows_out, gates_out)
    near_x, near_y, sibling = (y, 1 - x, core, z), (1 - y, x, core, z), (y, x, 1 - core, z)
    last = 24
    greet(line)

    def span(n, block):
        count = owns[n].shape[0]
        return outs[n].at[pl.ds(block * count, count)]

    def spot(m):
        q = m % 4
        i = m // 4 - (q + 1) // 2
        live = (i >= 0) & (i < line)
        held = i * live.astype(jnp.int32)
        yy, xx = (y + q // 2) % 2, (x + q % 2) % 2
        return q, held, live, yy, xx, near_first(z, held)

    def sends(m):
        q, i, live, yy, xx, zz = spot(m)
        block = block_of(yy, xx, core, zz)
        own = live & (q == 0)
        table = (
            (own & (zz <= z) & (z < line - 1), (y, x, core, z + 1)),
            (own & (zz >= z) & (z > 0), (y, x, core, z - 1)),
            (own | (live & (q == 2) & (zz % 2 == 1)), near_x),
            (own | (live & (q == 1) & (zz % 2 == 0)), near_y),
            (live, sibling),
        )
        for lane, (wanted, where) in enumerate(table):
            for n in range(2):
                part = span(n, block)
                yield wanted, remote(part, part, send_sem.at[n, lane, m], recv_sem.at[n, block], where)

    def load_c(chip):
        yy, xx, zz = chip // 8, chip // 4 % 2, chip % 4
        for c in range(2):
            b = block_of(yy, xx, c, zz)
            yield pltpu.make_async_copy(
                cots_ref.at[pl.ds(b * tokens, tokens)], in_c.at[pl.ds(c * tokens, tokens)], load_sem.at[0, c]
            )

    def load_x(yy, xx, zz):
        for c in range(2):
            b = block_of(yy, xx, c, zz)
            yield pltpu.make_async_copy(
                rows_out.at[pl.ds(b * tokens, tokens)], in_x.at[pl.ds(c * tokens, tokens)], load_sem.at[1, c]
            )
            yield pltpu.make_async_copy(
                gates_out.at[pl.ds(b * gates_ref.shape[0] + first_expert, experts)], in_gate.at[c], load_sem.at[2, c]
            )

    def store(stage, target, lane, chip):
        return pltpu.make_async_copy(stage, target.at[:, pl.ds(chip * 2 * rows, 2 * rows)], store_sem.at[lane])

    def pick(source, target, yy, xx, zz, gated):
        picks = []
        for c in range(2):
            slots = slots_ref[block_of(yy, xx, c, zz)]
            pieces = []
            for e in range(experts):
                hit = slot_hits(slots, e, rows)
                pieces.append(hit.astype(jnp.float32))
                if gated:
                    gate = jnp.sum(jnp.where(hit, in_gate[c, e : e + 1, :], 0.0), axis=1, keepdims=True)
                    stage_gate[e, c * rows : (c + 1) * rows, :] = jnp.broadcast_to(gate, (rows, 128))
            picks.append(jnp.concatenate(pieces, axis=0).astype(jnp.bfloat16))
        step = min(512, width)
        for first in range(0, width, step):
            parts = [
                jnp.dot(
                    picks[c], source[c * tokens : (c + 1) * tokens, first : first + step],
                    preferred_element_type=jnp.float32,
                )
                for c in range(2)
            ]
            for e in range(experts):
                target[e, :, first : first + step] = jnp.concatenate(
                    [part[e * rows : (e + 1) * rows] for part in parts], axis=0
                ).astype(jnp.bfloat16)

    mine = block_of(y, x, core, z)
    local = [pltpu.make_async_copy(owns[n], span(n, mine), local_sem.at[n]) for n in range(2)]
    for copy in local:
        copy.start()
    for copy in load_c(0):
        copy.start()
    for copy in local:
        copy.wait()
    chips = 4 * line
    lag = 2

    def work(m, carry):
        q, i, live, yy, xx, zz = spot(m)

        @pl.when((m < last) & live & (q + i > 0))
        def _():
            for n in range(2):
                landed(span(n, block_of(yy, xx, core, zz)), recv_sem.at[n, block_of(yy, xx, core, zz)])

        for wanted, copy in sends(m):
            pl.when((m < last) & wanted)(copy.start)

        back = m - lag
        q = (back + 8) % 4
        i = (back + 8) // 4 - 2 - (q + 1) // 2
        live = (i >= 0) & (i < line)
        held = i * live.astype(jnp.int32)
        yy, xx = (y + q // 2) % 2, (x + q % 2) % 2
        zz = near_first(z, held)
        chip = (yy * 2 + xx) * 4 + zz

        @pl.when(live)
        def _():
            block = block_of(yy, xx, 1 - core, zz)
            for n in range(2):
                landed(span(n, block), recv_sem.at[n, block])
            for copy in load_x(yy, xx, zz):
                copy.start()

        @pl.when(m < chips)
        def _():
            for copy in load_c(m):
                copy.wait()

            @pl.when(m > 0)
            def _():
                store(stage_c, c_out, 0, m - 1).wait()

            pick(in_c, stage_c, m // 8, m // 4 % 2, m % 4, False)
            store(stage_c, c_out, 0, m).start()

            @pl.when(m + 1 < chips)
            def _():
                for copy in load_c(m + 1):
                    copy.start()

        @pl.when(live)
        def _():
            @pl.when(q + held > 0)
            def _():
                store(stage_x, x_out, 1, chip).wait()
                store(stage_gate, gate_out, 2, chip).wait()

            for copy in load_x(yy, xx, zz):
                copy.wait()
            pick(in_x, stage_x, yy, xx, zz, True)
            store(stage_x, x_out, 1, chip).start()
            store(stage_gate, gate_out, 2, chip).start()

        return carry

    lax.fori_loop(0, last + lag, work, 0)
    store(stage_c, c_out, 0, chips - 1).wait()
    store(stage_x, x_out, 1, 0).wait()
    store(stage_gate, gate_out, 2, 0).wait()

    def finish(m, carry):
        for wanted, copy in sends(m):
            pl.when(wanted)(copy.wait_send)
        return carry

    lax.fori_loop(0, last, finish, 0)


def gather_dispatch(slots, hidden, gates, cots_all, rows, collective_id):
    line = 4
    blocks, experts, tokens = slots.shape
    width = hidden.shape[1]
    pair = 2 * rows
    low, wide = jnp.bfloat16, jnp.float32
    any_ref = pl.BlockSpec(memory_space=pl.ANY)
    vmem = pl.BlockSpec(memory_space=pltpu.VMEM)
    dma = pltpu.SemaphoreType.DMA
    slot_shape = jax.ShapeDtypeStruct((experts, blocks * rows, width), low)
    return pl.pallas_call(
        functools.partial(gather_dispatch_kernel, line, rows),
        out_shape=(
            jax.ShapeDtypeStruct((blocks * tokens, width), low),
            jax.ShapeDtypeStruct((blocks * gates.shape[0], tokens), wide),
            slot_shape,
            slot_shape,
            jax.ShapeDtypeStruct((experts, blocks * rows, 128), wide),
        ),
        in_specs=[vmem, any_ref, any_ref, any_ref],
        out_specs=[any_ref] * 5,
        scratch_shapes=[
            pltpu.VMEM((2 * tokens, width), low),
            pltpu.VMEM((2 * tokens, width), low),
            pltpu.VMEM((2, experts, tokens), wide),
            pltpu.VMEM((experts, pair, width), low),
            pltpu.VMEM((experts, pair, width), low),
            pltpu.VMEM((experts, pair, 128), wide),
            dma((2,)),
            dma((2, 5, 24)),
            dma((2, blocks)),
            dma((3, 2)),
            dma((3,)),
        ],
        compiler_params=pltpu.CompilerParams(
            collective_id=collective_id, has_side_effects=True, vmem_limit_bytes=40 << 20
        ),
        cost_estimate=pl.CostEstimate(
            flops=4 * blocks * experts * rows * tokens * width, bytes_accessed=200 << 20, transcendentals=0
        ),
        name="gather_dispatch",
    )(slots, hidden, gates, cots_all)[2:]


def reduce_kernel(line, slots_ref, grads_ref, outs_ref, sum_ref, part_ref,
                  grad_in, out_in, out_stage, stage, near, far_x, far_y, from_x, from_y, up, down,
                  in_sem, part_sem, stage_sem, near_sem, send_sem, far_sem, x_sem, y_sem, line_sem):
    y, x, core, z = place()
    tokens, width = sum_ref.shape
    half = tokens // 2
    experts, room = grads_ref.shape[1:3]
    rounds = line
    greet(line)

    def goal(r):
        early = 1 - r // 2
        return (line - 1) * (r % 2) * early + (r - 1) * (1 - early)

    def spot_at(q):
        r, p = q // 8, q % 8
        own = (1 - p % 2) * ((p + 7) // 8) + p // 7
        column = own * (p // 2 - 1 + p // 7) + (1 - own) * ((p + 1) // 2)
        dy, dx = (column + 1) % 2, 1 - column // 2
        target_core = core * own + (1 - core) * (1 - own)
        return (y + dy) % 2, (x + dx) % 2, target_core, goal(r)

    def load(q):
        b = slot_order(*spot_at(q))
        return (
            pltpu.make_async_copy(grads_ref.at[b], grad_in.at[q % 2], in_sem.at[0, q % 2]),
            pltpu.make_async_copy(outs_ref.at[b], out_in.at[q % 2], in_sem.at[1, q % 2]),
        )

    def to_part(q):
        b = block_of(*spot_at(q))
        return pltpu.make_async_copy(out_stage.at[q % 2], part_ref.at[pl.ds(b * tokens, tokens)], part_sem.at[q % 2])

    def to_sibling(r, j):
        return pltpu.make_async_remote_copy(
            src_ref=stage.at[j], dst_ref=near.at[r * 4 + j], send_sem=stage_sem.at[j], recv_sem=near_sem.at[r * 4 + j],
            device_id=peer(y, x, 1 - core, z), device_id_type=MESH,
        )

    near_x, near_y = peer(y, 1 - x, core, z), peer(1 - y, x, core, z)

    def rows(h):
        return pl.ds(h * half, half)

    def cross(kind, r):
        column, h, target, sem, index, lane = {
            "far_x": (0, 0, far_x.at[r], far_sem.at[0, r], near_x, 0),
            "far_y": (0, 1, far_y.at[r], far_sem.at[1, r], near_y, 1),
            "x0": (1, 0, from_x.at[r, rows(0)], x_sem.at[r, 0], near_x, 2),
            "x1": (1, 1, from_x.at[r, rows(1)], x_sem.at[r, 1], near_x, 3),
            "y0": (2, 0, from_y.at[r, rows(0)], y_sem.at[r, 0], near_y, 4),
            "y1": (2, 1, from_y.at[r, rows(1)], y_sem.at[r, 1], near_y, 5),
        }[kind]
        return pltpu.make_async_remote_copy(
            src_ref=near.at[r * 4 + column, rows(h)], dst_ref=target, send_sem=send_sem.at[lane, r], recv_sem=sem,
            device_id=index, device_id_type=MESH,
        )

    def along(sign, r):
        target = up if sign > 0 else down
        lane = 0 if sign > 0 else 1
        return pltpu.make_async_remote_copy(
            src_ref=near.at[r * 4 + 3], dst_ref=target.at[r], send_sem=send_sem.at[6 + lane, r], recv_sem=line_sem.at[lane, r],
            device_id=peer(y, x, core, z + sign), device_id_type=MESH,
        )

    def term(q, source, target_width, store):
        picks = jnp.concatenate(
            [slot_hits(slots_ref[block_of(*spot_at(q))], e, room).astype(jnp.float32) for e in range(experts)], axis=0
        ).astype(jnp.bfloat16)
        for first in range(0, target_width, 512):
            part = slice(first, min(first + 512, target_width))
            values = source[q % 2, :, :, part].reshape(experts * room, part.stop - first)
            store(part, turned(picks, values))

    for copy in load(0):
        copy.start()

    def one(r, p, j, own):
        q = r * 8 + p
        for copy in load(q):
            copy.wait()

        @pl.when(q + 1 < rounds * 8)
        def _():
            for copy in load(q + 1):
                copy.start()

        if own:
            near_slot = r * 4 + j
            to_sibling(r, j).wait_recv()

            def keep(part, value):
                near[near_slot, :, part] = (value + near[near_slot, :, part].astype(jnp.float32)).astype(jnp.bfloat16)

            term(q, grad_in, width, keep)
        else:

            @pl.when(r > 0)
            def _():
                to_sibling(r - 1, j).wait_send()

            def keep(part, value):
                stage[j, :, part] = value.astype(jnp.bfloat16)

            term(q, grad_in, width, keep)
            to_sibling(r, j).start()

        @pl.when(q >= 2)
        def _():
            to_part(q - 2).wait()

        def put(part, value):
            out_stage[q % 2, :, part] = value.astype(jnp.bfloat16)

        term(q, out_in, out_stage.shape[2], put)
        to_part(q).start()

    def add(target, h, *sources):
        for first in range(0, width, 512):
            part = slice(first, min(first + 512, width))
            total = near[target, h, part].astype(jnp.float32)
            for source in sources:
                total = total + source(part).astype(jnp.float32)
            near[target, h, part] = total.astype(jnp.bfloat16)

    def work(s, carry):
        @pl.when(s < rounds)
        def _():
            r = s
            one(r, 0, 0, 0)
            for j in range(4):
                if j < 3:
                    one(r, 2 * j + 1, j + 1, 0)
                one(r, min(2 * j + 2, 7), j, 1)
                for kind in (("far_x", "far_y"), ("x0",), ("y1",), ())[j]:
                    cross(kind, r).start()
            cross("far_y", r).wait_recv()
            add(r * 4 + 1, rows(1), lambda part: far_y[r, :, part])
            cross("x1", r).start()
            cross("far_x", r).wait_recv()
            add(r * 4 + 2, rows(0), lambda part: far_x[r, :, part])
            cross("y0", r).start()

        @pl.when((s >= 1) & (s < rounds + 1))
        def _():
            r = s - 1
            for kind in ("x0", "x1", "y0", "y1"):
                cross(kind, r).wait_recv()
            for h in range(2):
                add(
                    r * 4 + 3,
                    rows(h),
                    lambda part: from_x[r, rows(h), part],
                    lambda part: from_y[r, rows(h), part],
                )

        for hop in range(line - 1):
            r = s - 1 - hop
            live = (r >= 0) & (r < rounds)
            held = r * live.astype(jnp.int32)

            @pl.when(live & (goal(held) > z) & (z == hop))
            def _():
                if hop:
                    along(1, held).wait_recv()
                    for h in range(2):
                        add(held * 4 + 3, rows(h), lambda part: up[held, rows(h), part])
                along(1, held).start()

            @pl.when(live & (goal(held) < z) & (line - 1 - z == hop))
            def _():
                if hop:
                    along(-1, held).wait_recv()
                    for h in range(2):
                        add(held * 4 + 3, rows(h), lambda part: down[held, rows(h), part])
                along(-1, held).start()

        return carry

    lax.fori_loop(0, rounds + line - 1, work, 0)

    mine = (z + (z + 2) // 3) % 4 + z // 3
    sum_ref[...] = near[mine * 4 + 3].astype(jnp.float32)

    @pl.when(z > 0)
    def _():
        along(1, mine).wait_recv()
        sum_ref[...] += up[mine].astype(jnp.float32)

    @pl.when(z < line - 1)
    def _():
        along(-1, mine).wait_recv()
        sum_ref[...] += down[mine].astype(jnp.float32)

    def finish(r, carry):
        for kind in ("far_x", "far_y", "x0", "x1", "y0", "y1"):
            cross(kind, r).wait_send()

        @pl.when(goal(r) > z)
        def _():
            along(1, r).wait_send()

        @pl.when(goal(r) < z)
        def _():
            along(-1, r).wait_send()

        return carry

    lax.fori_loop(0, rounds, finish, 0)
    for j in range(4):
        to_sibling(rounds - 1, j).wait_send()
    for q in (rounds * 8 - 2, rounds * 8 - 1):
        to_part(q).wait()


def reduce_all(slots, outs, grads, collective_id):
    blocks, experts, tokens = slots.shape
    room, width = outs.shape[2:]
    wider = grads.shape[3]
    line = 4
    low = jnp.bfloat16
    any_ref = pl.BlockSpec(memory_space=pl.ANY)
    vmem = pl.BlockSpec(memory_space=pltpu.VMEM)
    dma = pltpu.SemaphoreType.DMA
    return pl.pallas_call(
        functools.partial(reduce_kernel, line),
        out_shape=(
            jax.ShapeDtypeStruct((tokens, wider), jnp.float32),
            jax.ShapeDtypeStruct((blocks * tokens, width), low),
        ),
        in_specs=[vmem, any_ref, any_ref],
        out_specs=[vmem, any_ref],
        scratch_shapes=[
            pltpu.VMEM((2, experts, room, wider), low),
            pltpu.VMEM((2, experts, room, width), low),
            pltpu.VMEM((2, tokens, width), low),
            pltpu.VMEM((4, tokens, wider), low),
            pltpu.VMEM((line * 4, tokens, wider), low),
            pltpu.VMEM((line, tokens // 2, wider), low),
            pltpu.VMEM((line, tokens // 2, wider), low),
            pltpu.VMEM((line, tokens, wider), low),
            pltpu.VMEM((line, tokens, wider), low),
            pltpu.VMEM((line, tokens, wider), low),
            pltpu.VMEM((line, tokens, wider), low),
            dma((2, 2)),
            dma((2,)),
            dma((4,)),
            dma((line * 4,)),
            dma((8, line)),
            dma((2, line)),
            dma((line, 2)),
            dma((line, 2)),
            dma((2, line)),
        ],
        compiler_params=pltpu.CompilerParams(
            collective_id=collective_id, has_side_effects=True, vmem_limit_bytes=62 << 20
        ),
        cost_estimate=pl.CostEstimate(
            flops=2 * blocks * experts * room * tokens * (width + wider),
            bytes_accessed=2 * blocks * experts * room * (width + wider),
            transcendentals=0,
        ),
        name="reduce_all",
    )(slots, grads, outs)


class LineGather:
    def __init__(self, own, out, send_sem, recv_sem, line):
        self.own, self.out, self.send_sem, self.recv_sem, self.line = own, out, send_sem, recv_sem, line
        self.spot = place()
        self.rows = own.shape[0]

    def view(self, block):
        return self.out.at[pl.ds(block * self.rows, self.rows)]

    def inside(self, block):
        return (block >= 0) & (block < self.line)

    def copy(self, sign, step):
        y, x, core, z = self.spot
        block = z - sign * step
        lane = (1 - sign) // 2
        source = self.own if step == 0 else self.view(block)
        return remote(
            source, self.view(block), self.send_sem.at[lane, step], self.recv_sem.at[lane, step], (y, x, core, z + sign)
        )

    def sends(self, sign, step):
        z = self.spot[3]
        return self.inside(z - sign * step) & self.inside(z + sign)

    def begin(self):
        for sign in (1, -1):
            pl.when(self.sends(sign, 0))(self.copy(sign, 0).start)

    def advance(self, step):
        z = self.spot[3]
        for sign in (1, -1):
            block = z - sign * (step + 1)
            lane = (1 - sign) // 2

            @pl.when(self.inside(block))
            def _():
                landed(self.view(block), self.recv_sem.at[lane, step])

            if step + 1 < self.line - 1:
                pl.when(self.sends(sign, step + 1))(self.copy(sign, step + 1).start)

    def finish(self):
        for sign in (1, -1):
            for step in range(self.line - 1):
                pl.when(self.sends(sign, step))(self.copy(sign, step).wait_send)


def start_kernel(line, hidden_ref, wq_ref, wk_ref, wv_ref, wo_ref, slots_ref, hidden_out, joined_out, wo_out, slots_out,
                 local_sem, line_send, line_recv, plane_send, plane_recv, slot_send, slot_recv, slot_line_send, slot_line_recv):
    y, x, core, z = place()
    owns = (wq_ref, wk_ref, wv_ref, wo_ref)
    near_x, near_y, sibling = (y, 1 - x, core, z), (1 - y, x, core, z), (y, x, 1 - core, z)

    def view(n, yy, xx, half=None):
        group = yy * 4 + xx * 2 + core
        rows, columns = owns[n].shape
        first, count = (0, rows) if half is None else (half * (rows // 2), rows // 2)
        if n < 3:
            return joined_out.at[pl.ds(group * rows + first, count), pl.ds(n * columns, columns)]
        return wo_out.at[pl.ds(first, count), pl.ds(pl.multiple_of(group * columns, columns), columns)]

    kinds = ("x", "y", "s", "fy", "fx", "sx", "sy", "sf")

    def copy(kind, n):
        source, target, where = {
            "x": (owns[n], view(n, y, x), near_x),
            "y": (owns[n], view(n, y, x), near_y),
            "s": (owns[n], view(n, y, x), sibling),
            "fy": (view(n, y, 1 - x, 0), view(n, y, 1 - x, 0), near_y),
            "fx": (view(n, 1 - y, x, 1), view(n, 1 - y, x, 1), near_x),
            "sx": (view(n, y, 1 - x), view(n, y, 1 - x), sibling),
            "sy": (view(n, 1 - y, x), view(n, 1 - y, x), sibling),
            "sf": (view(n, 1 - y, 1 - x), view(n, 1 - y, 1 - x), sibling),
        }[kind]
        lane = kinds.index(kind)
        return remote(source, target, plane_send.at[lane, n], plane_recv.at[lane, n], where)

    def other(n, yy, xx):
        group = yy * 4 + xx * 2 + 1 - core
        rows, columns = owns[n].shape
        if n < 3:
            return joined_out.at[pl.ds(group * rows, rows), pl.ds(n * columns, columns)]
        return wo_out.at[pl.ds(0, rows), pl.ds(pl.multiple_of(group * columns, columns), columns)]

    barrier = pltpu.get_barrier_semaphore()
    shifts = [(dy, dx, dc) for dy in range(2) for dx in range(2) for dc in range(2) if dy + dx + dc]
    plane = [((y + dy) % 2, (x + dx) % 2, (core + dc) % 2, z) for dy, dx, dc in shifts]
    for other_spot in plane:
        pl.semaphore_signal(barrier, inc=1, device_id=peer(*other_spot), device_id_type=MESH)
    for step in (-1, 1):

        @pl.when((z + step >= 0) & (z + step < line))
        def _():
            pl.semaphore_signal(barrier, inc=1, device_id=peer(y, x, core, z + step), device_id_type=MESH)

    pl.semaphore_wait(barrier, 7 + (z + line - 1) // line + (2 * line - 2 - z) // line)
    experts = slots_out.shape[1]
    group = peer(y, x, core, z)[0]
    slot_copies = []
    for n, other_spot in enumerate(plane):
        their_group = peer(*other_spot)[0]
        slot_copies.append(
            remote(
                slots_ref.at[pl.ds(their_group * experts, experts)], slots_out.at[z * 8 + group],
                slot_send.at[n], slot_recv.at[group], other_spot,
            )
        )
    own_slots = pltpu.make_async_copy(
        slots_ref.at[pl.ds(group * experts, experts)], slots_out.at[z * 8 + group], local_sem.at[5]
    )
    own_slots.start()
    slot_line = LineGather(slots_out.at[pl.ds(z * 8, 8)], slots_out, slot_line_send, slot_line_recv, line)
    hidden = LineGather(hidden_ref, hidden_out, line_send, line_recv, line)
    locals_ = [pltpu.make_async_copy(hidden_ref, hidden.view(z), local_sem.at[4])]
    locals_ += [pltpu.make_async_copy(owns[n], view(n, y, x), local_sem.at[n]) for n in range(4)]
    for slot_copy in slot_copies:
        slot_copy.start()
    hidden.begin()
    for n in range(4):
        for kind in ("x", "y", "s"):
            copy(kind, n).start()
    for local in locals_:
        local.start()
    for n in range(4):
        landed(view(n, y, 1 - x), plane_recv.at[0, n])
        copy("fy", n).start()
        copy("sx", n).start()
        landed(view(n, 1 - y, x), plane_recv.at[1, n])
        copy("fx", n).start()
        copy("sy", n).start()
    own_slots.wait()
    for other_spot in plane:
        their_group = peer(*other_spot)[0]
        landed(slots_out.at[z * 8 + their_group], slot_recv.at[their_group])
    slot_line.begin()
    hidden.advance(0)
    slot_line.advance(0)
    for n in range(4):
        landed(view(n, 1 - y, 1 - x, 0), plane_recv.at[3, n])
        landed(view(n, 1 - y, 1 - x, 1), plane_recv.at[4, n])
        copy("sf", n).start()
    for step in range(1, line - 1):
        slot_line.advance(step)
        hidden.advance(step)
    for n in range(4):
        landed(other(n, y, x), plane_recv.at[2, n])
        landed(other(n, y, 1 - x), plane_recv.at[5, n])
        landed(other(n, 1 - y, x), plane_recv.at[6, n])
        landed(other(n, 1 - y, 1 - x), plane_recv.at[7, n])
    hidden.finish()
    slot_line.finish()
    for slot_copy in slot_copies:
        slot_copy.wait_send()
    for n in range(4):
        for kind in kinds:
            copy(kind, n).wait_send()
    for local in locals_:
        local.wait()


def start_exchange(hidden, w_query, w_key, w_value, w_out, slots, collective_id):
    line = 4
    any_ref = pl.BlockSpec(memory_space=pl.ANY)
    dma = pltpu.SemaphoreType.DMA
    rows, width = hidden.shape
    part, columns = w_query.shape
    low = jnp.bfloat16
    return pl.pallas_call(
        functools.partial(start_kernel, line),
        out_shape=(
            jax.ShapeDtypeStruct((line * rows, width), low),
            jax.ShapeDtypeStruct((8 * part, 3 * columns), low),
            jax.ShapeDtypeStruct((w_out.shape[0], 8 * w_out.shape[1]), low),
            jax.ShapeDtypeStruct((line * 8, slots.shape[0] // 8, slots.shape[1]), slots.dtype),
        ),
        in_specs=[any_ref] * 6,
        out_specs=[any_ref] * 4,
        scratch_shapes=[
            dma((6,)), dma((2, line)), dma((2, line)), dma((8, 4)), dma((8, 4)),
            dma((7,)), dma((8,)), dma((2, line)), dma((2, line)),
        ],
        compiler_params=pltpu.CompilerParams(collective_id=collective_id, has_side_effects=True),
        cost_estimate=pl.CostEstimate(flops=0, bytes_accessed=150 << 20, transcendentals=0),
        name="start_exchange",
    )(hidden, w_query, w_key, w_value, w_out, slots)


class LineReduce:
    def __init__(self, part, up, down, send_sem, recv_sem, line):
        self.part, self.up, self.down = part, up, down
        self.send_sem, self.recv_sem, self.line = send_sem, recv_sem, line
        self.spot = place()

    def copy(self, sign, goal):
        y, x, core, z = self.spot
        lane = (1 - sign) // 2
        target = self.up if sign > 0 else self.down
        return remote(
            self.part.at[goal], target.at[goal], self.send_sem.at[lane, goal], self.recv_sem.at[lane, goal],
            (y, x, core, z + sign),
        )

    def order(self, i):
        z = self.spot[3]
        return either(self.line - 1 - i, i, z * 2 // self.line)

    def lead(self, goal):
        z = self.spot[3]
        pl.when((z == 0) & (goal > 0))(self.copy(1, goal).start)
        pl.when((z == self.line - 1) & (goal < z))(self.copy(-1, goal).start)

    def advance(self, unit, total_ref):
        z, line = self.spot[3], self.line
        for sign in (1, -1):
            goal = line - 1 - unit + z if sign > 0 else unit - line + 1 + z
            live = ((z > 0) & (goal < line)) if sign > 0 else ((z < line - 1) & (goal >= 0))
            inbox = self.up if sign > 0 else self.down

            @pl.when(live)
            def _():
                self.copy(sign, goal).wait_recv()
                if unit < line - 1:
                    self.part[goal] = (
                        self.part[goal].astype(jnp.float32) + inbox[goal].astype(jnp.float32)
                    ).astype(jnp.bfloat16)
                    self.copy(sign, goal).start()
                else:
                    total_ref[...] += inbox[goal].astype(jnp.float32)

    def finish(self):
        z = self.spot[3]

        def step(goal, carry):
            pl.when(goal > z)(self.copy(1, goal).wait_send)
            pl.when(goal < z)(self.copy(-1, goal).wait_send)
            return carry

        lax.fori_loop(0, self.line, step, 0)


def mixed_out_kernel(line, mixed_ref, w_ref, residual_ref, gain_ref, router_ref,
                     x_ref, hidden_ref, probs_ref, part, up, down, send_sem, recv_sem):
    rows, width = x_ref.shape
    greet(line)
    reduce = LineReduce(part, up, down, send_sem, recv_sem, line)
    z = reduce.spot[3]

    def term(i, carry):
        goal = reduce.order(i)
        first = pl.multiple_of(goal * rows, rows)
        for column in range(0, width, 512):
            piece = slice(column, column + 512)
            value = jnp.dot(mixed_ref[pl.ds(first, rows), :], w_ref[:, piece], preferred_element_type=jnp.float32)

            @pl.when(goal == z)
            def _():
                x_ref[:, piece] = value

            part[goal, :, piece] = value.astype(jnp.bfloat16)
        reduce.lead(goal)
        return carry

    lax.fori_loop(0, line, term, 0)
    for unit in range(1, line):
        reduce.advance(unit, x_ref)
    x_one = x_ref[...] + residual_ref[...].astype(jnp.float32)
    x_ref[...] = x_one
    scale = lax.rsqrt(jnp.mean(x_one * x_one, axis=-1, keepdims=True) + norm_eps)
    hidden = (x_one * scale * gain_ref[...]).astype(jnp.bfloat16)
    hidden_ref[...] = hidden
    logits = lax.dot_general(
        router_ref[...], hidden, (((1,), (1,)), ((), ())), preferred_element_type=jnp.float32
    )
    shifted = jnp.exp(logits - jnp.max(logits, axis=0, keepdims=True))
    probs_ref[...] = shifted / jnp.sum(shifted, axis=0, keepdims=True)
    reduce.finish()


def mixed_out(mixed, w_out, residual, gain, router_turned, collective_id):
    line = 4
    rows, width = residual.shape
    experts = router_turned.shape[0]
    vmem = pl.BlockSpec(memory_space=pltpu.VMEM)
    dma = pltpu.SemaphoreType.DMA
    block = pltpu.VMEM((line, rows, width), jnp.bfloat16)
    return pl.pallas_call(
        functools.partial(mixed_out_kernel, line),
        out_shape=(
            jax.ShapeDtypeStruct((rows, width), jnp.float32),
            jax.ShapeDtypeStruct((rows, width), jnp.bfloat16),
            jax.ShapeDtypeStruct((experts, rows), jnp.float32),
        ),
        in_specs=[vmem] * 5,
        out_specs=[vmem] * 3,
        scratch_shapes=[block, block, block, dma((2, line)), dma((2, line))],
        compiler_params=pltpu.CompilerParams(
            collective_id=collective_id, has_side_effects=True, vmem_limit_bytes=56 << 20
        ),
        cost_estimate=pl.CostEstimate(flops=0, bytes_accessed=150 << 20, transcendentals=0),
        name="mixed_out",
    )(mixed, w_out, residual, gain.reshape(1, width), router_turned)


class Butterfly:
    def __init__(self, data, total, from_core, from_x, from_y, from_z, sums, send_sem, recv_sem):
        self.data, self.total, self.sums = data, total, sums
        self.boxes = {"core": from_core, "x": from_x, "y": from_y}
        self.from_z, self.send_sem, self.recv_sem = from_z, send_sem, recv_sem
        y, x, core, z = self.spot = place()
        self.width = data.shape[1]
        self.near = {"core": (y, x, 1 - core, z), "x": (y, 1 - x, core, z), "y": (1 - y, x, core, z)}
        half, quarter, eighth = self.width // 2, self.width // 4, self.width // 8
        first = core * half
        self.kept = {"core": (first, half), "x": (first + x * quarter, quarter)}
        self.kept["y"] = (first + x * quarter + y * eighth, eighth)
        self.away = {
            "core": ((1 - core) * half, half),
            "x": (first + (1 - x) * quarter, quarter),
            "y": (first + x * quarter + (1 - y) * eighth, eighth),
        }

    def part(self, span):
        return pl.ds(pl.multiple_of(span[0], span[1]), span[1])

    def fold_copy(self, axis):
        lane = ("core", "x", "y").index(axis)
        return remote(
            self.data.at[:, self.part(self.away[axis])], self.boxes[axis], self.send_sem.at[lane],
            self.recv_sem.at[lane], self.near[axis],
        )

    def fold(self, axis):
        copy = self.fold_copy(axis)
        copy.start()
        copy.wait()
        self.data[:, self.part(self.kept[axis])] += self.boxes[axis][...]

    def line_step(self, step):
        y, x, core, z = self.spot
        other = (z + 1 - 2 * (z % 2)) if step == 0 else (z + 2) % 4
        piece = self.part(self.kept["y"])
        source = self.data.at[:, piece] if step == 0 else self.sums
        copy = remote(
            source, self.from_z.at[step], self.send_sem.at[3 + step], self.recv_sem.at[3 + step], (y, x, core, other)
        )
        copy.start()
        copy.wait()
        if step == 0:
            self.sums[...] = self.data[:, piece] + self.from_z[0]
        else:
            self.total[:, piece] = self.sums[...] + self.from_z[1]

    def unfold(self, axis):
        lane = 5 + ("core", "x", "y").index(axis)
        mine = self.total.at[:, self.part(self.kept[axis])]
        copy = remote(mine, mine, self.send_sem.at[lane], self.recv_sem.at[lane], self.near[axis])
        copy.start()
        copy.wait_send()
        landed(self.total.at[:, self.part(self.away[axis])], self.recv_sem.at[lane])

    def scratch(rows, width):
        low = jnp.float32
        return [
            pltpu.VMEM((rows, width // 2), low),
            pltpu.VMEM((rows, width // 4), low),
            pltpu.VMEM((rows, width // 8), low),
            pltpu.VMEM((2, rows, width // 8), low),
            pltpu.VMEM((rows, width // 8), low),
            pltpu.SemaphoreType.DMA((8,)),
            pltpu.SemaphoreType.DMA((8,)),
        ]


def greet_far(line):
    y, x, core, z = place()
    barrier = pltpu.get_barrier_semaphore()
    for near in ((y, x, 1 - core, z), (y, 1 - x, core, z), (1 - y, x, core, z)):
        pl.semaphore_signal(barrier, inc=1, device_id=peer(*near), device_id_type=MESH)
    for step in range(1, line):
        pl.semaphore_signal(barrier, inc=1, device_id=peer(y, x, core, (z + step) % line), device_id_type=MESH)
    pl.semaphore_wait(barrier, 3 + line - 1)


def back_gather_kernel(line, own_ref, sums_ref, out_ref, total_ref, data, local_sem, send_sem, recv_sem, *fly):
    greet_far(line)
    gather = LineGather(own_ref, out_ref, send_sem, recv_sem, line)
    local = pltpu.make_async_copy(own_ref, gather.view(gather.spot[3]), local_sem)
    gather.begin()
    local.start()
    data[...] = sums_ref[...]
    butterfly = Butterfly(data, total_ref, *fly)
    for axis in ("core", "x", "y"):
        butterfly.fold(axis)
    gather.advance(0)
    butterfly.line_step(0)
    gather.advance(1)
    butterfly.line_step(1)
    for axis in ("y", "x", "core"):
        butterfly.unfold(axis)
    gather.advance(2)
    gather.finish()
    local.wait()


def back_gather(own, sums, collective_id):
    line = 4
    any_ref = pl.BlockSpec(memory_space=pl.ANY)
    vmem = pl.BlockSpec(memory_space=pltpu.VMEM)
    dma = pltpu.SemaphoreType.DMA
    return pl.pallas_call(
        functools.partial(back_gather_kernel, line),
        out_shape=(
            jax.ShapeDtypeStruct((line * own.shape[0], own.shape[1]), own.dtype),
            jax.ShapeDtypeStruct(sums.shape, jnp.float32),
        ),
        in_specs=[any_ref, vmem],
        out_specs=[any_ref, vmem],
        scratch_shapes=[
            pltpu.VMEM(sums.shape, jnp.float32), dma(()), dma((2, line)), dma((2, line)),
            *Butterfly.scratch(*sums.shape),
        ],
        compiler_params=pltpu.CompilerParams(collective_id=collective_id, has_side_effects=True),
        cost_estimate=pl.CostEstimate(flops=0, bytes_accessed=150 << 20, transcendentals=0),
        name="back_gather",
    )(own, sums)


def last_kernel(line, joined_ref, weight_ref, hidden_ref, mixed_ref, attn_ref, residual_ref, gain_ref, x_grad_ref, gains_ref,
                input_ref, wq_ref, wk_ref, wv_ref, wo_ref, total_ref,
                part, up, down, stage, near, far_x, far_y, from_x, from_y, data,
                line_send, line_recv, stage_sem, near_sem, send_sem, recv_sem, *fly):
    y, x, core, z = place()
    rows, width = input_ref.shape
    columns = joined_ref.shape[1]
    half = rows // 2
    low = jnp.bfloat16
    greet_far(line)
    reduce = LineReduce(part, up, down, line_send, line_recv, line)

    def term(i, carry):
        goal = reduce.order(i)
        first = pl.multiple_of(goal * rows, rows)
        for column in range(0, width, 512):
            piece = slice(column, column + 512)
            value = across(joined_ref[pl.ds(first, rows), :], weight_ref[piece, :])

            @pl.when(goal == z)
            def _():
                input_ref[:, piece] = value

            part[goal, :, piece] = value.astype(low)
        reduce.lead(goal)
        return carry

    lax.fori_loop(0, line, term, 0)
    near_x, near_y, sibling = (y, 1 - x, core, z), (1 - y, x, core, z), (y, x, 1 - core, z)

    def terms(j, own, store):
        dy, dx = (j + 1) % 2, 1 - j // 2
        group = (y + dy) % 2 * 4 + (x + dx) % 2 * 2 + (core if own else 1 - core)
        span = pl.ds(pl.multiple_of(group * rows, rows), rows)
        turned_rows = hidden_ref[:, span]
        for column in range(0, columns, 512):
            piece = slice(column, column + 512)
            store(piece, turned(turned_rows, joined_ref[:, piece]))
        value = turned(mixed_ref[...], attn_ref[:, span])
        store(slice(columns, columns + rows), value[:rows])
        store(slice(columns + rows, columns + 2 * rows), value[rows:])

    def to_sibling(j):
        return remote(stage.at[j], near.at[j], stage_sem.at[j], near_sem.at[j], sibling)

    def away(j, carry):
        def store(piece, value):
            stage[j, :, piece] = value.astype(low)

        terms(j, False, store)
        to_sibling(j).start()
        return carry

    def own(j, carry):
        to_sibling(j).wait_recv()

        def store(piece, value):
            near[j, :, piece] = (value + near[j, :, piece].astype(jnp.float32)).astype(low)

        terms(j, True, store)
        return carry

    lax.fori_loop(0, 4, away, 0)
    lax.fori_loop(0, 4, own, 0)

    def line_rows(h):
        return pl.ds(h * half, half)

    def cross(kind):
        column, h, target, where = {
            "far_x": (0, 0, far_x, near_x),
            "far_y": (0, 1, far_y, near_y),
            "x0": (1, 0, from_x.at[line_rows(0)], near_x),
            "x1": (1, 1, from_x.at[line_rows(1)], near_x),
            "y0": (2, 0, from_y.at[line_rows(0)], near_y),
            "y1": (2, 1, from_y.at[line_rows(1)], near_y),
        }[kind]
        lane = kinds.index(kind)
        return remote(near.at[column, line_rows(h)], target, send_sem.at[lane], recv_sem.at[lane], where)

    kinds = ("far_x", "far_y", "x0", "y1", "x1", "y0")
    for kind in kinds[:4]:
        cross(kind).start()

    def add(column, h, source):
        near[column, line_rows(h), :] = (
            near[column, line_rows(h), :].astype(jnp.float32) + source[...].astype(jnp.float32)
        ).astype(low)

    reduce.advance(1, input_ref)
    cross("far_y").wait_recv()
    add(1, 1, far_y)
    cross("x1").start()
    cross("far_x").wait_recv()
    add(2, 0, far_x)
    cross("y0").start()
    reduce.advance(2, input_ref)
    for kind in kinds[2:]:
        cross(kind).wait_recv()
    for n, ref in enumerate((wq_ref, wk_ref, wv_ref, wo_ref, wo_ref)):
        count = columns // 3 if n < 3 else rows
        first = n * (columns // 3) if n < 3 else columns + (n - 3) * rows
        piece = slice(first, first + count)
        total = sum(r[:, piece].astype(jnp.float32) for r in (near.at[3], from_x, from_y))
        if n < 3:
            ref[...] = total
        else:
            ref[(n - 3) * rows : (n - 2) * rows, :] = total
    reduce.advance(3, input_ref)
    grad = input_ref[...]
    values = residual_ref[...].astype(jnp.float32)
    scale = lax.rsqrt(jnp.mean(values * values, axis=-1, keepdims=True) + norm_eps)
    gained = grad * gain_ref[...]
    inner = jnp.sum(gained * values, axis=-1, keepdims=True)
    data[...] = gains_ref[...]
    data[2:3, :] = jnp.sum(grad * values * scale, axis=0, keepdims=True)
    input_ref[...] = x_grad_ref[...] + scale * gained - values * (scale * scale * scale * inner / width)
    butterfly = Butterfly(data, total_ref, *fly)
    for axis in ("core", "x", "y"):
        butterfly.fold(axis)
    butterfly.line_step(0)
    butterfly.line_step(1)
    for axis in ("y", "x", "core"):
        butterfly.unfold(axis)
    reduce.finish()
    for j in range(4):
        to_sibling(j).wait_send()
    for kind in kinds:
        cross(kind).wait_send()


def last_exchange(joined, weight, hidden, mixed, attn, residual, gain, x_grad, gains, collective_id):
    line = 4
    rows, width = residual.shape
    columns = joined.shape[1] // 3
    low, wide = jnp.bfloat16, jnp.float32
    vmem = pl.BlockSpec(memory_space=pltpu.VMEM)
    dma = pltpu.SemaphoreType.DMA
    block = pltpu.VMEM((line, rows, width), low)
    one = pltpu.VMEM((rows, width), low)
    part = pltpu.VMEM((rows // 2, width), low)
    square = jax.ShapeDtypeStruct((rows, columns), wide)
    return pl.pallas_call(
        functools.partial(last_kernel, line),
        out_shape=(
            jax.ShapeDtypeStruct((rows, width), wide), square, square, square,
            jax.ShapeDtypeStruct((2 * rows, rows), wide),
            jax.ShapeDtypeStruct(gains.shape, wide),
        ),
        in_specs=[vmem] * 9,
        out_specs=[vmem] * 6,
        scratch_shapes=[
            block, block, block, pltpu.VMEM((4, rows, width), low), pltpu.VMEM((4, rows, width), low),
            part, part, one, one, pltpu.VMEM(gains.shape, wide),
            dma((2, line)), dma((2, line)), dma((4,)), dma((4,)), dma((6,)), dma((6,)),
            *Butterfly.scratch(*gains.shape),
        ],
        compiler_params=pltpu.CompilerParams(
            collective_id=collective_id, has_side_effects=True, vmem_limit_bytes=62 << 20
        ),
        cost_estimate=pl.CostEstimate(flops=0, bytes_accessed=250 << 20, transcendentals=0),
        name="last_exchange",
    )(joined, weight, hidden, mixed, attn, residual, gain.reshape(1, width), x_grad, gains)


def visible_block(row_paths, key_paths, key_valid, row_first):
    row_count = row_paths.shape[1]
    key_count = key_paths.shape[1]
    key_segment = key_paths[0][None, :]
    on_path = (
        (key_segment == row_paths[0][:, None])
        | (key_segment == row_paths[1][:, None])
        | (key_segment == row_paths[2][:, None])
    )
    row_place = row_first + lax.iota(jnp.int32, row_count)
    key_place = lax.iota(jnp.int32, key_count)
    earlier = key_place[None, :] <= row_place[:, None]
    return on_path & earlier & (key_valid[None, :] == 1) | (
        key_place[None, :] == row_place[:, None]
    )


def rotation(positions, head_dim):
    half = head_dim // 2
    freqs = jnp.exp(-jnp.log(rope_base) * 2.0 * lax.iota(jnp.float32, half) / head_dim)
    angles = positions.astype(jnp.float32)[:, None] * freqs[None, :]
    return (jnp.cos(angles), jnp.sin(angles))


def visible_bias(row_first, row_paths, row_places, key_segment, key_valid, key_places):
    on_path = (key_segment == row_paths[0]) | (key_segment == row_paths[1]) | (key_segment == row_paths[2])
    seen = (on_path & (key_places <= row_places) & (key_valid == 1)) | (key_places == row_places)
    return jnp.where(seen, 0.0, masked_score)


def attend_kernel(step, raw_ref, scale_ref, gain_ref, cos_ref, sin_ref, column_ref, line_ref,
                  query_ref, key_ref, value_ref, mixed_ref, log_ref, bias, logs):
    seq, columns = query_ref.shape
    heads = columns // HD

    def prepare(i, carry):
        rows = pl.ds(pl.multiple_of(i * step, step), step)
        cosine, sine = cos_ref[rows, :], sin_ref[rows, :]
        for n, ref in enumerate((query_ref, key_ref)):
            scale = scale_ref[rows, n : n + 1]
            for h in range(heads):
                span = slice(h * HD, (h + 1) * HD)
                values = raw_ref[rows, n * columns + h * HD : n * columns + (h + 1) * HD]
                values = values * scale * gain_ref[n : n + 1, span]
                turn = pltpu.roll(values, HD // 2, 1)
                ref[rows, span] = (values * cosine + turn * sine).astype(jnp.bfloat16)
        value_ref[rows, :] = raw_ref[rows, 2 * columns :].astype(jnp.bfloat16)
        return carry

    lax.fori_loop(0, seq // step, prepare, 0)
    for i in range(seq // step):
        rows = slice(i * step, (i + 1) * step)
        wide = (i + 1) * step
        places = lax.broadcasted_iota(jnp.int32, (step, wide), 0) + i * step
        bias[:, :wide] = visible_bias(
            i * step,
            [column_ref[rows, n : n + 1] for n in range(3)],
            places,
            line_ref[0:1, :wide],
            line_ref[3:4, :wide],
            lax.broadcasted_iota(jnp.int32, (step, wide), 1),
        )

        def head(h, carry):
            span = pl.ds(pl.multiple_of(h * HD, HD), HD)
            scores = across(query_ref[rows, span], key_ref[:wide, span]) * HD ** (-0.5) + bias[:, :wide]
            top = jnp.max(scores, axis=1, keepdims=True)
            weights = jnp.exp(scores - top)
            total = jnp.sum(weights, axis=1, keepdims=True)
            low = (weights / total).astype(jnp.bfloat16)
            mixed = jnp.dot(low, value_ref[:wide, span], preferred_element_type=jnp.float32)
            mixed_ref[rows, span] = mixed.astype(jnp.bfloat16)
            lanes = lax.broadcasted_iota(jnp.int32, (step, 128), 1)
            logs[...] = jnp.where(lanes == h, top + jnp.log(total), logs[...])
            return carry

        logs[...] = jnp.zeros_like(logs)
        lax.fori_loop(0, heads, head, 0)
        log_ref[:, rows] = jnp.transpose(logs[...])[: log_ref.shape[0]]


def attend(raw, scales, gains, cosine, sine, path_columns, path_lines):
    seq = raw.shape[0]
    columns = raw.shape[1] // 3
    step = min(256, seq)
    vmem = pl.BlockSpec(memory_space=pltpu.VMEM)
    low = jax.ShapeDtypeStruct((seq, columns), jnp.bfloat16)
    return pl.pallas_call(
        functools.partial(attend_kernel, step),
        out_shape=(low, low, low, low, jax.ShapeDtypeStruct((8, seq), jnp.float32)),
        in_specs=[vmem] * 7,
        out_specs=[vmem] * 5,
        scratch_shapes=[pltpu.VMEM((step, seq), jnp.float32), pltpu.VMEM((step, 128), jnp.float32)],
        compiler_params=pltpu.CompilerParams(vmem_limit_bytes=50 << 20),
        cost_estimate=pl.CostEstimate(
            flops=4 * seq * seq * columns, bytes_accessed=16 * seq * columns, transcendentals=seq * seq
        ),
        name="attend",
    )(raw, scales, gains, cosine, sine, path_columns, path_lines)


def attend_back_kernel(step, grad_ref, w_ref, query_ref, key_ref, value_ref, log_ref, cos_ref, sin_ref,
                       column_ref, line_ref, dq_ref, dk_ref, dv_ref, bias, mixed):
    seq, columns = query_ref.shape
    heads = columns // HD
    dk_ref[...] = jnp.zeros_like(dk_ref)
    dv_ref[...] = jnp.zeros_like(dv_ref)

    def unturn(values, rows):
        return values * cos_ref[rows, :] - pltpu.roll(values, HD // 2, 1) * sin_ref[rows, :]

    for i in range(seq // step):
        rows = slice(i * step, (i + 1) * step)
        wide = (i + 1) * step
        mixed[...] = across(grad_ref[rows, :], w_ref[...]).astype(jnp.bfloat16)
        places = lax.broadcasted_iota(jnp.int32, (wide, step), 1) + i * step
        bias[:wide, :] = visible_bias(
            i * step,
            [line_ref[n : n + 1, rows] for n in range(3)],
            places,
            column_ref[:wide, 0:1],
            column_ref[:wide, 3:4],
            lax.broadcasted_iota(jnp.int32, (wide, step), 0),
        )

        def head(h, carry):
            span = pl.ds(pl.multiple_of(h * HD, HD), HD)
            query, key, grad = query_ref[rows, span], key_ref[:wide, span], mixed[:, span]
            scores = across(key, query) * HD ** (-0.5) + bias[:wide, :]
            weights = jnp.exp(scores - log_ref[pl.ds(h, 1), rows])
            grad_weights = across(value_ref[:wide, span], grad)
            inner = jnp.sum(weights * grad_weights, axis=0, keepdims=True)
            grad_scores = (weights * (grad_weights - inner)).astype(jnp.bfloat16)
            dq_ref[rows, span] = unturn(turned(grad_scores, key) * HD ** (-0.5), rows)
            dk_ref[:wide, span] += jnp.dot(grad_scores, query, preferred_element_type=jnp.float32)
            dv_ref[:wide, span] += jnp.dot(
                weights.astype(jnp.bfloat16), grad, preferred_element_type=jnp.float32
            )
            return carry

        lax.fori_loop(0, heads, head, 0)
    for i in range(seq // step):
        rows = slice(i * step, (i + 1) * step)
        for h in range(heads):
            span = slice(h * HD, (h + 1) * HD)
            dk_ref[rows, span] = unturn(dk_ref[rows, span] * HD ** (-0.5), rows)


def attend_back(grads, w_out, query, key, value, logs, cosine, sine, path_columns, path_lines):
    seq, columns = query.shape
    step = min(256, seq)
    vmem = pl.BlockSpec(memory_space=pltpu.VMEM)
    wide = jax.ShapeDtypeStruct((seq, columns), jnp.float32)
    return pl.pallas_call(
        functools.partial(attend_back_kernel, step),
        out_shape=(wide, wide, wide),
        in_specs=[vmem] * 10,
        out_specs=[vmem] * 3,
        scratch_shapes=[pltpu.VMEM((seq, step), jnp.float32), pltpu.VMEM((step, columns), jnp.bfloat16)],
        compiler_params=pltpu.CompilerParams(vmem_limit_bytes=56 << 20),
        cost_estimate=pl.CostEstimate(
            flops=10 * seq * seq * columns, bytes_accessed=24 * seq * columns, transcendentals=seq * seq
        ),
        name="attend_back",
    )(grads, w_out, query, key, value, logs, cosine, sine, path_columns, path_lines)


def rms_apply(values, gain):
    scale = lax.rsqrt(jnp.mean(values * values, axis=-1, keepdims=True) + norm_eps)
    return (values * scale * gain, scale)


def rms_grad(values, scale, gain, grads, inner, width):
    grad_values = scale * gain * grads - values * scale**3 * inner / width
    grad_gain = jnp.sum(grads * values * scale, axis=0)
    return (grad_values, grad_gain)


def tensor_sums(pair):
    return lax.psum((pair[0], pair[1]), "tensor")


def heads_to_rows(term, rows):
    return lax.psum_scatter(
        term(jnp.int32(0), rows * lax.axis_size("tensor")).astype(jnp.bfloat16),
        "tensor",
        scatter_dimension=0,
        tiled=True,
    ).astype(jnp.float32)


def sum_over_dp(rows):
    dp = lax.axis_size("dp")
    pieces = rows.reshape(dp, rows.shape[0] // dp, rows.shape[1])
    return lax.psum_scatter(pieces, "dp", scatter_dimension=0, tiled=False)


def sum_over_tensor(part):
    return lax.psum_scatter(part, "tensor", scatter_dimension=0, tiled=True)


def body(
    residual,
    attn_gain,
    w_query,
    w_key,
    w_value,
    query_gain,
    key_gain,
    w_out,
    moe_gain,
    router,
    w_gate,
    w_up,
    w_down,
    segment_path,
    token_valid,
    routes,
    route_order,
    cotangent,
):
    tensor_rank = lax.axis_index("tensor")
    tok_dev, width = residual.shape
    seq_len = segment_path.shape[1]
    top_count = routes.shape[1]
    experts = router.shape[1]
    local_experts = w_gate.shape[0]
    dp_groups = experts // local_experts
    capacity = 9 * tok_dev * top_count // (8 * experts)
    full_width = H * HD
    everyone = ("dp", "tensor")
    direct = dp_groups == 8 and lax.axis_size("tensor") == 4
    first_expert = lax.axis_index("dp") * local_experts
    slot_rows = padded(capacity, 8)
    valid_dev = lax.dynamic_slice_in_dim(token_valid, tensor_rank * tok_dev, tok_dev)
    slots_own = slot_table(routes, route_order, valid_dev, experts, capacity)
    cots_all = lax.all_gather(cotangent, everyone, axis=0, tiled=True)
    head_cols = w_query.shape[1]
    residual_float = residual.astype(jnp.float32)
    normed_one, scale_one = rms_apply(residual_float, attn_gain)
    hidden = normed_one.astype(jnp.bfloat16)
    path_lines = jnp.concatenate((segment_path, token_valid[None]), axis=0)
    path_columns = path_lines.T
    positions = jnp.sum(visible_block(segment_path, segment_path, token_valid, 0).astype(jnp.int32), axis=1) - 1
    cosine, sine = rotation(positions, HD)
    cosine = jnp.concatenate((cosine, cosine), axis=1)
    sine = jnp.concatenate((-sine, sine), axis=1)
    if direct:
        hidden_all, joined_weight, gathered_out, slots = start_exchange(
            hidden, w_query, w_key, w_value, w_out, slots_own, 3
        )
        slots = jnp.swapaxes(slots.reshape(4, 8, local_experts, tok_dev), 0, 1).reshape(32, local_experts, tok_dev)
    else:
        hidden_all = lax.all_gather(hidden, "tensor", axis=0, tiled=True)
        joined_weight = jnp.concatenate(
            [lax.all_gather(w, "dp", axis=0, tiled=True) for w in (w_query, w_key, w_value)], axis=1
        )
        gathered_out = lax.all_gather(w_out, "dp", axis=1, tiled=True)
        slots_all = lax.all_gather(slots_own.astype(jnp.bfloat16), everyone, axis=0)
        slots = lax.dynamic_slice_in_dim(slots_all, first_expert, local_experts, 1).astype(jnp.int32)
    projected = jnp.dot(hidden_all, joined_weight, preferred_element_type=jnp.float32)
    blocks = slots.shape[0]
    q_raw = projected[:, :head_cols]
    k_raw = projected[:, head_cols : 2 * head_cols]
    query_sq, key_sq = tensor_sums((jnp.sum(q_raw * q_raw, axis=1), jnp.sum(k_raw * k_raw, axis=1)))
    query_scale = lax.rsqrt(query_sq / full_width + norm_eps)[:, None]
    key_scale = lax.rsqrt(key_sq / full_width + norm_eps)[:, None]
    query_gain_dev = lax.dynamic_slice_in_dim(query_gain, tensor_rank * head_cols, head_cols)
    key_gain_dev = lax.dynamic_slice_in_dim(key_gain, tensor_rank * head_cols, head_cols)
    query_low, key_low, value_low, attn_mixed, log_totals = attend(
        projected,
        jnp.concatenate((query_scale, key_scale), axis=1),
        jnp.stack((query_gain_dev, key_gain_dev)),
        cosine,
        sine,
        path_columns,
        path_lines,
    )
    if direct:
        x_one, hidden_two, gates_own = mixed_out(attn_mixed, gathered_out, residual, moe_gain, router.T, 4)
        probs = gates_own.T
    else:

        def attn_term(first_row, row_count):
            return jnp.dot(attn_mixed, gathered_out, preferred_element_type=jnp.float32)

        x_one = residual_float + heads_to_rows(attn_term, tok_dev)
        hidden_two = rms_apply(x_one, moe_gain)[0].astype(jnp.bfloat16)
        logits = jnp.dot(hidden_two, router, preferred_element_type=jnp.float32)
        probs = jax.nn.softmax(logits, axis=-1)
        gates_own = probs.T
    scale_two = lax.rsqrt(jnp.mean(x_one * x_one, axis=-1, keepdims=True) + norm_eps)
    if direct:
        x_slots, c_slots, gate_slots = gather_dispatch(slots, hidden_two, gates_own, cots_all, slot_rows, 1)
    else:
        gates_all = lax.all_gather(gates_own, everyone, axis=0)
        rows_all = lax.all_gather(hidden_two, everyone, axis=0, tiled=True)
        gates = lax.dynamic_slice_in_dim(gates_all, first_expert, local_experts, 1)
        x_slots, gate_slots = dispatch(slots, gates, rows_all, slot_rows)
        c_slots = dispatch(slots, None, cots_all, slot_rows)
    outs, grads, pre, gated = expert_pass(
        first_expert.reshape(1),
        x_slots,
        c_slots,
        gate_slots,
        w_gate,
        w_up,
        w_down,
        blocks,
        padded(slot_rows, 16),
    )
    if direct:
        grad_rows, out_part = reduce_all(slots, outs, grads, 2)
    else:
        out_part, grad_part = combine(slots, outs, grads)
        grad_rows = sum_over_tensor(sum_over_dp(grad_part)).astype(jnp.float32)
    out_part = sum_over_dp(out_part)
    grad_out = cotangent.astype(jnp.float32)
    grad_hidden_two = grad_rows[:, :width]
    grad_probs = grad_rows[:, width : width + experts]
    grad_logits = probs * (grad_probs - jnp.sum(probs * grad_probs, axis=-1, keepdims=True))
    router_float = router.astype(jnp.float32)
    grad_hidden_two = grad_hidden_two + lax.dot_general(
        grad_logits, router_float, (((1,), (1,)), ((), ())), precision=lax.Precision.HIGHEST
    )
    grad_router_part = lax.dot_general(
        grad_logits,
        hidden_two.astype(jnp.float32),
        (((0,), (0,)), ((), ())),
        precision=lax.Precision.HIGHEST,
    )
    inner_two = jnp.sum(grad_hidden_two * moe_gain * x_one, axis=-1, keepdims=True)
    grad_norm_two, grad_moe_gain_part = rms_grad(
        x_one, scale_two, moe_gain, grad_hidden_two, inner_two, width
    )
    grad_x_one = grad_out + grad_norm_two
    grad_attn_low = grad_x_one.astype(jnp.bfloat16)
    early_sums = jnp.concatenate(
        (grad_router_part, grad_moe_gain_part[None], jnp.zeros((7, width), jnp.float32)), axis=0
    )
    if direct:
        grad_attn_all, early_sums = back_gather(grad_attn_low, early_sums, 5)
    else:
        grad_attn_all = lax.all_gather(grad_attn_low, "tensor", axis=0, tiled=True)
        early_sums = lax.psum(early_sums, everyone)
    grad_q_norm, grad_k_norm, grad_value_all = attend_back(
        grad_attn_all,
        gathered_out,
        query_low,
        key_low,
        value_low,
        log_totals,
        cosine,
        sine,
        path_columns,
        path_lines,
    )
    query_inner, key_inner = tensor_sums(
        (
            jnp.sum(grad_q_norm * query_gain_dev * q_raw, axis=1),
            jnp.sum(grad_k_norm * key_gain_dev * k_raw, axis=1),
        )
    )
    grad_q_raw, grad_query_gain_dev = rms_grad(
        q_raw, query_scale, query_gain_dev, grad_q_norm, query_inner[:, None], full_width
    )
    grad_k_raw, grad_key_gain_dev = rms_grad(
        k_raw, key_scale, key_gain_dev, grad_k_norm, key_inner[:, None], full_width
    )
    grad_joined = jnp.concatenate(
        (grad_q_raw, grad_k_raw, grad_value_all), axis=1
    ).astype(jnp.bfloat16)
    zero_width = jnp.zeros((full_width,), jnp.float32)
    grad_query_full = lax.dynamic_update_slice_in_dim(
        zero_width, grad_query_gain_dev, tensor_rank * head_cols, 0
    )
    grad_key_full = lax.dynamic_update_slice_in_dim(
        zero_width, grad_key_gain_dev, tensor_rank * head_cols, 0
    )
    if direct:
        gains = jnp.concatenate(
            (grad_query_full[None], grad_key_full[None], jnp.zeros((6, width), jnp.float32)), axis=0
        )
        grad_input, grad_w_query, grad_w_key, grad_w_value, grad_w_out, gains = last_exchange(
            grad_joined,
            joined_weight,
            hidden_all,
            attn_mixed,
            grad_attn_all,
            residual,
            attn_gain,
            grad_x_one,
            gains,
            6,
        )
    else:
        grad_joined_weight = lax.dot_general(
            hidden_all, grad_joined, (((0,), (0,)), ((), ())), preferred_element_type=jnp.float32
        ).astype(jnp.bfloat16)
        grad_out_weight = lax.dot_general(
            attn_mixed, grad_attn_all, (((0,), (0,)), ((), ())), preferred_element_type=jnp.float32
        ).astype(jnp.bfloat16)

        def back_term(first_row, row_count):
            return lax.dot_general(
                grad_joined, joined_weight, (((1,), (1,)), ((), ())), preferred_element_type=jnp.float32
            )

        grad_hidden = heads_to_rows(back_term, tok_dev)
        inner_one = jnp.sum(grad_hidden * attn_gain * residual_float, axis=-1, keepdims=True)
        grad_norm_one, grad_attn_gain_part = rms_grad(
            residual_float, scale_one, attn_gain, grad_hidden, inner_one, width
        )
        grad_input = grad_x_one + grad_norm_one
        grad_w_query, grad_w_key, grad_w_value = (
            lax.psum_scatter(
                grad_joined_weight[:, n * head_cols : (n + 1) * head_cols],
                "dp",
                scatter_dimension=0,
                tiled=True,
            ).astype(jnp.float32)
            for n in range(3)
        )
        grad_w_out = lax.psum_scatter(
            grad_out_weight, "dp", scatter_dimension=1, tiled=True
        ).astype(jnp.float32)
        gains = lax.psum(jnp.stack((grad_query_full, grad_key_full, grad_attn_gain_part)), everyone)
    out_part, pre, grad_input = lax.optimization_barrier((out_part, pre, grad_input))
    grad_w_gate, grad_w_up, grad_w_down = weight_grads(x_slots, c_slots, pre, gated)
    moe_out, grad_w_gate, grad_w_up, grad_w_down = lax.optimization_barrier(
        (sum_over_tensor(out_part), grad_w_gate, grad_w_up, grad_w_down)
    )
    block_out = (x_one + moe_out.astype(jnp.float32)).astype(jnp.bfloat16)
    return (
        block_out,
        grad_input,
        gains[2],
        grad_w_query,
        grad_w_key,
        grad_w_value,
        gains[0],
        gains[1],
        grad_w_out,
        early_sums[experts],
        early_sums[:experts].T,
        grad_w_gate,
        grad_w_up,
        grad_w_down,
    )


def solution(mesh):
    in_specs = (
        P(("dp", "tensor"), None),
        P(),
        P("dp", "tensor"),
        P("dp", "tensor"),
        P("dp", "tensor"),
        P(),
        P(),
        P("tensor", "dp"),
        P(),
        P(),
        P("dp", None, "tensor"),
        P("dp", None, "tensor"),
        P("dp", "tensor", None),
        P(None, "dp"),
        P("dp"),
        P(("dp", "tensor"), None),
        P(("dp", "tensor"), None),
        P(("dp", "tensor"), None),
    )
    out_specs = (
        P(("dp", "tensor"), None),
        P(("dp", "tensor"), None),
        P(),
        P("dp", "tensor"),
        P("dp", "tensor"),
        P("dp", "tensor"),
        P(),
        P(),
        P("tensor", "dp"),
        P(),
        P(),
        P("dp", None, "tensor"),
        P("dp", None, "tensor"),
        P("dp", "tensor", None),
    )
    return jax.shard_map(body, mesh=mesh, in_specs=in_specs, out_specs=out_specs, check_vma=False)
```

```python
import functools

import jax
import jax.numpy as jnp
from jax import lax
from jax.experimental import pallas as pl
from jax.experimental.pallas import tpu as pltpu
from jax.sharding import PartitionSpec as P

H = 16
HD = 128


norm_eps = 1e-05
rope_base = 10000.0
masked_score = -1e30


def padded(count, step):
    return -(-count // step) * step


def slot_table(routes, route_order, valid, experts, capacity):
    far = jnp.int32(1 << 30)
    expert = lax.iota(jnp.int32, experts)[:, None, None]
    hits = (routes[None] == expert) & (valid[None, :, None] == 1)
    order = jnp.min(jnp.where(hits, route_order[None], far), axis=-1)
    ranks = jnp.sum((order[:, None, :] < order[:, :, None]).astype(jnp.int32), axis=-1)
    return jnp.where((order < far) & (ranks < capacity), ranks, -1)


def slot_hits(slots, expert, rows):
    tokens = slots.shape[-1]
    return lax.broadcasted_iota(jnp.int32, (rows, tokens), 0) == slots[expert : expert + 1, :]


def dispatch_kernel(slots_ref, gates_ref, rows_ref, x_ref, gate_ref):
    pair, experts, tokens = slots_ref.shape
    rows = x_ref.shape[1] // pair
    width = rows_ref.shape[1]
    picks = []
    for b in range(pair):
        slots = slots_ref[b]
        pieces = []
        for e in range(experts):
            hit = slot_hits(slots, e, rows)
            pieces.append(hit.astype(jnp.float32))
            if gate_ref is not None:
                gate = jnp.sum(jnp.where(hit, gates_ref[b, e : e + 1, :], 0.0), axis=1, keepdims=True)
                gate_ref[e, b * rows : (b + 1) * rows, :] = jnp.broadcast_to(gate, (rows, 128))
        picks.append(jnp.concatenate(pieces, axis=0).astype(jnp.bfloat16))
    step = min(512, width)
    for first in range(0, width, step):
        parts = [
            jnp.dot(
                picks[b],
                rows_ref[b * tokens : (b + 1) * tokens, first : first + step],
                preferred_element_type=jnp.float32,
            )
            for b in range(pair)
        ]
        for e in range(experts):
            x_ref[e, :, first : first + step] = jnp.concatenate(
                [part[e * rows : (e + 1) * rows] for part in parts], axis=0
            ).astype(jnp.bfloat16)


def plain_dispatch_kernel(slots_ref, rows_ref, x_ref):
    dispatch_kernel(slots_ref, None, rows_ref, x_ref, None)


def dispatch(slots, gates, rows_all, rows):
    blocks, experts, tokens = slots.shape
    width = rows_all.shape[1]
    pair = 2
    out = jax.ShapeDtypeStruct((experts, blocks * rows, width), jnp.bfloat16)
    table = pl.BlockSpec((pair, experts, tokens), lambda i: (i, 0, 0))
    source = pl.BlockSpec((pair * tokens, width), lambda i: (i, 0))
    target = pl.BlockSpec((experts, pair * rows, width), lambda i: (0, i, 0))
    settings = dict(
        grid=(blocks // pair,),
        compiler_params=pltpu.CompilerParams(vmem_limit_bytes=50 << 20),
        cost_estimate=pl.CostEstimate(
            flops=2 * blocks * experts * rows * tokens * width,
            bytes_accessed=2 * blocks * (tokens + experts * rows) * width,
            transcendentals=0,
        ),
    )
    if gates is None:
        return pl.pallas_call(
            plain_dispatch_kernel, out_shape=out, in_specs=[table, source], out_specs=target, name="pick", **settings
        )(slots, rows_all)
    return pl.pallas_call(
        dispatch_kernel,
        out_shape=(out, jax.ShapeDtypeStruct((experts, blocks * rows, 128), jnp.float32)),
        in_specs=[table, table, source],
        out_specs=[target, pl.BlockSpec((experts, pair * rows, 128), lambda i: (0, i, 0))],
        name="dispatch",
        **settings,
    )(slots, gates, rows_all)


def turned(left, right):
    return lax.dot_general(left, right, (((0,), (0,)), ((), ())), preferred_element_type=jnp.float32)


def across(left, right):
    return lax.dot_general(left, right, (((1,), (1,)), ((), ())), preferred_element_type=jnp.float32)


def expert_kernel(rows, first_ref, x_ref, c_ref, gate_ref, wg_ref, wu_ref, wd_ref,
                  o_ref, dx_ref, pre_ref, gated_ref):
    expert = pl.program_id(0)
    tile, width = x_ref.shape[1:]
    units = wg_ref.shape[2]
    room = o_ref.shape[2]
    blocks = tile // rows
    gate = gate_ref[0, :, 0:1]
    x = x_ref[0]
    c = c_ref[0]
    gate_pre = jnp.dot(x, wg_ref[0], preferred_element_type=jnp.float32)
    up_pre = jnp.dot(x, wu_ref[0], preferred_element_type=jnp.float32)
    back = across(c, wd_ref[0])
    sig = jax.nn.sigmoid(gate_pre)
    silu = gate_pre * sig
    act = (silu * up_pre).astype(jnp.bfloat16)
    act_float = act.astype(jnp.float32)
    grad_gate = jnp.sum(act_float * back, axis=1, keepdims=True)
    grad_act = back * gate
    grad_gate_pre = (grad_act * up_pre * sig * (1.0 + gate_pre * (1.0 - sig))).astype(jnp.bfloat16)
    grad_up_pre = (grad_act * silu).astype(jnp.bfloat16)
    gated = (act_float * gate).astype(jnp.bfloat16)

    def spread(values):
        values = values.reshape(blocks, rows, values.shape[1])
        if room > rows:
            empty = jnp.zeros((blocks, room - rows, values.shape[2]), jnp.float32)
            values = jnp.concatenate((values, empty), axis=1)
        return values.astype(jnp.bfloat16)

    step = min(512, width)
    for first in range(0, width, step):
        part = slice(first, first + step)
        out = jnp.dot(act, wd_ref[0, :, part], preferred_element_type=jnp.float32) * gate
        o_ref[:, 0, :, part] = spread(out)
        grad = across(grad_gate_pre, wg_ref[0, part, :]) + across(grad_up_pre, wu_ref[0, part, :])
        dx_ref[:, 0, :, part] = spread(grad)
    lanes = lax.broadcasted_iota(jnp.int32, (tile, 128), 1)
    dx_ref[:, 0, :, width:] = spread(jnp.where(lanes == first_ref[0] + expert, grad_gate, 0.0))

    pre_ref[0, :, :units] = grad_gate_pre
    pre_ref[0, :, units:] = grad_up_pre
    gated_ref[0] = gated


def weight_terms(x_ref, c_ref, pre_ref, gated_ref, gate_ref, up_ref, down_ref):
    units = gated_ref.shape[1]
    width = x_ref.shape[1]
    step = min(512, width)
    for first in range(0, width, step):
        part = slice(first, first + step)
        both = turned(x_ref[:, part], pre_ref[...])
        gate_ref[part, :] = both[:, :units]
        up_ref[part, :] = both[:, units:]
        down_ref[:, part] = turned(gated_ref[...], c_ref[:, part])


def weight_kernel(x_ref, c_ref, pre_ref, gated_ref, gate_ref, up_ref, down_ref):
    weight_terms(*(r.at[0] for r in (x_ref, c_ref, pre_ref, gated_ref, gate_ref, up_ref, down_ref)))


def weight_grads(x_slots, c_slots, pre, gated):
    experts, total, width = x_slots.shape
    units = gated.shape[2]
    step = min(512, width)
    part = pl.BlockSpec((1, total, step), lambda e, j: (e, 0, j))
    tall = pl.BlockSpec((1, step, units), lambda e, j: (e, j, 0))
    return pl.pallas_call(
        weight_kernel,
        grid=(experts, width // step),
        out_shape=(
            jax.ShapeDtypeStruct((experts, width, units), jnp.float32),
            jax.ShapeDtypeStruct((experts, width, units), jnp.float32),
            jax.ShapeDtypeStruct((experts, units, width), jnp.float32),
        ),
        in_specs=[
            part, part,
            pl.BlockSpec((1, total, 2 * units), lambda e, j: (e, 0, 0)),
            pl.BlockSpec((1, total, units), lambda e, j: (e, 0, 0)),
        ],
        out_specs=[tall, tall, pl.BlockSpec((1, units, step), lambda e, j: (e, 0, j))],
        compiler_params=pltpu.CompilerParams(vmem_limit_bytes=50 << 20),
        cost_estimate=pl.CostEstimate(
            flops=6 * experts * total * width * units,
            bytes_accessed=4 * experts * total * width + 12 * experts * width * units,
            transcendentals=0,
        ),
        name="weight_grads",
    )(x_slots, c_slots, pre, gated)


def expert_pass(first_expert, x_slots, c_slots, gate_slots, w_gate, w_up, w_down, blocks, room):
    experts, total, width = x_slots.shape
    units = w_gate.shape[2]
    rows = total // blocks
    group = next(n for n in (16, 8, 4, 2, 1) if blocks % n == 0 and (n * rows <= 768 or n == 1))
    tile = group * rows
    extra = 128
    tall = pl.BlockSpec((1, width, units), lambda e, r, _: (e, 0, 0))
    wide = pl.BlockSpec((1, units, width), lambda e, r, _: (e, 0, 0))
    slot = pl.BlockSpec((1, tile, width), lambda e, r, _: (e, r, 0))
    kernel = functools.partial(expert_kernel, rows)
    return pl.pallas_call(
        kernel,
        grid_spec=pltpu.PrefetchScalarGridSpec(
            num_scalar_prefetch=1,
            grid=(experts, total // tile),
            in_specs=[slot, slot, pl.BlockSpec((1, tile, 128), lambda e, r, _: (e, r, 0)), tall, tall, wide],
            out_specs=[
                pl.BlockSpec((group, 1, room, width), lambda e, r, _: (r, e, 0, 0)),
                pl.BlockSpec((group, 1, room, width + extra), lambda e, r, _: (r, e, 0, 0)),
                pl.BlockSpec((1, tile, 2 * units), lambda e, r, _: (e, r, 0)),
                pl.BlockSpec((1, tile, units), lambda e, r, _: (e, r, 0)),
            ],
        ),
        out_shape=(
            jax.ShapeDtypeStruct((blocks, experts, room, width), jnp.bfloat16),
            jax.ShapeDtypeStruct((blocks, experts, room, width + extra), jnp.bfloat16),
            jax.ShapeDtypeStruct((experts, total, 2 * units), jnp.bfloat16),
            jax.ShapeDtypeStruct((experts, total, units), jnp.bfloat16),
        ),
        compiler_params=pltpu.CompilerParams(vmem_limit_bytes=60 << 20),
        cost_estimate=pl.CostEstimate(
            flops=12 * experts * total * width * units,
            bytes_accessed=8 * experts * total * width + 6 * experts * width * units,
            transcendentals=experts * total * units,
        ),
        name="experts",
    )(first_expert, x_slots, c_slots, gate_slots, w_gate, w_up, w_down)


def combine_kernel(slots_ref, o_ref, dx_ref, out_ref, grad_ref):
    _, experts, tokens = slots_ref.shape
    room, width = o_ref.shape[2:]
    slots = slots_ref[0]
    picks = jnp.concatenate(
        [slot_hits(slots, e, room).astype(jnp.float32) for e in range(experts)], axis=0
    ).astype(jnp.bfloat16)
    for source, target in ((o_ref, out_ref), (dx_ref, grad_ref)):
        columns = target.shape[1]
        for first in range(0, columns, 512):
            part = slice(first, min(first + 512, columns))
            values = source[0, :, :, part].reshape(experts * room, part.stop - first)
            target[:, part] = turned(picks, values).astype(jnp.bfloat16)


def combine(slots, outs, grads):
    blocks, experts, tokens = slots.shape
    room, width = outs.shape[2:]
    wider = grads.shape[3]
    return pl.pallas_call(
        combine_kernel,
        grid=(blocks,),
        out_shape=(
            jax.ShapeDtypeStruct((blocks * tokens, width), jnp.bfloat16),
            jax.ShapeDtypeStruct((blocks * tokens, wider), jnp.bfloat16),
        ),
        in_specs=[
            pl.BlockSpec((1, experts, tokens), lambda i: (i, 0, 0)),
            pl.BlockSpec((1, experts, room, width), lambda i: (i, 0, 0, 0)),
            pl.BlockSpec((1, experts, room, wider), lambda i: (i, 0, 0, 0)),
        ],
        out_specs=[
            pl.BlockSpec((tokens, width), lambda i: (i, 0)),
            pl.BlockSpec((tokens, wider), lambda i: (i, 0)),
        ],
        compiler_params=pltpu.CompilerParams(vmem_limit_bytes=50 << 20),
        cost_estimate=pl.CostEstimate(
            flops=2 * blocks * experts * room * tokens * (width + wider),
            bytes_accessed=2 * blocks * (tokens + experts * room) * (width + wider),
            transcendentals=0,
        ),
        name="combine",
    )(slots, outs, grads)


MESH = pl.DeviceIdType.MESH


def place():
    dp, z = lax.axis_index("dp"), lax.axis_index("tensor")
    return dp // 4, dp // 2 % 2, dp % 2, z


def peer(y, x, core, z):
    return (y * 4 + x * 2 + core, z)


def block_of(y, x, core, z):
    return (y * 4 + x * 2 + core) * 4 + z


def greet(line):
    y, x, core, z = place()
    barrier = pltpu.get_barrier_semaphore()
    for near in ((y, x, 1 - core, z), (y, 1 - x, core, z), (1 - y, x, core, z)):
        pl.semaphore_signal(barrier, inc=1, device_id=peer(*near), device_id_type=MESH)

    @pl.when(z > 0)
    def _():
        pl.semaphore_signal(barrier, inc=1, device_id=peer(y, x, core, z - 1), device_id_type=MESH)

    @pl.when(z < line - 1)
    def _():
        pl.semaphore_signal(barrier, inc=1, device_id=peer(y, x, core, z + 1), device_id_type=MESH)

    pl.semaphore_wait(barrier, 3 + (z + line - 1) // line + (2 * line - 2 - z) // line)


def either(first, second, take):
    return first * (1 - take) + second * take


def remote(source, target, send_sem, recv_sem, where):
    return pltpu.make_async_remote_copy(
        src_ref=source, dst_ref=target, send_sem=send_sem, recv_sem=recv_sem,
        device_id=peer(*where), device_id_type=MESH,
    )


def landed(target, sem):
    pltpu.make_async_copy(target, target, sem).wait()


def slot_order(y, x, core, z):
    return ((y * 2 + x) * 4 + z) * 2 + core


def near_first(z, i):
    side = z // 2
    low = either(z, 3 - z, side)
    first, second = (4 - i) // 4, (5 - i) // 4 - (4 - i) // 4
    return either(i + low * (first - second), 3 - i - low * (first - second), side)


def gather_dispatch_kernel(line, rows, slots_ref, hidden_ref, gates_ref, cots_ref,
                           rows_out, gates_out, x_out, c_out, gate_out,
                           in_c, in_x, in_gate, stage_c, stage_x, stage_gate,
                           local_sem, send_sem, recv_sem, load_sem, store_sem):
    y, x, core, z = place()
    tokens, width = hidden_ref.shape
    experts = slots_ref.shape[1]
    first_expert = (y * 4 + x * 2 + core) * experts
    owns, outs = (hidden_ref, gates_ref), (rows_out, gates_out)
    near_x, near_y, sibling = (y, 1 - x, core, z), (1 - y, x, core, z), (y, x, 1 - core, z)
    last = 24
    greet(line)

    def span(n, block):
        count = owns[n].shape[0]
        return outs[n].at[pl.ds(block * count, count)]

    def spot(m):
        q = m % 4
        i = m // 4 - (q + 1) // 2
        live = (i >= 0) & (i < line)
        held = i * live.astype(jnp.int32)
        yy, xx = (y + q // 2) % 2, (x + q % 2) % 2
        return q, held, live, yy, xx, near_first(z, held)

    def sends(m):
        q, i, live, yy, xx, zz = spot(m)
        block = block_of(yy, xx, core, zz)
        own = live & (q == 0)
        table = (
            (own & (zz <= z) & (z < line - 1), (y, x, core, z + 1)),
            (own & (zz >= z) & (z > 0), (y, x, core, z - 1)),
            (own | (live & (q == 2) & (zz % 2 == 1)), near_x),
            (own | (live & (q == 1) & (zz % 2 == 0)), near_y),
            (live, sibling),
        )
        for lane, (wanted, where) in enumerate(table):
            for n in range(2):
                part = span(n, block)
                yield wanted, remote(part, part, send_sem.at[n, lane, m], recv_sem.at[n, block], where)

    def load_c(chip):
        yy, xx, zz = chip // 8, chip // 4 % 2, chip % 4
        for c in range(2):
            b = block_of(yy, xx, c, zz)
            yield pltpu.make_async_copy(
                cots_ref.at[pl.ds(b * tokens, tokens)], in_c.at[pl.ds(c * tokens, tokens)], load_sem.at[0, c]
            )

    def load_x(yy, xx, zz):
        for c in range(2):
            b = block_of(yy, xx, c, zz)
            yield pltpu.make_async_copy(
                rows_out.at[pl.ds(b * tokens, tokens)], in_x.at[pl.ds(c * tokens, tokens)], load_sem.at[1, c]
            )
            yield pltpu.make_async_copy(
                gates_out.at[pl.ds(b * gates_ref.shape[0] + first_expert, experts)], in_gate.at[c], load_sem.at[2, c]
            )

    def store(stage, target, lane, chip):
        return pltpu.make_async_copy(stage, target.at[:, pl.ds(chip * 2 * rows, 2 * rows)], store_sem.at[lane])

    def pick(source, target, yy, xx, zz, gated):
        picks = []
        for c in range(2):
            slots = slots_ref[block_of(yy, xx, c, zz)]
            pieces = []
            for e in range(experts):
                hit = slot_hits(slots, e, rows)
                pieces.append(hit.astype(jnp.float32))
                if gated:
                    gate = jnp.sum(jnp.where(hit, in_gate[c, e : e + 1, :], 0.0), axis=1, keepdims=True)
                    stage_gate[e, c * rows : (c + 1) * rows, :] = jnp.broadcast_to(gate, (rows, 128))
            picks.append(jnp.concatenate(pieces, axis=0).astype(jnp.bfloat16))
        step = min(512, width)
        for first in range(0, width, step):
            parts = [
                jnp.dot(
                    picks[c], source[c * tokens : (c + 1) * tokens, first : first + step],
                    preferred_element_type=jnp.float32,
                )
                for c in range(2)
            ]
            for e in range(experts):
                target[e, :, first : first + step] = jnp.concatenate(
                    [part[e * rows : (e + 1) * rows] for part in parts], axis=0
                ).astype(jnp.bfloat16)

    mine = block_of(y, x, core, z)
    local = [pltpu.make_async_copy(owns[n], span(n, mine), local_sem.at[n]) for n in range(2)]
    for copy in local:
        copy.start()
    for copy in load_c(0):
        copy.start()
    for copy in local:
        copy.wait()
    chips = 4 * line
    lag = 2

    def work(m, carry):
        q, i, live, yy, xx, zz = spot(m)

        @pl.when((m < last) & live & (q + i > 0))
        def _():
            for n in range(2):
                landed(span(n, block_of(yy, xx, core, zz)), recv_sem.at[n, block_of(yy, xx, core, zz)])

        for wanted, copy in sends(m):
            pl.when((m < last) & wanted)(copy.start)

        back = m - lag
        q = (back + 8) % 4
        i = (back + 8) // 4 - 2 - (q + 1) // 2
        live = (i >= 0) & (i < line)
        held = i * live.astype(jnp.int32)
        yy, xx = (y + q // 2) % 2, (x + q % 2) % 2
        zz = near_first(z, held)
        chip = (yy * 2 + xx) * 4 + zz

        @pl.when(live)
        def _():
            block = block_of(yy, xx, 1 - core, zz)
            for n in range(2):
                landed(span(n, block), recv_sem.at[n, block])
            for copy in load_x(yy, xx, zz):
                copy.start()

        @pl.when(m < chips)
        def _():
            for copy in load_c(m):
                copy.wait()

            @pl.when(m > 0)
            def _():
                store(stage_c, c_out, 0, m - 1).wait()

            pick(in_c, stage_c, m // 8, m // 4 % 2, m % 4, False)
            store(stage_c, c_out, 0, m).start()

            @pl.when(m + 1 < chips)
            def _():
                for copy in load_c(m + 1):
                    copy.start()

        @pl.when(live)
        def _():
            @pl.when(q + held > 0)
            def _():
                store(stage_x, x_out, 1, chip).wait()
                store(stage_gate, gate_out, 2, chip).wait()

            for copy in load_x(yy, xx, zz):
                copy.wait()
            pick(in_x, stage_x, yy, xx, zz, True)
            store(stage_x, x_out, 1, chip).start()
            store(stage_gate, gate_out, 2, chip).start()

        return carry

    lax.fori_loop(0, last + lag, work, 0)
    store(stage_c, c_out, 0, chips - 1).wait()
    store(stage_x, x_out, 1, 0).wait()
    store(stage_gate, gate_out, 2, 0).wait()

    def finish(m, carry):
        for wanted, copy in sends(m):
            pl.when(wanted)(copy.wait_send)
        return carry

    lax.fori_loop(0, last, finish, 0)


def gather_dispatch(slots, hidden, gates, cots_all, rows, collective_id):
    line = 4
    blocks, experts, tokens = slots.shape
    width = hidden.shape[1]
    pair = 2 * rows
    low, wide = jnp.bfloat16, jnp.float32
    any_ref = pl.BlockSpec(memory_space=pl.ANY)
    vmem = pl.BlockSpec(memory_space=pltpu.VMEM)
    dma = pltpu.SemaphoreType.DMA
    slot_shape = jax.ShapeDtypeStruct((experts, blocks * rows, width), low)
    return pl.pallas_call(
        functools.partial(gather_dispatch_kernel, line, rows),
        out_shape=(
            jax.ShapeDtypeStruct((blocks * tokens, width), low),
            jax.ShapeDtypeStruct((blocks * gates.shape[0], tokens), wide),
            slot_shape,
            slot_shape,
            jax.ShapeDtypeStruct((experts, blocks * rows, 128), wide),
        ),
        in_specs=[vmem, any_ref, any_ref, any_ref],
        out_specs=[any_ref] * 5,
        scratch_shapes=[
            pltpu.VMEM((2 * tokens, width), low),
            pltpu.VMEM((2 * tokens, width), low),
            pltpu.VMEM((2, experts, tokens), wide),
            pltpu.VMEM((experts, pair, width), low),
            pltpu.VMEM((experts, pair, width), low),
            pltpu.VMEM((experts, pair, 128), wide),
            dma((2,)),
            dma((2, 5, 24)),
            dma((2, blocks)),
            dma((3, 2)),
            dma((3,)),
        ],
        compiler_params=pltpu.CompilerParams(
            collective_id=collective_id, has_side_effects=True, vmem_limit_bytes=40 << 20
        ),
        cost_estimate=pl.CostEstimate(
            flops=4 * blocks * experts * rows * tokens * width, bytes_accessed=200 << 20, transcendentals=0
        ),
        name="gather_dispatch",
    )(slots, hidden, gates, cots_all)[2:]


def reduce_kernel(line, slots_ref, grads_ref, outs_ref, sum_ref, part_ref,
                  grad_in, out_in, out_stage, stage, near, far_x, far_y, from_x, from_y, up, down,
                  in_sem, part_sem, stage_sem, near_sem, send_sem, far_sem, x_sem, y_sem, line_sem):
    y, x, core, z = place()
    tokens, width = sum_ref.shape
    half = tokens // 2
    experts, room = grads_ref.shape[1:3]
    rounds = line
    greet(line)

    def goal(r):
        early = 1 - r // 2
        return (line - 1) * (r % 2) * early + (r - 1) * (1 - early)

    def spot_at(q):
        r, p = q // 8, q % 8
        own = (1 - p % 2) * ((p + 7) // 8) + p // 7
        column = own * (p // 2 - 1 + p // 7) + (1 - own) * ((p + 1) // 2)
        dy, dx = (column + 1) % 2, 1 - column // 2
        target_core = core * own + (1 - core) * (1 - own)
        return (y + dy) % 2, (x + dx) % 2, target_core, goal(r)

    def load(q):
        b = slot_order(*spot_at(q))
        return (
            pltpu.make_async_copy(grads_ref.at[b], grad_in.at[q % 2], in_sem.at[0, q % 2]),
            pltpu.make_async_copy(outs_ref.at[b], out_in.at[q % 2], in_sem.at[1, q % 2]),
        )

    def to_part(q):
        b = block_of(*spot_at(q))
        return pltpu.make_async_copy(out_stage.at[q % 2], part_ref.at[pl.ds(b * tokens, tokens)], part_sem.at[q % 2])

    def to_sibling(r, j):
        return pltpu.make_async_remote_copy(
            src_ref=stage.at[j], dst_ref=near.at[r * 4 + j], send_sem=stage_sem.at[j], recv_sem=near_sem.at[r * 4 + j],
            device_id=peer(y, x, 1 - core, z), device_id_type=MESH,
        )

    near_x, near_y = peer(y, 1 - x, core, z), peer(1 - y, x, core, z)

    def rows(h):
        return pl.ds(h * half, half)

    def cross(kind, r):
        column, h, target, sem, index, lane = {
            "far_x": (0, 0, far_x.at[r], far_sem.at[0, r], near_x, 0),
            "far_y": (0, 1, far_y.at[r], far_sem.at[1, r], near_y, 1),
            "x0": (1, 0, from_x.at[r, rows(0)], x_sem.at[r, 0], near_x, 2),
            "x1": (1, 1, from_x.at[r, rows(1)], x_sem.at[r, 1], near_x, 3),
            "y0": (2, 0, from_y.at[r, rows(0)], y_sem.at[r, 0], near_y, 4),
            "y1": (2, 1, from_y.at[r, rows(1)], y_sem.at[r, 1], near_y, 5),
        }[kind]
        return pltpu.make_async_remote_copy(
            src_ref=near.at[r * 4 + column, rows(h)], dst_ref=target, send_sem=send_sem.at[lane, r], recv_sem=sem,
            device_id=index, device_id_type=MESH,
        )

    def along(sign, r):
        target = up if sign > 0 else down
        lane = 0 if sign > 0 else 1
        return pltpu.make_async_remote_copy(
            src_ref=near.at[r * 4 + 3], dst_ref=target.at[r], send_sem=send_sem.at[6 + lane, r], recv_sem=line_sem.at[lane, r],
            device_id=peer(y, x, core, z + sign), device_id_type=MESH,
        )

    def term(q, source, target_width, store):
        picks = jnp.concatenate(
            [slot_hits(slots_ref[block_of(*spot_at(q))], e, room).astype(jnp.float32) for e in range(experts)], axis=0
        ).astype(jnp.bfloat16)
        for first in range(0, target_width, 512):
            part = slice(first, min(first + 512, target_width))
            values = source[q % 2, :, :, part].reshape(experts * room, part.stop - first)
            store(part, turned(picks, values))

    for copy in load(0):
        copy.start()

    def one(r, p, j, own):
        q = r * 8 + p
        for copy in load(q):
            copy.wait()

        @pl.when(q + 1 < rounds * 8)
        def _():
            for copy in load(q + 1):
                copy.start()

        if own:
            near_slot = r * 4 + j
            to_sibling(r, j).wait_recv()

            def keep(part, value):
                near[near_slot, :, part] = (value + near[near_slot, :, part].astype(jnp.float32)).astype(jnp.bfloat16)

            term(q, grad_in, width, keep)
        else:

            @pl.when(r > 0)
            def _():
                to_sibling(r - 1, j).wait_send()

            def keep(part, value):
                stage[j, :, part] = value.astype(jnp.bfloat16)

            term(q, grad_in, width, keep)
            to_sibling(r, j).start()

        @pl.when(q >= 2)
        def _():
            to_part(q - 2).wait()

        def put(part, value):
            out_stage[q % 2, :, part] = value.astype(jnp.bfloat16)

        term(q, out_in, out_stage.shape[2], put)
        to_part(q).start()

    def add(target, h, *sources):
        for first in range(0, width, 512):
            part = slice(first, min(first + 512, width))
            total = near[target, h, part].astype(jnp.float32)
            for source in sources:
                total = total + source(part).astype(jnp.float32)
            near[target, h, part] = total.astype(jnp.bfloat16)

    def work(s, carry):
        @pl.when(s < rounds)
        def _():
            r = s
            one(r, 0, 0, 0)
            for j in range(4):
                if j < 3:
                    one(r, 2 * j + 1, j + 1, 0)
                one(r, min(2 * j + 2, 7), j, 1)
                for kind in (("far_x", "far_y"), ("x0",), ("y1",), ())[j]:
                    cross(kind, r).start()
            cross("far_y", r).wait_recv()
            add(r * 4 + 1, rows(1), lambda part: far_y[r, :, part])
            cross("x1", r).start()
            cross("far_x", r).wait_recv()
            add(r * 4 + 2, rows(0), lambda part: far_x[r, :, part])
            cross("y0", r).start()

        @pl.when((s >= 1) & (s < rounds + 1))
        def _():
            r = s - 1
            for kind in ("x0", "x1", "y0", "y1"):
                cross(kind, r).wait_recv()
            for h in range(2):
                add(
                    r * 4 + 3,
                    rows(h),
                    lambda part: from_x[r, rows(h), part],
                    lambda part: from_y[r, rows(h), part],
                )

        for hop in range(line - 1):
            r = s - 1 - hop
            live = (r >= 0) & (r < rounds)
            held = r * live.astype(jnp.int32)

            @pl.when(live & (goal(held) > z) & (z == hop))
            def _():
                if hop:
                    along(1, held).wait_recv()
                    for h in range(2):
                        add(held * 4 + 3, rows(h), lambda part: up[held, rows(h), part])
                along(1, held).start()

            @pl.when(live & (goal(held) < z) & (line - 1 - z == hop))
            def _():
                if hop:
                    along(-1, held).wait_recv()
                    for h in range(2):
                        add(held * 4 + 3, rows(h), lambda part: down[held, rows(h), part])
                along(-1, held).start()

        return carry

    lax.fori_loop(0, rounds + line - 1, work, 0)

    mine = (z + (z + 2) // 3) % 4 + z // 3
    sum_ref[...] = near[mine * 4 + 3].astype(jnp.float32)

    @pl.when(z > 0)
    def _():
        along(1, mine).wait_recv()
        sum_ref[...] += up[mine].astype(jnp.float32)

    @pl.when(z < line - 1)
    def _():
        along(-1, mine).wait_recv()
        sum_ref[...] += down[mine].astype(jnp.float32)

    def finish(r, carry):
        for kind in ("far_x", "far_y", "x0", "x1", "y0", "y1"):
            cross(kind, r).wait_send()

        @pl.when(goal(r) > z)
        def _():
            along(1, r).wait_send()

        @pl.when(goal(r) < z)
        def _():
            along(-1, r).wait_send()

        return carry

    lax.fori_loop(0, rounds, finish, 0)
    for j in range(4):
        to_sibling(rounds - 1, j).wait_send()
    for q in (rounds * 8 - 2, rounds * 8 - 1):
        to_part(q).wait()


def reduce_all(slots, outs, grads, collective_id):
    blocks, experts, tokens = slots.shape
    room, width = outs.shape[2:]
    wider = grads.shape[3]
    line = 4
    low = jnp.bfloat16
    any_ref = pl.BlockSpec(memory_space=pl.ANY)
    vmem = pl.BlockSpec(memory_space=pltpu.VMEM)
    dma = pltpu.SemaphoreType.DMA
    return pl.pallas_call(
        functools.partial(reduce_kernel, line),
        out_shape=(
            jax.ShapeDtypeStruct((tokens, wider), jnp.float32),
            jax.ShapeDtypeStruct((blocks * tokens, width), low),
        ),
        in_specs=[vmem, any_ref, any_ref],
        out_specs=[vmem, any_ref],
        scratch_shapes=[
            pltpu.VMEM((2, experts, room, wider), low),
            pltpu.VMEM((2, experts, room, width), low),
            pltpu.VMEM((2, tokens, width), low),
            pltpu.VMEM((4, tokens, wider), low),
            pltpu.VMEM((line * 4, tokens, wider), low),
            pltpu.VMEM((line, tokens // 2, wider), low),
            pltpu.VMEM((line, tokens // 2, wider), low),
            pltpu.VMEM((line, tokens, wider), low),
            pltpu.VMEM((line, tokens, wider), low),
            pltpu.VMEM((line, tokens, wider), low),
            pltpu.VMEM((line, tokens, wider), low),
            dma((2, 2)),
            dma((2,)),
            dma((4,)),
            dma((line * 4,)),
            dma((8, line)),
            dma((2, line)),
            dma((line, 2)),
            dma((line, 2)),
            dma((2, line)),
        ],
        compiler_params=pltpu.CompilerParams(
            collective_id=collective_id, has_side_effects=True, vmem_limit_bytes=62 << 20
        ),
        cost_estimate=pl.CostEstimate(
            flops=2 * blocks * experts * room * tokens * (width + wider),
            bytes_accessed=2 * blocks * experts * room * (width + wider),
            transcendentals=0,
        ),
        name="reduce_all",
    )(slots, grads, outs)


class LineGather:
    def __init__(self, own, out, send_sem, recv_sem, line):
        self.own, self.out, self.send_sem, self.recv_sem, self.line = own, out, send_sem, recv_sem, line
        self.spot = place()
        self.rows = own.shape[0]

    def view(self, block):
        return self.out.at[pl.ds(block * self.rows, self.rows)]

    def inside(self, block):
        return (block >= 0) & (block < self.line)

    def copy(self, sign, step):
        y, x, core, z = self.spot
        block = z - sign * step
        lane = (1 - sign) // 2
        source = self.own if step == 0 else self.view(block)
        return remote(
            source, self.view(block), self.send_sem.at[lane, step], self.recv_sem.at[lane, step], (y, x, core, z + sign)
        )

    def sends(self, sign, step):
        z = self.spot[3]
        return self.inside(z - sign * step) & self.inside(z + sign)

    def begin(self):
        for sign in (1, -1):
            pl.when(self.sends(sign, 0))(self.copy(sign, 0).start)

    def advance(self, step):
        z = self.spot[3]
        for sign in (1, -1):
            block = z - sign * (step + 1)
            lane = (1 - sign) // 2

            @pl.when(self.inside(block))
            def _():
                landed(self.view(block), self.recv_sem.at[lane, step])

            if step + 1 < self.line - 1:
                pl.when(self.sends(sign, step + 1))(self.copy(sign, step + 1).start)

    def finish(self):
        for sign in (1, -1):
            for step in range(self.line - 1):
                pl.when(self.sends(sign, step))(self.copy(sign, step).wait_send)


def start_kernel(line, hidden_ref, wq_ref, wk_ref, wv_ref, wo_ref, slots_ref, hidden_out, joined_out, wo_out, slots_out, raw_out, scale_out,
                 weights, rows_in, sums, local_sem, line_send, line_recv, plane_send, plane_recv,
                 slot_send, slot_recv, slot_line_send, slot_line_recv, sum_send, sum_recv):
    y, x, core, z = place()
    owns = (wq_ref, wk_ref, wv_ref, wo_ref)
    near_x, near_y, sibling = (y, 1 - x, core, z), (1 - y, x, core, z), (y, x, 1 - core, z)

    def view(n, yy, xx, half=None):
        group = yy * 4 + xx * 2 + core
        rows, columns = owns[n].shape
        first, count = (0, rows) if half is None else (half * (rows // 2), rows // 2)
        if n < 3:
            return joined_out.at[pl.ds(group * rows + first, count), pl.ds(n * columns, columns)]
        return wo_out.at[pl.ds(first, count), pl.ds(pl.multiple_of(group * columns, columns), columns)]

    kinds = ("x", "y", "s", "fy", "fx", "sx", "sy", "sf")

    def copy(kind, n):
        source, target, where = {
            "x": (owns[n], view(n, y, x), near_x),
            "y": (owns[n], view(n, y, x), near_y),
            "s": (owns[n], view(n, y, x), sibling),
            "fy": (view(n, y, 1 - x, 0), view(n, y, 1 - x, 0), near_y),
            "fx": (view(n, 1 - y, x, 1), view(n, 1 - y, x, 1), near_x),
            "sx": (view(n, y, 1 - x), view(n, y, 1 - x), sibling),
            "sy": (view(n, 1 - y, x), view(n, 1 - y, x), sibling),
            "sf": (view(n, 1 - y, 1 - x), view(n, 1 - y, 1 - x), sibling),
        }[kind]
        lane = kinds.index(kind)
        return remote(source, target, plane_send.at[lane, n], plane_recv.at[lane, n], where)

    def other(n, yy, xx):
        group = yy * 4 + xx * 2 + 1 - core
        rows, columns = owns[n].shape
        if n < 3:
            return joined_out.at[pl.ds(group * rows, rows), pl.ds(n * columns, columns)]
        return wo_out.at[pl.ds(0, rows), pl.ds(pl.multiple_of(group * columns, columns), columns)]

    barrier = pltpu.get_barrier_semaphore()
    shifts = [(dy, dx, dc) for dy in range(2) for dx in range(2) for dc in range(2) if dy + dx + dc]
    plane = [((y + dy) % 2, (x + dx) % 2, (core + dc) % 2, z) for dy, dx, dc in shifts]
    for other_spot in plane:
        pl.semaphore_signal(barrier, inc=1, device_id=peer(*other_spot), device_id_type=MESH)
    for step in range(1, line):
        pl.semaphore_signal(barrier, inc=1, device_id=peer(y, x, core, (z + step) % line), device_id_type=MESH)
    pl.semaphore_wait(barrier, 7 + line - 1)
    experts = slots_out.shape[1]
    group = peer(y, x, core, z)[0]
    slot_copies = []
    for n, other_spot in enumerate(plane):
        their_group = peer(*other_spot)[0]
        slot_copies.append(
            remote(
                slots_ref.at[pl.ds(their_group * experts, experts)], slots_out.at[z * 8 + group],
                slot_send.at[n], slot_recv.at[group], other_spot,
            )
        )
    own_slots = pltpu.make_async_copy(
        slots_ref.at[pl.ds(group * experts, experts)], slots_out.at[z * 8 + group], local_sem.at[5]
    )
    own_slots.start()
    slot_line = LineGather(slots_out.at[pl.ds(z * 8, 8)], slots_out, slot_line_send, slot_line_recv, line)
    hidden = LineGather(hidden_ref, hidden_out, line_send, line_recv, line)
    locals_ = [pltpu.make_async_copy(hidden_ref, hidden.view(z), local_sem.at[4])]
    locals_ += [pltpu.make_async_copy(owns[n], view(n, y, x), local_sem.at[n]) for n in range(4)]
    for slot_copy in slot_copies:
        slot_copy.start()
    hidden.begin()
    for n in range(4):
        for kind in ("x", "y", "s"):
            copy(kind, n).start()
    for local in locals_:
        local.start()
    for n in range(4):
        landed(view(n, y, 1 - x), plane_recv.at[0, n])
        copy("fy", n).start()
        copy("sx", n).start()
        landed(view(n, 1 - y, x), plane_recv.at[1, n])
        copy("fx", n).start()
        copy("sy", n).start()
    own_slots.wait()
    for other_spot in plane:
        their_group = peer(*other_spot)[0]
        landed(slots_out.at[z * 8 + their_group], slot_recv.at[their_group])
    slot_line.begin()
    hidden.advance(0)
    slot_line.advance(0)
    for n in range(4):
        landed(view(n, 1 - y, 1 - x, 0), plane_recv.at[3, n])
        landed(view(n, 1 - y, 1 - x, 1), plane_recv.at[4, n])
        copy("sf", n).start()
    for n in range(4):
        landed(other(n, y, x), plane_recv.at[2, n])
        landed(other(n, y, 1 - x), plane_recv.at[5, n])
        landed(other(n, 1 - y, x), plane_recv.at[6, n])
        landed(other(n, 1 - y, 1 - x), plane_recv.at[7, n])
    for local in locals_:
        local.wait()
    columns = wq_ref.shape[1]
    rows = hidden_ref.shape[0]
    fetch = pltpu.make_async_copy(joined_out, weights, local_sem.at[0])
    fetch.start()
    fetch.wait()

    def project(block):
        rows_copy = pltpu.make_async_copy(hidden.view(block), rows_in, local_sem.at[1])
        rows_copy.start()
        rows_copy.wait()
        span = pl.ds(pl.multiple_of(block * rows, rows), rows)
        lanes = lax.broadcasted_iota(jnp.int32, (rows, 128), 1)
        tile = jnp.zeros((rows, 128), jnp.float32)
        for n in range(3):
            part = slice(n * columns, (n + 1) * columns)
            value = jnp.dot(rows_in[...], weights[:, part], preferred_element_type=jnp.float32)
            raw_out[span, part] = value
            if n < 2:
                tile = jnp.where(lanes == n, jnp.sum(value * value, axis=1, keepdims=True), tile)
        sums[z, :, span] = jnp.transpose(tile)[:8]

    project(z)
    for step in range(line - 1):
        if step:
            slot_line.advance(step)
            hidden.advance(step)
        for sign in (1, -1):
            block = z - sign * (step + 1)

            @pl.when((block >= 0) & (block < line))
            def _():
                project(block)

    sum_copies = [
        remote(sums.at[z], sums.at[z], sum_send.at[step - 1], sum_recv.at[z], (y, x, core, (z + step) % line))
        for step in range(1, line)
    ]
    for sum_copy in sum_copies:
        sum_copy.start()
    for step in range(1, line):
        other_z = (z + step) % line
        landed(sums.at[other_z], sum_recv.at[other_z])
    total = sums[0]
    for other_z in range(1, line):
        total = total + sums[other_z]
    scale = lax.rsqrt(total / (line * columns) + norm_eps)
    for block in range(line):
        piece = scale[:, block * rows : (block + 1) * rows]
        tall = jnp.concatenate((piece, jnp.zeros((120, rows), jnp.float32)), axis=0)
        scale_out[block * rows : (block + 1) * rows, :] = jnp.transpose(tall)
    for sum_copy in sum_copies:
        sum_copy.wait_send()
    hidden.finish()
    slot_line.finish()
    for slot_copy in slot_copies:
        slot_copy.wait_send()
    for n in range(4):
        for kind in kinds:
            copy(kind, n).wait_send()


def start_exchange(hidden, w_query, w_key, w_value, w_out, slots, collective_id):
    line = 4
    any_ref = pl.BlockSpec(memory_space=pl.ANY)
    dma = pltpu.SemaphoreType.DMA
    rows, width = hidden.shape
    part, columns = w_query.shape
    low = jnp.bfloat16
    return pl.pallas_call(
        functools.partial(start_kernel, line),
        out_shape=(
            jax.ShapeDtypeStruct((line * rows, width), low),
            jax.ShapeDtypeStruct((8 * part, 3 * columns), low),
            jax.ShapeDtypeStruct((w_out.shape[0], 8 * w_out.shape[1]), low),
            jax.ShapeDtypeStruct((line * 8, slots.shape[0] // 8, slots.shape[1]), slots.dtype),
            jax.ShapeDtypeStruct((line * rows, 3 * columns), jnp.float32),
            jax.ShapeDtypeStruct((line * rows, 128), jnp.float32),
        ),
        in_specs=[any_ref] * 6,
        out_specs=[any_ref] * 4 + [pl.BlockSpec(memory_space=pltpu.VMEM)] * 2,
        scratch_shapes=[
            pltpu.VMEM((8 * part, 3 * columns), low),
            pltpu.VMEM((rows, width), low),
            pltpu.VMEM((line, 8, line * rows), jnp.float32),
            dma((6,)), dma((2, line)), dma((2, line)), dma((8, 4)), dma((8, 4)),
            dma((7,)), dma((8,)), dma((2, line)), dma((2, line)), dma((line - 1,)), dma((line,)),
        ],
        compiler_params=pltpu.CompilerParams(
            collective_id=collective_id, has_side_effects=True, vmem_limit_bytes=40 << 20
        ),
        cost_estimate=pl.CostEstimate(flops=0, bytes_accessed=150 << 20, transcendentals=0),
        name="start_exchange",
    )(hidden, w_query, w_key, w_value, w_out, slots)


class LineReduce:
    def __init__(self, part, up, down, send_sem, recv_sem, line):
        self.part, self.up, self.down = part, up, down
        self.send_sem, self.recv_sem, self.line = send_sem, recv_sem, line
        self.spot = place()

    def copy(self, sign, goal):
        y, x, core, z = self.spot
        lane = (1 - sign) // 2
        target = self.up if sign > 0 else self.down
        return remote(
            self.part.at[goal], target.at[goal], self.send_sem.at[lane, goal], self.recv_sem.at[lane, goal],
            (y, x, core, z + sign),
        )

    def order(self, i):
        z = self.spot[3]
        return either(self.line - 1 - i, i, z * 2 // self.line)

    def lead(self, goal):
        z = self.spot[3]
        pl.when((z == 0) & (goal > 0))(self.copy(1, goal).start)
        pl.when((z == self.line - 1) & (goal < z))(self.copy(-1, goal).start)

    def advance(self, unit, total_ref):
        z, line = self.spot[3], self.line
        for sign in (1, -1):
            goal = line - 1 - unit + z if sign > 0 else unit - line + 1 + z
            live = ((z > 0) & (goal < line)) if sign > 0 else ((z < line - 1) & (goal >= 0))
            inbox = self.up if sign > 0 else self.down

            @pl.when(live)
            def _():
                self.copy(sign, goal).wait_recv()
                if unit < line - 1:
                    self.part[goal] = (
                        self.part[goal].astype(jnp.float32) + inbox[goal].astype(jnp.float32)
                    ).astype(jnp.bfloat16)
                    self.copy(sign, goal).start()
                else:
                    total_ref[...] += inbox[goal].astype(jnp.float32)

    def finish(self):
        z = self.spot[3]

        def step(goal, carry):
            pl.when(goal > z)(self.copy(1, goal).wait_send)
            pl.when(goal < z)(self.copy(-1, goal).wait_send)
            return carry

        lax.fori_loop(0, self.line, step, 0)


def mixed_out_kernel(line, mixed_ref, w_ref, residual_ref, gain_ref, router_ref,
                     x_ref, hidden_ref, probs_ref, part, up, down, send_sem, recv_sem):
    rows, width = x_ref.shape
    greet(line)
    reduce = LineReduce(part, up, down, send_sem, recv_sem, line)
    z = reduce.spot[3]

    def term(i, carry):
        goal = reduce.order(i)
        first = pl.multiple_of(goal * rows, rows)
        for column in range(0, width, 512):
            piece = slice(column, column + 512)
            value = jnp.dot(mixed_ref[pl.ds(first, rows), :], w_ref[:, piece], preferred_element_type=jnp.float32)

            @pl.when(goal == z)
            def _():
                x_ref[:, piece] = value

            part[goal, :, piece] = value.astype(jnp.bfloat16)
        reduce.lead(goal)
        return carry

    lax.fori_loop(0, line, term, 0)
    for unit in range(1, line):
        reduce.advance(unit, x_ref)
    x_one = x_ref[...] + residual_ref[...].astype(jnp.float32)
    x_ref[...] = x_one
    scale = lax.rsqrt(jnp.mean(x_one * x_one, axis=-1, keepdims=True) + norm_eps)
    hidden = (x_one * scale * gain_ref[...]).astype(jnp.bfloat16)
    hidden_ref[...] = hidden
    logits = lax.dot_general(
        router_ref[...], hidden, (((1,), (1,)), ((), ())), preferred_element_type=jnp.float32
    )
    shifted = jnp.exp(logits - jnp.max(logits, axis=0, keepdims=True))
    probs_ref[...] = shifted / jnp.sum(shifted, axis=0, keepdims=True)
    reduce.finish()


def mixed_out(mixed, w_out, residual, gain, router_turned, collective_id):
    line = 4
    rows, width = residual.shape
    experts = router_turned.shape[0]
    vmem = pl.BlockSpec(memory_space=pltpu.VMEM)
    dma = pltpu.SemaphoreType.DMA
    block = pltpu.VMEM((line, rows, width), jnp.bfloat16)
    return pl.pallas_call(
        functools.partial(mixed_out_kernel, line),
        out_shape=(
            jax.ShapeDtypeStruct((rows, width), jnp.float32),
            jax.ShapeDtypeStruct((rows, width), jnp.bfloat16),
            jax.ShapeDtypeStruct((experts, rows), jnp.float32),
        ),
        in_specs=[vmem] * 5,
        out_specs=[vmem] * 3,
        scratch_shapes=[block, block, block, dma((2, line)), dma((2, line))],
        compiler_params=pltpu.CompilerParams(
            collective_id=collective_id, has_side_effects=True, vmem_limit_bytes=56 << 20
        ),
        cost_estimate=pl.CostEstimate(flops=0, bytes_accessed=150 << 20, transcendentals=0),
        name="mixed_out",
    )(mixed, w_out, residual, gain.reshape(1, width), router_turned)


class Butterfly:
    def __init__(self, data, total, from_core, from_x, from_y, from_z, sums, send_sem, recv_sem):
        self.data, self.total, self.sums = data, total, sums
        self.boxes = {"core": from_core, "x": from_x, "y": from_y}
        self.from_z, self.send_sem, self.recv_sem = from_z, send_sem, recv_sem
        y, x, core, z = self.spot = place()
        self.width = data.shape[1]
        self.near = {"core": (y, x, 1 - core, z), "x": (y, 1 - x, core, z), "y": (1 - y, x, core, z)}
        half, quarter, eighth = self.width // 2, self.width // 4, self.width // 8
        first = core * half
        self.kept = {"core": (first, half), "x": (first + x * quarter, quarter)}
        self.kept["y"] = (first + x * quarter + y * eighth, eighth)
        self.away = {
            "core": ((1 - core) * half, half),
            "x": (first + (1 - x) * quarter, quarter),
            "y": (first + x * quarter + (1 - y) * eighth, eighth),
        }

    def part(self, span):
        return pl.ds(pl.multiple_of(span[0], span[1]), span[1])

    def fold_copy(self, axis):
        lane = ("core", "x", "y").index(axis)
        return remote(
            self.data.at[:, self.part(self.away[axis])], self.boxes[axis], self.send_sem.at[lane],
            self.recv_sem.at[lane], self.near[axis],
        )

    def fold(self, axis):
        copy = self.fold_copy(axis)
        copy.start()
        copy.wait()
        self.data[:, self.part(self.kept[axis])] += self.boxes[axis][...]

    def line_step(self, step):
        y, x, core, z = self.spot
        other = (z + 1 - 2 * (z % 2)) if step == 0 else (z + 2) % 4
        piece = self.part(self.kept["y"])
        source = self.data.at[:, piece] if step == 0 else self.sums
        copy = remote(
            source, self.from_z.at[step], self.send_sem.at[3 + step], self.recv_sem.at[3 + step], (y, x, core, other)
        )
        copy.start()
        copy.wait()
        if step == 0:
            self.sums[...] = self.data[:, piece] + self.from_z[0]
        else:
            self.total[:, piece] = self.sums[...] + self.from_z[1]

    def unfold(self, axis):
        lane = 5 + ("core", "x", "y").index(axis)
        mine = self.total.at[:, self.part(self.kept[axis])]
        copy = remote(mine, mine, self.send_sem.at[lane], self.recv_sem.at[lane], self.near[axis])
        copy.start()
        copy.wait_send()
        landed(self.total.at[:, self.part(self.away[axis])], self.recv_sem.at[lane])

    def scratch(rows, width):
        low = jnp.float32
        return [
            pltpu.VMEM((rows, width // 2), low),
            pltpu.VMEM((rows, width // 4), low),
            pltpu.VMEM((rows, width // 8), low),
            pltpu.VMEM((2, rows, width // 8), low),
            pltpu.VMEM((rows, width // 8), low),
            pltpu.SemaphoreType.DMA((8,)),
            pltpu.SemaphoreType.DMA((8,)),
        ]


def greet_far(line):
    y, x, core, z = place()
    barrier = pltpu.get_barrier_semaphore()
    for near in ((y, x, 1 - core, z), (y, 1 - x, core, z), (1 - y, x, core, z)):
        pl.semaphore_signal(barrier, inc=1, device_id=peer(*near), device_id_type=MESH)
    for step in range(1, line):
        pl.semaphore_signal(barrier, inc=1, device_id=peer(y, x, core, (z + step) % line), device_id_type=MESH)
    pl.semaphore_wait(barrier, 3 + line - 1)


def back_gather_kernel(line, own_ref, sums_ref, out_ref, total_ref, data, local_sem, send_sem, recv_sem, *fly):
    greet_far(line)
    gather = LineGather(own_ref, out_ref, send_sem, recv_sem, line)
    local = pltpu.make_async_copy(own_ref, gather.view(gather.spot[3]), local_sem)
    gather.begin()
    local.start()
    data[...] = sums_ref[...]
    butterfly = Butterfly(data, total_ref, *fly)
    for axis in ("core", "x", "y"):
        butterfly.fold(axis)
    gather.advance(0)
    butterfly.line_step(0)
    gather.advance(1)
    butterfly.line_step(1)
    for axis in ("y", "x", "core"):
        butterfly.unfold(axis)
    gather.advance(2)
    gather.finish()
    local.wait()


def back_gather(own, sums, collective_id):
    line = 4
    any_ref = pl.BlockSpec(memory_space=pl.ANY)
    vmem = pl.BlockSpec(memory_space=pltpu.VMEM)
    dma = pltpu.SemaphoreType.DMA
    return pl.pallas_call(
        functools.partial(back_gather_kernel, line),
        out_shape=(
            jax.ShapeDtypeStruct((line * own.shape[0], own.shape[1]), own.dtype),
            jax.ShapeDtypeStruct(sums.shape, jnp.float32),
        ),
        in_specs=[any_ref, vmem],
        out_specs=[any_ref, vmem],
        scratch_shapes=[
            pltpu.VMEM(sums.shape, jnp.float32), dma(()), dma((2, line)), dma((2, line)),
            *Butterfly.scratch(*sums.shape),
        ],
        compiler_params=pltpu.CompilerParams(collective_id=collective_id, has_side_effects=True),
        cost_estimate=pl.CostEstimate(flops=0, bytes_accessed=150 << 20, transcendentals=0),
        name="back_gather",
    )(own, sums)


def last_kernel(line, joined_ref, weight_ref, hidden_ref, mixed_ref, attn_ref, residual_ref, gain_ref, x_grad_ref, gains_ref,
                input_ref, wq_ref, wk_ref, wv_ref, wo_ref, total_ref,
                part, up, down, stage, near, far_x, far_y, from_x, from_y, data,
                line_send, line_recv, stage_sem, near_sem, send_sem, recv_sem, *fly):
    y, x, core, z = place()
    rows, width = input_ref.shape
    columns = joined_ref.shape[1]
    half = rows // 2
    low = jnp.bfloat16
    greet_far(line)
    reduce = LineReduce(part, up, down, line_send, line_recv, line)

    def term(i, carry):
        goal = reduce.order(i)
        first = pl.multiple_of(goal * rows, rows)
        for column in range(0, width, 512):
            piece = slice(column, column + 512)
            value = across(joined_ref[pl.ds(first, rows), :], weight_ref[piece, :])

            @pl.when(goal == z)
            def _():
                input_ref[:, piece] = value

            part[goal, :, piece] = value.astype(low)
        reduce.lead(goal)
        return carry

    lax.fori_loop(0, line, term, 0)
    near_x, near_y, sibling = (y, 1 - x, core, z), (1 - y, x, core, z), (y, x, 1 - core, z)

    def terms(j, own, store):
        dy, dx = (j + 1) % 2, 1 - j // 2
        group = (y + dy) % 2 * 4 + (x + dx) % 2 * 2 + (core if own else 1 - core)
        span = pl.ds(pl.multiple_of(group * rows, rows), rows)
        turned_rows = hidden_ref[:, span]
        for column in range(0, columns, 512):
            piece = slice(column, column + 512)
            store(piece, turned(turned_rows, joined_ref[:, piece]))
        value = turned(mixed_ref[...], attn_ref[:, span])
        store(slice(columns, columns + rows), value[:rows])
        store(slice(columns + rows, columns + 2 * rows), value[rows:])

    def to_sibling(j):
        return remote(stage.at[j], near.at[j], stage_sem.at[j], near_sem.at[j], sibling)

    def away(j, carry):
        def store(piece, value):
            stage[j, :, piece] = value.astype(low)

        terms(j, False, store)
        to_sibling(j).start()
        return carry

    def own(j, carry):
        to_sibling(j).wait_recv()

        def store(piece, value):
            near[j, :, piece] = (value + near[j, :, piece].astype(jnp.float32)).astype(low)

        terms(j, True, store)
        return carry

    lax.fori_loop(0, 4, away, 0)
    lax.fori_loop(0, 4, own, 0)

    def line_rows(h):
        return pl.ds(h * half, half)

    def cross(kind):
        column, h, target, where = {
            "far_x": (0, 0, far_x, near_x),
            "far_y": (0, 1, far_y, near_y),
            "x0": (1, 0, from_x.at[line_rows(0)], near_x),
            "x1": (1, 1, from_x.at[line_rows(1)], near_x),
            "y0": (2, 0, from_y.at[line_rows(0)], near_y),
            "y1": (2, 1, from_y.at[line_rows(1)], near_y),
        }[kind]
        lane = kinds.index(kind)
        return remote(near.at[column, line_rows(h)], target, send_sem.at[lane], recv_sem.at[lane], where)

    kinds = ("far_x", "far_y", "x0", "y1", "x1", "y0")
    for kind in kinds[:4]:
        cross(kind).start()

    def add(column, h, source):
        near[column, line_rows(h), :] = (
            near[column, line_rows(h), :].astype(jnp.float32) + source[...].astype(jnp.float32)
        ).astype(low)

    reduce.advance(1, input_ref)
    cross("far_y").wait_recv()
    add(1, 1, far_y)
    cross("x1").start()
    cross("far_x").wait_recv()
    add(2, 0, far_x)
    cross("y0").start()
    reduce.advance(2, input_ref)
    for kind in kinds[2:]:
        cross(kind).wait_recv()
    for n, ref in enumerate((wq_ref, wk_ref, wv_ref, wo_ref, wo_ref)):
        count = columns // 3 if n < 3 else rows
        first = n * (columns // 3) if n < 3 else columns + (n - 3) * rows
        piece = slice(first, first + count)
        total = sum(r[:, piece].astype(jnp.float32) for r in (near.at[3], from_x, from_y))
        if n < 3:
            ref[...] = total
        else:
            ref[(n - 3) * rows : (n - 2) * rows, :] = total
    reduce.advance(3, input_ref)
    grad = input_ref[...]
    values = residual_ref[...].astype(jnp.float32)
    scale = lax.rsqrt(jnp.mean(values * values, axis=-1, keepdims=True) + norm_eps)
    gained = grad * gain_ref[...]
    inner = jnp.sum(gained * values, axis=-1, keepdims=True)
    data[...] = gains_ref[...]
    data[2:3, :] = jnp.sum(grad * values * scale, axis=0, keepdims=True)
    input_ref[...] = x_grad_ref[...] + scale * gained - values * (scale * scale * scale * inner / width)
    butterfly = Butterfly(data, total_ref, *fly)
    for axis in ("core", "x", "y"):
        butterfly.fold(axis)
    butterfly.line_step(0)
    butterfly.line_step(1)
    for axis in ("y", "x", "core"):
        butterfly.unfold(axis)
    reduce.finish()
    for j in range(4):
        to_sibling(j).wait_send()
    for kind in kinds:
        cross(kind).wait_send()


def last_exchange(joined, weight, hidden, mixed, attn, residual, gain, x_grad, gains, collective_id):
    line = 4
    rows, width = residual.shape
    columns = joined.shape[1] // 3
    low, wide = jnp.bfloat16, jnp.float32
    vmem = pl.BlockSpec(memory_space=pltpu.VMEM)
    dma = pltpu.SemaphoreType.DMA
    block = pltpu.VMEM((line, rows, width), low)
    one = pltpu.VMEM((rows, width), low)
    part = pltpu.VMEM((rows // 2, width), low)
    square = jax.ShapeDtypeStruct((rows, columns), wide)
    return pl.pallas_call(
        functools.partial(last_kernel, line),
        out_shape=(
            jax.ShapeDtypeStruct((rows, width), wide), square, square, square,
            jax.ShapeDtypeStruct((2 * rows, rows), wide),
            jax.ShapeDtypeStruct(gains.shape, wide),
        ),
        in_specs=[vmem] * 9,
        out_specs=[vmem] * 6,
        scratch_shapes=[
            block, block, block, pltpu.VMEM((4, rows, width), low), pltpu.VMEM((4, rows, width), low),
            part, part, one, one, pltpu.VMEM(gains.shape, wide),
            dma((2, line)), dma((2, line)), dma((4,)), dma((4,)), dma((6,)), dma((6,)),
            *Butterfly.scratch(*gains.shape),
        ],
        compiler_params=pltpu.CompilerParams(
            collective_id=collective_id, has_side_effects=True, vmem_limit_bytes=62 << 20
        ),
        cost_estimate=pl.CostEstimate(flops=0, bytes_accessed=250 << 20, transcendentals=0),
        name="last_exchange",
    )(joined, weight, hidden, mixed, attn, residual, gain.reshape(1, width), x_grad, gains)


def visible_block(row_paths, key_paths, key_valid, row_first):
    row_count = row_paths.shape[1]
    key_count = key_paths.shape[1]
    key_segment = key_paths[0][None, :]
    on_path = (
        (key_segment == row_paths[0][:, None])
        | (key_segment == row_paths[1][:, None])
        | (key_segment == row_paths[2][:, None])
    )
    row_place = row_first + lax.iota(jnp.int32, row_count)
    key_place = lax.iota(jnp.int32, key_count)
    earlier = key_place[None, :] <= row_place[:, None]
    return on_path & earlier & (key_valid[None, :] == 1) | (
        key_place[None, :] == row_place[:, None]
    )


def rotation(positions, head_dim):
    half = head_dim // 2
    freqs = jnp.exp(-jnp.log(rope_base) * 2.0 * lax.iota(jnp.float32, half) / head_dim)
    angles = positions.astype(jnp.float32)[:, None] * freqs[None, :]
    return (jnp.cos(angles), jnp.sin(angles))


def visible_bias(row_first, row_paths, row_places, key_segment, key_valid, key_places):
    on_path = (key_segment == row_paths[0]) | (key_segment == row_paths[1]) | (key_segment == row_paths[2])
    seen = (on_path & (key_places <= row_places) & (key_valid == 1)) | (key_places == row_places)
    return jnp.where(seen, 0.0, masked_score)


def attend_kernel(step, raw_ref, scale_ref, gain_ref, cos_ref, sin_ref, column_ref, line_ref,
                  query_ref, key_ref, value_ref, mixed_ref, log_ref, bias, logs):
    seq, columns = query_ref.shape
    heads = columns // HD

    def prepare(i, carry):
        rows = pl.ds(pl.multiple_of(i * step, step), step)
        cosine, sine = cos_ref[rows, :], sin_ref[rows, :]
        for n, ref in enumerate((query_ref, key_ref)):
            scale = scale_ref[rows, n : n + 1]
            for h in range(heads):
                span = slice(h * HD, (h + 1) * HD)
                values = raw_ref[rows, n * columns + h * HD : n * columns + (h + 1) * HD]
                values = values * scale * gain_ref[n : n + 1, span]
                turn = pltpu.roll(values, HD // 2, 1)
                ref[rows, span] = (values * cosine + turn * sine).astype(jnp.bfloat16)
        value_ref[rows, :] = raw_ref[rows, 2 * columns :].astype(jnp.bfloat16)
        return carry

    lax.fori_loop(0, seq // step, prepare, 0)
    for i in range(seq // step):
        rows = slice(i * step, (i + 1) * step)
        wide = (i + 1) * step
        places = lax.broadcasted_iota(jnp.int32, (step, wide), 0) + i * step
        bias[:, :wide] = visible_bias(
            i * step,
            [column_ref[rows, n : n + 1] for n in range(3)],
            places,
            line_ref[0:1, :wide],
            line_ref[3:4, :wide],
            lax.broadcasted_iota(jnp.int32, (step, wide), 1),
        )

        def head(h, carry):
            span = pl.ds(pl.multiple_of(h * HD, HD), HD)
            scores = across(query_ref[rows, span], key_ref[:wide, span]) * HD ** (-0.5) + bias[:, :wide]
            top = jnp.max(scores, axis=1, keepdims=True)
            weights = jnp.exp(scores - top)
            total = jnp.sum(weights, axis=1, keepdims=True)
            low = (weights / total).astype(jnp.bfloat16)
            mixed = jnp.dot(low, value_ref[:wide, span], preferred_element_type=jnp.float32)
            mixed_ref[rows, span] = mixed.astype(jnp.bfloat16)
            lanes = lax.broadcasted_iota(jnp.int32, (step, 128), 1)
            logs[...] = jnp.where(lanes == h, top + jnp.log(total), logs[...])
            return carry

        logs[...] = jnp.zeros_like(logs)
        lax.fori_loop(0, heads, head, 0)
        log_ref[:, rows] = jnp.transpose(logs[...])[: log_ref.shape[0]]


def attend(raw, scales, gains, cosine, sine, path_columns, path_lines):
    seq = raw.shape[0]
    columns = raw.shape[1] // 3
    step = min(256, seq)
    vmem = pl.BlockSpec(memory_space=pltpu.VMEM)
    low = jax.ShapeDtypeStruct((seq, columns), jnp.bfloat16)
    return pl.pallas_call(
        functools.partial(attend_kernel, step),
        out_shape=(low, low, low, low, jax.ShapeDtypeStruct((8, seq), jnp.float32)),
        in_specs=[vmem] * 7,
        out_specs=[vmem] * 5,
        scratch_shapes=[pltpu.VMEM((step, seq), jnp.float32), pltpu.VMEM((step, 128), jnp.float32)],
        compiler_params=pltpu.CompilerParams(vmem_limit_bytes=50 << 20),
        cost_estimate=pl.CostEstimate(
            flops=4 * seq * seq * columns, bytes_accessed=16 * seq * columns, transcendentals=seq * seq
        ),
        name="attend",
    )(raw, scales, gains, cosine, sine, path_columns, path_lines)


def attend_back_kernel(step, grad_ref, w_ref, query_ref, key_ref, value_ref, log_ref, cos_ref, sin_ref,
                       column_ref, line_ref, dq_ref, dk_ref, dv_ref, bias, mixed):
    seq, columns = query_ref.shape
    heads = columns // HD
    dk_ref[...] = jnp.zeros_like(dk_ref)
    dv_ref[...] = jnp.zeros_like(dv_ref)

    def unturn(values, rows):
        return values * cos_ref[rows, :] - pltpu.roll(values, HD // 2, 1) * sin_ref[rows, :]

    for i in range(seq // step):
        rows = slice(i * step, (i + 1) * step)
        wide = (i + 1) * step
        mixed[...] = across(grad_ref[rows, :], w_ref[...]).astype(jnp.bfloat16)
        places = lax.broadcasted_iota(jnp.int32, (wide, step), 1) + i * step
        bias[:wide, :] = visible_bias(
            i * step,
            [line_ref[n : n + 1, rows] for n in range(3)],
            places,
            column_ref[:wide, 0:1],
            column_ref[:wide, 3:4],
            lax.broadcasted_iota(jnp.int32, (wide, step), 0),
        )

        def head(h, carry):
            span = pl.ds(pl.multiple_of(h * HD, HD), HD)
            query, key, grad = query_ref[rows, span], key_ref[:wide, span], mixed[:, span]
            scores = across(key, query) * HD ** (-0.5) + bias[:wide, :]
            weights = jnp.exp(scores - log_ref[pl.ds(h, 1), rows])
            grad_weights = across(value_ref[:wide, span], grad)
            inner = jnp.sum(weights * grad_weights, axis=0, keepdims=True)
            grad_scores = (weights * (grad_weights - inner)).astype(jnp.bfloat16)
            dq_ref[rows, span] = unturn(turned(grad_scores, key) * HD ** (-0.5), rows)
            dk_ref[:wide, span] += jnp.dot(grad_scores, query, preferred_element_type=jnp.float32)
            dv_ref[:wide, span] += jnp.dot(
                weights.astype(jnp.bfloat16), grad, preferred_element_type=jnp.float32
            )
            return carry

        lax.fori_loop(0, heads, head, 0)
    for i in range(seq // step):
        rows = slice(i * step, (i + 1) * step)
        for h in range(heads):
            span = slice(h * HD, (h + 1) * HD)
            dk_ref[rows, span] = unturn(dk_ref[rows, span] * HD ** (-0.5), rows)


def attend_back(grads, w_out, query, key, value, logs, cosine, sine, path_columns, path_lines):
    seq, columns = query.shape
    step = min(256, seq)
    vmem = pl.BlockSpec(memory_space=pltpu.VMEM)
    wide = jax.ShapeDtypeStruct((seq, columns), jnp.float32)
    return pl.pallas_call(
        functools.partial(attend_back_kernel, step),
        out_shape=(wide, wide, wide),
        in_specs=[vmem] * 10,
        out_specs=[vmem] * 3,
        scratch_shapes=[pltpu.VMEM((seq, step), jnp.float32), pltpu.VMEM((step, columns), jnp.bfloat16)],
        compiler_params=pltpu.CompilerParams(vmem_limit_bytes=56 << 20),
        cost_estimate=pl.CostEstimate(
            flops=10 * seq * seq * columns, bytes_accessed=24 * seq * columns, transcendentals=seq * seq
        ),
        name="attend_back",
    )(grads, w_out, query, key, value, logs, cosine, sine, path_columns, path_lines)


def rms_apply(values, gain):
    scale = lax.rsqrt(jnp.mean(values * values, axis=-1, keepdims=True) + norm_eps)
    return (values * scale * gain, scale)


def rms_grad(values, scale, gain, grads, inner, width):
    grad_values = scale * gain * grads - values * scale**3 * inner / width
    grad_gain = jnp.sum(grads * values * scale, axis=0)
    return (grad_values, grad_gain)


def tensor_sums(pair):
    return lax.psum((pair[0], pair[1]), "tensor")


def heads_to_rows(term, rows):
    return lax.psum_scatter(
        term(jnp.int32(0), rows * lax.axis_size("tensor")).astype(jnp.bfloat16),
        "tensor",
        scatter_dimension=0,
        tiled=True,
    ).astype(jnp.float32)


def sum_over_dp(rows):
    dp = lax.axis_size("dp")
    pieces = rows.reshape(dp, rows.shape[0] // dp, rows.shape[1])
    return lax.psum_scatter(pieces, "dp", scatter_dimension=0, tiled=False)


def sum_over_tensor(part):
    return lax.psum_scatter(part, "tensor", scatter_dimension=0, tiled=True)


def body(
    residual,
    attn_gain,
    w_query,
    w_key,
    w_value,
    query_gain,
    key_gain,
    w_out,
    moe_gain,
    router,
    w_gate,
    w_up,
    w_down,
    segment_path,
    token_valid,
    routes,
    route_order,
    cotangent,
):
    tensor_rank = lax.axis_index("tensor")
    tok_dev, width = residual.shape
    seq_len = segment_path.shape[1]
    top_count = routes.shape[1]
    experts = router.shape[1]
    local_experts = w_gate.shape[0]
    dp_groups = experts // local_experts
    capacity = 9 * tok_dev * top_count // (8 * experts)
    full_width = H * HD
    everyone = ("dp", "tensor")
    direct = dp_groups == 8 and lax.axis_size("tensor") == 4
    first_expert = lax.axis_index("dp") * local_experts
    slot_rows = padded(capacity, 8)
    valid_dev = lax.dynamic_slice_in_dim(token_valid, tensor_rank * tok_dev, tok_dev)
    slots_own = slot_table(routes, route_order, valid_dev, experts, capacity)
    cots_all = lax.all_gather(cotangent, everyone, axis=0, tiled=True)
    head_cols = w_query.shape[1]
    residual_float = residual.astype(jnp.float32)
    normed_one, scale_one = rms_apply(residual_float, attn_gain)
    hidden = normed_one.astype(jnp.bfloat16)
    path_lines = jnp.concatenate((segment_path, token_valid[None]), axis=0)
    path_columns = path_lines.T
    positions = jnp.sum(visible_block(segment_path, segment_path, token_valid, 0).astype(jnp.int32), axis=1) - 1
    cosine, sine = rotation(positions, HD)
    cosine = jnp.concatenate((cosine, cosine), axis=1)
    sine = jnp.concatenate((-sine, sine), axis=1)
    if direct:
        hidden, cosine, sine, path_columns = lax.optimization_barrier((hidden, cosine, sine, path_columns))
        hidden_all, joined_weight, gathered_out, slots, projected, scales = start_exchange(
            hidden, w_query, w_key, w_value, w_out, slots_own, 3
        )
        slots = jnp.swapaxes(slots.reshape(4, 8, local_experts, tok_dev), 0, 1).reshape(32, local_experts, tok_dev)
    else:
        hidden_all = lax.all_gather(hidden, "tensor", axis=0, tiled=True)
        joined_weight = jnp.concatenate(
            [lax.all_gather(w, "dp", axis=0, tiled=True) for w in (w_query, w_key, w_value)], axis=1
        )
        gathered_out = lax.all_gather(w_out, "dp", axis=1, tiled=True)
        slots_all = lax.all_gather(slots_own.astype(jnp.bfloat16), everyone, axis=0)
        slots = lax.dynamic_slice_in_dim(slots_all, first_expert, local_experts, 1).astype(jnp.int32)
    if not direct:
        projected = jnp.dot(hidden_all, joined_weight, preferred_element_type=jnp.float32)
        squares = [jnp.sum(projected[:, n * head_cols : (n + 1) * head_cols] ** 2, axis=1) for n in range(2)]
        scales = lax.rsqrt(jnp.stack(tensor_sums(squares), axis=1) / full_width + norm_eps)
    blocks = slots.shape[0]
    q_raw = projected[:, :head_cols]
    k_raw = projected[:, head_cols : 2 * head_cols]
    query_scale, key_scale = scales[:, 0:1], scales[:, 1:2]
    query_gain_dev = lax.dynamic_slice_in_dim(query_gain, tensor_rank * head_cols, head_cols)
    key_gain_dev = lax.dynamic_slice_in_dim(key_gain, tensor_rank * head_cols, head_cols)
    query_low, key_low, value_low, attn_mixed, log_totals = attend(
        projected,
        scales,
        jnp.stack((query_gain_dev, key_gain_dev)),
        cosine,
        sine,
        path_columns,
        path_lines,
    )
    if direct:
        x_one, hidden_two, gates_own = mixed_out(attn_mixed, gathered_out, residual, moe_gain, router.T, 4)
        probs = gates_own.T
    else:

        def attn_term(first_row, row_count):
            return jnp.dot(attn_mixed, gathered_out, preferred_element_type=jnp.float32)

        x_one = residual_float + heads_to_rows(attn_term, tok_dev)
        hidden_two = rms_apply(x_one, moe_gain)[0].astype(jnp.bfloat16)
        logits = jnp.dot(hidden_two, router, preferred_element_type=jnp.float32)
        probs = jax.nn.softmax(logits, axis=-1)
        gates_own = probs.T
    scale_two = lax.rsqrt(jnp.mean(x_one * x_one, axis=-1, keepdims=True) + norm_eps)
    if direct:
        x_slots, c_slots, gate_slots = gather_dispatch(slots, hidden_two, gates_own, cots_all, slot_rows, 1)
    else:
        gates_all = lax.all_gather(gates_own, everyone, axis=0)
        rows_all = lax.all_gather(hidden_two, everyone, axis=0, tiled=True)
        gates = lax.dynamic_slice_in_dim(gates_all, first_expert, local_experts, 1)
        x_slots, gate_slots = dispatch(slots, gates, rows_all, slot_rows)
        c_slots = dispatch(slots, None, cots_all, slot_rows)
    outs, grads, pre, gated = expert_pass(
        first_expert.reshape(1),
        x_slots,
        c_slots,
        gate_slots,
        w_gate,
        w_up,
        w_down,
        blocks,
        padded(slot_rows, 16),
    )
    if direct:
        grad_rows, out_part = reduce_all(slots, outs, grads, 2)
    else:
        out_part, grad_part = combine(slots, outs, grads)
        grad_rows = sum_over_tensor(sum_over_dp(grad_part)).astype(jnp.float32)
    out_part = sum_over_dp(out_part)
    grad_out = cotangent.astype(jnp.float32)
    grad_hidden_two = grad_rows[:, :width]
    grad_probs = grad_rows[:, width : width + experts]
    grad_logits = probs * (grad_probs - jnp.sum(probs * grad_probs, axis=-1, keepdims=True))
    router_float = router.astype(jnp.float32)
    grad_hidden_two = grad_hidden_two + lax.dot_general(
        grad_logits, router_float, (((1,), (1,)), ((), ())), precision=lax.Precision.HIGHEST
    )
    grad_router_part = lax.dot_general(
        grad_logits,
        hidden_two.astype(jnp.float32),
        (((0,), (0,)), ((), ())),
        precision=lax.Precision.HIGHEST,
    )
    inner_two = jnp.sum(grad_hidden_two * moe_gain * x_one, axis=-1, keepdims=True)
    grad_norm_two, grad_moe_gain_part = rms_grad(
        x_one, scale_two, moe_gain, grad_hidden_two, inner_two, width
    )
    grad_x_one = grad_out + grad_norm_two
    grad_attn_low = grad_x_one.astype(jnp.bfloat16)
    early_sums = jnp.concatenate(
        (grad_router_part, grad_moe_gain_part[None], jnp.zeros((7, width), jnp.float32)), axis=0
    )
    if direct:
        grad_attn_all, early_sums = back_gather(grad_attn_low, early_sums, 5)
    else:
        grad_attn_all = lax.all_gather(grad_attn_low, "tensor", axis=0, tiled=True)
        early_sums = lax.psum(early_sums, everyone)
    grad_q_norm, grad_k_norm, grad_value_all = attend_back(
        grad_attn_all,
        gathered_out,
        query_low,
        key_low,
        value_low,
        log_totals,
        cosine,
        sine,
        path_columns,
        path_lines,
    )
    query_inner, key_inner = tensor_sums(
        (
            jnp.sum(grad_q_norm * query_gain_dev * q_raw, axis=1),
            jnp.sum(grad_k_norm * key_gain_dev * k_raw, axis=1),
        )
    )
    grad_q_raw, grad_query_gain_dev = rms_grad(
        q_raw, query_scale, query_gain_dev, grad_q_norm, query_inner[:, None], full_width
    )
    grad_k_raw, grad_key_gain_dev = rms_grad(
        k_raw, key_scale, key_gain_dev, grad_k_norm, key_inner[:, None], full_width
    )
    grad_joined = jnp.concatenate(
        (grad_q_raw, grad_k_raw, grad_value_all), axis=1
    ).astype(jnp.bfloat16)
    zero_width = jnp.zeros((full_width,), jnp.float32)
    grad_query_full = lax.dynamic_update_slice_in_dim(
        zero_width, grad_query_gain_dev, tensor_rank * head_cols, 0
    )
    grad_key_full = lax.dynamic_update_slice_in_dim(
        zero_width, grad_key_gain_dev, tensor_rank * head_cols, 0
    )
    if direct:
        gains = jnp.concatenate(
            (grad_query_full[None], grad_key_full[None], jnp.zeros((6, width), jnp.float32)), axis=0
        )
        grad_input, grad_w_query, grad_w_key, grad_w_value, grad_w_out, gains = last_exchange(
            grad_joined,
            joined_weight,
            hidden_all,
            attn_mixed,
            grad_attn_all,
            residual,
            attn_gain,
            grad_x_one,
            gains,
            6,
        )
    else:
        grad_joined_weight = lax.dot_general(
            hidden_all, grad_joined, (((0,), (0,)), ((), ())), preferred_element_type=jnp.float32
        ).astype(jnp.bfloat16)
        grad_out_weight = lax.dot_general(
            attn_mixed, grad_attn_all, (((0,), (0,)), ((), ())), preferred_element_type=jnp.float32
        ).astype(jnp.bfloat16)

        def back_term(first_row, row_count):
            return lax.dot_general(
                grad_joined, joined_weight, (((1,), (1,)), ((), ())), preferred_element_type=jnp.float32
            )

        grad_hidden = heads_to_rows(back_term, tok_dev)
        inner_one = jnp.sum(grad_hidden * attn_gain * residual_float, axis=-1, keepdims=True)
        grad_norm_one, grad_attn_gain_part = rms_grad(
            residual_float, scale_one, attn_gain, grad_hidden, inner_one, width
        )
        grad_input = grad_x_one + grad_norm_one
        grad_w_query, grad_w_key, grad_w_value = (
            lax.psum_scatter(
                grad_joined_weight[:, n * head_cols : (n + 1) * head_cols],
                "dp",
                scatter_dimension=0,
                tiled=True,
            ).astype(jnp.float32)
            for n in range(3)
        )
        grad_w_out = lax.psum_scatter(
            grad_out_weight, "dp", scatter_dimension=1, tiled=True
        ).astype(jnp.float32)
        gains = lax.psum(jnp.stack((grad_query_full, grad_key_full, grad_attn_gain_part)), everyone)
    out_part, pre, grad_input = lax.optimization_barrier((out_part, pre, grad_input))
    grad_w_gate, grad_w_up, grad_w_down = weight_grads(x_slots, c_slots, pre, gated)
    moe_out, grad_w_gate, grad_w_up, grad_w_down = lax.optimization_barrier(
        (sum_over_tensor(out_part), grad_w_gate, grad_w_up, grad_w_down)
    )
    block_out = (x_one + moe_out.astype(jnp.float32)).astype(jnp.bfloat16)
    return (
        block_out,
        grad_input,
        gains[2],
        grad_w_query,
        grad_w_key,
        grad_w_value,
        gains[0],
        gains[1],
        grad_w_out,
        early_sums[experts],
        early_sums[:experts].T,
        grad_w_gate,
        grad_w_up,
        grad_w_down,
    )


def solution(mesh):
    in_specs = (
        P(("dp", "tensor"), None),
        P(),
        P("dp", "tensor"),
        P("dp", "tensor"),
        P("dp", "tensor"),
        P(),
        P(),
        P("tensor", "dp"),
        P(),
        P(),
        P("dp", None, "tensor"),
        P("dp", None, "tensor"),
        P("dp", "tensor", None),
        P(None, "dp"),
        P("dp"),
        P(("dp", "tensor"), None),
        P(("dp", "tensor"), None),
        P(("dp", "tensor"), None),
    )
    out_specs = (
        P(("dp", "tensor"), None),
        P(("dp", "tensor"), None),
        P(),
        P("dp", "tensor"),
        P("dp", "tensor"),
        P("dp", "tensor"),
        P(),
        P(),
        P("tensor", "dp"),
        P(),
        P(),
        P("dp", None, "tensor"),
        P("dp", None, "tensor"),
        P("dp", "tensor", None),
    )
    return jax.shard_map(body, mesh=mesh, in_specs=in_specs, out_specs=out_specs, check_vma=False)
```

```python
import functools

import jax
import jax.numpy as jnp
from jax import lax
from jax.experimental import pallas as pl
from jax.experimental.pallas import tpu as pltpu
from jax.sharding import PartitionSpec as P

H = 16
HD = 128


norm_eps = 1e-05
rope_base = 10000.0
masked_score = -1e30


def padded(count, step):
    return -(-count // step) * step


def slot_table(routes, route_order, valid, experts, capacity):
    far = jnp.int32(1 << 30)
    expert = lax.iota(jnp.int32, experts)[:, None, None]
    hits = (routes[None] == expert) & (valid[None, :, None] == 1)
    order = jnp.min(jnp.where(hits, route_order[None], far), axis=-1)
    ranks = jnp.sum((order[:, None, :] < order[:, :, None]).astype(jnp.int32), axis=-1)
    return jnp.where((order < far) & (ranks < capacity), ranks, -1)


def slot_hits(slots, expert, rows):
    tokens = slots.shape[-1]
    return lax.broadcasted_iota(jnp.int32, (rows, tokens), 0) == slots[expert : expert + 1, :]


def dispatch_kernel(slots_ref, gates_ref, rows_ref, x_ref, gate_ref):
    pair, experts, tokens = slots_ref.shape
    rows = x_ref.shape[1] // pair
    width = rows_ref.shape[1]
    picks = []
    for b in range(pair):
        slots = slots_ref[b]
        pieces = []
        for e in range(experts):
            hit = slot_hits(slots, e, rows)
            pieces.append(hit.astype(jnp.float32))
            if gate_ref is not None:
                gate = jnp.sum(jnp.where(hit, gates_ref[b, e : e + 1, :], 0.0), axis=1, keepdims=True)
                gate_ref[e, b * rows : (b + 1) * rows, :] = jnp.broadcast_to(gate, (rows, 128))
        picks.append(jnp.concatenate(pieces, axis=0).astype(jnp.bfloat16))
    step = min(512, width)
    for first in range(0, width, step):
        parts = [
            jnp.dot(
                picks[b],
                rows_ref[b * tokens : (b + 1) * tokens, first : first + step],
                preferred_element_type=jnp.float32,
            )
            for b in range(pair)
        ]
        for e in range(experts):
            x_ref[e, :, first : first + step] = jnp.concatenate(
                [part[e * rows : (e + 1) * rows] for part in parts], axis=0
            ).astype(jnp.bfloat16)


def plain_dispatch_kernel(slots_ref, rows_ref, x_ref):
    dispatch_kernel(slots_ref, None, rows_ref, x_ref, None)


def dispatch(slots, gates, rows_all, rows):
    blocks, experts, tokens = slots.shape
    width = rows_all.shape[1]
    pair = 2
    out = jax.ShapeDtypeStruct((experts, blocks * rows, width), jnp.bfloat16)
    table = pl.BlockSpec((pair, experts, tokens), lambda i: (i, 0, 0))
    source = pl.BlockSpec((pair * tokens, width), lambda i: (i, 0))
    target = pl.BlockSpec((experts, pair * rows, width), lambda i: (0, i, 0))
    settings = dict(
        grid=(blocks // pair,),
        compiler_params=pltpu.CompilerParams(vmem_limit_bytes=50 << 20),
        cost_estimate=pl.CostEstimate(
            flops=2 * blocks * experts * rows * tokens * width,
            bytes_accessed=2 * blocks * (tokens + experts * rows) * width,
            transcendentals=0,
        ),
    )
    if gates is None:
        return pl.pallas_call(
            plain_dispatch_kernel, out_shape=out, in_specs=[table, source], out_specs=target, name="pick", **settings
        )(slots, rows_all)
    return pl.pallas_call(
        dispatch_kernel,
        out_shape=(out, jax.ShapeDtypeStruct((experts, blocks * rows, 128), jnp.float32)),
        in_specs=[table, table, source],
        out_specs=[target, pl.BlockSpec((experts, pair * rows, 128), lambda i: (0, i, 0))],
        name="dispatch",
        **settings,
    )(slots, gates, rows_all)


def turned(left, right):
    return lax.dot_general(left, right, (((0,), (0,)), ((), ())), preferred_element_type=jnp.float32)


def across(left, right):
    return lax.dot_general(left, right, (((1,), (1,)), ((), ())), preferred_element_type=jnp.float32)


def expert_kernel(rows, first_ref, x_ref, c_ref, gate_ref, wg_ref, wu_ref, wd_ref,
                  o_ref, dx_ref, pre_ref, gated_ref):
    expert = pl.program_id(0)
    tile, width = x_ref.shape[1:]
    units = wg_ref.shape[2]
    room = o_ref.shape[2]
    blocks = tile // rows
    gate = gate_ref[0, :, 0:1]
    x = x_ref[0]
    c = c_ref[0]
    gate_pre = jnp.dot(x, wg_ref[0], preferred_element_type=jnp.float32)
    up_pre = jnp.dot(x, wu_ref[0], preferred_element_type=jnp.float32)
    back = across(c, wd_ref[0])
    sig = jax.nn.sigmoid(gate_pre)
    silu = gate_pre * sig
    act = (silu * up_pre).astype(jnp.bfloat16)
    act_float = act.astype(jnp.float32)
    grad_gate = jnp.sum(act_float * back, axis=1, keepdims=True)
    grad_act = back * gate
    grad_gate_pre = (grad_act * up_pre * sig * (1.0 + gate_pre * (1.0 - sig))).astype(jnp.bfloat16)
    grad_up_pre = (grad_act * silu).astype(jnp.bfloat16)
    gated = (act_float * gate).astype(jnp.bfloat16)

    def spread(values):
        values = values.reshape(blocks, rows, values.shape[1])
        if room > rows:
            empty = jnp.zeros((blocks, room - rows, values.shape[2]), jnp.float32)
            values = jnp.concatenate((values, empty), axis=1)
        return values.astype(jnp.bfloat16)

    step = min(512, width)
    for first in range(0, width, step):
        part = slice(first, first + step)
        out = jnp.dot(act, wd_ref[0, :, part], preferred_element_type=jnp.float32) * gate
        o_ref[:, 0, :, part] = spread(out)
        grad = across(grad_gate_pre, wg_ref[0, part, :]) + across(grad_up_pre, wu_ref[0, part, :])
        dx_ref[:, 0, :, part] = spread(grad)
    lanes = lax.broadcasted_iota(jnp.int32, (tile, 128), 1)
    dx_ref[:, 0, :, width:] = spread(jnp.where(lanes == first_ref[0] + expert, grad_gate, 0.0))

    pre_ref[0, :, :units] = grad_gate_pre
    pre_ref[0, :, units:] = grad_up_pre
    gated_ref[0] = gated


def weight_terms(x_ref, c_ref, pre_ref, gated_ref, gate_ref, up_ref, down_ref):
    units = gated_ref.shape[1]
    width = x_ref.shape[1]
    step = min(512, width)
    for first in range(0, width, step):
        part = slice(first, first + step)
        both = turned(x_ref[:, part], pre_ref[...])
        gate_ref[part, :] = both[:, :units]
        up_ref[part, :] = both[:, units:]
        down_ref[:, part] = turned(gated_ref[...], c_ref[:, part])


def weight_kernel(x_ref, c_ref, pre_ref, gated_ref, gate_ref, up_ref, down_ref):
    weight_terms(*(r.at[0] for r in (x_ref, c_ref, pre_ref, gated_ref, gate_ref, up_ref, down_ref)))


def weight_grads(x_slots, c_slots, pre, gated):
    experts, total, width = x_slots.shape
    units = gated.shape[2]
    step = min(512, width)
    part = pl.BlockSpec((1, total, step), lambda e, j: (e, 0, j))
    tall = pl.BlockSpec((1, step, units), lambda e, j: (e, j, 0))
    return pl.pallas_call(
        weight_kernel,
        grid=(experts, width // step),
        out_shape=(
            jax.ShapeDtypeStruct((experts, width, units), jnp.float32),
            jax.ShapeDtypeStruct((experts, width, units), jnp.float32),
            jax.ShapeDtypeStruct((experts, units, width), jnp.float32),
        ),
        in_specs=[
            part, part,
            pl.BlockSpec((1, total, 2 * units), lambda e, j: (e, 0, 0)),
            pl.BlockSpec((1, total, units), lambda e, j: (e, 0, 0)),
        ],
        out_specs=[tall, tall, pl.BlockSpec((1, units, step), lambda e, j: (e, 0, j))],
        compiler_params=pltpu.CompilerParams(vmem_limit_bytes=50 << 20),
        cost_estimate=pl.CostEstimate(
            flops=6 * experts * total * width * units,
            bytes_accessed=4 * experts * total * width + 12 * experts * width * units,
            transcendentals=0,
        ),
        name="weight_grads",
    )(x_slots, c_slots, pre, gated)


def expert_pass(first_expert, x_slots, c_slots, gate_slots, w_gate, w_up, w_down, blocks, room):
    experts, total, width = x_slots.shape
    units = w_gate.shape[2]
    rows = total // blocks
    group = next(n for n in (16, 8, 4, 2, 1) if blocks % n == 0 and (n * rows <= 768 or n == 1))
    tile = group * rows
    extra = 128
    tall = pl.BlockSpec((1, width, units), lambda e, r, _: (e, 0, 0))
    wide = pl.BlockSpec((1, units, width), lambda e, r, _: (e, 0, 0))
    slot = pl.BlockSpec((1, tile, width), lambda e, r, _: (e, r, 0))
    kernel = functools.partial(expert_kernel, rows)
    return pl.pallas_call(
        kernel,
        grid_spec=pltpu.PrefetchScalarGridSpec(
            num_scalar_prefetch=1,
            grid=(experts, total // tile),
            in_specs=[slot, slot, pl.BlockSpec((1, tile, 128), lambda e, r, _: (e, r, 0)), tall, tall, wide],
            out_specs=[
                pl.BlockSpec((group, 1, room, width), lambda e, r, _: (r, e, 0, 0)),
                pl.BlockSpec((group, 1, room, width + extra), lambda e, r, _: (r, e, 0, 0)),
                pl.BlockSpec((1, tile, 2 * units), lambda e, r, _: (e, r, 0)),
                pl.BlockSpec((1, tile, units), lambda e, r, _: (e, r, 0)),
            ],
        ),
        out_shape=(
            jax.ShapeDtypeStruct((blocks, experts, room, width), jnp.bfloat16),
            jax.ShapeDtypeStruct((blocks, experts, room, width + extra), jnp.bfloat16),
            jax.ShapeDtypeStruct((experts, total, 2 * units), jnp.bfloat16),
            jax.ShapeDtypeStruct((experts, total, units), jnp.bfloat16),
        ),
        compiler_params=pltpu.CompilerParams(vmem_limit_bytes=60 << 20),
        cost_estimate=pl.CostEstimate(
            flops=12 * experts * total * width * units,
            bytes_accessed=8 * experts * total * width + 6 * experts * width * units,
            transcendentals=experts * total * units,
        ),
        name="experts",
    )(first_expert, x_slots, c_slots, gate_slots, w_gate, w_up, w_down)


def combine_kernel(slots_ref, o_ref, dx_ref, out_ref, grad_ref):
    _, experts, tokens = slots_ref.shape
    room, width = o_ref.shape[2:]
    slots = slots_ref[0]
    picks = jnp.concatenate(
        [slot_hits(slots, e, room).astype(jnp.float32) for e in range(experts)], axis=0
    ).astype(jnp.bfloat16)
    for source, target in ((o_ref, out_ref), (dx_ref, grad_ref)):
        columns = target.shape[1]
        for first in range(0, columns, 512):
            part = slice(first, min(first + 512, columns))
            values = source[0, :, :, part].reshape(experts * room, part.stop - first)
            target[:, part] = turned(picks, values).astype(jnp.bfloat16)


def combine(slots, outs, grads):
    blocks, experts, tokens = slots.shape
    room, width = outs.shape[2:]
    wider = grads.shape[3]
    return pl.pallas_call(
        combine_kernel,
        grid=(blocks,),
        out_shape=(
            jax.ShapeDtypeStruct((blocks * tokens, width), jnp.bfloat16),
            jax.ShapeDtypeStruct((blocks * tokens, wider), jnp.bfloat16),
        ),
        in_specs=[
            pl.BlockSpec((1, experts, tokens), lambda i: (i, 0, 0)),
            pl.BlockSpec((1, experts, room, width), lambda i: (i, 0, 0, 0)),
            pl.BlockSpec((1, experts, room, wider), lambda i: (i, 0, 0, 0)),
        ],
        out_specs=[
            pl.BlockSpec((tokens, width), lambda i: (i, 0)),
            pl.BlockSpec((tokens, wider), lambda i: (i, 0)),
        ],
        compiler_params=pltpu.CompilerParams(vmem_limit_bytes=50 << 20),
        cost_estimate=pl.CostEstimate(
            flops=2 * blocks * experts * room * tokens * (width + wider),
            bytes_accessed=2 * blocks * (tokens + experts * room) * (width + wider),
            transcendentals=0,
        ),
        name="combine",
    )(slots, outs, grads)


MESH = pl.DeviceIdType.MESH


def place():
    dp, z = lax.axis_index("dp"), lax.axis_index("tensor")
    return dp // 4, dp // 2 % 2, dp % 2, z


def peer(y, x, core, z):
    return (y * 4 + x * 2 + core, z)


def block_of(y, x, core, z):
    return (y * 4 + x * 2 + core) * 4 + z


def greet(line):
    y, x, core, z = place()
    barrier = pltpu.get_barrier_semaphore()
    for near in ((y, x, 1 - core, z), (y, 1 - x, core, z), (1 - y, x, core, z)):
        pl.semaphore_signal(barrier, inc=1, device_id=peer(*near), device_id_type=MESH)

    @pl.when(z > 0)
    def _():
        pl.semaphore_signal(barrier, inc=1, device_id=peer(y, x, core, z - 1), device_id_type=MESH)

    @pl.when(z < line - 1)
    def _():
        pl.semaphore_signal(barrier, inc=1, device_id=peer(y, x, core, z + 1), device_id_type=MESH)

    pl.semaphore_wait(barrier, 3 + (z + line - 1) // line + (2 * line - 2 - z) // line)


def either(first, second, take):
    return first * (1 - take) + second * take


def remote(source, target, send_sem, recv_sem, where):
    return pltpu.make_async_remote_copy(
        src_ref=source, dst_ref=target, send_sem=send_sem, recv_sem=recv_sem,
        device_id=peer(*where), device_id_type=MESH,
    )


def landed(target, sem):
    pltpu.make_async_copy(target, target, sem).wait()


def slot_order(y, x, core, z):
    return ((y * 2 + x) * 4 + z) * 2 + core


def near_first(z, i):
    side = z // 2
    low = either(z, 3 - z, side)
    first, second = (4 - i) // 4, (5 - i) // 4 - (4 - i) // 4
    return either(i + low * (first - second), 3 - i - low * (first - second), side)


def gather_dispatch_kernel(line, rows, slots_ref, hidden_ref, gates_ref, cots_left, cots_right,
                           rows_out, gates_out, x_out, c_out, gate_out,
                           in_c, in_x, in_gate, stage_c, stage_x, stage_gate,
                           local_sem, send_sem, recv_sem, load_sem, store_sem):
    y, x, core, z = place()
    tokens, width = hidden_ref.shape
    experts = slots_ref.shape[1]
    first_expert = (y * 4 + x * 2 + core) * experts
    owns, outs = (hidden_ref, gates_ref), (rows_out, gates_out)
    near_x, near_y, sibling = (y, 1 - x, core, z), (1 - y, x, core, z), (y, x, 1 - core, z)
    last = 24
    greet(line)

    def span(n, block):
        count = owns[n].shape[0]
        return outs[n].at[pl.ds(block * count, count)]

    def spot(m):
        q = m % 4
        i = m // 4 - (q + 1) // 2
        live = (i >= 0) & (i < line)
        held = i * live.astype(jnp.int32)
        yy, xx = (y + q // 2) % 2, (x + q % 2) % 2
        return q, held, live, yy, xx, near_first(z, held)

    def sends(m):
        q, i, live, yy, xx, zz = spot(m)
        block = block_of(yy, xx, core, zz)
        own = live & (q == 0)
        table = (
            (own & (zz <= z) & (z < line - 1), (y, x, core, z + 1)),
            (own & (zz >= z) & (z > 0), (y, x, core, z - 1)),
            (own | (live & (q == 2) & (zz % 2 == 1)), near_x),
            (own | (live & (q == 1) & (zz % 2 == 0)), near_y),
            (live, sibling),
        )
        for lane, (wanted, where) in enumerate(table):
            for n in range(2):
                part = span(n, block)
                yield wanted, remote(part, part, send_sem.at[n, lane, m], recv_sem.at[n, block], where)

    def load_c(chip):
        yy, xx, zz = chip // 8, chip // 4 % 2, chip % 4
        for c in range(2):
            b = block_of(yy, xx, c, zz)
            half = width // 2
            for n, source in enumerate((cots_left, cots_right)):
                yield pltpu.make_async_copy(
                    source.at[pl.ds(b * tokens, tokens)],
                    in_c.at[pl.ds(c * tokens, tokens), pl.ds(n * half, half)],
                    load_sem.at[3 * n, c],
                )

    def load_x(yy, xx, zz):
        for c in range(2):
            b = block_of(yy, xx, c, zz)
            yield pltpu.make_async_copy(
                rows_out.at[pl.ds(b * tokens, tokens)], in_x.at[pl.ds(c * tokens, tokens)], load_sem.at[1, c]
            )
            yield pltpu.make_async_copy(
                gates_out.at[pl.ds(b * gates_ref.shape[0] + first_expert, experts)], in_gate.at[c], load_sem.at[2, c]
            )

    def store(stage, target, lane, chip):
        return pltpu.make_async_copy(stage, target.at[:, pl.ds(chip * 2 * rows, 2 * rows)], store_sem.at[lane])

    def pick(source, target, yy, xx, zz, gated):
        picks = []
        for c in range(2):
            slots = slots_ref[block_of(yy, xx, c, zz)]
            pieces = []
            for e in range(experts):
                hit = slot_hits(slots, e, rows)
                pieces.append(hit.astype(jnp.float32))
                if gated:
                    gate = jnp.sum(jnp.where(hit, in_gate[c, e : e + 1, :], 0.0), axis=1, keepdims=True)
                    stage_gate[e, c * rows : (c + 1) * rows, :] = jnp.broadcast_to(gate, (rows, 128))
            picks.append(jnp.concatenate(pieces, axis=0).astype(jnp.bfloat16))
        step = min(512, width)
        for first in range(0, width, step):
            parts = [
                jnp.dot(
                    picks[c], source[c * tokens : (c + 1) * tokens, first : first + step],
                    preferred_element_type=jnp.float32,
                )
                for c in range(2)
            ]
            for e in range(experts):
                target[e, :, first : first + step] = jnp.concatenate(
                    [part[e * rows : (e + 1) * rows] for part in parts], axis=0
                ).astype(jnp.bfloat16)

    mine = block_of(y, x, core, z)
    local = [pltpu.make_async_copy(owns[n], span(n, mine), local_sem.at[n]) for n in range(2)]
    for copy in local:
        copy.start()
    for copy in load_c(0):
        copy.start()
    for copy in local:
        copy.wait()
    chips = 4 * line
    lag = 2

    def work(m, carry):
        q, i, live, yy, xx, zz = spot(m)

        @pl.when((m < last) & live & (q + i > 0))
        def _():
            for n in range(2):
                landed(span(n, block_of(yy, xx, core, zz)), recv_sem.at[n, block_of(yy, xx, core, zz)])

        for wanted, copy in sends(m):
            pl.when((m < last) & wanted)(copy.start)

        back = m - lag
        q = (back + 8) % 4
        i = (back + 8) // 4 - 2 - (q + 1) // 2
        live = (i >= 0) & (i < line)
        held = i * live.astype(jnp.int32)
        yy, xx = (y + q // 2) % 2, (x + q % 2) % 2
        zz = near_first(z, held)
        chip = (yy * 2 + xx) * 4 + zz

        @pl.when(live)
        def _():
            block = block_of(yy, xx, 1 - core, zz)
            for n in range(2):
                landed(span(n, block), recv_sem.at[n, block])
            for copy in load_x(yy, xx, zz):
                copy.start()

        @pl.when(m < chips)
        def _():
            for copy in load_c(m):
                copy.wait()

            @pl.when(m > 0)
            def _():
                store(stage_c, c_out, 0, m - 1).wait()

            pick(in_c, stage_c, m // 8, m // 4 % 2, m % 4, False)
            store(stage_c, c_out, 0, m).start()

            @pl.when(m + 1 < chips)
            def _():
                for copy in load_c(m + 1):
                    copy.start()

        @pl.when(live)
        def _():
            @pl.when(q + held > 0)
            def _():
                store(stage_x, x_out, 1, chip).wait()
                store(stage_gate, gate_out, 2, chip).wait()

            for copy in load_x(yy, xx, zz):
                copy.wait()
            pick(in_x, stage_x, yy, xx, zz, True)
            store(stage_x, x_out, 1, chip).start()
            store(stage_gate, gate_out, 2, chip).start()

        return carry

    lax.fori_loop(0, last + lag, work, 0)
    store(stage_c, c_out, 0, chips - 1).wait()
    store(stage_x, x_out, 1, 0).wait()
    store(stage_gate, gate_out, 2, 0).wait()

    def finish(m, carry):
        for wanted, copy in sends(m):
            pl.when(wanted)(copy.wait_send)
        return carry

    lax.fori_loop(0, last, finish, 0)


def gather_dispatch(slots, hidden, gates, cots, rows, collective_id):
    line = 4
    blocks, experts, tokens = slots.shape
    width = hidden.shape[1]
    pair = 2 * rows
    low, wide = jnp.bfloat16, jnp.float32
    any_ref = pl.BlockSpec(memory_space=pl.ANY)
    vmem = pl.BlockSpec(memory_space=pltpu.VMEM)
    dma = pltpu.SemaphoreType.DMA
    slot_shape = jax.ShapeDtypeStruct((experts, blocks * rows, width), low)
    return pl.pallas_call(
        functools.partial(gather_dispatch_kernel, line, rows),
        out_shape=(
            jax.ShapeDtypeStruct((blocks * tokens, width), low),
            jax.ShapeDtypeStruct((blocks * gates.shape[0], tokens), wide),
            slot_shape,
            slot_shape,
            jax.ShapeDtypeStruct((experts, blocks * rows, 128), wide),
        ),
        in_specs=[vmem, any_ref, any_ref, any_ref, any_ref],
        out_specs=[any_ref] * 5,
        scratch_shapes=[
            pltpu.VMEM((2 * tokens, width), low),
            pltpu.VMEM((2 * tokens, width), low),
            pltpu.VMEM((2, experts, tokens), wide),
            pltpu.VMEM((experts, pair, width), low),
            pltpu.VMEM((experts, pair, width), low),
            pltpu.VMEM((experts, pair, 128), wide),
            dma((2,)),
            dma((2, 5, 24)),
            dma((2, blocks)),
            dma((4, 2)),
            dma((3,)),
        ],
        compiler_params=pltpu.CompilerParams(
            collective_id=collective_id, has_side_effects=True, vmem_limit_bytes=40 << 20
        ),
        cost_estimate=pl.CostEstimate(
            flops=4 * blocks * experts * rows * tokens * width, bytes_accessed=200 << 20, transcendentals=0
        ),
        name="gather_dispatch",
    )(slots, hidden, gates, *cots)[2:]


def reduce_kernel(line, slots_ref, grads_ref, outs_ref, sum_ref, part_ref,
                  grad_in, out_in, out_stage, stage, near, far_x, far_y, from_x, from_y, up, down,
                  in_sem, part_sem, stage_sem, near_sem, send_sem, far_sem, x_sem, y_sem, line_sem):
    y, x, core, z = place()
    tokens, width = sum_ref.shape
    half = tokens // 2
    experts, room = grads_ref.shape[1:3]
    rounds = line
    greet(line)

    def goal(r):
        early = 1 - r // 2
        return (line - 1) * (r % 2) * early + (r - 1) * (1 - early)

    def spot_at(q):
        r, p = q // 8, q % 8
        own = (1 - p % 2) * ((p + 7) // 8) + p // 7
        column = own * (p // 2 - 1 + p // 7) + (1 - own) * ((p + 1) // 2)
        dy, dx = (column + 1) % 2, 1 - column // 2
        target_core = core * own + (1 - core) * (1 - own)
        return (y + dy) % 2, (x + dx) % 2, target_core, goal(r)

    def load(q):
        b = slot_order(*spot_at(q))
        return (
            pltpu.make_async_copy(grads_ref.at[b], grad_in.at[q % 2], in_sem.at[0, q % 2]),
            pltpu.make_async_copy(outs_ref.at[b], out_in.at[q % 2], in_sem.at[1, q % 2]),
        )

    def to_part(q):
        b = block_of(*spot_at(q))
        return pltpu.make_async_copy(out_stage.at[q % 2], part_ref.at[pl.ds(b * tokens, tokens)], part_sem.at[q % 2])

    def to_sibling(r, j):
        return pltpu.make_async_remote_copy(
            src_ref=stage.at[j], dst_ref=near.at[r * 4 + j], send_sem=stage_sem.at[j], recv_sem=near_sem.at[r * 4 + j],
            device_id=peer(y, x, 1 - core, z), device_id_type=MESH,
        )

    near_x, near_y = peer(y, 1 - x, core, z), peer(1 - y, x, core, z)

    def rows(h):
        return pl.ds(h * half, half)

    def cross(kind, r):
        column, h, target, sem, index, lane = {
            "far_x": (0, 0, far_x.at[r], far_sem.at[0, r], near_x, 0),
            "far_y": (0, 1, far_y.at[r], far_sem.at[1, r], near_y, 1),
            "x0": (1, 0, from_x.at[r, rows(0)], x_sem.at[r, 0], near_x, 2),
            "x1": (1, 1, from_x.at[r, rows(1)], x_sem.at[r, 1], near_x, 3),
            "y0": (2, 0, from_y.at[r, rows(0)], y_sem.at[r, 0], near_y, 4),
            "y1": (2, 1, from_y.at[r, rows(1)], y_sem.at[r, 1], near_y, 5),
        }[kind]
        return pltpu.make_async_remote_copy(
            src_ref=near.at[r * 4 + column, rows(h)], dst_ref=target, send_sem=send_sem.at[lane, r], recv_sem=sem,
            device_id=index, device_id_type=MESH,
        )

    def along(sign, r):
        target = up if sign > 0 else down
        lane = 0 if sign > 0 else 1
        return pltpu.make_async_remote_copy(
            src_ref=near.at[r * 4 + 3], dst_ref=target.at[r], send_sem=send_sem.at[6 + lane, r], recv_sem=line_sem.at[lane, r],
            device_id=peer(y, x, core, z + sign), device_id_type=MESH,
        )

    def term(q, source, target_width, store):
        picks = jnp.concatenate(
            [slot_hits(slots_ref[block_of(*spot_at(q))], e, room).astype(jnp.float32) for e in range(experts)], axis=0
        ).astype(jnp.bfloat16)
        for first in range(0, target_width, 512):
            part = slice(first, min(first + 512, target_width))
            values = source[q % 2, :, :, part].reshape(experts * room, part.stop - first)
            store(part, turned(picks, values))

    for copy in load(0):
        copy.start()

    def one(r, p, j, own):
        q = r * 8 + p
        for copy in load(q):
            copy.wait()

        @pl.when(q + 1 < rounds * 8)
        def _():
            for copy in load(q + 1):
                copy.start()

        if own:
            near_slot = r * 4 + j
            to_sibling(r, j).wait_recv()

            def keep(part, value):
                near[near_slot, :, part] = (value + near[near_slot, :, part].astype(jnp.float32)).astype(jnp.bfloat16)

            term(q, grad_in, width, keep)
        else:

            @pl.when(r > 0)
            def _():
                to_sibling(r - 1, j).wait_send()

            def keep(part, value):
                stage[j, :, part] = value.astype(jnp.bfloat16)

            term(q, grad_in, width, keep)
            to_sibling(r, j).start()

        @pl.when(q >= 2)
        def _():
            to_part(q - 2).wait()

        def put(part, value):
            out_stage[q % 2, :, part] = value.astype(jnp.bfloat16)

        term(q, out_in, out_stage.shape[2], put)
        to_part(q).start()

    def add(target, h, *sources):
        for first in range(0, width, 512):
            part = slice(first, min(first + 512, width))
            total = near[target, h, part].astype(jnp.float32)
            for source in sources:
                total = total + source(part).astype(jnp.float32)
            near[target, h, part] = total.astype(jnp.bfloat16)

    def work(s, carry):
        @pl.when(s < rounds)
        def _():
            r = s
            one(r, 0, 0, 0)
            for j in range(4):
                if j < 3:
                    one(r, 2 * j + 1, j + 1, 0)
                one(r, min(2 * j + 2, 7), j, 1)
                for kind in (("far_x", "far_y"), ("x0",), ("y1",), ())[j]:
                    cross(kind, r).start()
            cross("far_y", r).wait_recv()
            add(r * 4 + 1, rows(1), lambda part: far_y[r, :, part])
            cross("x1", r).start()
            cross("far_x", r).wait_recv()
            add(r * 4 + 2, rows(0), lambda part: far_x[r, :, part])
            cross("y0", r).start()

        @pl.when((s >= 1) & (s < rounds + 1))
        def _():
            r = s - 1
            for kind in ("x0", "x1", "y0", "y1"):
                cross(kind, r).wait_recv()
            for h in range(2):
                add(
                    r * 4 + 3,
                    rows(h),
                    lambda part: from_x[r, rows(h), part],
                    lambda part: from_y[r, rows(h), part],
                )

        for hop in range(line - 1):
            r = s - 1 - hop
            live = (r >= 0) & (r < rounds)
            held = r * live.astype(jnp.int32)

            @pl.when(live & (goal(held) > z) & (z == hop))
            def _():
                if hop:
                    along(1, held).wait_recv()
                    for h in range(2):
                        add(held * 4 + 3, rows(h), lambda part: up[held, rows(h), part])
                along(1, held).start()

            @pl.when(live & (goal(held) < z) & (line - 1 - z == hop))
            def _():
                if hop:
                    along(-1, held).wait_recv()
                    for h in range(2):
                        add(held * 4 + 3, rows(h), lambda part: down[held, rows(h), part])
                along(-1, held).start()

        return carry

    lax.fori_loop(0, rounds + line - 1, work, 0)

    mine = (z + (z + 2) // 3) % 4 + z // 3
    sum_ref[...] = near[mine * 4 + 3].astype(jnp.float32)

    @pl.when(z > 0)
    def _():
        along(1, mine).wait_recv()
        sum_ref[...] += up[mine].astype(jnp.float32)

    @pl.when(z < line - 1)
    def _():
        along(-1, mine).wait_recv()
        sum_ref[...] += down[mine].astype(jnp.float32)

    def finish(r, carry):
        for kind in ("far_x", "far_y", "x0", "x1", "y0", "y1"):
            cross(kind, r).wait_send()

        @pl.when(goal(r) > z)
        def _():
            along(1, r).wait_send()

        @pl.when(goal(r) < z)
        def _():
            along(-1, r).wait_send()

        return carry

    lax.fori_loop(0, rounds, finish, 0)
    for j in range(4):
        to_sibling(rounds - 1, j).wait_send()
    for q in (rounds * 8 - 2, rounds * 8 - 1):
        to_part(q).wait()


def reduce_all(slots, outs, grads, collective_id):
    blocks, experts, tokens = slots.shape
    room, width = outs.shape[2:]
    wider = grads.shape[3]
    line = 4
    low = jnp.bfloat16
    any_ref = pl.BlockSpec(memory_space=pl.ANY)
    vmem = pl.BlockSpec(memory_space=pltpu.VMEM)
    dma = pltpu.SemaphoreType.DMA
    return pl.pallas_call(
        functools.partial(reduce_kernel, line),
        out_shape=(
            jax.ShapeDtypeStruct((tokens, wider), jnp.float32),
            jax.ShapeDtypeStruct((blocks * tokens, width), low),
        ),
        in_specs=[vmem, any_ref, any_ref],
        out_specs=[vmem, any_ref],
        scratch_shapes=[
            pltpu.VMEM((2, experts, room, wider), low),
            pltpu.VMEM((2, experts, room, width), low),
            pltpu.VMEM((2, tokens, width), low),
            pltpu.VMEM((4, tokens, wider), low),
            pltpu.VMEM((line * 4, tokens, wider), low),
            pltpu.VMEM((line, tokens // 2, wider), low),
            pltpu.VMEM((line, tokens // 2, wider), low),
            pltpu.VMEM((line, tokens, wider), low),
            pltpu.VMEM((line, tokens, wider), low),
            pltpu.VMEM((line, tokens, wider), low),
            pltpu.VMEM((line, tokens, wider), low),
            dma((2, 2)),
            dma((2,)),
            dma((4,)),
            dma((line * 4,)),
            dma((8, line)),
            dma((2, line)),
            dma((line, 2)),
            dma((line, 2)),
            dma((2, line)),
        ],
        compiler_params=pltpu.CompilerParams(
            collective_id=collective_id, has_side_effects=True, vmem_limit_bytes=62 << 20
        ),
        cost_estimate=pl.CostEstimate(
            flops=2 * blocks * experts * room * tokens * (width + wider),
            bytes_accessed=2 * blocks * experts * room * (width + wider),
            transcendentals=0,
        ),
        name="reduce_all",
    )(slots, grads, outs)


class LineGather:
    def __init__(self, own, out, send_sem, recv_sem, line):
        self.own, self.out, self.send_sem, self.recv_sem, self.line = own, out, send_sem, recv_sem, line
        self.spot = place()
        self.rows = own.shape[0]

    def view(self, block):
        return self.out.at[pl.ds(block * self.rows, self.rows)]

    def inside(self, block):
        return (block >= 0) & (block < self.line)

    def copy(self, sign, step):
        y, x, core, z = self.spot
        block = z - sign * step
        lane = (1 - sign) // 2
        source = self.own if step == 0 else self.view(block)
        return remote(
            source, self.view(block), self.send_sem.at[lane, step], self.recv_sem.at[lane, step], (y, x, core, z + sign)
        )

    def sends(self, sign, step):
        z = self.spot[3]
        return self.inside(z - sign * step) & self.inside(z + sign)

    def begin(self):
        for sign in (1, -1):
            pl.when(self.sends(sign, 0))(self.copy(sign, 0).start)

    def advance(self, step):
        z = self.spot[3]
        for sign in (1, -1):
            block = z - sign * (step + 1)
            lane = (1 - sign) // 2

            @pl.when(self.inside(block))
            def _():
                landed(self.view(block), self.recv_sem.at[lane, step])

            if step + 1 < self.line - 1:
                pl.when(self.sends(sign, step + 1))(self.copy(sign, step + 1).start)

    def finish(self):
        for sign in (1, -1):
            for step in range(self.line - 1):
                pl.when(self.sends(sign, step))(self.copy(sign, step).wait_send)


def start_kernel(line, hidden_ref, wq_ref, wk_ref, wv_ref, wo_ref, slots_ref, hidden_out, joined_out, wo_out, slots_out,
                 local_sem, line_send, line_recv, plane_send, plane_recv, slot_send, slot_recv, slot_line_send, slot_line_recv):
    y, x, core, z = place()
    owns = (wq_ref, wk_ref, wv_ref, wo_ref)
    near_x, near_y, sibling = (y, 1 - x, core, z), (1 - y, x, core, z), (y, x, 1 - core, z)

    def view(n, yy, xx, half=None):
        group = yy * 4 + xx * 2 + core
        rows, columns = owns[n].shape
        first, count = (0, rows) if half is None else (half * (rows // 2), rows // 2)
        if n < 3:
            return joined_out.at[pl.ds(group * rows + first, count), pl.ds(n * columns, columns)]
        return wo_out.at[pl.ds(first, count), pl.ds(pl.multiple_of(group * columns, columns), columns)]

    kinds = ("x", "y", "s", "fy", "fx", "sx", "sy", "sf")

    def copy(kind, n):
        source, target, where = {
            "x": (owns[n], view(n, y, x), near_x),
            "y": (owns[n], view(n, y, x), near_y),
            "s": (owns[n], view(n, y, x), sibling),
            "fy": (view(n, y, 1 - x, 0), view(n, y, 1 - x, 0), near_y),
            "fx": (view(n, 1 - y, x, 1), view(n, 1 - y, x, 1), near_x),
            "sx": (view(n, y, 1 - x), view(n, y, 1 - x), sibling),
            "sy": (view(n, 1 - y, x), view(n, 1 - y, x), sibling),
            "sf": (view(n, 1 - y, 1 - x), view(n, 1 - y, 1 - x), sibling),
        }[kind]
        lane = kinds.index(kind)
        return remote(source, target, plane_send.at[lane, n], plane_recv.at[lane, n], where)

    def other(n, yy, xx):
        group = yy * 4 + xx * 2 + 1 - core
        rows, columns = owns[n].shape
        if n < 3:
            return joined_out.at[pl.ds(group * rows, rows), pl.ds(n * columns, columns)]
        return wo_out.at[pl.ds(0, rows), pl.ds(pl.multiple_of(group * columns, columns), columns)]

    barrier = pltpu.get_barrier_semaphore()
    shifts = [(dy, dx, dc) for dy in range(2) for dx in range(2) for dc in range(2) if dy + dx + dc]
    plane = [((y + dy) % 2, (x + dx) % 2, (core + dc) % 2, z) for dy, dx, dc in shifts]
    for other_spot in plane:
        pl.semaphore_signal(barrier, inc=1, device_id=peer(*other_spot), device_id_type=MESH)
    for step in (-1, 1):

        @pl.when((z + step >= 0) & (z + step < line))
        def _():
            pl.semaphore_signal(barrier, inc=1, device_id=peer(y, x, core, z + step), device_id_type=MESH)

    pl.semaphore_wait(barrier, 7 + (z + line - 1) // line + (2 * line - 2 - z) // line)
    experts = slots_out.shape[1]
    group = peer(y, x, core, z)[0]
    slot_copies = []
    for n, other_spot in enumerate(plane):
        their_group = peer(*other_spot)[0]
        slot_copies.append(
            remote(
                slots_ref.at[pl.ds(their_group * experts, experts)], slots_out.at[z * 8 + group],
                slot_send.at[n], slot_recv.at[group], other_spot,
            )
        )
    own_slots = pltpu.make_async_copy(
        slots_ref.at[pl.ds(group * experts, experts)], slots_out.at[z * 8 + group], local_sem.at[5]
    )
    own_slots.start()
    slot_line = LineGather(slots_out.at[pl.ds(z * 8, 8)], slots_out, slot_line_send, slot_line_recv, line)
    hidden = LineGather(hidden_ref, hidden_out, line_send, line_recv, line)
    locals_ = [pltpu.make_async_copy(hidden_ref, hidden.view(z), local_sem.at[4])]
    locals_ += [pltpu.make_async_copy(owns[n], view(n, y, x), local_sem.at[n]) for n in range(4)]
    for slot_copy in slot_copies:
        slot_copy.start()
    hidden.begin()
    for n in range(4):
        for kind in ("x", "y", "s"):
            copy(kind, n).start()
    for local in locals_:
        local.start()
    for n in range(4):
        landed(view(n, y, 1 - x), plane_recv.at[0, n])
        copy("fy", n).start()
        copy("sx", n).start()
        landed(view(n, 1 - y, x), plane_recv.at[1, n])
        copy("fx", n).start()
        copy("sy", n).start()
    own_slots.wait()
    for other_spot in plane:
        their_group = peer(*other_spot)[0]
        landed(slots_out.at[z * 8 + their_group], slot_recv.at[their_group])
    slot_line.begin()
    hidden.advance(0)
    slot_line.advance(0)
    for n in range(4):
        landed(view(n, 1 - y, 1 - x, 0), plane_recv.at[3, n])
        landed(view(n, 1 - y, 1 - x, 1), plane_recv.at[4, n])
        copy("sf", n).start()
    for step in range(1, line - 1):
        slot_line.advance(step)
        hidden.advance(step)
    for n in range(4):
        landed(other(n, y, x), plane_recv.at[2, n])
        landed(other(n, y, 1 - x), plane_recv.at[5, n])
        landed(other(n, 1 - y, x), plane_recv.at[6, n])
        landed(other(n, 1 - y, 1 - x), plane_recv.at[7, n])
    hidden.finish()
    slot_line.finish()
    for slot_copy in slot_copies:
        slot_copy.wait_send()
    for n in range(4):
        for kind in kinds:
            copy(kind, n).wait_send()
    for local in locals_:
        local.wait()


def start_exchange(hidden, w_query, w_key, w_value, w_out, slots, collective_id):
    line = 4
    any_ref = pl.BlockSpec(memory_space=pl.ANY)
    dma = pltpu.SemaphoreType.DMA
    rows, width = hidden.shape
    part, columns = w_query.shape
    low = jnp.bfloat16
    return pl.pallas_call(
        functools.partial(start_kernel, line),
        out_shape=(
            jax.ShapeDtypeStruct((line * rows, width), low),
            jax.ShapeDtypeStruct((8 * part, 3 * columns), low),
            jax.ShapeDtypeStruct((w_out.shape[0], 8 * w_out.shape[1]), low),
            jax.ShapeDtypeStruct((line * 8, slots.shape[0] // 8, slots.shape[1]), slots.dtype),
        ),
        in_specs=[any_ref] * 6,
        out_specs=[any_ref] * 4,
        scratch_shapes=[
            dma((6,)), dma((2, line)), dma((2, line)), dma((8, 4)), dma((8, 4)),
            dma((7,)), dma((8,)), dma((2, line)), dma((2, line)),
        ],
        compiler_params=pltpu.CompilerParams(collective_id=collective_id, has_side_effects=True),
        cost_estimate=pl.CostEstimate(flops=0, bytes_accessed=150 << 20, transcendentals=0),
        name="start_exchange",
    )(hidden, w_query, w_key, w_value, w_out, slots)


class LineReduce:
    def __init__(self, part, up, down, send_sem, recv_sem, line):
        self.part, self.up, self.down = part, up, down
        self.send_sem, self.recv_sem, self.line = send_sem, recv_sem, line
        self.spot = place()

    def copy(self, sign, goal):
        y, x, core, z = self.spot
        lane = (1 - sign) // 2
        target = self.up if sign > 0 else self.down
        return remote(
            self.part.at[goal], target.at[goal], self.send_sem.at[lane, goal], self.recv_sem.at[lane, goal],
            (y, x, core, z + sign),
        )

    def order(self, i):
        z = self.spot[3]
        return either(self.line - 1 - i, i, z * 2 // self.line)

    def lead(self, goal):
        z = self.spot[3]
        pl.when((z == 0) & (goal > 0))(self.copy(1, goal).start)
        pl.when((z == self.line - 1) & (goal < z))(self.copy(-1, goal).start)

    def advance(self, unit, total_ref):
        z, line = self.spot[3], self.line
        for sign in (1, -1):
            goal = line - 1 - unit + z if sign > 0 else unit - line + 1 + z
            live = ((z > 0) & (goal < line)) if sign > 0 else ((z < line - 1) & (goal >= 0))
            inbox = self.up if sign > 0 else self.down

            @pl.when(live)
            def _():
                self.copy(sign, goal).wait_recv()
                if unit < line - 1:
                    self.part[goal] = (
                        self.part[goal].astype(jnp.float32) + inbox[goal].astype(jnp.float32)
                    ).astype(jnp.bfloat16)
                    self.copy(sign, goal).start()
                else:
                    total_ref[...] += inbox[goal].astype(jnp.float32)

    def finish(self):
        z = self.spot[3]

        def step(goal, carry):
            pl.when(goal > z)(self.copy(1, goal).wait_send)
            pl.when(goal < z)(self.copy(-1, goal).wait_send)
            return carry

        lax.fori_loop(0, self.line, step, 0)


def mixed_out_kernel(line, mixed_ref, w_ref, residual_ref, gain_ref, router_ref,
                     x_ref, hidden_ref, probs_ref, part, up, down, send_sem, recv_sem):
    rows, width = x_ref.shape
    greet(line)
    reduce = LineReduce(part, up, down, send_sem, recv_sem, line)
    z = reduce.spot[3]

    def term(i, carry):
        goal = reduce.order(i)
        first = pl.multiple_of(goal * rows, rows)
        for column in range(0, width, 512):
            piece = slice(column, column + 512)
            value = jnp.dot(mixed_ref[pl.ds(first, rows), :], w_ref[:, piece], preferred_element_type=jnp.float32)

            @pl.when(goal == z)
            def _():
                x_ref[:, piece] = value

            part[goal, :, piece] = value.astype(jnp.bfloat16)
        reduce.lead(goal)
        return carry

    lax.fori_loop(0, line, term, 0)
    for unit in range(1, line):
        reduce.advance(unit, x_ref)
    x_one = x_ref[...] + residual_ref[...].astype(jnp.float32)
    x_ref[...] = x_one
    scale = lax.rsqrt(jnp.mean(x_one * x_one, axis=-1, keepdims=True) + norm_eps)
    hidden = (x_one * scale * gain_ref[...]).astype(jnp.bfloat16)
    hidden_ref[...] = hidden
    logits = lax.dot_general(
        router_ref[...], hidden, (((1,), (1,)), ((), ())), preferred_element_type=jnp.float32
    )
    shifted = jnp.exp(logits - jnp.max(logits, axis=0, keepdims=True))
    probs_ref[...] = shifted / jnp.sum(shifted, axis=0, keepdims=True)
    reduce.finish()


def mixed_out(mixed, w_out, residual, gain, router_turned, collective_id):
    line = 4
    rows, width = residual.shape
    experts = router_turned.shape[0]
    vmem = pl.BlockSpec(memory_space=pltpu.VMEM)
    dma = pltpu.SemaphoreType.DMA
    block = pltpu.VMEM((line, rows, width), jnp.bfloat16)
    return pl.pallas_call(
        functools.partial(mixed_out_kernel, line),
        out_shape=(
            jax.ShapeDtypeStruct((rows, width), jnp.float32),
            jax.ShapeDtypeStruct((rows, width), jnp.bfloat16),
            jax.ShapeDtypeStruct((experts, rows), jnp.float32),
        ),
        in_specs=[vmem] * 5,
        out_specs=[vmem] * 3,
        scratch_shapes=[block, block, block, dma((2, line)), dma((2, line))],
        compiler_params=pltpu.CompilerParams(
            collective_id=collective_id, has_side_effects=True, vmem_limit_bytes=56 << 20
        ),
        cost_estimate=pl.CostEstimate(flops=0, bytes_accessed=150 << 20, transcendentals=0),
        name="mixed_out",
    )(mixed, w_out, residual, gain.reshape(1, width), router_turned)


class Butterfly:
    def __init__(self, data, total, from_core, from_x, from_y, from_z, sums, send_sem, recv_sem):
        self.data, self.total, self.sums = data, total, sums
        self.boxes = {"core": from_core, "x": from_x, "y": from_y}
        self.from_z, self.send_sem, self.recv_sem = from_z, send_sem, recv_sem
        y, x, core, z = self.spot = place()
        self.width = data.shape[1]
        self.near = {"core": (y, x, 1 - core, z), "x": (y, 1 - x, core, z), "y": (1 - y, x, core, z)}
        half, quarter, eighth = self.width // 2, self.width // 4, self.width // 8
        first = core * half
        self.kept = {"core": (first, half), "x": (first + x * quarter, quarter)}
        self.kept["y"] = (first + x * quarter + y * eighth, eighth)
        self.away = {
            "core": ((1 - core) * half, half),
            "x": (first + (1 - x) * quarter, quarter),
            "y": (first + x * quarter + (1 - y) * eighth, eighth),
        }

    def part(self, span):
        return pl.ds(pl.multiple_of(span[0], span[1]), span[1])

    def fold_copy(self, axis):
        lane = ("core", "x", "y").index(axis)
        return remote(
            self.data.at[:, self.part(self.away[axis])], self.boxes[axis], self.send_sem.at[lane],
            self.recv_sem.at[lane], self.near[axis],
        )

    def fold(self, axis):
        copy = self.fold_copy(axis)
        copy.start()
        copy.wait()
        self.data[:, self.part(self.kept[axis])] += self.boxes[axis][...]

    def line_step(self, step):
        y, x, core, z = self.spot
        other = (z + 1 - 2 * (z % 2)) if step == 0 else (z + 2) % 4
        piece = self.part(self.kept["y"])
        source = self.data.at[:, piece] if step == 0 else self.sums
        copy = remote(
            source, self.from_z.at[step], self.send_sem.at[3 + step], self.recv_sem.at[3 + step], (y, x, core, other)
        )
        copy.start()
        copy.wait()
        if step == 0:
            self.sums[...] = self.data[:, piece] + self.from_z[0]
        else:
            self.total[:, piece] = self.sums[...] + self.from_z[1]

    def unfold(self, axis):
        lane = 5 + ("core", "x", "y").index(axis)
        mine = self.total.at[:, self.part(self.kept[axis])]
        copy = remote(mine, mine, self.send_sem.at[lane], self.recv_sem.at[lane], self.near[axis])
        copy.start()
        copy.wait_send()
        landed(self.total.at[:, self.part(self.away[axis])], self.recv_sem.at[lane])

    def scratch(rows, width):
        low = jnp.float32
        return [
            pltpu.VMEM((rows, width // 2), low),
            pltpu.VMEM((rows, width // 4), low),
            pltpu.VMEM((rows, width // 8), low),
            pltpu.VMEM((2, rows, width // 8), low),
            pltpu.VMEM((rows, width // 8), low),
            pltpu.SemaphoreType.DMA((8,)),
            pltpu.SemaphoreType.DMA((8,)),
        ]


def greet_far(line):
    y, x, core, z = place()
    barrier = pltpu.get_barrier_semaphore()
    for near in ((y, x, 1 - core, z), (y, 1 - x, core, z), (1 - y, x, core, z)):
        pl.semaphore_signal(barrier, inc=1, device_id=peer(*near), device_id_type=MESH)
    for step in range(1, line):
        pl.semaphore_signal(barrier, inc=1, device_id=peer(y, x, core, (z + step) % line), device_id_type=MESH)
    pl.semaphore_wait(barrier, 3 + line - 1)


def back_gather_kernel(line, own_ref, sums_ref, out_ref, total_ref, data, local_sem, send_sem, recv_sem, *fly):
    greet_far(line)
    gather = LineGather(own_ref, out_ref, send_sem, recv_sem, line)
    local = pltpu.make_async_copy(own_ref, gather.view(gather.spot[3]), local_sem)
    gather.begin()
    local.start()
    data[...] = sums_ref[...]
    butterfly = Butterfly(data, total_ref, *fly)
    for axis in ("core", "x", "y"):
        butterfly.fold(axis)
    gather.advance(0)
    butterfly.line_step(0)
    gather.advance(1)
    butterfly.line_step(1)
    for axis in ("y", "x", "core"):
        butterfly.unfold(axis)
    gather.advance(2)
    gather.finish()
    local.wait()


def back_gather(own, sums, collective_id):
    line = 4
    any_ref = pl.BlockSpec(memory_space=pl.ANY)
    vmem = pl.BlockSpec(memory_space=pltpu.VMEM)
    dma = pltpu.SemaphoreType.DMA
    return pl.pallas_call(
        functools.partial(back_gather_kernel, line),
        out_shape=(
            jax.ShapeDtypeStruct((line * own.shape[0], own.shape[1]), own.dtype),
            jax.ShapeDtypeStruct(sums.shape, jnp.float32),
        ),
        in_specs=[any_ref, vmem],
        out_specs=[any_ref, vmem],
        scratch_shapes=[
            pltpu.VMEM(sums.shape, jnp.float32), dma(()), dma((2, line)), dma((2, line)),
            *Butterfly.scratch(*sums.shape),
        ],
        compiler_params=pltpu.CompilerParams(collective_id=collective_id, has_side_effects=True),
        cost_estimate=pl.CostEstimate(flops=0, bytes_accessed=150 << 20, transcendentals=0),
        name="back_gather",
    )(own, sums)


def last_kernel(line, joined_ref, weight_ref, hidden_ref, mixed_ref, attn_ref, residual_ref, gain_ref, x_grad_ref, gains_ref,
                input_ref, wq_ref, wk_ref, wv_ref, wo_ref, total_ref,
                part, up, down, stage, near, far_x, far_y, from_x, from_y, data,
                line_send, line_recv, stage_sem, near_sem, send_sem, recv_sem, *fly):
    y, x, core, z = place()
    rows, width = input_ref.shape
    columns = joined_ref.shape[1]
    half = rows // 2
    low = jnp.bfloat16
    greet_far(line)
    reduce = LineReduce(part, up, down, line_send, line_recv, line)

    def term(i, carry):
        goal = reduce.order(i)
        first = pl.multiple_of(goal * rows, rows)
        for column in range(0, width, 512):
            piece = slice(column, column + 512)
            value = across(joined_ref[pl.ds(first, rows), :], weight_ref[piece, :])

            @pl.when(goal == z)
            def _():
                input_ref[:, piece] = value

            part[goal, :, piece] = value.astype(low)
        reduce.lead(goal)
        return carry

    lax.fori_loop(0, line, term, 0)
    near_x, near_y, sibling = (y, 1 - x, core, z), (1 - y, x, core, z), (y, x, 1 - core, z)

    def terms(j, own, store):
        dy, dx = (j + 1) % 2, 1 - j // 2
        group = (y + dy) % 2 * 4 + (x + dx) % 2 * 2 + (core if own else 1 - core)
        span = pl.ds(pl.multiple_of(group * rows, rows), rows)
        turned_rows = hidden_ref[:, span]
        for column in range(0, columns, 512):
            piece = slice(column, column + 512)
            store(piece, turned(turned_rows, joined_ref[:, piece]))
        value = turned(mixed_ref[...], attn_ref[:, span])
        store(slice(columns, columns + rows), value[:rows])
        store(slice(columns + rows, columns + 2 * rows), value[rows:])

    def to_sibling(j):
        return remote(stage.at[j], near.at[j], stage_sem.at[j], near_sem.at[j], sibling)

    def away(j, carry):
        def store(piece, value):
            stage[j, :, piece] = value.astype(low)

        terms(j, False, store)
        to_sibling(j).start()
        return carry

    def own(j, carry):
        to_sibling(j).wait_recv()

        def store(piece, value):
            near[j, :, piece] = (value + near[j, :, piece].astype(jnp.float32)).astype(low)

        terms(j, True, store)
        return carry

    lax.fori_loop(0, 4, away, 0)
    lax.fori_loop(0, 4, own, 0)

    def line_rows(h):
        return pl.ds(h * half, half)

    def cross(kind):
        column, h, target, where = {
            "far_x": (0, 0, far_x, near_x),
            "far_y": (0, 1, far_y, near_y),
            "x0": (1, 0, from_x.at[line_rows(0)], near_x),
            "x1": (1, 1, from_x.at[line_rows(1)], near_x),
            "y0": (2, 0, from_y.at[line_rows(0)], near_y),
            "y1": (2, 1, from_y.at[line_rows(1)], near_y),
        }[kind]
        lane = kinds.index(kind)
        return remote(near.at[column, line_rows(h)], target, send_sem.at[lane], recv_sem.at[lane], where)

    kinds = ("far_x", "far_y", "x0", "y1", "x1", "y0")
    for kind in kinds[:4]:
        cross(kind).start()

    def add(column, h, source):
        near[column, line_rows(h), :] = (
            near[column, line_rows(h), :].astype(jnp.float32) + source[...].astype(jnp.float32)
        ).astype(low)

    reduce.advance(1, input_ref)
    cross("far_y").wait_recv()
    add(1, 1, far_y)
    cross("x1").start()
    cross("far_x").wait_recv()
    add(2, 0, far_x)
    cross("y0").start()
    reduce.advance(2, input_ref)
    for kind in kinds[2:]:
        cross(kind).wait_recv()
    for n, ref in enumerate((wq_ref, wk_ref, wv_ref, wo_ref, wo_ref)):
        count = columns // 3 if n < 3 else rows
        first = n * (columns // 3) if n < 3 else columns + (n - 3) * rows
        piece = slice(first, first + count)
        total = sum(r[:, piece].astype(jnp.float32) for r in (near.at[3], from_x, from_y))
        if n < 3:
            ref[...] = total
        else:
            ref[(n - 3) * rows : (n - 2) * rows, :] = total
    reduce.advance(3, input_ref)
    grad = input_ref[...]
    values = residual_ref[...].astype(jnp.float32)
    scale = lax.rsqrt(jnp.mean(values * values, axis=-1, keepdims=True) + norm_eps)
    gained = grad * gain_ref[...]
    inner = jnp.sum(gained * values, axis=-1, keepdims=True)
    data[...] = gains_ref[...]
    data[2:3, :] = jnp.sum(grad * values * scale, axis=0, keepdims=True)
    input_ref[...] = x_grad_ref[...] + scale * gained - values * (scale * scale * scale * inner / width)
    butterfly = Butterfly(data, total_ref, *fly)
    for axis in ("core", "x", "y"):
        butterfly.fold(axis)
    butterfly.line_step(0)
    butterfly.line_step(1)
    for axis in ("y", "x", "core"):
        butterfly.unfold(axis)
    reduce.finish()
    for j in range(4):
        to_sibling(j).wait_send()
    for kind in kinds:
        cross(kind).wait_send()


def last_exchange(joined, weight, hidden, mixed, attn, residual, gain, x_grad, gains, collective_id):
    line = 4
    rows, width = residual.shape
    columns = joined.shape[1] // 3
    low, wide = jnp.bfloat16, jnp.float32
    vmem = pl.BlockSpec(memory_space=pltpu.VMEM)
    dma = pltpu.SemaphoreType.DMA
    block = pltpu.VMEM((line, rows, width), low)
    one = pltpu.VMEM((rows, width), low)
    part = pltpu.VMEM((rows // 2, width), low)
    square = jax.ShapeDtypeStruct((rows, columns), wide)
    return pl.pallas_call(
        functools.partial(last_kernel, line),
        out_shape=(
            jax.ShapeDtypeStruct((rows, width), wide), square, square, square,
            jax.ShapeDtypeStruct((2 * rows, rows), wide),
            jax.ShapeDtypeStruct(gains.shape, wide),
        ),
        in_specs=[vmem] * 9,
        out_specs=[vmem] * 6,
        scratch_shapes=[
            block, block, block, pltpu.VMEM((4, rows, width), low), pltpu.VMEM((4, rows, width), low),
            part, part, one, one, pltpu.VMEM(gains.shape, wide),
            dma((2, line)), dma((2, line)), dma((4,)), dma((4,)), dma((6,)), dma((6,)),
            *Butterfly.scratch(*gains.shape),
        ],
        compiler_params=pltpu.CompilerParams(
            collective_id=collective_id, has_side_effects=True, vmem_limit_bytes=62 << 20
        ),
        cost_estimate=pl.CostEstimate(flops=0, bytes_accessed=250 << 20, transcendentals=0),
        name="last_exchange",
    )(joined, weight, hidden, mixed, attn, residual, gain.reshape(1, width), x_grad, gains)


def visible_block(row_paths, key_paths, key_valid, row_first):
    row_count = row_paths.shape[1]
    key_count = key_paths.shape[1]
    key_segment = key_paths[0][None, :]
    on_path = (
        (key_segment == row_paths[0][:, None])
        | (key_segment == row_paths[1][:, None])
        | (key_segment == row_paths[2][:, None])
    )
    row_place = row_first + lax.iota(jnp.int32, row_count)
    key_place = lax.iota(jnp.int32, key_count)
    earlier = key_place[None, :] <= row_place[:, None]
    return on_path & earlier & (key_valid[None, :] == 1) | (
        key_place[None, :] == row_place[:, None]
    )


def rotation(positions, head_dim):
    half = head_dim // 2
    freqs = jnp.exp(-jnp.log(rope_base) * 2.0 * lax.iota(jnp.float32, half) / head_dim)
    angles = positions.astype(jnp.float32)[:, None] * freqs[None, :]
    return (jnp.cos(angles), jnp.sin(angles))


def visible_bias(row_first, row_paths, row_places, key_segment, key_valid, key_places):
    on_path = (key_segment == row_paths[0]) | (key_segment == row_paths[1]) | (key_segment == row_paths[2])
    seen = (on_path & (key_places <= row_places) & (key_valid == 1)) | (key_places == row_places)
    return jnp.where(seen, 0.0, masked_score)


def attend_kernel(step, raw_ref, scale_ref, gain_ref, cos_ref, sin_ref, column_ref, line_ref,
                  query_ref, key_ref, value_ref, mixed_ref, log_ref, bias, logs):
    seq, columns = query_ref.shape
    heads = columns // HD

    def prepare(i, carry):
        rows = pl.ds(pl.multiple_of(i * step, step), step)
        cosine, sine = cos_ref[rows, :], sin_ref[rows, :]
        for n, ref in enumerate((query_ref, key_ref)):
            scale = scale_ref[rows, n : n + 1]
            for h in range(heads):
                span = slice(h * HD, (h + 1) * HD)
                values = raw_ref[rows, n * columns + h * HD : n * columns + (h + 1) * HD]
                values = values * scale * gain_ref[n : n + 1, span]
                turn = pltpu.roll(values, HD // 2, 1)
                ref[rows, span] = (values * cosine + turn * sine).astype(jnp.bfloat16)
        value_ref[rows, :] = raw_ref[rows, 2 * columns :].astype(jnp.bfloat16)
        return carry

    lax.fori_loop(0, seq // step, prepare, 0)
    for i in range(seq // step):
        rows = slice(i * step, (i + 1) * step)
        wide = (i + 1) * step
        places = lax.broadcasted_iota(jnp.int32, (step, wide), 0) + i * step
        bias[:, :wide] = visible_bias(
            i * step,
            [column_ref[rows, n : n + 1] for n in range(3)],
            places,
            line_ref[0:1, :wide],
            line_ref[3:4, :wide],
            lax.broadcasted_iota(jnp.int32, (step, wide), 1),
        )

        def head(h, carry):
            span = pl.ds(pl.multiple_of(h * HD, HD), HD)
            scores = across(query_ref[rows, span], key_ref[:wide, span]) * HD ** (-0.5) + bias[:, :wide]
            top = jnp.max(scores, axis=1, keepdims=True)
            weights = jnp.exp(scores - top)
            total = jnp.sum(weights, axis=1, keepdims=True)
            low = (weights / total).astype(jnp.bfloat16)
            mixed = jnp.dot(low, value_ref[:wide, span], preferred_element_type=jnp.float32)
            mixed_ref[rows, span] = mixed.astype(jnp.bfloat16)
            lanes = lax.broadcasted_iota(jnp.int32, (step, 128), 1)
            logs[...] = jnp.where(lanes == h, top + jnp.log(total), logs[...])
            return carry

        logs[...] = jnp.zeros_like(logs)
        lax.fori_loop(0, heads, head, 0)
        log_ref[:, rows] = jnp.transpose(logs[...])[: log_ref.shape[0]]


def attend(raw, scales, gains, cosine, sine, path_columns, path_lines):
    seq = raw.shape[0]
    columns = raw.shape[1] // 3
    step = min(256, seq)
    vmem = pl.BlockSpec(memory_space=pltpu.VMEM)
    low = jax.ShapeDtypeStruct((seq, columns), jnp.bfloat16)
    return pl.pallas_call(
        functools.partial(attend_kernel, step),
        out_shape=(low, low, low, low, jax.ShapeDtypeStruct((8, seq), jnp.float32)),
        in_specs=[vmem] * 7,
        out_specs=[vmem] * 5,
        scratch_shapes=[pltpu.VMEM((step, seq), jnp.float32), pltpu.VMEM((step, 128), jnp.float32)],
        compiler_params=pltpu.CompilerParams(vmem_limit_bytes=50 << 20),
        cost_estimate=pl.CostEstimate(
            flops=4 * seq * seq * columns, bytes_accessed=16 * seq * columns, transcendentals=seq * seq
        ),
        name="attend",
    )(raw, scales, gains, cosine, sine, path_columns, path_lines)


def attend_back_kernel(step, grad_ref, w_ref, query_ref, key_ref, value_ref, log_ref, cos_ref, sin_ref,
                       column_ref, line_ref, dq_ref, dk_ref, dv_ref, bias, mixed):
    seq, columns = query_ref.shape
    heads = columns // HD
    dk_ref[...] = jnp.zeros_like(dk_ref)
    dv_ref[...] = jnp.zeros_like(dv_ref)

    def unturn(values, rows):
        return values * cos_ref[rows, :] - pltpu.roll(values, HD // 2, 1) * sin_ref[rows, :]

    for i in range(seq // step):
        rows = slice(i * step, (i + 1) * step)
        wide = (i + 1) * step
        mixed[...] = across(grad_ref[rows, :], w_ref[...]).astype(jnp.bfloat16)
        places = lax.broadcasted_iota(jnp.int32, (wide, step), 1) + i * step
        bias[:wide, :] = visible_bias(
            i * step,
            [line_ref[n : n + 1, rows] for n in range(3)],
            places,
            column_ref[:wide, 0:1],
            column_ref[:wide, 3:4],
            lax.broadcasted_iota(jnp.int32, (wide, step), 0),
        )

        def head(h, carry):
            span = pl.ds(pl.multiple_of(h * HD, HD), HD)
            query, key, grad = query_ref[rows, span], key_ref[:wide, span], mixed[:, span]
            scores = across(key, query) * HD ** (-0.5) + bias[:wide, :]
            weights = jnp.exp(scores - log_ref[pl.ds(h, 1), rows])
            grad_weights = across(value_ref[:wide, span], grad)
            inner = jnp.sum(weights * grad_weights, axis=0, keepdims=True)
            grad_scores = (weights * (grad_weights - inner)).astype(jnp.bfloat16)
            dq_ref[rows, span] = unturn(turned(grad_scores, key) * HD ** (-0.5), rows)
            dk_ref[:wide, span] += jnp.dot(grad_scores, query, preferred_element_type=jnp.float32)
            dv_ref[:wide, span] += jnp.dot(
                weights.astype(jnp.bfloat16), grad, preferred_element_type=jnp.float32
            )
            return carry

        lax.fori_loop(0, heads, head, 0)
    for i in range(seq // step):
        rows = slice(i * step, (i + 1) * step)
        for h in range(heads):
            span = slice(h * HD, (h + 1) * HD)
            dk_ref[rows, span] = unturn(dk_ref[rows, span] * HD ** (-0.5), rows)


def attend_back(grads, w_out, query, key, value, logs, cosine, sine, path_columns, path_lines):
    seq, columns = query.shape
    step = min(256, seq)
    vmem = pl.BlockSpec(memory_space=pltpu.VMEM)
    wide = jax.ShapeDtypeStruct((seq, columns), jnp.float32)
    return pl.pallas_call(
        functools.partial(attend_back_kernel, step),
        out_shape=(wide, wide, wide),
        in_specs=[vmem] * 10,
        out_specs=[vmem] * 3,
        scratch_shapes=[pltpu.VMEM((seq, step), jnp.float32), pltpu.VMEM((step, columns), jnp.bfloat16)],
        compiler_params=pltpu.CompilerParams(vmem_limit_bytes=56 << 20),
        cost_estimate=pl.CostEstimate(
            flops=10 * seq * seq * columns, bytes_accessed=24 * seq * columns, transcendentals=seq * seq
        ),
        name="attend_back",
    )(grads, w_out, query, key, value, logs, cosine, sine, path_columns, path_lines)


def rms_apply(values, gain):
    scale = lax.rsqrt(jnp.mean(values * values, axis=-1, keepdims=True) + norm_eps)
    return (values * scale * gain, scale)


def rms_grad(values, scale, gain, grads, inner, width):
    grad_values = scale * gain * grads - values * scale**3 * inner / width
    grad_gain = jnp.sum(grads * values * scale, axis=0)
    return (grad_values, grad_gain)


def tensor_sums(pair):
    return lax.psum((pair[0], pair[1]), "tensor")


def heads_to_rows(term, rows):
    return lax.psum_scatter(
        term(jnp.int32(0), rows * lax.axis_size("tensor")).astype(jnp.bfloat16),
        "tensor",
        scatter_dimension=0,
        tiled=True,
    ).astype(jnp.float32)


def sum_over_dp(rows):
    dp = lax.axis_size("dp")
    pieces = rows.reshape(dp, rows.shape[0] // dp, rows.shape[1])
    return lax.psum_scatter(pieces, "dp", scatter_dimension=0, tiled=False)


def sum_over_tensor(part):
    return lax.psum_scatter(part, "tensor", scatter_dimension=0, tiled=True)


def body(
    residual,
    attn_gain,
    w_query,
    w_key,
    w_value,
    query_gain,
    key_gain,
    w_out,
    moe_gain,
    router,
    w_gate,
    w_up,
    w_down,
    segment_path,
    token_valid,
    routes,
    route_order,
    cotangent,
):
    tensor_rank = lax.axis_index("tensor")
    tok_dev, width = residual.shape
    seq_len = segment_path.shape[1]
    top_count = routes.shape[1]
    experts = router.shape[1]
    local_experts = w_gate.shape[0]
    dp_groups = experts // local_experts
    capacity = 9 * tok_dev * top_count // (8 * experts)
    full_width = H * HD
    everyone = ("dp", "tensor")
    direct = dp_groups == 8 and lax.axis_size("tensor") == 4
    first_expert = lax.axis_index("dp") * local_experts
    slot_rows = padded(capacity, 8)
    valid_dev = lax.dynamic_slice_in_dim(token_valid, tensor_rank * tok_dev, tok_dev)
    slots_own = slot_table(routes, route_order, valid_dev, experts, capacity)
    if direct:
        cots_left = lax.all_gather(cotangent[:, : width // 2], everyone, axis=0, tiled=True)
    else:
        cots_all = lax.all_gather(cotangent, everyone, axis=0, tiled=True)
    head_cols = w_query.shape[1]
    residual_float = residual.astype(jnp.float32)
    normed_one, scale_one = rms_apply(residual_float, attn_gain)
    hidden = normed_one.astype(jnp.bfloat16)
    path_lines = jnp.concatenate((segment_path, token_valid[None]), axis=0)
    path_columns = path_lines.T
    positions = jnp.sum(visible_block(segment_path, segment_path, token_valid, 0).astype(jnp.int32), axis=1) - 1
    cosine, sine = rotation(positions, HD)
    cosine = jnp.concatenate((cosine, cosine), axis=1)
    sine = jnp.concatenate((-sine, sine), axis=1)
    if direct:
        hidden_all, joined_weight, gathered_out, slots = start_exchange(
            hidden, w_query, w_key, w_value, w_out, slots_own, 3
        )
        right, hidden_all = lax.optimization_barrier((cotangent[:, width // 2 :], hidden_all))
        cots_right = lax.all_gather(right, everyone, axis=0, tiled=True)
        slots = jnp.swapaxes(slots.reshape(4, 8, local_experts, tok_dev), 0, 1).reshape(32, local_experts, tok_dev)
    else:
        hidden_all = lax.all_gather(hidden, "tensor", axis=0, tiled=True)
        joined_weight = jnp.concatenate(
            [lax.all_gather(w, "dp", axis=0, tiled=True) for w in (w_query, w_key, w_value)], axis=1
        )
        gathered_out = lax.all_gather(w_out, "dp", axis=1, tiled=True)
        slots_all = lax.all_gather(slots_own.astype(jnp.bfloat16), everyone, axis=0)
        slots = lax.dynamic_slice_in_dim(slots_all, first_expert, local_experts, 1).astype(jnp.int32)
    projected = jnp.dot(hidden_all, joined_weight, preferred_element_type=jnp.float32)
    blocks = slots.shape[0]
    q_raw = projected[:, :head_cols]
    k_raw = projected[:, head_cols : 2 * head_cols]
    query_sq, key_sq = tensor_sums((jnp.sum(q_raw * q_raw, axis=1), jnp.sum(k_raw * k_raw, axis=1)))
    query_scale = lax.rsqrt(query_sq / full_width + norm_eps)[:, None]
    key_scale = lax.rsqrt(key_sq / full_width + norm_eps)[:, None]
    query_gain_dev = lax.dynamic_slice_in_dim(query_gain, tensor_rank * head_cols, head_cols)
    key_gain_dev = lax.dynamic_slice_in_dim(key_gain, tensor_rank * head_cols, head_cols)
    query_low, key_low, value_low, attn_mixed, log_totals = attend(
        projected,
        jnp.concatenate((query_scale, key_scale), axis=1),
        jnp.stack((query_gain_dev, key_gain_dev)),
        cosine,
        sine,
        path_columns,
        path_lines,
    )
    if direct:
        x_one, hidden_two, gates_own = mixed_out(attn_mixed, gathered_out, residual, moe_gain, router.T, 4)
        probs = gates_own.T
    else:

        def attn_term(first_row, row_count):
            return jnp.dot(attn_mixed, gathered_out, preferred_element_type=jnp.float32)

        x_one = residual_float + heads_to_rows(attn_term, tok_dev)
        hidden_two = rms_apply(x_one, moe_gain)[0].astype(jnp.bfloat16)
        logits = jnp.dot(hidden_two, router, preferred_element_type=jnp.float32)
        probs = jax.nn.softmax(logits, axis=-1)
        gates_own = probs.T
    scale_two = lax.rsqrt(jnp.mean(x_one * x_one, axis=-1, keepdims=True) + norm_eps)
    if direct:
        x_slots, c_slots, gate_slots = gather_dispatch(
            slots, hidden_two, gates_own, (cots_left, cots_right), slot_rows, 1
        )
    else:
        gates_all = lax.all_gather(gates_own, everyone, axis=0)
        rows_all = lax.all_gather(hidden_two, everyone, axis=0, tiled=True)
        gates = lax.dynamic_slice_in_dim(gates_all, first_expert, local_experts, 1)
        x_slots, gate_slots = dispatch(slots, gates, rows_all, slot_rows)
        c_slots = dispatch(slots, None, cots_all, slot_rows)
    outs, grads, pre, gated = expert_pass(
        first_expert.reshape(1),
        x_slots,
        c_slots,
        gate_slots,
        w_gate,
        w_up,
        w_down,
        blocks,
        padded(slot_rows, 16),
    )
    if direct:
        grad_rows, out_part = reduce_all(slots, outs, grads, 2)
    else:
        out_part, grad_part = combine(slots, outs, grads)
        grad_rows = sum_over_tensor(sum_over_dp(grad_part)).astype(jnp.float32)
    out_part = sum_over_dp(out_part)
    grad_out = cotangent.astype(jnp.float32)
    grad_hidden_two = grad_rows[:, :width]
    grad_probs = grad_rows[:, width : width + experts]
    grad_logits = probs * (grad_probs - jnp.sum(probs * grad_probs, axis=-1, keepdims=True))
    router_float = router.astype(jnp.float32)
    grad_hidden_two = grad_hidden_two + lax.dot_general(
        grad_logits, router_float, (((1,), (1,)), ((), ())), precision=lax.Precision.HIGHEST
    )
    grad_router_part = lax.dot_general(
        grad_logits,
        hidden_two.astype(jnp.float32),
        (((0,), (0,)), ((), ())),
        precision=lax.Precision.HIGHEST,
    )
    inner_two = jnp.sum(grad_hidden_two * moe_gain * x_one, axis=-1, keepdims=True)
    grad_norm_two, grad_moe_gain_part = rms_grad(
        x_one, scale_two, moe_gain, grad_hidden_two, inner_two, width
    )
    grad_x_one = grad_out + grad_norm_two
    grad_attn_low = grad_x_one.astype(jnp.bfloat16)
    early_sums = jnp.concatenate(
        (grad_router_part, grad_moe_gain_part[None], jnp.zeros((7, width), jnp.float32)), axis=0
    )
    if direct:
        grad_attn_all, early_sums = back_gather(grad_attn_low, early_sums, 5)
    else:
        grad_attn_all = lax.all_gather(grad_attn_low, "tensor", axis=0, tiled=True)
        early_sums = lax.psum(early_sums, everyone)
    grad_q_norm, grad_k_norm, grad_value_all = attend_back(
        grad_attn_all,
        gathered_out,
        query_low,
        key_low,
        value_low,
        log_totals,
        cosine,
        sine,
        path_columns,
        path_lines,
    )
    query_inner, key_inner = tensor_sums(
        (
            jnp.sum(grad_q_norm * query_gain_dev * q_raw, axis=1),
            jnp.sum(grad_k_norm * key_gain_dev * k_raw, axis=1),
        )
    )
    grad_q_raw, grad_query_gain_dev = rms_grad(
        q_raw, query_scale, query_gain_dev, grad_q_norm, query_inner[:, None], full_width
    )
    grad_k_raw, grad_key_gain_dev = rms_grad(
        k_raw, key_scale, key_gain_dev, grad_k_norm, key_inner[:, None], full_width
    )
    grad_joined = jnp.concatenate(
        (grad_q_raw, grad_k_raw, grad_value_all), axis=1
    ).astype(jnp.bfloat16)
    zero_width = jnp.zeros((full_width,), jnp.float32)
    grad_query_full = lax.dynamic_update_slice_in_dim(
        zero_width, grad_query_gain_dev, tensor_rank * head_cols, 0
    )
    grad_key_full = lax.dynamic_update_slice_in_dim(
        zero_width, grad_key_gain_dev, tensor_rank * head_cols, 0
    )
    if direct:
        gains = jnp.concatenate(
            (grad_query_full[None], grad_key_full[None], jnp.zeros((6, width), jnp.float32)), axis=0
        )
        grad_input, grad_w_query, grad_w_key, grad_w_value, grad_w_out, gains = last_exchange(
            grad_joined,
            joined_weight,
            hidden_all,
            attn_mixed,
            grad_attn_all,
            residual,
            attn_gain,
            grad_x_one,
            gains,
            6,
        )
    else:
        grad_joined_weight = lax.dot_general(
            hidden_all, grad_joined, (((0,), (0,)), ((), ())), preferred_element_type=jnp.float32
        ).astype(jnp.bfloat16)
        grad_out_weight = lax.dot_general(
            attn_mixed, grad_attn_all, (((0,), (0,)), ((), ())), preferred_element_type=jnp.float32
        ).astype(jnp.bfloat16)

        def back_term(first_row, row_count):
            return lax.dot_general(
                grad_joined, joined_weight, (((1,), (1,)), ((), ())), preferred_element_type=jnp.float32
            )

        grad_hidden = heads_to_rows(back_term, tok_dev)
        inner_one = jnp.sum(grad_hidden * attn_gain * residual_float, axis=-1, keepdims=True)
        grad_norm_one, grad_attn_gain_part = rms_grad(
            residual_float, scale_one, attn_gain, grad_hidden, inner_one, width
        )
        grad_input = grad_x_one + grad_norm_one
        grad_w_query, grad_w_key, grad_w_value = (
            lax.psum_scatter(
                grad_joined_weight[:, n * head_cols : (n + 1) * head_cols],
                "dp",
                scatter_dimension=0,
                tiled=True,
            ).astype(jnp.float32)
            for n in range(3)
        )
        grad_w_out = lax.psum_scatter(
            grad_out_weight, "dp", scatter_dimension=1, tiled=True
        ).astype(jnp.float32)
        gains = lax.psum(jnp.stack((grad_query_full, grad_key_full, grad_attn_gain_part)), everyone)
    out_part, pre, grad_input = lax.optimization_barrier((out_part, pre, grad_input))
    grad_w_gate, grad_w_up, grad_w_down = weight_grads(x_slots, c_slots, pre, gated)
    moe_out, grad_w_gate, grad_w_up, grad_w_down = lax.optimization_barrier(
        (sum_over_tensor(out_part), grad_w_gate, grad_w_up, grad_w_down)
    )
    block_out = (x_one + moe_out.astype(jnp.float32)).astype(jnp.bfloat16)
    return (
        block_out,
        grad_input,
        gains[2],
        grad_w_query,
        grad_w_key,
        grad_w_value,
        gains[0],
        gains[1],
        grad_w_out,
        early_sums[experts],
        early_sums[:experts].T,
        grad_w_gate,
        grad_w_up,
        grad_w_down,
    )


def solution(mesh):
    in_specs = (
        P(("dp", "tensor"), None),
        P(),
        P("dp", "tensor"),
        P("dp", "tensor"),
        P("dp", "tensor"),
        P(),
        P(),
        P("tensor", "dp"),
        P(),
        P(),
        P("dp", None, "tensor"),
        P("dp", None, "tensor"),
        P("dp", "tensor", None),
        P(None, "dp"),
        P("dp"),
        P(("dp", "tensor"), None),
        P(("dp", "tensor"), None),
        P(("dp", "tensor"), None),
    )
    out_specs = (
        P(("dp", "tensor"), None),
        P(("dp", "tensor"), None),
        P(),
        P("dp", "tensor"),
        P("dp", "tensor"),
        P("dp", "tensor"),
        P(),
        P(),
        P("tensor", "dp"),
        P(),
        P(),
        P("dp", None, "tensor"),
        P("dp", None, "tensor"),
        P("dp", "tensor", None),
    )
    return jax.shard_map(body, mesh=mesh, in_specs=in_specs, out_specs=out_specs, check_vma=False)
```

```python
import functools

import jax
import jax.numpy as jnp
from jax import lax
from jax.experimental import pallas as pl
from jax.experimental.pallas import tpu as pltpu
from jax.sharding import PartitionSpec as P

H = 16
HD = 128


norm_eps = 1e-05
rope_base = 10000.0
masked_score = -1e30


def padded(count, step):
    return -(-count // step) * step


def slot_table(routes, route_order, valid, experts, capacity):
    far = jnp.int32(1 << 30)
    expert = lax.iota(jnp.int32, experts)[:, None, None]
    hits = (routes[None] == expert) & (valid[None, :, None] == 1)
    order = jnp.min(jnp.where(hits, route_order[None], far), axis=-1)
    ranks = jnp.sum((order[:, None, :] < order[:, :, None]).astype(jnp.int32), axis=-1)
    return jnp.where((order < far) & (ranks < capacity), ranks, -1)


def slot_hits(slots, expert, rows):
    tokens = slots.shape[-1]
    return lax.broadcasted_iota(jnp.int32, (rows, tokens), 0) == slots[expert : expert + 1, :]


def dispatch_kernel(slots_ref, gates_ref, rows_ref, x_ref, gate_ref):
    pair, experts, tokens = slots_ref.shape
    rows = x_ref.shape[1] // pair
    width = rows_ref.shape[1]
    picks = []
    for b in range(pair):
        slots = slots_ref[b]
        pieces = []
        for e in range(experts):
            hit = slot_hits(slots, e, rows)
            pieces.append(hit.astype(jnp.float32))
            if gate_ref is not None:
                gate = jnp.sum(jnp.where(hit, gates_ref[b, e : e + 1, :], 0.0), axis=1, keepdims=True)
                gate_ref[e, b * rows : (b + 1) * rows, :] = jnp.broadcast_to(gate, (rows, 128))
        picks.append(jnp.concatenate(pieces, axis=0).astype(jnp.bfloat16))
    step = min(512, width)
    for first in range(0, width, step):
        parts = [
            jnp.dot(
                picks[b],
                rows_ref[b * tokens : (b + 1) * tokens, first : first + step],
                preferred_element_type=jnp.float32,
            )
            for b in range(pair)
        ]
        for e in range(experts):
            x_ref[e, :, first : first + step] = jnp.concatenate(
                [part[e * rows : (e + 1) * rows] for part in parts], axis=0
            ).astype(jnp.bfloat16)


def plain_dispatch_kernel(slots_ref, rows_ref, x_ref):
    dispatch_kernel(slots_ref, None, rows_ref, x_ref, None)


def dispatch(slots, gates, rows_all, rows):
    blocks, experts, tokens = slots.shape
    width = rows_all.shape[1]
    pair = 2
    out = jax.ShapeDtypeStruct((experts, blocks * rows, width), jnp.bfloat16)
    table = pl.BlockSpec((pair, experts, tokens), lambda i: (i, 0, 0))
    source = pl.BlockSpec((pair * tokens, width), lambda i: (i, 0))
    target = pl.BlockSpec((experts, pair * rows, width), lambda i: (0, i, 0))
    settings = dict(
        grid=(blocks // pair,),
        compiler_params=pltpu.CompilerParams(vmem_limit_bytes=50 << 20),
        cost_estimate=pl.CostEstimate(
            flops=2 * blocks * experts * rows * tokens * width,
            bytes_accessed=2 * blocks * (tokens + experts * rows) * width,
            transcendentals=0,
        ),
    )
    if gates is None:
        return pl.pallas_call(
            plain_dispatch_kernel, out_shape=out, in_specs=[table, source], out_specs=target, name="pick", **settings
        )(slots, rows_all)
    return pl.pallas_call(
        dispatch_kernel,
        out_shape=(out, jax.ShapeDtypeStruct((experts, blocks * rows, 128), jnp.float32)),
        in_specs=[table, table, source],
        out_specs=[target, pl.BlockSpec((experts, pair * rows, 128), lambda i: (0, i, 0))],
        name="dispatch",
        **settings,
    )(slots, gates, rows_all)


def turned(left, right):
    return lax.dot_general(left, right, (((0,), (0,)), ((), ())), preferred_element_type=jnp.float32)


def across(left, right):
    return lax.dot_general(left, right, (((1,), (1,)), ((), ())), preferred_element_type=jnp.float32)


def expert_kernel(rows, first_ref, x_ref, c_ref, gate_ref, wg_ref, wu_ref, wd_ref,
                  o_ref, dx_ref, pre_ref, gated_ref):
    expert = pl.program_id(0)
    tile, width = x_ref.shape[1:]
    units = wg_ref.shape[2]
    room = o_ref.shape[2]
    blocks = tile // rows
    gate = gate_ref[0, :, 0:1]
    x = x_ref[0]
    c = c_ref[0]
    gate_pre = jnp.dot(x, wg_ref[0], preferred_element_type=jnp.float32)
    up_pre = jnp.dot(x, wu_ref[0], preferred_element_type=jnp.float32)
    back = across(c, wd_ref[0])
    sig = jax.nn.sigmoid(gate_pre)
    silu = gate_pre * sig
    act = (silu * up_pre).astype(jnp.bfloat16)
    act_float = act.astype(jnp.float32)
    grad_gate = jnp.sum(act_float * back, axis=1, keepdims=True)
    grad_act = back * gate
    grad_gate_pre = (grad_act * up_pre * sig * (1.0 + gate_pre * (1.0 - sig))).astype(jnp.bfloat16)
    grad_up_pre = (grad_act * silu).astype(jnp.bfloat16)
    gated = (act_float * gate).astype(jnp.bfloat16)

    def spread(values):
        values = values.reshape(blocks, rows, values.shape[1])
        if room > rows:
            empty = jnp.zeros((blocks, room - rows, values.shape[2]), jnp.float32)
            values = jnp.concatenate((values, empty), axis=1)
        return values.astype(jnp.bfloat16)

    step = min(512, width)
    for first in range(0, width, step):
        part = slice(first, first + step)
        out = jnp.dot(act, wd_ref[0, :, part], preferred_element_type=jnp.float32) * gate
        o_ref[:, 0, :, part] = spread(out)
        grad = across(grad_gate_pre, wg_ref[0, part, :]) + across(grad_up_pre, wu_ref[0, part, :])
        dx_ref[:, 0, :, part] = spread(grad)
    lanes = lax.broadcasted_iota(jnp.int32, (tile, 128), 1)
    dx_ref[:, 0, :, width:] = spread(jnp.where(lanes == first_ref[0] + expert, grad_gate, 0.0))

    pre_ref[0, :, :units] = grad_gate_pre
    pre_ref[0, :, units:] = grad_up_pre
    gated_ref[0] = gated


def weight_terms(x_ref, c_ref, pre_ref, gated_ref, gate_ref, up_ref, down_ref):
    units = gated_ref.shape[1]
    width = x_ref.shape[1]
    step = min(512, width)
    for first in range(0, width, step):
        part = slice(first, first + step)
        both = turned(x_ref[:, part], pre_ref[...])
        gate_ref[part, :] = both[:, :units]
        up_ref[part, :] = both[:, units:]
        down_ref[:, part] = turned(gated_ref[...], c_ref[:, part])


def weight_kernel(x_ref, c_ref, pre_ref, gated_ref, gate_ref, up_ref, down_ref):
    weight_terms(*(r.at[0] for r in (x_ref, c_ref, pre_ref, gated_ref, gate_ref, up_ref, down_ref)))


def weight_grads(x_slots, c_slots, pre, gated):
    experts, total, width = x_slots.shape
    units = gated.shape[2]
    step = min(512, width)
    part = pl.BlockSpec((1, total, step), lambda e, j: (e, 0, j))
    tall = pl.BlockSpec((1, step, units), lambda e, j: (e, j, 0))
    return pl.pallas_call(
        weight_kernel,
        grid=(experts, width // step),
        out_shape=(
            jax.ShapeDtypeStruct((experts, width, units), jnp.float32),
            jax.ShapeDtypeStruct((experts, width, units), jnp.float32),
            jax.ShapeDtypeStruct((experts, units, width), jnp.float32),
        ),
        in_specs=[
            part, part,
            pl.BlockSpec((1, total, 2 * units), lambda e, j: (e, 0, 0)),
            pl.BlockSpec((1, total, units), lambda e, j: (e, 0, 0)),
        ],
        out_specs=[tall, tall, pl.BlockSpec((1, units, step), lambda e, j: (e, 0, j))],
        compiler_params=pltpu.CompilerParams(vmem_limit_bytes=50 << 20),
        cost_estimate=pl.CostEstimate(
            flops=6 * experts * total * width * units,
            bytes_accessed=4 * experts * total * width + 12 * experts * width * units,
            transcendentals=0,
        ),
        name="weight_grads",
    )(x_slots, c_slots, pre, gated)


def expert_pass(first_expert, x_slots, c_slots, gate_slots, w_gate, w_up, w_down, blocks, room):
    experts, total, width = x_slots.shape
    units = w_gate.shape[2]
    rows = total // blocks
    group = next(n for n in (16, 8, 4, 2, 1) if blocks % n == 0 and (n * rows <= 768 or n == 1))
    tile = group * rows
    extra = 128
    tall = pl.BlockSpec((1, width, units), lambda e, r, _: (e, 0, 0))
    wide = pl.BlockSpec((1, units, width), lambda e, r, _: (e, 0, 0))
    slot = pl.BlockSpec((1, tile, width), lambda e, r, _: (e, r, 0))
    kernel = functools.partial(expert_kernel, rows)
    return pl.pallas_call(
        kernel,
        grid_spec=pltpu.PrefetchScalarGridSpec(
            num_scalar_prefetch=1,
            grid=(experts, total // tile),
            in_specs=[slot, slot, pl.BlockSpec((1, tile, 128), lambda e, r, _: (e, r, 0)), tall, tall, wide],
            out_specs=[
                pl.BlockSpec((group, 1, room, width), lambda e, r, _: (r, e, 0, 0)),
                pl.BlockSpec((group, 1, room, width + extra), lambda e, r, _: (r, e, 0, 0)),
                pl.BlockSpec((1, tile, 2 * units), lambda e, r, _: (e, r, 0)),
                pl.BlockSpec((1, tile, units), lambda e, r, _: (e, r, 0)),
            ],
        ),
        out_shape=(
            jax.ShapeDtypeStruct((blocks, experts, room, width), jnp.bfloat16),
            jax.ShapeDtypeStruct((blocks, experts, room, width + extra), jnp.bfloat16),
            jax.ShapeDtypeStruct((experts, total, 2 * units), jnp.bfloat16),
            jax.ShapeDtypeStruct((experts, total, units), jnp.bfloat16),
        ),
        compiler_params=pltpu.CompilerParams(vmem_limit_bytes=60 << 20),
        cost_estimate=pl.CostEstimate(
            flops=12 * experts * total * width * units,
            bytes_accessed=8 * experts * total * width + 6 * experts * width * units,
            transcendentals=experts * total * units,
        ),
        name="experts",
    )(first_expert, x_slots, c_slots, gate_slots, w_gate, w_up, w_down)


def combine_kernel(slots_ref, o_ref, dx_ref, out_ref, grad_ref):
    _, experts, tokens = slots_ref.shape
    room, width = o_ref.shape[2:]
    slots = slots_ref[0]
    picks = jnp.concatenate(
        [slot_hits(slots, e, room).astype(jnp.float32) for e in range(experts)], axis=0
    ).astype(jnp.bfloat16)
    for source, target in ((o_ref, out_ref), (dx_ref, grad_ref)):
        columns = target.shape[1]
        for first in range(0, columns, 512):
            part = slice(first, min(first + 512, columns))
            values = source[0, :, :, part].reshape(experts * room, part.stop - first)
            target[:, part] = turned(picks, values).astype(jnp.bfloat16)


def combine(slots, outs, grads):
    blocks, experts, tokens = slots.shape
    room, width = outs.shape[2:]
    wider = grads.shape[3]
    return pl.pallas_call(
        combine_kernel,
        grid=(blocks,),
        out_shape=(
            jax.ShapeDtypeStruct((blocks * tokens, width), jnp.bfloat16),
            jax.ShapeDtypeStruct((blocks * tokens, wider), jnp.bfloat16),
        ),
        in_specs=[
            pl.BlockSpec((1, experts, tokens), lambda i: (i, 0, 0)),
            pl.BlockSpec((1, experts, room, width), lambda i: (i, 0, 0, 0)),
            pl.BlockSpec((1, experts, room, wider), lambda i: (i, 0, 0, 0)),
        ],
        out_specs=[
            pl.BlockSpec((tokens, width), lambda i: (i, 0)),
            pl.BlockSpec((tokens, wider), lambda i: (i, 0)),
        ],
        compiler_params=pltpu.CompilerParams(vmem_limit_bytes=50 << 20),
        cost_estimate=pl.CostEstimate(
            flops=2 * blocks * experts * room * tokens * (width + wider),
            bytes_accessed=2 * blocks * (tokens + experts * room) * (width + wider),
            transcendentals=0,
        ),
        name="combine",
    )(slots, outs, grads)


MESH = pl.DeviceIdType.MESH


def place():
    dp, z = lax.axis_index("dp"), lax.axis_index("tensor")
    return dp // 4, dp // 2 % 2, dp % 2, z


def peer(y, x, core, z):
    return (y * 4 + x * 2 + core, z)


def block_of(y, x, core, z):
    return (y * 4 + x * 2 + core) * 4 + z


def greet(line):
    y, x, core, z = place()
    barrier = pltpu.get_barrier_semaphore()
    for near in ((y, x, 1 - core, z), (y, 1 - x, core, z), (1 - y, x, core, z)):
        pl.semaphore_signal(barrier, inc=1, device_id=peer(*near), device_id_type=MESH)

    @pl.when(z > 0)
    def _():
        pl.semaphore_signal(barrier, inc=1, device_id=peer(y, x, core, z - 1), device_id_type=MESH)

    @pl.when(z < line - 1)
    def _():
        pl.semaphore_signal(barrier, inc=1, device_id=peer(y, x, core, z + 1), device_id_type=MESH)

    pl.semaphore_wait(barrier, 3 + (z + line - 1) // line + (2 * line - 2 - z) // line)


def either(first, second, take):
    return first * (1 - take) + second * take


def remote(source, target, send_sem, recv_sem, where):
    return pltpu.make_async_remote_copy(
        src_ref=source, dst_ref=target, send_sem=send_sem, recv_sem=recv_sem,
        device_id=peer(*where), device_id_type=MESH,
    )


def landed(target, sem):
    pltpu.make_async_copy(target, target, sem).wait()


def slot_order(y, x, core, z):
    return ((y * 2 + x) * 4 + z) * 2 + core


def near_first(z, i):
    side = z // 2
    low = either(z, 3 - z, side)
    first, second = (4 - i) // 4, (5 - i) // 4 - (4 - i) // 4
    return either(i + low * (first - second), 3 - i - low * (first - second), side)


def gather_dispatch_kernel(line, rows, slots_ref, hidden_ref, gates_ref, cots_ref,
                           rows_out, gates_out, x_out, c_out, gate_out,
                           in_c, in_x, in_gate, stage_c, stage_x, stage_gate,
                           local_sem, send_sem, recv_sem, load_sem, store_sem):
    y, x, core, z = place()
    tokens, width = hidden_ref.shape
    experts = slots_ref.shape[1]
    first_expert = (y * 4 + x * 2 + core) * experts
    owns, outs = (hidden_ref, gates_ref), (rows_out, gates_out)
    near_x, near_y, sibling = (y, 1 - x, core, z), (1 - y, x, core, z), (y, x, 1 - core, z)
    last = 24
    greet(line)

    def span(n, block):
        count = owns[n].shape[0]
        return outs[n].at[pl.ds(block * count, count)]

    def spot(m):
        q = m % 4
        i = m // 4 - (q + 1) // 2
        live = (i >= 0) & (i < line)
        held = i * live.astype(jnp.int32)
        yy, xx = (y + q // 2) % 2, (x + q % 2) % 2
        return q, held, live, yy, xx, near_first(z, held)

    def sends(m):
        q, i, live, yy, xx, zz = spot(m)
        block = block_of(yy, xx, core, zz)
        own = live & (q == 0)
        table = (
            (own & (zz <= z) & (z < line - 1), (y, x, core, z + 1)),
            (own & (zz >= z) & (z > 0), (y, x, core, z - 1)),
            (own | (live & (q == 2) & (zz % 2 == 1)), near_x),
            (own | (live & (q == 1) & (zz % 2 == 0)), near_y),
            (live, sibling),
        )
        for lane, (wanted, where) in enumerate(table):
            for n in range(2):
                part = span(n, block)
                yield wanted, remote(part, part, send_sem.at[n, lane, m], recv_sem.at[n, block], where)

    def load_c(chip):
        yy, xx, zz = chip // 8, chip // 4 % 2, chip % 4
        for c in range(2):
            b = block_of(yy, xx, c, zz)
            yield pltpu.make_async_copy(
                cots_ref.at[pl.ds(b * tokens, tokens)], in_c.at[pl.ds(c * tokens, tokens)], load_sem.at[0, c]
            )

    def load_x(yy, xx, zz):
        for c in range(2):
            b = block_of(yy, xx, c, zz)
            yield pltpu.make_async_copy(
                rows_out.at[pl.ds(b * tokens, tokens)], in_x.at[pl.ds(c * tokens, tokens)], load_sem.at[1, c]
            )
            yield pltpu.make_async_copy(
                gates_out.at[pl.ds(b * gates_ref.shape[0] + first_expert, experts)], in_gate.at[c], load_sem.at[2, c]
            )

    def store(stage, target, lane, chip):
        return pltpu.make_async_copy(stage, target.at[:, pl.ds(chip * 2 * rows, 2 * rows)], store_sem.at[lane])

    def pick(source, target, yy, xx, zz, gated):
        picks = []
        for c in range(2):
            slots = slots_ref[block_of(yy, xx, c, zz)]
            pieces = []
            for e in range(experts):
                hit = slot_hits(slots, e, rows)
                pieces.append(hit.astype(jnp.float32))
                if gated:
                    gate = jnp.sum(jnp.where(hit, in_gate[c, e : e + 1, :], 0.0), axis=1, keepdims=True)
                    stage_gate[e, c * rows : (c + 1) * rows, :] = jnp.broadcast_to(gate, (rows, 128))
            picks.append(jnp.concatenate(pieces, axis=0).astype(jnp.bfloat16))
        step = min(512, width)
        for first in range(0, width, step):
            parts = [
                jnp.dot(
                    picks[c], source[c * tokens : (c + 1) * tokens, first : first + step],
                    preferred_element_type=jnp.float32,
                )
                for c in range(2)
            ]
            for e in range(experts):
                target[e, :, first : first + step] = jnp.concatenate(
                    [part[e * rows : (e + 1) * rows] for part in parts], axis=0
                ).astype(jnp.bfloat16)

    mine = block_of(y, x, core, z)
    local = [pltpu.make_async_copy(owns[n], span(n, mine), local_sem.at[n]) for n in range(2)]
    for copy in local:
        copy.start()
    for copy in load_c(0):
        copy.start()
    for copy in local:
        copy.wait()
    chips = 4 * line
    lag = 2

    def work(m, carry):
        q, i, live, yy, xx, zz = spot(m)

        @pl.when((m < last) & live & (q + i > 0))
        def _():
            for n in range(2):
                landed(span(n, block_of(yy, xx, core, zz)), recv_sem.at[n, block_of(yy, xx, core, zz)])

        for wanted, copy in sends(m):
            pl.when((m < last) & wanted)(copy.start)

        back = m - lag
        q = (back + 8) % 4
        i = (back + 8) // 4 - 2 - (q + 1) // 2
        live = (i >= 0) & (i < line)
        held = i * live.astype(jnp.int32)
        yy, xx = (y + q // 2) % 2, (x + q % 2) % 2
        zz = near_first(z, held)
        chip = (yy * 2 + xx) * 4 + zz

        @pl.when(live)
        def _():
            block = block_of(yy, xx, 1 - core, zz)
            for n in range(2):
                landed(span(n, block), recv_sem.at[n, block])
            for copy in load_x(yy, xx, zz):
                copy.start()

        @pl.when(m < chips)
        def _():
            for copy in load_c(m):
                copy.wait()

            @pl.when(m > 0)
            def _():
                store(stage_c, c_out, 0, m - 1).wait()

            pick(in_c, stage_c, m // 8, m // 4 % 2, m % 4, False)
            store(stage_c, c_out, 0, m).start()

            @pl.when(m + 1 < chips)
            def _():
                for copy in load_c(m + 1):
                    copy.start()

        @pl.when(live)
        def _():
            @pl.when(q + held > 0)
            def _():
                store(stage_x, x_out, 1, chip).wait()
                store(stage_gate, gate_out, 2, chip).wait()

            for copy in load_x(yy, xx, zz):
                copy.wait()
            pick(in_x, stage_x, yy, xx, zz, True)
            store(stage_x, x_out, 1, chip).start()
            store(stage_gate, gate_out, 2, chip).start()

        return carry

    lax.fori_loop(0, last + lag, work, 0)
    store(stage_c, c_out, 0, chips - 1).wait()
    store(stage_x, x_out, 1, 0).wait()
    store(stage_gate, gate_out, 2, 0).wait()

    def finish(m, carry):
        for wanted, copy in sends(m):
            pl.when(wanted)(copy.wait_send)
        return carry

    lax.fori_loop(0, last, finish, 0)


def gather_dispatch(slots, hidden, gates, cots_all, rows, collective_id):
    line = 4
    blocks, experts, tokens = slots.shape
    width = hidden.shape[1]
    pair = 2 * rows
    low, wide = jnp.bfloat16, jnp.float32
    any_ref = pl.BlockSpec(memory_space=pl.ANY)
    vmem = pl.BlockSpec(memory_space=pltpu.VMEM)
    dma = pltpu.SemaphoreType.DMA
    slot_shape = jax.ShapeDtypeStruct((experts, blocks * rows, width), low)
    return pl.pallas_call(
        functools.partial(gather_dispatch_kernel, line, rows),
        out_shape=(
            jax.ShapeDtypeStruct((blocks * tokens, width), low),
            jax.ShapeDtypeStruct((blocks * gates.shape[0], tokens), wide),
            slot_shape,
            slot_shape,
            jax.ShapeDtypeStruct((experts, blocks * rows, 128), wide),
        ),
        in_specs=[vmem, any_ref, any_ref, any_ref],
        out_specs=[any_ref] * 5,
        scratch_shapes=[
            pltpu.VMEM((2 * tokens, width), low),
            pltpu.VMEM((2 * tokens, width), low),
            pltpu.VMEM((2, experts, tokens), wide),
            pltpu.VMEM((experts, pair, width), low),
            pltpu.VMEM((experts, pair, width), low),
            pltpu.VMEM((experts, pair, 128), wide),
            dma((2,)),
            dma((2, 5, 24)),
            dma((2, blocks)),
            dma((3, 2)),
            dma((3,)),
        ],
        compiler_params=pltpu.CompilerParams(
            collective_id=collective_id, has_side_effects=True, vmem_limit_bytes=40 << 20
        ),
        cost_estimate=pl.CostEstimate(
            flops=4 * blocks * experts * rows * tokens * width, bytes_accessed=200 << 20, transcendentals=0
        ),
        name="gather_dispatch",
    )(slots, hidden, gates, cots_all)[2:]


def reduce_kernel(line, slots_ref, grads_ref, outs_ref, sum_ref, part_ref,
                  grad_in, out_in, out_stage, stage, near, far_x, far_y, from_x, from_y, up, down,
                  in_sem, part_sem, stage_sem, near_sem, send_sem, far_sem, x_sem, y_sem, line_sem):
    y, x, core, z = place()
    tokens, width = sum_ref.shape
    half = tokens // 2
    experts, room = grads_ref.shape[1:3]
    rounds = line
    greet(line)

    def goal(r):
        early = 1 - r // 2
        return (line - 1) * (r % 2) * early + (r - 1) * (1 - early)

    def spot_at(q):
        r, p = q // 8, q % 8
        own = (1 - p % 2) * ((p + 7) // 8) + p // 7
        column = own * (p // 2 - 1 + p // 7) + (1 - own) * ((p + 1) // 2)
        dy, dx = (column + 1) % 2, 1 - column // 2
        target_core = core * own + (1 - core) * (1 - own)
        return (y + dy) % 2, (x + dx) % 2, target_core, goal(r)

    def load(q):
        b = slot_order(*spot_at(q))
        return (
            pltpu.make_async_copy(grads_ref.at[b], grad_in.at[q % 2], in_sem.at[0, q % 2]),
            pltpu.make_async_copy(outs_ref.at[b], out_in.at[q % 2], in_sem.at[1, q % 2]),
        )

    def to_part(q):
        b = block_of(*spot_at(q))
        return pltpu.make_async_copy(out_stage.at[q % 2], part_ref.at[pl.ds(b * tokens, tokens)], part_sem.at[q % 2])

    def to_sibling(r, j):
        return pltpu.make_async_remote_copy(
            src_ref=stage.at[j], dst_ref=near.at[r * 4 + j], send_sem=stage_sem.at[j], recv_sem=near_sem.at[r * 4 + j],
            device_id=peer(y, x, 1 - core, z), device_id_type=MESH,
        )

    near_x, near_y = peer(y, 1 - x, core, z), peer(1 - y, x, core, z)

    def rows(h):
        return pl.ds(h * half, half)

    def cross(kind, r):
        column, h, target, sem, index, lane = {
            "far_x": (0, 0, far_x.at[r], far_sem.at[0, r], near_x, 0),
            "far_y": (0, 1, far_y.at[r], far_sem.at[1, r], near_y, 1),
            "x0": (1, 0, from_x.at[r, rows(0)], x_sem.at[r, 0], near_x, 2),
            "x1": (1, 1, from_x.at[r, rows(1)], x_sem.at[r, 1], near_x, 3),
            "y0": (2, 0, from_y.at[r, rows(0)], y_sem.at[r, 0], near_y, 4),
            "y1": (2, 1, from_y.at[r, rows(1)], y_sem.at[r, 1], near_y, 5),
        }[kind]
        return pltpu.make_async_remote_copy(
            src_ref=near.at[r * 4 + column, rows(h)], dst_ref=target, send_sem=send_sem.at[lane, r], recv_sem=sem,
            device_id=index, device_id_type=MESH,
        )

    def along(sign, r, h):
        target = up if sign > 0 else down
        lane = 0 if sign > 0 else 1
        return pltpu.make_async_remote_copy(
            src_ref=near.at[r * 4 + 3, rows(h)], dst_ref=target.at[r, rows(h)],
            send_sem=send_sem.at[6 + lane + 2 * h, r], recv_sem=line_sem.at[lane, r, h],
            device_id=peer(y, x, core, z + sign), device_id_type=MESH,
        )

    def term(q, source, target_width, store):
        picks = jnp.concatenate(
            [slot_hits(slots_ref[block_of(*spot_at(q))], e, room).astype(jnp.float32) for e in range(experts)], axis=0
        ).astype(jnp.bfloat16)
        for first in range(0, target_width, 512):
            part = slice(first, min(first + 512, target_width))
            values = source[q % 2, :, :, part].reshape(experts * room, part.stop - first)
            store(part, turned(picks, values))

    for copy in load(0):
        copy.start()

    def one(r, p, j, own):
        q = r * 8 + p
        for copy in load(q):
            copy.wait()

        @pl.when(q + 1 < rounds * 8)
        def _():
            for copy in load(q + 1):
                copy.start()

        if own:
            near_slot = r * 4 + j
            to_sibling(r, j).wait_recv()

            def keep(part, value):
                near[near_slot, :, part] = (value + near[near_slot, :, part].astype(jnp.float32)).astype(jnp.bfloat16)

            term(q, grad_in, width, keep)
        else:

            @pl.when(r > 0)
            def _():
                to_sibling(r - 1, j).wait_send()

            def keep(part, value):
                stage[j, :, part] = value.astype(jnp.bfloat16)

            term(q, grad_in, width, keep)
            to_sibling(r, j).start()

        @pl.when(q >= 2)
        def _():
            to_part(q - 2).wait()

        def put(part, value):
            out_stage[q % 2, :, part] = value.astype(jnp.bfloat16)

        term(q, out_in, out_stage.shape[2], put)
        to_part(q).start()

    def add(target, h, *sources):
        for first in range(0, width, 512):
            part = slice(first, min(first + 512, width))
            total = near[target, h, part].astype(jnp.float32)
            for source in sources:
                total = total + source(part).astype(jnp.float32)
            near[target, h, part] = total.astype(jnp.bfloat16)

    def work(s, carry):
        @pl.when(s < rounds)
        def _():
            r = s
            one(r, 0, 0, 0)
            for j in range(4):
                if j < 3:
                    one(r, 2 * j + 1, j + 1, 0)
                one(r, min(2 * j + 2, 7), j, 1)
                for kind in (("far_x", "far_y"), ("x0",), ("y1",), ())[j]:
                    cross(kind, r).start()
            cross("far_y", r).wait_recv()
            add(r * 4 + 1, rows(1), lambda part: far_y[r, :, part])
            cross("x1", r).start()
            cross("far_x", r).wait_recv()
            add(r * 4 + 2, rows(0), lambda part: far_x[r, :, part])
            cross("y0", r).start()

        @pl.when((s >= 1) & (s < rounds + 1))
        def _():
            r = s - 1
            for kind in ("x0", "x1", "y0", "y1"):
                cross(kind, r).wait_recv()
            for h in range(2):
                add(
                    r * 4 + 3,
                    rows(h),
                    lambda part: from_x[r, rows(h), part],
                    lambda part: from_y[r, rows(h), part],
                )

        for hop in range(line - 1):
            r = s - 1 - hop
            live = (r >= 0) & (r < rounds)
            held = r * live.astype(jnp.int32)

            @pl.when(live & (goal(held) > z) & (z == hop))
            def _():
                for h in range(2):
                    if hop:
                        along(1, held, h).wait_recv()
                        add(held * 4 + 3, rows(h), lambda part: up[held, rows(h), part])
                    along(1, held, h).start()

            @pl.when(live & (goal(held) < z) & (line - 1 - z == hop))
            def _():
                for h in range(2):
                    if hop:
                        along(-1, held, h).wait_recv()
                        add(held * 4 + 3, rows(h), lambda part: down[held, rows(h), part])
                    along(-1, held, h).start()

        return carry

    lax.fori_loop(0, rounds + line - 1, work, 0)

    mine = (z + (z + 2) // 3) % 4 + z // 3
    sum_ref[...] = near[mine * 4 + 3].astype(jnp.float32)

    @pl.when(z > 0)
    def _():
        for h in range(2):
            along(1, mine, h).wait_recv()
        sum_ref[...] += up[mine].astype(jnp.float32)

    @pl.when(z < line - 1)
    def _():
        for h in range(2):
            along(-1, mine, h).wait_recv()
        sum_ref[...] += down[mine].astype(jnp.float32)

    def finish(r, carry):
        for kind in ("far_x", "far_y", "x0", "x1", "y0", "y1"):
            cross(kind, r).wait_send()

        @pl.when(goal(r) > z)
        def _():
            for h in range(2):
                along(1, r, h).wait_send()

        @pl.when(goal(r) < z)
        def _():
            for h in range(2):
                along(-1, r, h).wait_send()

        return carry

    lax.fori_loop(0, rounds, finish, 0)
    for j in range(4):
        to_sibling(rounds - 1, j).wait_send()
    for q in (rounds * 8 - 2, rounds * 8 - 1):
        to_part(q).wait()


def reduce_all(slots, outs, grads, collective_id):
    blocks, experts, tokens = slots.shape
    room, width = outs.shape[2:]
    wider = grads.shape[3]
    line = 4
    low = jnp.bfloat16
    any_ref = pl.BlockSpec(memory_space=pl.ANY)
    vmem = pl.BlockSpec(memory_space=pltpu.VMEM)
    dma = pltpu.SemaphoreType.DMA
    return pl.pallas_call(
        functools.partial(reduce_kernel, line),
        out_shape=(
            jax.ShapeDtypeStruct((tokens, wider), jnp.float32),
            jax.ShapeDtypeStruct((blocks * tokens, width), low),
        ),
        in_specs=[vmem, any_ref, any_ref],
        out_specs=[vmem, any_ref],
        scratch_shapes=[
            pltpu.VMEM((2, experts, room, wider), low),
            pltpu.VMEM((2, experts, room, width), low),
            pltpu.VMEM((2, tokens, width), low),
            pltpu.VMEM((4, tokens, wider), low),
            pltpu.VMEM((line * 4, tokens, wider), low),
            pltpu.VMEM((line, tokens // 2, wider), low),
            pltpu.VMEM((line, tokens // 2, wider), low),
            pltpu.VMEM((line, tokens, wider), low),
            pltpu.VMEM((line, tokens, wider), low),
            pltpu.VMEM((line, tokens, wider), low),
            pltpu.VMEM((line, tokens, wider), low),
            dma((2, 2)),
            dma((2,)),
            dma((4,)),
            dma((line * 4,)),
            dma((10, line)),
            dma((2, line)),
            dma((line, 2)),
            dma((line, 2)),
            dma((2, line, 2)),
        ],
        compiler_params=pltpu.CompilerParams(
            collective_id=collective_id, has_side_effects=True, vmem_limit_bytes=62 << 20
        ),
        cost_estimate=pl.CostEstimate(
            flops=2 * blocks * experts * room * tokens * (width + wider),
            bytes_accessed=2 * blocks * experts * room * (width + wider),
            transcendentals=0,
        ),
        name="reduce_all",
    )(slots, grads, outs)


class LineGather:
    def __init__(self, own, out, send_sem, recv_sem, line):
        self.own, self.out, self.send_sem, self.recv_sem, self.line = own, out, send_sem, recv_sem, line
        self.spot = place()
        self.rows = own.shape[0]

    def view(self, block):
        return self.out.at[pl.ds(block * self.rows, self.rows)]

    def inside(self, block):
        return (block >= 0) & (block < self.line)

    def copy(self, sign, step):
        y, x, core, z = self.spot
        block = z - sign * step
        lane = (1 - sign) // 2
        source = self.own if step == 0 else self.view(block)
        return remote(
            source, self.view(block), self.send_sem.at[lane, step], self.recv_sem.at[lane, step], (y, x, core, z + sign)
        )

    def sends(self, sign, step):
        z = self.spot[3]
        return self.inside(z - sign * step) & self.inside(z + sign)

    def begin(self):
        for sign in (1, -1):
            pl.when(self.sends(sign, 0))(self.copy(sign, 0).start)

    def advance(self, step):
        z = self.spot[3]
        for sign in (1, -1):
            block = z - sign * (step + 1)
            lane = (1 - sign) // 2

            @pl.when(self.inside(block))
            def _():
                landed(self.view(block), self.recv_sem.at[lane, step])

            if step + 1 < self.line - 1:
                pl.when(self.sends(sign, step + 1))(self.copy(sign, step + 1).start)

    def finish(self):
        for sign in (1, -1):
            for step in range(self.line - 1):
                pl.when(self.sends(sign, step))(self.copy(sign, step).wait_send)


def start_kernel(line, hidden_ref, wq_ref, wk_ref, wv_ref, wo_ref, slots_ref, hidden_out, joined_out, wo_out, slots_out,
                 local_sem, line_send, line_recv, plane_send, plane_recv, slot_send, slot_recv, slot_line_send, slot_line_recv):
    y, x, core, z = place()
    owns = (wq_ref, wk_ref, wv_ref, wo_ref)
    near_x, near_y, sibling = (y, 1 - x, core, z), (1 - y, x, core, z), (y, x, 1 - core, z)

    def view(n, yy, xx, half=None):
        group = yy * 4 + xx * 2 + core
        rows, columns = owns[n].shape
        first, count = (0, rows) if half is None else (half * (rows // 2), rows // 2)
        if n < 3:
            return joined_out.at[pl.ds(group * rows + first, count), pl.ds(n * columns, columns)]
        return wo_out.at[pl.ds(first, count), pl.ds(pl.multiple_of(group * columns, columns), columns)]

    kinds = ("x", "y", "s", "fy", "fx", "sx", "sy", "sf")

    def copy(kind, n):
        source, target, where = {
            "x": (owns[n], view(n, y, x), near_x),
            "y": (owns[n], view(n, y, x), near_y),
            "s": (owns[n], view(n, y, x), sibling),
            "fy": (view(n, y, 1 - x, 0), view(n, y, 1 - x, 0), near_y),
            "fx": (view(n, 1 - y, x, 1), view(n, 1 - y, x, 1), near_x),
            "sx": (view(n, y, 1 - x), view(n, y, 1 - x), sibling),
            "sy": (view(n, 1 - y, x), view(n, 1 - y, x), sibling),
            "sf": (view(n, 1 - y, 1 - x), view(n, 1 - y, 1 - x), sibling),
        }[kind]
        lane = kinds.index(kind)
        return remote(source, target, plane_send.at[lane, n], plane_recv.at[lane, n], where)

    def other(n, yy, xx):
        group = yy * 4 + xx * 2 + 1 - core
        rows, columns = owns[n].shape
        if n < 3:
            return joined_out.at[pl.ds(group * rows, rows), pl.ds(n * columns, columns)]
        return wo_out.at[pl.ds(0, rows), pl.ds(pl.multiple_of(group * columns, columns), columns)]

    barrier = pltpu.get_barrier_semaphore()
    shifts = [(dy, dx, dc) for dy in range(2) for dx in range(2) for dc in range(2) if dy + dx + dc]
    plane = [((y + dy) % 2, (x + dx) % 2, (core + dc) % 2, z) for dy, dx, dc in shifts]
    for other_spot in plane:
        pl.semaphore_signal(barrier, inc=1, device_id=peer(*other_spot), device_id_type=MESH)
    for step in (-1, 1):

        @pl.when((z + step >= 0) & (z + step < line))
        def _():
            pl.semaphore_signal(barrier, inc=1, device_id=peer(y, x, core, z + step), device_id_type=MESH)

    pl.semaphore_wait(barrier, 7 + (z + line - 1) // line + (2 * line - 2 - z) // line)
    experts = slots_out.shape[1]
    group = peer(y, x, core, z)[0]
    slot_copies = []
    for n, other_spot in enumerate(plane):
        their_group = peer(*other_spot)[0]
        slot_copies.append(
            remote(
                slots_ref.at[pl.ds(their_group * experts, experts)], slots_out.at[z * 8 + group],
                slot_send.at[n], slot_recv.at[group], other_spot,
            )
        )
    own_slots = pltpu.make_async_copy(
        slots_ref.at[pl.ds(group * experts, experts)], slots_out.at[z * 8 + group], local_sem.at[5]
    )
    own_slots.start()
    slot_line = LineGather(slots_out.at[pl.ds(z * 8, 8)], slots_out, slot_line_send, slot_line_recv, line)
    hidden = LineGather(hidden_ref, hidden_out, line_send, line_recv, line)
    locals_ = [pltpu.make_async_copy(hidden_ref, hidden.view(z), local_sem.at[4])]
    locals_ += [pltpu.make_async_copy(owns[n], view(n, y, x), local_sem.at[n]) for n in range(4)]
    for slot_copy in slot_copies:
        slot_copy.start()
    hidden.begin()
    for n in range(4):
        for kind in ("x", "y", "s"):
            copy(kind, n).start()
    for local in locals_:
        local.start()
    for n in range(4):
        landed(view(n, y, 1 - x), plane_recv.at[0, n])
        copy("fy", n).start()
        copy("sx", n).start()
        landed(view(n, 1 - y, x), plane_recv.at[1, n])
        copy("fx", n).start()
        copy("sy", n).start()
    own_slots.wait()
    for other_spot in plane:
        their_group = peer(*other_spot)[0]
        landed(slots_out.at[z * 8 + their_group], slot_recv.at[their_group])
    slot_line.begin()
    hidden.advance(0)
    slot_line.advance(0)
    for n in range(4):
        landed(view(n, 1 - y, 1 - x, 0), plane_recv.at[3, n])
        landed(view(n, 1 - y, 1 - x, 1), plane_recv.at[4, n])
        copy("sf", n).start()
    for step in range(1, line - 1):
        slot_line.advance(step)
        hidden.advance(step)
    for n in range(4):
        landed(other(n, y, x), plane_recv.at[2, n])
        landed(other(n, y, 1 - x), plane_recv.at[5, n])
        landed(other(n, 1 - y, x), plane_recv.at[6, n])
        landed(other(n, 1 - y, 1 - x), plane_recv.at[7, n])
    hidden.finish()
    slot_line.finish()
    for slot_copy in slot_copies:
        slot_copy.wait_send()
    for n in range(4):
        for kind in kinds:
            copy(kind, n).wait_send()
    for local in locals_:
        local.wait()


def start_exchange(hidden, w_query, w_key, w_value, w_out, slots, collective_id):
    line = 4
    any_ref = pl.BlockSpec(memory_space=pl.ANY)
    dma = pltpu.SemaphoreType.DMA
    rows, width = hidden.shape
    part, columns = w_query.shape
    low = jnp.bfloat16
    return pl.pallas_call(
        functools.partial(start_kernel, line),
        out_shape=(
            jax.ShapeDtypeStruct((line * rows, width), low),
            jax.ShapeDtypeStruct((8 * part, 3 * columns), low),
            jax.ShapeDtypeStruct((w_out.shape[0], 8 * w_out.shape[1]), low),
            jax.ShapeDtypeStruct((line * 8, slots.shape[0] // 8, slots.shape[1]), slots.dtype),
        ),
        in_specs=[any_ref] * 6,
        out_specs=[any_ref] * 4,
        scratch_shapes=[
            dma((6,)), dma((2, line)), dma((2, line)), dma((8, 4)), dma((8, 4)),
            dma((7,)), dma((8,)), dma((2, line)), dma((2, line)),
        ],
        compiler_params=pltpu.CompilerParams(collective_id=collective_id, has_side_effects=True),
        cost_estimate=pl.CostEstimate(flops=0, bytes_accessed=150 << 20, transcendentals=0),
        name="start_exchange",
    )(hidden, w_query, w_key, w_value, w_out, slots)


class LineReduce:
    def __init__(self, part, up, down, send_sem, recv_sem, line):
        self.part, self.up, self.down = part, up, down
        self.send_sem, self.recv_sem, self.line = send_sem, recv_sem, line
        self.spot = place()

    def copy(self, sign, goal):
        y, x, core, z = self.spot
        lane = (1 - sign) // 2
        target = self.up if sign > 0 else self.down
        return remote(
            self.part.at[goal], target.at[goal], self.send_sem.at[lane, goal], self.recv_sem.at[lane, goal],
            (y, x, core, z + sign),
        )

    def order(self, i):
        z = self.spot[3]
        return either(self.line - 1 - i, i, z * 2 // self.line)

    def lead(self, goal):
        z = self.spot[3]
        pl.when((z == 0) & (goal > 0))(self.copy(1, goal).start)
        pl.when((z == self.line - 1) & (goal < z))(self.copy(-1, goal).start)

    def advance(self, unit, total_ref):
        z, line = self.spot[3], self.line
        for sign in (1, -1):
            goal = line - 1 - unit + z if sign > 0 else unit - line + 1 + z
            live = ((z > 0) & (goal < line)) if sign > 0 else ((z < line - 1) & (goal >= 0))
            inbox = self.up if sign > 0 else self.down

            @pl.when(live)
            def _():
                self.copy(sign, goal).wait_recv()
                if unit < line - 1:
                    self.part[goal] = (
                        self.part[goal].astype(jnp.float32) + inbox[goal].astype(jnp.float32)
                    ).astype(jnp.bfloat16)
                    self.copy(sign, goal).start()
                else:
                    total_ref[...] += inbox[goal].astype(jnp.float32)

    def finish(self):
        z = self.spot[3]

        def step(goal, carry):
            pl.when(goal > z)(self.copy(1, goal).wait_send)
            pl.when(goal < z)(self.copy(-1, goal).wait_send)
            return carry

        lax.fori_loop(0, self.line, step, 0)


def mixed_out_kernel(line, mixed_ref, w_ref, residual_ref, gain_ref, router_ref,
                     x_ref, hidden_ref, probs_ref, part, up, down, send_sem, recv_sem):
    rows, width = x_ref.shape
    greet(line)
    reduce = LineReduce(part, up, down, send_sem, recv_sem, line)
    z = reduce.spot[3]

    def term(i, carry):
        goal = reduce.order(i)
        first = pl.multiple_of(goal * rows, rows)
        for column in range(0, width, 512):
            piece = slice(column, column + 512)
            value = jnp.dot(mixed_ref[pl.ds(first, rows), :], w_ref[:, piece], preferred_element_type=jnp.float32)

            @pl.when(goal == z)
            def _():
                x_ref[:, piece] = value

            part[goal, :, piece] = value.astype(jnp.bfloat16)
        reduce.lead(goal)
        return carry

    lax.fori_loop(0, line, term, 0)
    for unit in range(1, line):
        reduce.advance(unit, x_ref)
    x_one = x_ref[...] + residual_ref[...].astype(jnp.float32)
    x_ref[...] = x_one
    scale = lax.rsqrt(jnp.mean(x_one * x_one, axis=-1, keepdims=True) + norm_eps)
    hidden = (x_one * scale * gain_ref[...]).astype(jnp.bfloat16)
    hidden_ref[...] = hidden
    logits = lax.dot_general(
        router_ref[...], hidden, (((1,), (1,)), ((), ())), preferred_element_type=jnp.float32
    )
    shifted = jnp.exp(logits - jnp.max(logits, axis=0, keepdims=True))
    probs_ref[...] = shifted / jnp.sum(shifted, axis=0, keepdims=True)
    reduce.finish()


def mixed_out(mixed, w_out, residual, gain, router_turned, collective_id):
    line = 4
    rows, width = residual.shape
    experts = router_turned.shape[0]
    vmem = pl.BlockSpec(memory_space=pltpu.VMEM)
    dma = pltpu.SemaphoreType.DMA
    block = pltpu.VMEM((line, rows, width), jnp.bfloat16)
    return pl.pallas_call(
        functools.partial(mixed_out_kernel, line),
        out_shape=(
            jax.ShapeDtypeStruct((rows, width), jnp.float32),
            jax.ShapeDtypeStruct((rows, width), jnp.bfloat16),
            jax.ShapeDtypeStruct((experts, rows), jnp.float32),
        ),
        in_specs=[vmem] * 5,
        out_specs=[vmem] * 3,
        scratch_shapes=[block, block, block, dma((2, line)), dma((2, line))],
        compiler_params=pltpu.CompilerParams(
            collective_id=collective_id, has_side_effects=True, vmem_limit_bytes=56 << 20
        ),
        cost_estimate=pl.CostEstimate(flops=0, bytes_accessed=150 << 20, transcendentals=0),
        name="mixed_out",
    )(mixed, w_out, residual, gain.reshape(1, width), router_turned)


class Butterfly:
    def __init__(self, data, total, from_core, from_x, from_y, from_z, sums, send_sem, recv_sem):
        self.data, self.total, self.sums = data, total, sums
        self.boxes = {"core": from_core, "x": from_x, "y": from_y}
        self.from_z, self.send_sem, self.recv_sem = from_z, send_sem, recv_sem
        y, x, core, z = self.spot = place()
        self.width = data.shape[1]
        self.near = {"core": (y, x, 1 - core, z), "x": (y, 1 - x, core, z), "y": (1 - y, x, core, z)}
        half, quarter, eighth = self.width // 2, self.width // 4, self.width // 8
        first = core * half
        self.kept = {"core": (first, half), "x": (first + x * quarter, quarter)}
        self.kept["y"] = (first + x * quarter + y * eighth, eighth)
        self.away = {
            "core": ((1 - core) * half, half),
            "x": (first + (1 - x) * quarter, quarter),
            "y": (first + x * quarter + (1 - y) * eighth, eighth),
        }

    def part(self, span):
        return pl.ds(pl.multiple_of(span[0], span[1]), span[1])

    def fold_copy(self, axis):
        lane = ("core", "x", "y").index(axis)
        return remote(
            self.data.at[:, self.part(self.away[axis])], self.boxes[axis], self.send_sem.at[lane],
            self.recv_sem.at[lane], self.near[axis],
        )

    def fold(self, axis):
        copy = self.fold_copy(axis)
        copy.start()
        copy.wait()
        self.data[:, self.part(self.kept[axis])] += self.boxes[axis][...]

    def line_step(self, step):
        y, x, core, z = self.spot
        other = (z + 1 - 2 * (z % 2)) if step == 0 else (z + 2) % 4
        piece = self.part(self.kept["y"])
        source = self.data.at[:, piece] if step == 0 else self.sums
        copy = remote(
            source, self.from_z.at[step], self.send_sem.at[3 + step], self.recv_sem.at[3 + step], (y, x, core, other)
        )
        copy.start()
        copy.wait()
        if step == 0:
            self.sums[...] = self.data[:, piece] + self.from_z[0]
        else:
            self.total[:, piece] = self.sums[...] + self.from_z[1]

    def unfold(self, axis):
        lane = 5 + ("core", "x", "y").index(axis)
        mine = self.total.at[:, self.part(self.kept[axis])]
        copy = remote(mine, mine, self.send_sem.at[lane], self.recv_sem.at[lane], self.near[axis])
        copy.start()
        copy.wait_send()
        landed(self.total.at[:, self.part(self.away[axis])], self.recv_sem.at[lane])

    def scratch(rows, width):
        low = jnp.float32
        return [
            pltpu.VMEM((rows, width // 2), low),
            pltpu.VMEM((rows, width // 4), low),
            pltpu.VMEM((rows, width // 8), low),
            pltpu.VMEM((2, rows, width // 8), low),
            pltpu.VMEM((rows, width // 8), low),
            pltpu.SemaphoreType.DMA((8,)),
            pltpu.SemaphoreType.DMA((8,)),
        ]


def greet_far(line):
    y, x, core, z = place()
    barrier = pltpu.get_barrier_semaphore()
    for near in ((y, x, 1 - core, z), (y, 1 - x, core, z), (1 - y, x, core, z)):
        pl.semaphore_signal(barrier, inc=1, device_id=peer(*near), device_id_type=MESH)
    for step in range(1, line):
        pl.semaphore_signal(barrier, inc=1, device_id=peer(y, x, core, (z + step) % line), device_id_type=MESH)
    pl.semaphore_wait(barrier, 3 + line - 1)


def back_gather_kernel(line, own_ref, sums_ref, out_ref, total_ref, data, local_sem, send_sem, recv_sem, *fly):
    greet_far(line)
    gather = LineGather(own_ref, out_ref, send_sem, recv_sem, line)
    local = pltpu.make_async_copy(own_ref, gather.view(gather.spot[3]), local_sem)
    gather.begin()
    local.start()
    data[...] = sums_ref[...]
    butterfly = Butterfly(data, total_ref, *fly)
    for axis in ("core", "x", "y"):
        butterfly.fold(axis)
    gather.advance(0)
    butterfly.line_step(0)
    gather.advance(1)
    butterfly.line_step(1)
    for axis in ("y", "x", "core"):
        butterfly.unfold(axis)
    gather.advance(2)
    gather.finish()
    local.wait()


def back_gather(own, sums, collective_id):
    line = 4
    any_ref = pl.BlockSpec(memory_space=pl.ANY)
    vmem = pl.BlockSpec(memory_space=pltpu.VMEM)
    dma = pltpu.SemaphoreType.DMA
    return pl.pallas_call(
        functools.partial(back_gather_kernel, line),
        out_shape=(
            jax.ShapeDtypeStruct((line * own.shape[0], own.shape[1]), own.dtype),
            jax.ShapeDtypeStruct(sums.shape, jnp.float32),
        ),
        in_specs=[any_ref, vmem],
        out_specs=[any_ref, vmem],
        scratch_shapes=[
            pltpu.VMEM(sums.shape, jnp.float32), dma(()), dma((2, line)), dma((2, line)),
            *Butterfly.scratch(*sums.shape),
        ],
        compiler_params=pltpu.CompilerParams(collective_id=collective_id, has_side_effects=True),
        cost_estimate=pl.CostEstimate(flops=0, bytes_accessed=150 << 20, transcendentals=0),
        name="back_gather",
    )(own, sums)


def last_kernel(line, joined_ref, weight_ref, hidden_ref, mixed_ref, attn_ref, residual_ref, gain_ref, x_grad_ref, gains_ref,
                input_ref, wq_ref, wk_ref, wv_ref, wo_ref, total_ref,
                part, up, down, stage, near, far_x, far_y, from_x, from_y, data,
                line_send, line_recv, stage_sem, near_sem, send_sem, recv_sem, *fly):
    y, x, core, z = place()
    rows, width = input_ref.shape
    columns = joined_ref.shape[1]
    half = rows // 2
    low = jnp.bfloat16
    greet_far(line)
    reduce = LineReduce(part, up, down, line_send, line_recv, line)

    def term(i, carry):
        goal = reduce.order(i)
        first = pl.multiple_of(goal * rows, rows)
        for column in range(0, width, 512):
            piece = slice(column, column + 512)
            value = across(joined_ref[pl.ds(first, rows), :], weight_ref[piece, :])

            @pl.when(goal == z)
            def _():
                input_ref[:, piece] = value

            part[goal, :, piece] = value.astype(low)
        reduce.lead(goal)
        return carry

    lax.fori_loop(0, line, term, 0)
    near_x, near_y, sibling = (y, 1 - x, core, z), (1 - y, x, core, z), (y, x, 1 - core, z)

    def terms(j, own, store):
        dy, dx = (j + 1) % 2, 1 - j // 2
        group = (y + dy) % 2 * 4 + (x + dx) % 2 * 2 + (core if own else 1 - core)
        span = pl.ds(pl.multiple_of(group * rows, rows), rows)
        turned_rows = hidden_ref[:, span]
        for column in range(0, columns, 512):
            piece = slice(column, column + 512)
            store(piece, turned(turned_rows, joined_ref[:, piece]))
        value = turned(mixed_ref[...], attn_ref[:, span])
        store(slice(columns, columns + rows), value[:rows])
        store(slice(columns + rows, columns + 2 * rows), value[rows:])

    def to_sibling(j):
        return remote(stage.at[j], near.at[j], stage_sem.at[j], near_sem.at[j], sibling)

    def away(j, carry):
        def store(piece, value):
            stage[j, :, piece] = value.astype(low)

        terms(j, False, store)
        to_sibling(j).start()
        return carry

    def own(j, carry):
        to_sibling(j).wait_recv()

        def store(piece, value):
            near[j, :, piece] = (value + near[j, :, piece].astype(jnp.float32)).astype(low)

        terms(j, True, store)
        return carry

    lax.fori_loop(0, 4, away, 0)
    lax.fori_loop(0, 4, own, 0)

    def line_rows(h):
        return pl.ds(h * half, half)

    def cross(kind):
        column, h, target, where = {
            "far_x": (0, 0, far_x, near_x),
            "far_y": (0, 1, far_y, near_y),
            "x0": (1, 0, from_x.at[line_rows(0)], near_x),
            "x1": (1, 1, from_x.at[line_rows(1)], near_x),
            "y0": (2, 0, from_y.at[line_rows(0)], near_y),
            "y1": (2, 1, from_y.at[line_rows(1)], near_y),
        }[kind]
        lane = kinds.index(kind)
        return remote(near.at[column, line_rows(h)], target, send_sem.at[lane], recv_sem.at[lane], where)

    kinds = ("far_x", "far_y", "x0", "y1", "x1", "y0")
    for kind in kinds[:4]:
        cross(kind).start()

    def add(column, h, source):
        near[column, line_rows(h), :] = (
            near[column, line_rows(h), :].astype(jnp.float32) + source[...].astype(jnp.float32)
        ).astype(low)

    reduce.advance(1, input_ref)
    cross("far_y").wait_recv()
    add(1, 1, far_y)
    cross("x1").start()
    cross("far_x").wait_recv()
    add(2, 0, far_x)
    cross("y0").start()
    reduce.advance(2, input_ref)
    for kind in kinds[2:]:
        cross(kind).wait_recv()
    for n, ref in enumerate((wq_ref, wk_ref, wv_ref, wo_ref, wo_ref)):
        count = columns // 3 if n < 3 else rows
        first = n * (columns // 3) if n < 3 else columns + (n - 3) * rows
        piece = slice(first, first + count)
        total = sum(r[:, piece].astype(jnp.float32) for r in (near.at[3], from_x, from_y))
        if n < 3:
            ref[...] = total
        else:
            ref[(n - 3) * rows : (n - 2) * rows, :] = total
    reduce.advance(3, input_ref)
    grad = input_ref[...]
    values = residual_ref[...].astype(jnp.float32)
    scale = lax.rsqrt(jnp.mean(values * values, axis=-1, keepdims=True) + norm_eps)
    gained = grad * gain_ref[...]
    inner = jnp.sum(gained * values, axis=-1, keepdims=True)
    data[...] = gains_ref[...]
    data[2:3, :] = jnp.sum(grad * values * scale, axis=0, keepdims=True)
    input_ref[...] = x_grad_ref[...] + scale * gained - values * (scale * scale * scale * inner / width)
    butterfly = Butterfly(data, total_ref, *fly)
    for axis in ("core", "x", "y"):
        butterfly.fold(axis)
    butterfly.line_step(0)
    butterfly.line_step(1)
    for axis in ("y", "x", "core"):
        butterfly.unfold(axis)
    reduce.finish()
    for j in range(4):
        to_sibling(j).wait_send()
    for kind in kinds:
        cross(kind).wait_send()


def last_exchange(joined, weight, hidden, mixed, attn, residual, gain, x_grad, gains, collective_id):
    line = 4
    rows, width = residual.shape
    columns = joined.shape[1] // 3
    low, wide = jnp.bfloat16, jnp.float32
    vmem = pl.BlockSpec(memory_space=pltpu.VMEM)
    dma = pltpu.SemaphoreType.DMA
    block = pltpu.VMEM((line, rows, width), low)
    one = pltpu.VMEM((rows, width), low)
    part = pltpu.VMEM((rows // 2, width), low)
    square = jax.ShapeDtypeStruct((rows, columns), wide)
    return pl.pallas_call(
        functools.partial(last_kernel, line),
        out_shape=(
            jax.ShapeDtypeStruct((rows, width), wide), square, square, square,
            jax.ShapeDtypeStruct((2 * rows, rows), wide),
            jax.ShapeDtypeStruct(gains.shape, wide),
        ),
        in_specs=[vmem] * 9,
        out_specs=[vmem] * 6,
        scratch_shapes=[
            block, block, block, pltpu.VMEM((4, rows, width), low), pltpu.VMEM((4, rows, width), low),
            part, part, one, one, pltpu.VMEM(gains.shape, wide),
            dma((2, line)), dma((2, line)), dma((4,)), dma((4,)), dma((6,)), dma((6,)),
            *Butterfly.scratch(*gains.shape),
        ],
        compiler_params=pltpu.CompilerParams(
            collective_id=collective_id, has_side_effects=True, vmem_limit_bytes=62 << 20
        ),
        cost_estimate=pl.CostEstimate(flops=0, bytes_accessed=250 << 20, transcendentals=0),
        name="last_exchange",
    )(joined, weight, hidden, mixed, attn, residual, gain.reshape(1, width), x_grad, gains)


def visible_block(row_paths, key_paths, key_valid, row_first):
    row_count = row_paths.shape[1]
    key_count = key_paths.shape[1]
    key_segment = key_paths[0][None, :]
    on_path = (
        (key_segment == row_paths[0][:, None])
        | (key_segment == row_paths[1][:, None])
        | (key_segment == row_paths[2][:, None])
    )
    row_place = row_first + lax.iota(jnp.int32, row_count)
    key_place = lax.iota(jnp.int32, key_count)
    earlier = key_place[None, :] <= row_place[:, None]
    return on_path & earlier & (key_valid[None, :] == 1) | (
        key_place[None, :] == row_place[:, None]
    )


def rotation(positions, head_dim):
    half = head_dim // 2
    freqs = jnp.exp(-jnp.log(rope_base) * 2.0 * lax.iota(jnp.float32, half) / head_dim)
    angles = positions.astype(jnp.float32)[:, None] * freqs[None, :]
    return (jnp.cos(angles), jnp.sin(angles))


def visible_bias(row_first, row_paths, row_places, key_segment, key_valid, key_places):
    on_path = (key_segment == row_paths[0]) | (key_segment == row_paths[1]) | (key_segment == row_paths[2])
    seen = (on_path & (key_places <= row_places) & (key_valid == 1)) | (key_places == row_places)
    return jnp.where(seen, 0.0, masked_score)


def attend_kernel(step, raw_ref, scale_ref, gain_ref, cos_ref, sin_ref, column_ref, line_ref,
                  query_ref, key_ref, value_ref, mixed_ref, log_ref, bias, logs):
    seq, columns = query_ref.shape
    heads = columns // HD

    def prepare(i, carry):
        rows = pl.ds(pl.multiple_of(i * step, step), step)
        cosine, sine = cos_ref[rows, :], sin_ref[rows, :]
        for n, ref in enumerate((query_ref, key_ref)):
            scale = scale_ref[rows, n : n + 1]
            for h in range(heads):
                span = slice(h * HD, (h + 1) * HD)
                values = raw_ref[rows, n * columns + h * HD : n * columns + (h + 1) * HD]
                values = values * scale * gain_ref[n : n + 1, span]
                turn = pltpu.roll(values, HD // 2, 1)
                ref[rows, span] = (values * cosine + turn * sine).astype(jnp.bfloat16)
        value_ref[rows, :] = raw_ref[rows, 2 * columns :].astype(jnp.bfloat16)
        return carry

    lax.fori_loop(0, seq // step, prepare, 0)
    for i in range(seq // step):
        rows = slice(i * step, (i + 1) * step)
        wide = (i + 1) * step
        places = lax.broadcasted_iota(jnp.int32, (step, wide), 0) + i * step
        bias[:, :wide] = visible_bias(
            i * step,
            [column_ref[rows, n : n + 1] for n in range(3)],
            places,
            line_ref[0:1, :wide],
            line_ref[3:4, :wide],
            lax.broadcasted_iota(jnp.int32, (step, wide), 1),
        )

        def head(h, carry):
            span = pl.ds(pl.multiple_of(h * HD, HD), HD)
            scores = across(query_ref[rows, span], key_ref[:wide, span]) * HD ** (-0.5) + bias[:, :wide]
            top = jnp.max(scores, axis=1, keepdims=True)
            weights = jnp.exp(scores - top)
            total = jnp.sum(weights, axis=1, keepdims=True)
            low = (weights / total).astype(jnp.bfloat16)
            mixed = jnp.dot(low, value_ref[:wide, span], preferred_element_type=jnp.float32)
            mixed_ref[rows, span] = mixed.astype(jnp.bfloat16)
            lanes = lax.broadcasted_iota(jnp.int32, (step, 128), 1)
            logs[...] = jnp.where(lanes == h, top + jnp.log(total), logs[...])
            return carry

        logs[...] = jnp.zeros_like(logs)
        lax.fori_loop(0, heads, head, 0)
        log_ref[:, rows] = jnp.transpose(logs[...])[: log_ref.shape[0]]


def attend(raw, scales, gains, cosine, sine, path_columns, path_lines):
    seq = raw.shape[0]
    columns = raw.shape[1] // 3
    step = min(256, seq)
    vmem = pl.BlockSpec(memory_space=pltpu.VMEM)
    low = jax.ShapeDtypeStruct((seq, columns), jnp.bfloat16)
    return pl.pallas_call(
        functools.partial(attend_kernel, step),
        out_shape=(low, low, low, low, jax.ShapeDtypeStruct((8, seq), jnp.float32)),
        in_specs=[vmem] * 7,
        out_specs=[vmem] * 5,
        scratch_shapes=[pltpu.VMEM((step, seq), jnp.float32), pltpu.VMEM((step, 128), jnp.float32)],
        compiler_params=pltpu.CompilerParams(vmem_limit_bytes=50 << 20),
        cost_estimate=pl.CostEstimate(
            flops=4 * seq * seq * columns, bytes_accessed=16 * seq * columns, transcendentals=seq * seq
        ),
        name="attend",
    )(raw, scales, gains, cosine, sine, path_columns, path_lines)


def attend_back_kernel(step, grad_ref, w_ref, query_ref, key_ref, value_ref, log_ref, cos_ref, sin_ref,
                       column_ref, line_ref, dq_ref, dk_ref, dv_ref, bias, mixed):
    seq, columns = query_ref.shape
    heads = columns // HD
    dk_ref[...] = jnp.zeros_like(dk_ref)
    dv_ref[...] = jnp.zeros_like(dv_ref)

    def unturn(values, rows):
        return values * cos_ref[rows, :] - pltpu.roll(values, HD // 2, 1) * sin_ref[rows, :]

    for i in range(seq // step):
        rows = slice(i * step, (i + 1) * step)
        wide = (i + 1) * step
        mixed[...] = across(grad_ref[rows, :], w_ref[...]).astype(jnp.bfloat16)
        places = lax.broadcasted_iota(jnp.int32, (wide, step), 1) + i * step
        bias[:wide, :] = visible_bias(
            i * step,
            [line_ref[n : n + 1, rows] for n in range(3)],
            places,
            column_ref[:wide, 0:1],
            column_ref[:wide, 3:4],
            lax.broadcasted_iota(jnp.int32, (wide, step), 0),
        )

        def head(h, carry):
            span = pl.ds(pl.multiple_of(h * HD, HD), HD)
            query, key, grad = query_ref[rows, span], key_ref[:wide, span], mixed[:, span]
            scores = across(key, query) * HD ** (-0.5) + bias[:wide, :]
            weights = jnp.exp(scores - log_ref[pl.ds(h, 1), rows])
            grad_weights = across(value_ref[:wide, span], grad)
            inner = jnp.sum(weights * grad_weights, axis=0, keepdims=True)
            grad_scores = (weights * (grad_weights - inner)).astype(jnp.bfloat16)
            dq_ref[rows, span] = unturn(turned(grad_scores, key) * HD ** (-0.5), rows)
            dk_ref[:wide, span] += jnp.dot(grad_scores, query, preferred_element_type=jnp.float32)
            dv_ref[:wide, span] += jnp.dot(
                weights.astype(jnp.bfloat16), grad, preferred_element_type=jnp.float32
            )
            return carry

        lax.fori_loop(0, heads, head, 0)
    for i in range(seq // step):
        rows = slice(i * step, (i + 1) * step)
        for h in range(heads):
            span = slice(h * HD, (h + 1) * HD)
            dk_ref[rows, span] = unturn(dk_ref[rows, span] * HD ** (-0.5), rows)


def attend_back(grads, w_out, query, key, value, logs, cosine, sine, path_columns, path_lines):
    seq, columns = query.shape
    step = min(256, seq)
    vmem = pl.BlockSpec(memory_space=pltpu.VMEM)
    wide = jax.ShapeDtypeStruct((seq, columns), jnp.float32)
    return pl.pallas_call(
        functools.partial(attend_back_kernel, step),
        out_shape=(wide, wide, wide),
        in_specs=[vmem] * 10,
        out_specs=[vmem] * 3,
        scratch_shapes=[pltpu.VMEM((seq, step), jnp.float32), pltpu.VMEM((step, columns), jnp.bfloat16)],
        compiler_params=pltpu.CompilerParams(vmem_limit_bytes=56 << 20),
        cost_estimate=pl.CostEstimate(
            flops=10 * seq * seq * columns, bytes_accessed=24 * seq * columns, transcendentals=seq * seq
        ),
        name="attend_back",
    )(grads, w_out, query, key, value, logs, cosine, sine, path_columns, path_lines)


def rms_apply(values, gain):
    scale = lax.rsqrt(jnp.mean(values * values, axis=-1, keepdims=True) + norm_eps)
    return (values * scale * gain, scale)


def rms_grad(values, scale, gain, grads, inner, width):
    grad_values = scale * gain * grads - values * scale**3 * inner / width
    grad_gain = jnp.sum(grads * values * scale, axis=0)
    return (grad_values, grad_gain)


def tensor_sums(pair):
    return lax.psum((pair[0], pair[1]), "tensor")


def heads_to_rows(term, rows):
    return lax.psum_scatter(
        term(jnp.int32(0), rows * lax.axis_size("tensor")).astype(jnp.bfloat16),
        "tensor",
        scatter_dimension=0,
        tiled=True,
    ).astype(jnp.float32)


def sum_over_dp(rows):
    dp = lax.axis_size("dp")
    pieces = rows.reshape(dp, rows.shape[0] // dp, rows.shape[1])
    return lax.psum_scatter(pieces, "dp", scatter_dimension=0, tiled=False)


def sum_over_tensor(part):
    return lax.psum_scatter(part, "tensor", scatter_dimension=0, tiled=True)


def body(
    residual,
    attn_gain,
    w_query,
    w_key,
    w_value,
    query_gain,
    key_gain,
    w_out,
    moe_gain,
    router,
    w_gate,
    w_up,
    w_down,
    segment_path,
    token_valid,
    routes,
    route_order,
    cotangent,
):
    tensor_rank = lax.axis_index("tensor")
    tok_dev, width = residual.shape
    seq_len = segment_path.shape[1]
    top_count = routes.shape[1]
    experts = router.shape[1]
    local_experts = w_gate.shape[0]
    dp_groups = experts // local_experts
    capacity = 9 * tok_dev * top_count // (8 * experts)
    full_width = H * HD
    everyone = ("dp", "tensor")
    direct = dp_groups == 8 and lax.axis_size("tensor") == 4
    first_expert = lax.axis_index("dp") * local_experts
    slot_rows = padded(capacity, 8)
    valid_dev = lax.dynamic_slice_in_dim(token_valid, tensor_rank * tok_dev, tok_dev)
    slots_own = slot_table(routes, route_order, valid_dev, experts, capacity)
    cots_all = lax.all_gather(cotangent, everyone, axis=0, tiled=True)
    head_cols = w_query.shape[1]
    residual_float = residual.astype(jnp.float32)
    normed_one, scale_one = rms_apply(residual_float, attn_gain)
    hidden = normed_one.astype(jnp.bfloat16)
    path_lines = jnp.concatenate((segment_path, token_valid[None]), axis=0)
    path_columns = path_lines.T
    positions = jnp.sum(visible_block(segment_path, segment_path, token_valid, 0).astype(jnp.int32), axis=1) - 1
    cosine, sine = rotation(positions, HD)
    cosine = jnp.concatenate((cosine, cosine), axis=1)
    sine = jnp.concatenate((-sine, sine), axis=1)
    if direct:
        hidden_all, joined_weight, gathered_out, slots = start_exchange(
            hidden, w_query, w_key, w_value, w_out, slots_own, 3
        )
        slots = jnp.swapaxes(slots.reshape(4, 8, local_experts, tok_dev), 0, 1).reshape(32, local_experts, tok_dev)
    else:
        hidden_all = lax.all_gather(hidden, "tensor", axis=0, tiled=True)
        joined_weight = jnp.concatenate(
            [lax.all_gather(w, "dp", axis=0, tiled=True) for w in (w_query, w_key, w_value)], axis=1
        )
        gathered_out = lax.all_gather(w_out, "dp", axis=1, tiled=True)
        slots_all = lax.all_gather(slots_own.astype(jnp.bfloat16), everyone, axis=0)
        slots = lax.dynamic_slice_in_dim(slots_all, first_expert, local_experts, 1).astype(jnp.int32)
    projected = jnp.dot(hidden_all, joined_weight, preferred_element_type=jnp.float32)
    blocks = slots.shape[0]
    q_raw = projected[:, :head_cols]
    k_raw = projected[:, head_cols : 2 * head_cols]
    query_sq, key_sq = tensor_sums((jnp.sum(q_raw * q_raw, axis=1), jnp.sum(k_raw * k_raw, axis=1)))
    query_scale = lax.rsqrt(query_sq / full_width + norm_eps)[:, None]
    key_scale = lax.rsqrt(key_sq / full_width + norm_eps)[:, None]
    query_gain_dev = lax.dynamic_slice_in_dim(query_gain, tensor_rank * head_cols, head_cols)
    key_gain_dev = lax.dynamic_slice_in_dim(key_gain, tensor_rank * head_cols, head_cols)
    query_low, key_low, value_low, attn_mixed, log_totals = attend(
        projected,
        jnp.concatenate((query_scale, key_scale), axis=1),
        jnp.stack((query_gain_dev, key_gain_dev)),
        cosine,
        sine,
        path_columns,
        path_lines,
    )
    if direct:
        x_one, hidden_two, gates_own = mixed_out(attn_mixed, gathered_out, residual, moe_gain, router.T, 4)
        probs = gates_own.T
    else:

        def attn_term(first_row, row_count):
            return jnp.dot(attn_mixed, gathered_out, preferred_element_type=jnp.float32)

        x_one = residual_float + heads_to_rows(attn_term, tok_dev)
        hidden_two = rms_apply(x_one, moe_gain)[0].astype(jnp.bfloat16)
        logits = jnp.dot(hidden_two, router, preferred_element_type=jnp.float32)
        probs = jax.nn.softmax(logits, axis=-1)
        gates_own = probs.T
    scale_two = lax.rsqrt(jnp.mean(x_one * x_one, axis=-1, keepdims=True) + norm_eps)
    if direct:
        x_slots, c_slots, gate_slots = gather_dispatch(slots, hidden_two, gates_own, cots_all, slot_rows, 1)
    else:
        gates_all = lax.all_gather(gates_own, everyone, axis=0)
        rows_all = lax.all_gather(hidden_two, everyone, axis=0, tiled=True)
        gates = lax.dynamic_slice_in_dim(gates_all, first_expert, local_experts, 1)
        x_slots, gate_slots = dispatch(slots, gates, rows_all, slot_rows)
        c_slots = dispatch(slots, None, cots_all, slot_rows)
    outs, grads, pre, gated = expert_pass(
        first_expert.reshape(1),
        x_slots,
        c_slots,
        gate_slots,
        w_gate,
        w_up,
        w_down,
        blocks,
        padded(slot_rows, 16),
    )
    if direct:
        grad_rows, out_part = reduce_all(slots, outs, grads, 2)
    else:
        out_part, grad_part = combine(slots, outs, grads)
        grad_rows = sum_over_tensor(sum_over_dp(grad_part)).astype(jnp.float32)
    out_part = sum_over_dp(out_part)
    grad_out = cotangent.astype(jnp.float32)
    grad_hidden_two = grad_rows[:, :width]
    grad_probs = grad_rows[:, width : width + experts]
    grad_logits = probs * (grad_probs - jnp.sum(probs * grad_probs, axis=-1, keepdims=True))
    router_float = router.astype(jnp.float32)
    grad_hidden_two = grad_hidden_two + lax.dot_general(
        grad_logits, router_float, (((1,), (1,)), ((), ())), precision=lax.Precision.HIGHEST
    )
    grad_router_part = lax.dot_general(
        grad_logits,
        hidden_two.astype(jnp.float32),
        (((0,), (0,)), ((), ())),
        precision=lax.Precision.HIGHEST,
    )
    inner_two = jnp.sum(grad_hidden_two * moe_gain * x_one, axis=-1, keepdims=True)
    grad_norm_two, grad_moe_gain_part = rms_grad(
        x_one, scale_two, moe_gain, grad_hidden_two, inner_two, width
    )
    grad_x_one = grad_out + grad_norm_two
    grad_attn_low = grad_x_one.astype(jnp.bfloat16)
    early_sums = jnp.concatenate(
        (grad_router_part, grad_moe_gain_part[None], jnp.zeros((7, width), jnp.float32)), axis=0
    )
    if direct:
        grad_attn_all, early_sums = back_gather(grad_attn_low, early_sums, 5)
    else:
        grad_attn_all = lax.all_gather(grad_attn_low, "tensor", axis=0, tiled=True)
        early_sums = lax.psum(early_sums, everyone)
    grad_q_norm, grad_k_norm, grad_value_all = attend_back(
        grad_attn_all,
        gathered_out,
        query_low,
        key_low,
        value_low,
        log_totals,
        cosine,
        sine,
        path_columns,
        path_lines,
    )
    query_inner, key_inner = tensor_sums(
        (
            jnp.sum(grad_q_norm * query_gain_dev * q_raw, axis=1),
            jnp.sum(grad_k_norm * key_gain_dev * k_raw, axis=1),
        )
    )
    grad_q_raw, grad_query_gain_dev = rms_grad(
        q_raw, query_scale, query_gain_dev, grad_q_norm, query_inner[:, None], full_width
    )
    grad_k_raw, grad_key_gain_dev = rms_grad(
        k_raw, key_scale, key_gain_dev, grad_k_norm, key_inner[:, None], full_width
    )
    grad_joined = jnp.concatenate(
        (grad_q_raw, grad_k_raw, grad_value_all), axis=1
    ).astype(jnp.bfloat16)
    zero_width = jnp.zeros((full_width,), jnp.float32)
    grad_query_full = lax.dynamic_update_slice_in_dim(
        zero_width, grad_query_gain_dev, tensor_rank * head_cols, 0
    )
    grad_key_full = lax.dynamic_update_slice_in_dim(
        zero_width, grad_key_gain_dev, tensor_rank * head_cols, 0
    )
    if direct:
        gains = jnp.concatenate(
            (grad_query_full[None], grad_key_full[None], jnp.zeros((6, width), jnp.float32)), axis=0
        )
        grad_input, grad_w_query, grad_w_key, grad_w_value, grad_w_out, gains = last_exchange(
            grad_joined,
            joined_weight,
            hidden_all,
            attn_mixed,
            grad_attn_all,
            residual,
            attn_gain,
            grad_x_one,
            gains,
            6,
        )
    else:
        grad_joined_weight = lax.dot_general(
            hidden_all, grad_joined, (((0,), (0,)), ((), ())), preferred_element_type=jnp.float32
        ).astype(jnp.bfloat16)
        grad_out_weight = lax.dot_general(
            attn_mixed, grad_attn_all, (((0,), (0,)), ((), ())), preferred_element_type=jnp.float32
        ).astype(jnp.bfloat16)

        def back_term(first_row, row_count):
            return lax.dot_general(
                grad_joined, joined_weight, (((1,), (1,)), ((), ())), preferred_element_type=jnp.float32
            )

        grad_hidden = heads_to_rows(back_term, tok_dev)
        inner_one = jnp.sum(grad_hidden * attn_gain * residual_float, axis=-1, keepdims=True)
        grad_norm_one, grad_attn_gain_part = rms_grad(
            residual_float, scale_one, attn_gain, grad_hidden, inner_one, width
        )
        grad_input = grad_x_one + grad_norm_one
        grad_w_query, grad_w_key, grad_w_value = (
            lax.psum_scatter(
                grad_joined_weight[:, n * head_cols : (n + 1) * head_cols],
                "dp",
                scatter_dimension=0,
                tiled=True,
            ).astype(jnp.float32)
            for n in range(3)
        )
        grad_w_out = lax.psum_scatter(
            grad_out_weight, "dp", scatter_dimension=1, tiled=True
        ).astype(jnp.float32)
        gains = lax.psum(jnp.stack((grad_query_full, grad_key_full, grad_attn_gain_part)), everyone)
    out_part, pre, grad_input = lax.optimization_barrier((out_part, pre, grad_input))
    grad_w_gate, grad_w_up, grad_w_down = weight_grads(x_slots, c_slots, pre, gated)
    moe_out, grad_w_gate, grad_w_up, grad_w_down = lax.optimization_barrier(
        (sum_over_tensor(out_part), grad_w_gate, grad_w_up, grad_w_down)
    )
    block_out = (x_one + moe_out.astype(jnp.float32)).astype(jnp.bfloat16)
    return (
        block_out,
        grad_input,
        gains[2],
        grad_w_query,
        grad_w_key,
        grad_w_value,
        gains[0],
        gains[1],
        grad_w_out,
        early_sums[experts],
        early_sums[:experts].T,
        grad_w_gate,
        grad_w_up,
        grad_w_down,
    )


def solution(mesh):
    in_specs = (
        P(("dp", "tensor"), None),
        P(),
        P("dp", "tensor"),
        P("dp", "tensor"),
        P("dp", "tensor"),
        P(),
        P(),
        P("tensor", "dp"),
        P(),
        P(),
        P("dp", None, "tensor"),
        P("dp", None, "tensor"),
        P("dp", "tensor", None),
        P(None, "dp"),
        P("dp"),
        P(("dp", "tensor"), None),
        P(("dp", "tensor"), None),
        P(("dp", "tensor"), None),
    )
    out_specs = (
        P(("dp", "tensor"), None),
        P(("dp", "tensor"), None),
        P(),
        P("dp", "tensor"),
        P("dp", "tensor"),
        P("dp", "tensor"),
        P(),
        P(),
        P("tensor", "dp"),
        P(),
        P(),
        P("dp", None, "tensor"),
        P("dp", None, "tensor"),
        P("dp", "tensor", None),
    )
    return jax.shard_map(body, mesh=mesh, in_specs=in_specs, out_specs=out_specs, check_vma=False)
```
